32 devices in a mesh: section: 2 (over core), dp: 16 (over z, y, x).
Axes of the slice: x: 2, y: 2, z: 4, core: 2. Of those that a mesh axis runs over, the one named last changes fastest.
Arguments:
- pixels: bfloat16 [32, 196, 768], P('dp'), may hold values from -6 to 6
- ctx_idx: int32 [32, 128], P('dp'), may hold values from 0 to 195, as said below
- ctx_len: int32 [32], P('dp'), may hold values from 64 to 128
- tgt_idx: int32 [32, 4, 36], P('dp'), may hold values from 0 to 195, as said below
- tgt_len: int32 [32, 4], P('dp'), may hold values from 4 to 36, as said below
- slot_of: int32 [68], replicated, may hold values from 0 to 79, as said below
- weights: float32 [2, 80, 384, 384], P('section', 'dp')
- first_moment: float32 [2, 80, 384, 384], P('section', 'dp'), may hold values from -0.001953125 to 0.001953125
- second_moment: float32 [2, 80, 384, 384], P('section', 'dp'), may hold values from 4.9773828e-08 to 7.9638124e-07
- left_basis: float32 [2, 80, 384, 384], P('section', 'dp'), as said below
- right_basis: float32 [2, 80, 384, 384], P('section', 'dp'), as said below
- left_stats: float32 [2, 80, 384, 384], P('section', 'dp'), as said below
- right_stats: float32 [2, 80, 384, 384], P('section', 'dp'), as said below
- vectors: float32 [2, 18432], P('section')
- vector_first: float32 [2, 18432], P('section'), may hold values from -0.005859375 to 0.005859375
- vector_second: float32 [2, 18432], P('section'), may hold values from 9.9547655e-08 to 6.37105e-06
Outputs:
- loss_sum: float32 [], replicated
- loss_count: float32 [], replicated
- grad_norm: float32 [], replicated
- new_weights: float32 [2, 80, 384, 384], P('section', 'dp')
- new_first: float32 [2, 80, 384, 384], P('section', 'dp')
- new_second: float32 [2, 80, 384, 384], P('section', 'dp')
- new_left: float32 [2, 80, 384, 384], P('section', 'dp')
- new_right: float32 [2, 80, 384, 384], P('section', 'dp')
- new_left_stats: float32 [2, 80, 384, 384], P('section', 'dp')
- new_right_stats: float32 [2, 80, 384, 384], P('section', 'dp')
- new_vectors: float32 [2, 18432], P('section')
- new_vector_first: float32 [2, 18432], P('section')
- new_vector_second: float32 [2, 18432], P('section')
The draws below stay inside these ranges and needn't reach their ends.
Inputs may be any that keep to these rules, and one draw needn't show every extreme that they name: `ctx_idx`: each image's 128 context patch numbers are distinct; the first ctx_len of them count. `tgt_idx`: each target block is a rectangle of the 14 x 14 patch grid, listed row by row; entries past its length are 0. `tgt_len`: A block's height times its width, with heights 2 to 6 and widths 2 to 6. `slot_of`: distinct slot numbers. `left_basis`: each block is orthogonal. `right_basis`: each block is orthogonal. `left_stats`: each block is symmetric positive definite. `right_stats`: each block is symmetric positive definite.
All inputs are finite; a program needn't handle non-finite values.
Results may differ from the reference program's by a relative error of at most 0.00065.
The reference program's roundings to bfloat16 on the way count: a program that leaves them out, or rounds other values in their place, can miss the bound.
Values may be sent and summed in bfloat16 or wider, within the bound.
No kernel may reach another device: no remote copies, remote signals or barrier semaphores. Data moves between devices by JAX's collectives and lax.ppermute only.
A program may use at most 384 MiB of HBM per device.

```python
import math
import jax
import jax.numpy as jnp
from jax import lax

D = 768
FF = 3072
H = 12
PD = 384
PFF = 1536
PH = 12
PIX = 768
GRID = 14
B = 384
NT = 4
RH = 6
RW = 6
LC = 128
STEP = 10
P_SIZE = 196
LT = 36
IMAGES = 32
NBE = 52
NBP = 16
SLOT_ROWS = 80
VE = 11520
VP = 6912
VW = 18432
NPARAM = 10045440


def block_scales():
    layout = [(PIX, D, PIX), (D, 3 * D, D), (D, D, D / LC), (D, FF, D), (FF, D, FF), (D, PD, D), (PD, 3 * PD, PD), (PD, PD, PD / (LC + NT * LT)), (PD, PFF, PD), (PFF, PD, PFF), (PD, D, PD)]
    pieces = []
    for height, breadth, fan_in in layout:
        pieces.append(jnp.full((height * breadth // (B * B),), fan_in ** (-0.5), jnp.float32))
    return jnp.concatenate(pieces)


def slot_list(key):
    count_all = NBE + NBP
    middle = 1 + jax.random.permutation(jax.random.fold_in(key, 7), SLOT_ROWS - 2)[:count_all - 2]
    ends = jnp.array([0, SLOT_ROWS - 1], jnp.int32)
    full_list = jnp.concatenate([ends, middle.astype(jnp.int32)])
    return jax.random.permutation(jax.random.fold_in(key, 8), full_list).astype(jnp.int32)


def draw_slot_of(key, part):
    return slot_list(key)


def draw_weights(key, part):
    chosen = slot_list(key)
    scales = block_scales()
    filler = jnp.full((SLOT_ROWS,), 0.05, jnp.float32)
    first_row = filler.at[chosen[:NBE]].set(scales[:NBE])
    second_row = filler.at[chosen[NBE:]].set(scales[NBE:]).at[chosen[:NBE]].set(scales[:NBE])
    noise = jax.random.normal(jax.random.fold_in(key, 21), (2, SLOT_ROWS, B, B), jnp.float32)
    return noise * jnp.stack([first_row, second_row])[:, :, None, None]


def orthogonal_tables(key, salt):
    frequency = jnp.arange(B, dtype=jnp.float32)[:, None]
    sample_pos = jnp.arange(B, dtype=jnp.float32)[None, :]
    cosine = jnp.cos(math.pi * (sample_pos + 0.5) * frequency / B) * math.sqrt(2.0 / B)
    cosine = jnp.where(frequency == 0, math.sqrt(1.0 / B), cosine)
    columns = cosine.T
    subkeys = jax.random.split(jax.random.fold_in(key, salt), 2 * SLOT_ROWS)

    def single(subkey):
        order = jax.random.permutation(subkey, B)
        signs = jnp.where(jax.random.bernoulli(jax.random.fold_in(subkey, 3), 0.5, (B,)), 1.0, -1.0)
        return jnp.take(columns, order, 1) * signs[None, :]
    return jax.vmap(single)(subkeys).reshape(2, SLOT_ROWS, B, B)


def draw_left_basis(key, part):
    return orthogonal_tables(key, 51)


def draw_right_basis(key, part):
    return orthogonal_tables(key, 52)


def stat_tables(key, salt):
    stat_scale = B / NPARAM
    key_diag, key_off = jax.random.split(jax.random.fold_in(key, salt))
    diagonal = stat_scale * jnp.exp(jax.random.uniform(key_diag, (2, SLOT_ROWS, B), jnp.float32, 0.0, math.log(4.0)))
    uniform_part = jax.random.uniform(key_off, (2, SLOT_ROWS, B, B), jnp.float32, -1.0, 1.0) * (0.8 * stat_scale / B)
    mirror = 0.5 * (uniform_part + jnp.swapaxes(uniform_part, -1, -2))
    identity = jnp.eye(B, dtype=jnp.float32)
    return mirror * (1.0 - identity) + diagonal[..., None] * identity


def draw_left_stats(key, part):
    return stat_tables(key, 53)


def draw_right_stats(key, part):
    return stat_tables(key, 54)


def vector_kinds():
    enc_flags = [0, 1, 0, 0, 0, 0, 1, 0, 0, 0, 1, 0]
    enc_sizes = [D] * 8 + [FF, D, D, D]
    pred_flags = [0, 1, 0, 0, 0, 0, 1, 0, 0, 0, 1, 0, 0, 0]
    pred_sizes = [PD] * 8 + [PFF, PD, PD, PD, D, PD]

    def build_row(flag_list, size_list):
        return jnp.concatenate([jnp.full((length,), flag_value, jnp.int32) for flag_value, length in zip(flag_list, size_list)])
    enc_part = build_row(enc_flags, enc_sizes)
    pred_part = build_row(pred_flags, pred_sizes)
    first_row = jnp.concatenate([enc_part, jnp.zeros((VP,), jnp.int32)])
    second_row = jnp.concatenate([pred_part, enc_part])
    return jnp.stack([first_row, second_row])


def draw_vectors(key, part):
    kinds = vector_kinds()
    key_gain, key_bias = jax.random.split(jax.random.fold_in(key, 61))
    gains = jax.random.uniform(key_gain, (2, VW), jnp.float32, 0.5, 1.5)
    biases = 0.2 * jax.random.normal(key_bias, (2, VW), jnp.float32)
    return jnp.where(kinds == 1, gains, biases)


def context_parts(key):
    subkeys = jax.random.split(jax.random.fold_in(key, 31), IMAGES)
    chosen = jax.vmap(lambda subkey: jax.random.permutation(subkey, P_SIZE)[:LC])(subkeys)
    counts = jax.random.randint(jax.random.fold_in(key, 32), (IMAGES,), LC // 2, LC + 1)
    return (chosen.astype(jnp.int32), counts.at[0].set(LC).astype(jnp.int32))


def draw_ctx_idx(key, part):
    return context_parts(key)[0]


def draw_ctx_len(key, part):
    return context_parts(key)[1]


def target_parts(key):
    keys_all = jax.random.split(jax.random.fold_in(key, 41), 4)
    heights = jax.random.randint(keys_all[0], (IMAGES, NT), 2, RH + 1).at[0, 0].set(RH)
    widths = jax.random.randint(keys_all[1], (IMAGES, NT), 2, RW + 1).at[0, 0].set(RW)
    top_row = jax.random.randint(keys_all[2], (IMAGES, NT), 0, GRID - heights + 1)
    left_col = jax.random.randint(keys_all[3], (IMAGES, NT), 0, GRID - widths + 1)
    places = jnp.arange(LT)[None, None, :]
    patch_ids = (top_row[..., None] + places // widths[..., None]) * GRID + left_col[..., None] + places % widths[..., None]
    counts = heights * widths
    return (jnp.where(places < counts[..., None], patch_ids, 0).astype(jnp.int32), counts.astype(jnp.int32))


def draw_tgt_idx(key, part):
    return target_parts(key)[0]


def draw_tgt_len(key, part):
    return target_parts(key)[1]


def steps_of(key, extent, cuts, least, largest):
    gain, own = 1.0, jax.random.fold_in(key, 6)
    for dim, parts in cuts:
        steps = jnp.exp(jax.random.uniform(jax.random.fold_in(own, dim), (parts,), jnp.float32, least / len(cuts), largest / len(cuts)))
        gain = gain * jnp.repeat(steps, extent[dim] // parts).reshape([-1 if axis == dim else 1 for axis in range(len(extent))])
    return gain


def normal_values(stream_key, shape, scale, bound, cuts=(), kind=jnp.bfloat16):
    values = scale * jax.random.normal(stream_key, shape, jnp.float32)
    if cuts:
        values = values * steps_of(stream_key, shape, cuts, -0.22, 0.18)
    return jnp.clip(values, -bound, bound).astype(kind)


def setup_inputs(seed: int = 0) -> dict:
    splits = jax.random.split(jax.random.key(seed), 17)
    return {
        "pixels": normal_values(splits[0], (IMAGES, P_SIZE, PIX), 1.0, 6.0, ((0, 16),)),
        "ctx_idx": draw_ctx_idx(jax.random.fold_in(splits[16], 71), 0),
        "ctx_len": draw_ctx_len(jax.random.fold_in(splits[16], 71), 0),
        "tgt_idx": draw_tgt_idx(jax.random.fold_in(splits[16], 71), 0),
        "tgt_len": draw_tgt_len(jax.random.fold_in(splits[16], 71), 0),
        "slot_of": draw_slot_of(jax.random.fold_in(splits[16], 71), 0),
        "weights": draw_weights(jax.random.fold_in(splits[16], 71), 0),
        "first_moment": normal_values(splits[7], (2, SLOT_ROWS, B, B), (NPARAM ** -0.5), 0.001953125, ((0, 2), (1, 16)), jnp.float32),
        "second_moment": jnp.clip(jnp.exp(math.log(7.963812436173612e-07) - 2.7725887 * jax.random.uniform(splits[8], (2, SLOT_ROWS, B, B), jnp.float32) ** steps_of(splits[8], (2, SLOT_ROWS, B, B), ((0, 2), (1, 16)), -0.2, 0.2)), 4.9773827726085074e-08, 7.963812436173612e-07),
        "left_basis": draw_left_basis(jax.random.fold_in(splits[16], 71), 0),
        "right_basis": draw_right_basis(jax.random.fold_in(splits[16], 71), 0),
        "left_stats": draw_left_stats(jax.random.fold_in(splits[16], 71), 0),
        "right_stats": draw_right_stats(jax.random.fold_in(splits[16], 71), 0),
        "vectors": draw_vectors(jax.random.fold_in(splits[16], 71), 0),
        "vector_first": normal_values(splits[14], (2, VW), (3 * NPARAM ** -0.5), 0.005859375, ((0, 2),), jnp.float32),
        "vector_second": jnp.clip(jnp.exp(math.log(6.3710499489388894e-06) - 4.158883 * jax.random.uniform(splits[15], (2, VW), jnp.float32) ** steps_of(splits[15], (2, VW), ((0, 2),), -0.2, 0.2)), 9.954765545217015e-08, 6.3710499489388894e-06),
    }


TOP_PRECISION = lax.Precision.HIGHEST
NORM_EPS = 1e-06
ADAM_EPS = 1e-08
BETA_FIRST = 0.5
BETA_SECOND = 0.5
BETA_STATS = 0.95
RATE_MATRIX = 0.02
RATE_VECTOR = 0.05
DECAY_MATRIX = 0.04
EMA_KEEP = 0.996
CLIP_LIMIT = 1.0
NEG_FILL = -1000000000.0

@jax.custom_vjp
def low(v):
    return lax.optimization_barrier(v.astype(jnp.bfloat16)).astype(jnp.float32)

@jax.custom_vjp
def low_back(v):
    return v

def low_keep(v):
    return (low(v), None)

def low_pass(kept, grad):
    return (grad,)

def back_keep(v):
    return (v, None)

def back_low(kept, grad):
    return (low(grad),)
low.defvjp(low_keep, low_pass)
low_back.defvjp(back_keep, back_low)

def enc_shapes():
    return [(PIX, D), (D, 3 * D), (D, D), (D, FF), (FF, D)]

def pred_shapes():
    return [(D, PD), (PD, 3 * PD), (PD, PD), (PD, PFF), (PFF, PD), (PD, D)]

def enc_lengths():
    return [D] * 8 + [FF, D, D, D]

def pred_lengths():
    return [PD] * 8 + [PFF, PD, PD, PD, D, PD]

def assemble(blocks, height, breadth):
    block_edge = blocks.shape[-1]
    tiled = blocks.reshape(height // block_edge, breadth // block_edge, block_edge, block_edge)
    return tiled.transpose(0, 2, 1, 3).reshape(height, breadth)

def split_blocks(matrix, block_edge):
    height, breadth = matrix.shape
    tiled = matrix.reshape(height // block_edge, block_edge, breadth // block_edge, block_edge)
    return tiled.transpose(0, 2, 1, 3).reshape(-1, block_edge, block_edge)

def unpack_mats(blocks, shapes):
    block_edge = blocks.shape[-1]
    result = []
    offset = 0
    for height, breadth in shapes:
        amount = height * breadth // (block_edge * block_edge)
        result.append(assemble(blocks[offset:offset + amount], height, breadth))
        offset += amount
    return result

def pack_mats(matrices, block_edge):
    return jnp.concatenate([split_blocks(matrix, block_edge) for matrix in matrices], 0)

def unpack_vec(vector, lengths):
    result = []
    offset = 0
    for length in lengths:
        result.append(vector[offset:offset + length])
        offset += length
    return result

def sincos(width):
    quarter = width // 4
    frequency = 1.0 / 10000.0 ** (jnp.arange(quarter, dtype=jnp.float32) / quarter)
    cell_ids = jnp.arange(P_SIZE)
    row_pos = (cell_ids // GRID).astype(jnp.float32)[:, None] * frequency
    column_pos = (cell_ids % GRID).astype(jnp.float32)[:, None] * frequency
    return jnp.concatenate([jnp.sin(row_pos), jnp.cos(row_pos), jnp.sin(column_pos), jnp.cos(column_pos)], 1)

def layer_norm(inputs, gain_vec, shift_vec):
    center = inputs - lax.optimization_barrier(jnp.mean(inputs, -1, keepdims=True))
    spread = lax.optimization_barrier(jnp.mean(center * center, -1, keepdims=True))
    return center * lax.rsqrt(spread + NORM_EPS) * gain_vec + shift_vec

def plain_norm(inputs):
    center = inputs - lax.optimization_barrier(jnp.mean(inputs, -1, keepdims=True))
    spread = lax.optimization_barrier(jnp.mean(center * center, -1, keepdims=True))
    return center * lax.rsqrt(spread + NORM_EPS)

def linear(inputs, weight, bias):
    return low_back(jnp.einsum('...k,km->...m', low(inputs), low(weight), precision=TOP_PRECISION)) + bias

def attend(qkv, valid, heads):
    batch_size, length, triple = qkv.shape
    model_width = triple // 3
    head_dim = model_width // heads
    split_shape = (batch_size, length, heads, head_dim)
    queries = low(qkv[..., :model_width] * (1.0 / math.sqrt(head_dim))).reshape(split_shape)
    keys_low = low(qkv[..., model_width:2 * model_width]).reshape(split_shape)
    values_low = low(qkv[..., 2 * model_width:]).reshape(split_shape)
    scores = low_back(jnp.einsum('nqhd,nkhd->nhqk', queries, keys_low, precision=TOP_PRECISION))
    scores = jnp.where(valid[:, None, None, :], scores, NEG_FILL)
    softmax_out = jax.nn.softmax(scores, axis=-1)
    attended = jnp.einsum('nhqk,nkhd->nqhd', low(softmax_out), values_low, precision=TOP_PRECISION)
    return low_back(attended).reshape(batch_size, length, model_width)

def layer(inputs, valid, matrices, vector_list, heads):
    weight_proj, weight_out, weight_up, weight_down = matrices
    gain_one, shift_one, bias_query, bias_value, bias_output, gain_two, shift_two, bias_up, bias_down = vector_list
    bias_all = jnp.concatenate([bias_query, jnp.zeros_like(bias_query), bias_value])
    qkv = linear(layer_norm(inputs, gain_one, shift_one), weight_proj, bias_all)
    middle = inputs + linear(attend(qkv, valid, heads), weight_out, bias_output)
    pre_act = linear(layer_norm(middle, gain_two, shift_two), weight_up, bias_up)
    return middle + linear(jax.nn.gelu(pre_act, approximate=False), weight_down, bias_down)

def encode(pixel_rows, position, valid, matrices, vector_list):
    embedded = linear(pixel_rows, matrices[0], vector_list[0]) + position
    hidden = layer(embedded, valid, matrices[1:], vector_list[1:10], H)
    return layer_norm(hidden, vector_list[10], vector_list[11])

def predict(context, ctx_pos, tgt_pos, valid, matrices, vector_list):
    entry = linear(low_back(context), matrices[0], vector_list[0]) + ctx_pos
    joined = jnp.concatenate([entry, vector_list[13] + tgt_pos], 1)
    hidden = layer(joined, valid, matrices[1:5], vector_list[1:10], PH)
    return linear(layer_norm(hidden[:, LC:], vector_list[10], vector_list[11]), matrices[5], vector_list[12])

def huber_sum(difference, target_mask):
    magnitude = jnp.abs(difference)
    return jnp.sum(jnp.where(magnitude < 1.0, 0.5 * difference * difference, magnitude - 0.5) * target_mask)

def mul(left_op, right_op):
    return jnp.dot(left_op, right_op, precision=TOP_PRECISION)

def orthonormal(matrix):
    factor = jnp.linalg.cholesky(mul(matrix.T, matrix))
    return jax.scipy.linalg.solve_triangular(factor, matrix.T, lower=True).T

def soap_update(weight, gradient, moment, second, left_op, right_op, left_stat, right_stat):
    correct_one = 1.0 - BETA_FIRST ** STEP
    correct_two = 1.0 - BETA_SECOND ** STEP
    rotated = mul(mul(left_op.T, gradient), right_op)
    moment_new = BETA_FIRST * moment + (1.0 - BETA_FIRST) * rotated
    second_new = BETA_SECOND * second + (1.0 - BETA_SECOND) * rotated * rotated
    normed = moment_new / correct_one / (jnp.sqrt(second_new / correct_two) + ADAM_EPS)
    weight_new = weight - RATE_MATRIX * (mul(mul(left_op, normed), right_op.T) + DECAY_MATRIX * weight)
    left_stat_new = BETA_STATS * left_stat + (1.0 - BETA_STATS) * mul(gradient, gradient.T)
    right_stat_new = BETA_STATS * right_stat + (1.0 - BETA_STATS) * mul(gradient.T, gradient)
    left_new = orthonormal(mul(left_stat_new, left_op))
    right_new = orthonormal(mul(right_stat_new, right_op))
    moment_out = mul(mul(mul(left_new.T, left_op), moment_new), mul(right_op.T, right_new))
    return (weight_new, moment_out, second_new, left_new, right_new, left_stat_new, right_stat_new)

def reference(pixels, ctx_idx, ctx_len, tgt_idx, tgt_len, slot_of, weights, first_moment, second_moment, left_basis, right_basis, left_stats, right_stats, vectors, vector_first, vector_second):
    enc_slots = slot_of[:NBE]
    pred_slots = slot_of[NBE:]
    online = (unpack_mats(weights[0][enc_slots], enc_shapes()), unpack_vec(vectors[0, :VE], enc_lengths()), unpack_mats(weights[1][pred_slots], pred_shapes()), unpack_vec(vectors[1, :VP], pred_lengths()))
    target_mats = unpack_mats(weights[1][enc_slots], enc_shapes())
    target_vectors = unpack_vec(vectors[1, VP:], enc_lengths())
    pos_enc = sincos(D)
    pos_pred = sincos(PD)
    ctx_valid = jnp.arange(LC)[None, :] < ctx_len[:, None]
    tgt_flat = tgt_idx.reshape(IMAGES, NT * LT)
    tgt_valid = (jnp.arange(LT)[None, None, :] < tgt_len[:, :, None]).reshape(IMAGES, NT * LT)
    group_size = 16

    def group_step(carried, inputs):
        loss_total, grad_total = carried
        group_pix, group_ctx, group_cvalid, group_tgt, group_tvalid = inputs
        pixel_rows = jnp.take_along_axis(group_pix, group_ctx[:, :, None], 1)
        all_valid = jnp.ones(group_pix.shape[:2], jnp.bool_)
        encoded_all = plain_norm(encode(group_pix, pos_enc[None], all_valid, target_mats, target_vectors))
        target = jnp.take_along_axis(encoded_all, group_tgt[:, :, None], 1)
        target_mask = group_tvalid.astype(jnp.float32)[:, :, None]
        joined_valid = jnp.concatenate([group_cvalid, group_tvalid], 1)

        def loss_of(params):
            enc_mats, enc_vectors, pred_mats, pred_vectors = params
            context = encode(pixel_rows, pos_enc[group_ctx], group_cvalid, enc_mats, enc_vectors)
            predicted = predict(context, pos_pred[group_ctx], pos_pred[group_tgt], joined_valid, pred_mats, pred_vectors)
            return huber_sum(predicted - target, target_mask)
        loss_value, backward = jax.vjp(loss_of, online)
        group_grads = backward(jnp.ones_like(loss_value))[0]
        return ((loss_total + loss_value, jax.tree.map(jnp.add, grad_total, group_grads)), None)
    reshaped = tuple((array_in.reshape((IMAGES // group_size, group_size) + array_in.shape[1:]) for array_in in (pixels.astype(jnp.float32), ctx_idx, ctx_valid, tgt_flat, tgt_valid)))
    initial = (jnp.zeros((), jnp.float32), jax.tree.map(jnp.zeros_like, online))
    (loss_sum, grad_sums), _ = lax.scan(group_step, initial, reshaped)
    loss_count = jnp.sum(tgt_len).astype(jnp.float32)
    enc_mat_grads, enc_vec_grads, pred_mat_grads, pred_vec_grads = grad_sums
    block_grads = jnp.concatenate([pack_mats(enc_mat_grads, B), pack_mats(pred_mat_grads, B)]) / loss_count
    vector_grads = jnp.concatenate(enc_vec_grads + pred_vec_grads) / loss_count
    grad_norm = jnp.sqrt(jnp.sum(block_grads * block_grads) + jnp.sum(vector_grads * vector_grads))
    factor = jnp.minimum(1.0, CLIP_LIMIT / (grad_norm + 1e-06))
    block_grads = block_grads * factor
    vector_grads = vector_grads * factor

    def pick_blocks(state_table):
        return jnp.concatenate([state_table[0][enc_slots], state_table[1][pred_slots]])
    tables = (weights, first_moment, second_moment, left_basis, right_basis, left_stats, right_stats)
    olds = [pick_blocks(state_table) for state_table in tables]
    results = lax.map(lambda members: soap_update(*members), (olds[0], block_grads) + tuple(olds[1:]))
    outputs = []
    for position, state_table in enumerate(tables):
        first_row = state_table[0].at[enc_slots].set(results[position][:NBE])
        second_row = state_table[1].at[pred_slots].set(results[position][NBE:])
        if position == 0:
            second_row = second_row.at[enc_slots].set(EMA_KEEP * state_table[1][enc_slots] + (1.0 - EMA_KEEP) * results[0][:NBE])
        outputs.append(jnp.stack([first_row, second_row]))
    correct_one = 1.0 - BETA_FIRST ** STEP
    correct_two = 1.0 - BETA_SECOND ** STEP
    old_params = jnp.concatenate([vectors[0, :VE], vectors[1, :VP]])
    old_first = jnp.concatenate([vector_first[0, :VE], vector_first[1, :VP]])
    old_second = jnp.concatenate([vector_second[0, :VE], vector_second[1, :VP]])
    fresh_first = BETA_FIRST * old_first + (1.0 - BETA_FIRST) * vector_grads
    fresh_second = BETA_SECOND * old_second + (1.0 - BETA_SECOND) * vector_grads * vector_grads
    fresh_params = old_params - RATE_VECTOR * (fresh_first / correct_one) / (jnp.sqrt(fresh_second / correct_two) + ADAM_EPS)

    def place_vec(state_table, fresh, tail_part):
        return jnp.stack([state_table[0].at[:VE].set(fresh[:VE]), jnp.concatenate([fresh[VE:], tail_part])])
    new_vectors = place_vec(vectors, fresh_params, EMA_KEEP * vectors[1, VP:] + (1.0 - EMA_KEEP) * fresh_params[:VE])
    new_vector_first = place_vec(vector_first, fresh_first, vector_first[1, VP:])
    new_vector_second = place_vec(vector_second, fresh_second, vector_second[1, VP:])
    return (loss_sum, loss_count, grad_norm, outputs[0], outputs[1], outputs[2], outputs[3], outputs[4], outputs[5], outputs[6], new_vectors, new_vector_first, new_vector_second)
```

```python
import math

import jax
import jax.numpy as jnp
from jax import lax
from jax.experimental import pallas as pl
from jax.experimental.pallas import tpu as pltpu
from jax.sharding import PartitionSpec as P

D = 768
FF = 3072
H = 12
PD = 384
PFF = 1536
PH = 12
PIX = 768
GRID = 14
NT = 4
LC = 128
STEP = 10
P_SIZE = 196
LT = 36
NBE = 52
NBP = 16
VE = 11520
VP = 6912
VW = 18432


NORM_EPS = 1e-06
ADAM_EPS = 1e-08
BETA_FIRST = 0.5
BETA_SECOND = 0.5
BETA_STATS = 0.95
RATE_MATRIX = 0.02
RATE_VECTOR = 0.05
DECAY_MATRIX = 0.04
EMA_KEEP = 0.996
CLIP_LIMIT = 1.0
NEG_FILL = -1000000000.0
WIRE = jnp.float16
WIRE_TOP = 16384.0
f32 = jnp.float32
bf = jnp.bfloat16


def from_behind(shard, axis, by):
    size = lax.axis_size(axis)
    pairs = [(i, i + by) for i in range(size) if 0 <= i + by < size]
    return lax.ppermute(shard, axis, pairs)


def enc_shapes():
    return [(PIX, D), (D, 3 * D), (D, D), (D, FF), (FF, D)]


def pred_shapes():
    return [(D, PD), (PD, 3 * PD), (PD, PD), (PD, PFF), (PFF, PD), (PD, D)]


def enc_lengths():
    return [D] * 8 + [FF, D, D, D]


def pred_lengths():
    return [PD] * 8 + [PFF, PD, PD, PD, D, PD]


def unpack_vec(vector, lengths):
    result = []
    offset = 0
    for length in lengths:
        result.append(vector[offset : offset + length])
        offset += length
    return result


def sincos(width):
    quarter = width // 4
    frequency = 1.0 / 10000.0 ** (jnp.arange(quarter, dtype=jnp.float32) / quarter)
    cell_ids = jnp.arange(P_SIZE)
    row_pos = (cell_ids // GRID).astype(jnp.float32)[:, None] * frequency
    column_pos = (cell_ids % GRID).astype(jnp.float32)[:, None] * frequency
    return jnp.concatenate(
        [jnp.sin(row_pos), jnp.cos(row_pos), jnp.sin(column_pos), jnp.cos(column_pos)], 1
    )


def layer_norm(inputs, gain_vec, shift_vec):
    center = inputs - jnp.mean(inputs, -1, keepdims=True)
    spread = jnp.mean(center * center, -1, keepdims=True)
    return center * lax.rsqrt(spread + NORM_EPS) * gain_vec + shift_vec


def plain_norm(inputs):
    center = inputs - jnp.mean(inputs, -1, keepdims=True)
    spread = jnp.mean(center * center, -1, keepdims=True)
    return center * lax.rsqrt(spread + NORM_EPS)


def gelu_exact(inputs):
    return jax.nn.gelu(inputs, approximate=False)


def dense(left_op, right_op):
    return jnp.einsum("...k,km->...m", left_op, right_op, preferred_element_type=jnp.float32)


def dense_back(inputs, weight, grad_out):
    grad_low = grad_out.astype(jnp.bfloat16)
    grad_in = jnp.einsum("...m,km->...k", grad_low, weight, preferred_element_type=jnp.float32)
    grad_weight = jnp.einsum("...k,...m->km", inputs, grad_low, preferred_element_type=jnp.float32)
    return (grad_in, grad_weight)


def lead_sum(values):
    return jnp.sum(values.reshape(-1, values.shape[-1]), 0)


def attend_forward(qkv, valid, heads):
    batch_size, length, triple = qkv.shape
    model_width = triple // 3
    head_dim = model_width // heads
    split_shape = (batch_size, length, heads, head_dim)
    queries = (
        (qkv[..., :model_width] * (1.0 / math.sqrt(head_dim)))
        .astype(jnp.bfloat16)
        .reshape(split_shape)
    )
    keys_low = qkv[..., model_width : 2 * model_width].astype(jnp.bfloat16).reshape(split_shape)
    values_low = qkv[..., 2 * model_width :].astype(jnp.bfloat16).reshape(split_shape)
    scores = jnp.einsum("nqhd,nkhd->nhqk", queries, keys_low, preferred_element_type=jnp.float32)
    scores = jnp.where(valid[:, None, None, :], scores, NEG_FILL)
    softmax_out = jax.nn.softmax(scores, axis=-1)
    softmax_low = softmax_out.astype(jnp.bfloat16)
    attended = jnp.einsum(
        "nhqk,nkhd->nqhd", softmax_low, values_low, preferred_element_type=jnp.float32
    )
    return (
        attended.reshape(batch_size, length, model_width),
        (queries, keys_low, values_low, softmax_out, softmax_low),
    )


def attend_backward(kept, grad_out):
    queries, keys_low, values_low, softmax_out, softmax_low = kept
    batch_size, length, heads, head_dim = queries.shape
    grad_low = grad_out.astype(jnp.bfloat16).reshape(batch_size, length, heads, head_dim)
    grad_values = jnp.einsum(
        "nhqk,nqhd->nkhd", softmax_low, grad_low, preferred_element_type=jnp.float32
    )
    grad_probs = jnp.einsum(
        "nqhd,nkhd->nhqk", grad_low, values_low, preferred_element_type=jnp.float32
    )
    grad_scores = softmax_out * (grad_probs - jnp.sum(grad_probs * softmax_out, -1, keepdims=True))
    scores_low = grad_scores.astype(jnp.bfloat16)
    grad_queries = jnp.einsum(
        "nhqk,nkhd->nqhd", scores_low, keys_low, preferred_element_type=jnp.float32
    ) * (1.0 / math.sqrt(head_dim))
    grad_keys = jnp.einsum(
        "nhqk,nqhd->nkhd", scores_low, queries, preferred_element_type=jnp.float32
    )
    flat_shape = (batch_size, length, heads * head_dim)
    return jnp.concatenate(
        [
            grad_queries.reshape(flat_shape),
            grad_keys.reshape(flat_shape),
            grad_values.reshape(flat_shape),
        ],
        -1,
    )


def block_forward(inputs, valid, matrices, vector_list, heads):
    weight_proj, weight_out, weight_up, weight_down = matrices
    (
        gain_one,
        shift_one,
        bias_query,
        bias_value,
        bias_output,
        gain_two,
        shift_two,
        bias_up,
        bias_down,
    ) = vector_list
    bias_all = jnp.concatenate([bias_query, jnp.zeros_like(bias_query), bias_value])
    normed_low = layer_norm(inputs, gain_one, shift_one).astype(jnp.bfloat16)
    qkv = dense(normed_low, weight_proj) + bias_all
    attended, attn_kept = attend_forward(qkv, valid, heads)
    attended_low = attended.astype(jnp.bfloat16)
    middle = inputs + dense(attended_low, weight_out) + bias_output
    hidden_low = layer_norm(middle, gain_two, shift_two).astype(jnp.bfloat16)
    pre_act = dense(hidden_low, weight_up) + bias_up
    act_low = gelu_exact(pre_act).astype(jnp.bfloat16)
    output = middle + dense(act_low, weight_down) + bias_down
    return (
        output,
        (inputs, normed_low, attn_kept, attended_low, middle, hidden_low, pre_act, act_low),
    )


def block_backward(kept, grad_out, matrices, vector_list):
    inputs, normed_low, attn_kept, attended_low, middle, hidden_low, pre_act, act_low = kept
    weight_proj, weight_out, weight_up, weight_down = matrices
    (
        gain_one,
        shift_one,
        bias_query,
        bias_value,
        bias_output,
        gain_two,
        shift_two,
        bias_up,
        bias_down,
    ) = vector_list
    grad_act, grad_down = dense_back(act_low, weight_down, grad_out)
    grad_pre = jax.vjp(gelu_exact, pre_act)[1](grad_act)[0]
    grad_hidden, grad_up = dense_back(hidden_low, weight_up, grad_pre)
    grad_middle, grad_gain_two, grad_shift_two = jax.vjp(layer_norm, middle, gain_two, shift_two)[
        1
    ](grad_hidden)
    grad_middle = grad_middle + grad_out
    grad_attn, grad_output = dense_back(attended_low, weight_out, grad_middle)
    grad_qkv = attend_backward(attn_kept, grad_attn)
    bias_sums = lead_sum(grad_qkv)
    model_width = inputs.shape[-1]
    grad_normed, grad_proj = dense_back(normed_low, weight_proj, grad_qkv)
    grad_inputs, grad_gain_one, grad_shift_one = jax.vjp(layer_norm, inputs, gain_one, shift_one)[
        1
    ](grad_normed)
    mats_out = [grad_proj, grad_output, grad_up, grad_down]
    vecs_out = [
        grad_gain_one,
        grad_shift_one,
        bias_sums[:model_width],
        bias_sums[2 * model_width :],
        lead_sum(grad_middle),
        grad_gain_two,
        grad_shift_two,
        lead_sum(grad_pre),
        lead_sum(grad_out),
    ]
    return (grad_inputs + grad_middle, mats_out, vecs_out)


def encode_forward(pixel_rows, position, valid, matrices, vector_list):
    embedded = dense(pixel_rows, matrices[0]) + vector_list[0] + position
    hidden, saved = block_forward(embedded, valid, matrices[1:], vector_list[1:10], H)
    return (layer_norm(hidden, vector_list[10], vector_list[11]), (hidden, saved))


def encode_backward(pixel_rows, kept, grad_out, matrices, vector_list):
    hidden, saved = kept
    grad_hidden, grad_gain, grad_shift = jax.vjp(
        layer_norm, hidden, vector_list[10], vector_list[11]
    )[1](grad_out)
    grad_embed, layer_mats, layer_vecs = block_backward(
        saved, grad_hidden, matrices[1:], vector_list[1:10]
    )
    grad_patch = jnp.einsum(
        "...k,...m->km",
        pixel_rows,
        grad_embed.astype(jnp.bfloat16),
        preferred_element_type=jnp.float32,
    )
    return (
        [grad_patch] + layer_mats,
        [lead_sum(grad_embed)] + layer_vecs + [grad_gain, grad_shift],
    )


def target_forward(pixel_all, tgt_rows, position, matrices, vector_list):
    all_valid = jnp.ones(pixel_all.shape[:2], jnp.bool_)
    encoded, _ = encode_forward(pixel_all, position, all_valid, matrices, vector_list)
    return jnp.take_along_axis(plain_norm(encoded), tgt_rows[:, :, None], 1)


def predict_forward(context, ctx_pos, tgt_pos, valid, matrices, vector_list):
    entry = dense(context, matrices[0]) + vector_list[0] + ctx_pos
    joined = jnp.concatenate([entry, vector_list[13] + tgt_pos], 1)
    hidden, saved = block_forward(joined, valid, matrices[1:5], vector_list[1:10], PH)
    tail = hidden[:, LC:]
    normed = layer_norm(tail, vector_list[10], vector_list[11]).astype(jnp.bfloat16)
    return (dense(normed, matrices[5]) + vector_list[12], (saved, tail, normed))


def predict_backward(context, kept, grad_out, matrices, vector_list):
    saved, tail, normed = kept
    grad_normed, grad_final = dense_back(normed, matrices[5], grad_out)
    grad_tail, grad_gain, grad_shift = jax.vjp(layer_norm, tail, vector_list[10], vector_list[11])[
        1
    ](grad_normed)
    grad_hidden = jnp.concatenate(
        [jnp.zeros((tail.shape[0], LC, tail.shape[2]), jnp.float32), grad_tail], 1
    )
    grad_joined, layer_mats, layer_vecs = block_backward(
        saved, grad_hidden, matrices[1:5], vector_list[1:10]
    )
    grad_entry = grad_joined[:, :LC]
    grad_queries = grad_joined[:, LC:]
    grad_context, grad_first = dense_back(context, matrices[0], grad_entry)
    mats_out = [grad_first] + layer_mats + [grad_final]
    vecs_out = (
        [lead_sum(grad_entry)]
        + layer_vecs
        + [grad_gain, grad_shift, lead_sum(grad_out), lead_sum(grad_queries)]
    )
    return (grad_context, mats_out, vecs_out)


DIMS = {"nn": (1, 0), "nt": (1, 1), "tn": (0, 0)}

def parts_of(a, count):
    found = []
    for index in range(count):
        piece = a.astype(bf)
        found.append(piece)
        if index + 1 < count:
            a = a - piece.astype(f32)
    return found

def product(left, right, form, pairs):
    ld, rd = DIMS[form]
    lhs = jnp.concatenate([left[i] for i, _ in pairs], ld)
    rhs = jnp.concatenate([right[j] for _, j in pairs], rd)
    return lax.dot_general(lhs, rhs, (((ld,), (rd,)), ((), ())), preferred_element_type=f32)

THREE = ((0, 1), (1, 0), (0, 0))
SIX = ((0, 2), (2, 0), (1, 1), (0, 1), (1, 0), (0, 0))
def mul3(left, right, form="nn"):
    return product(left, right, form, THREE)
def mul6(left, right, form="nn"):
    return product(left, right, form, SIX)

def invert_factors(mats):
    n = mats[0].shape[0]
    lane = lax.broadcasted_iota(jnp.int32, (8, n), 1)
    sub = lax.broadcasted_iota(jnp.int32, (8, n), 0)
    groups = [[a[8 * t : 8 * t + 8, :] for t in range(n // 8)] for a in mats]
    for j in range(n):
        top, at_row = divmod(j, 8)
        here = lane == j
        pick = jnp.full((8, n), j, jnp.int32)
        for tiles in groups:
            column = jnp.take_along_axis(tiles[top], pick, axis=1)
            pivot = jnp.broadcast_to(column[at_row : at_row + 1, :], (8, n))
            row = jnp.broadcast_to(tiles[top][at_row : at_row + 1, :], (8, n))
            scaled = jnp.where(here, 1.0, row) * (1.0 / pivot)
            for t in range(top, n // 8):
                if t > top:
                    column = jnp.take_along_axis(tiles[t], pick, axis=1)
                fresh = jnp.where(here, 0.0, tiles[t]) - column * scaled
                tiles[t] = jnp.where(sub > at_row, fresh, tiles[t]) if t == top else fresh
    results = []
    for tiles in groups:
        rows = []
        for t in range(n // 8):
            at = sub + 8 * t
            pivots = jnp.sum(jnp.where(lane == at, tiles[t], 0.0), axis=1, keepdims=True)
            unit = jnp.where(lane < at, tiles[t], jnp.where(lane == at, 1.0, 0.0))
            rows.append(unit * lax.rsqrt(pivots))
        results.append(jnp.concatenate(rows, 0))
    return results

def first_kernel(flag, factor, g_ref, w_ref, m_ref, v_ref, l_ref, r_ref, e_ref, f_ref,
                 w_out, m_out, v_out, e_out, f_out, base_out, gram_out):
    on = flag[pl.program_id(0)] != 0

    @pl.when(jnp.logical_not(on))
    def keep():
        for source, target in ((w_ref, w_out), (m_ref, m_out), (v_ref, v_out), (e_ref, e_out), (f_ref, f_out)):
            target[...] = source[...]

    @pl.when(on)
    def update():
        correct_one = 1.0 - BETA_FIRST**STEP
        correct_two = 1.0 - BETA_SECOND**STEP
        grad = parts_of(g_ref[0] * factor[0], 3)
        left = parts_of(l_ref[0], 3)
        right = parts_of(r_ref[0], 3)
        rotated = mul3(left, parts_of(mul3(grad, right), 2), "tn")
        moment = BETA_FIRST * m_ref[0] + (1.0 - BETA_FIRST) * rotated
        second = BETA_SECOND * v_ref[0] + (1.0 - BETA_SECOND) * rotated * rotated
        m_out[0] = moment
        v_out[0] = second
        normed = moment / correct_one / (jnp.sqrt(second / correct_two) + ADAM_EPS)
        weight = w_ref[0]
        step = mul3(left, parts_of(mul3(parts_of(normed, 2), right, "nt"), 2))
        w_out[0] = weight - RATE_MATRIX * (step + DECAY_MATRIX * weight)
        for index, (stat, target, basis, form) in enumerate(
            ((e_ref, e_out, left, "nt"), (f_ref, f_out, right, "tn"))
        ):
            fresh = BETA_STATS * stat[0] + (1.0 - BETA_STATS) * mul6(grad, grad, form)
            target[0] = fresh
            moved = mul6(parts_of(fresh, 3), basis)
            base_out[0, index] = moved
            pieces = parts_of(moved, 3)
            gram_out[0, index] = mul6(pieces, pieces, "tn")

def factor_kernel(flag, base_ref, gram_ref, q_out, base, gram, inverse):
    blocks, edge = base_ref.shape[0], base_ref.shape[-1]
    panel = 128
    count = edge // panel
    base[...] = base_ref[...]
    gram[...] = gram_ref[...]

    def stage(k):
        at = pl.ds(panel * k, panel)
        start = panel * k
        spot = slice(start, start + panel)
        rest = slice(start + panel, edge)

        def block(b, carry):
            @pl.when(flag[b] != 0)
            def run():
                for side in range(2):
                    inv = parts_of(inverse[b, side], 3)
                    q = mul6(parts_of(base[b, side, :, spot], 3), inv, "nt")
                    q_out[b, side, :, spot] = q
                    if k + 1 < count:
                        p = parts_of(mul6(inv, parts_of(gram[b, side, spot, rest], 3)), 3)
                        gram[b, side, rest, rest] = gram[b, side, rest, rest] - mul6(p, p, "tn")
                        base[b, side, :, rest] = base[b, side, :, rest] - mul6(parts_of(q, 3), p)
            return carry

        lax.fori_loop(0, blocks, block, 0)

    def turn(k, carry):
        for which in range(count):
            @pl.when(k == which)
            def load():
                spot = slice(panel * which, panel * which + panel)
                for b in range(blocks):
                    for side in range(2):
                        inverse[b, side] = gram[b, side, spot, spot]
        mats = invert_factors([inverse[b, side] for b in range(blocks) for side in range(2)])
        for b in range(blocks):
            for side in range(2):
                inverse[b, side] = mats[2 * b + side]
        for which in range(count):
            @pl.when(k == which)
            def run():
                stage(which)
        return carry

    lax.fori_loop(0, count, turn, 0)

def last_kernel(flag, l_ref, r_ref, m_ref, q_ref, l_out, r_out, m_out):
    on = flag[pl.program_id(0)] != 0

    @pl.when(jnp.logical_not(on))
    def keep():
        l_out[...] = l_ref[...]
        r_out[...] = r_ref[...]
        m_out[...] = m_ref[...]

    @pl.when(on)
    def update():
        l_out[0] = q_ref[0, 0]
        r_out[0] = q_ref[0, 1]
        turn_left = mul3(parts_of(q_ref[0, 0], 2), parts_of(l_ref[0], 2), "tn")
        turn_right = mul3(parts_of(r_ref[0], 2), parts_of(q_ref[0, 1], 2), "tn")
        half = mul3(parts_of(turn_left, 2), parts_of(m_ref[0], 2))
        m_out[0] = mul3(parts_of(half, 2), parts_of(turn_right, 2))

def soap_first(flags, factor, *arrays):
    n, e = arrays[0].shape[:2]
    one = pl.BlockSpec((1, e, e), lambda i, *_: (i, 0, 0))
    two = pl.BlockSpec((1, 2, e, e), lambda i, *_: (i, 0, 0, 0))
    single = jax.ShapeDtypeStruct((n, e, e), f32)
    double = jax.ShapeDtypeStruct((n, 2, e, e), f32)
    return pl.pallas_call(
        first_kernel,
        grid_spec=pltpu.PrefetchScalarGridSpec(
            num_scalar_prefetch=2, grid=(n,), in_specs=[one] * 8, out_specs=[one] * 5 + [two] * 2
        ),
        out_shape=[single] * 5 + [double] * 2,
        compiler_params=pltpu.CompilerParams(vmem_limit_bytes=56 << 20),
        name="soap_first",
    )(flags, factor, *arrays)


def soap_factor(flags, base, gram):
    n, _, e, _ = base.shape
    whole = pl.BlockSpec(memory_space=pltpu.VMEM)
    return pl.pallas_call(
        factor_kernel,
        grid_spec=pltpu.PrefetchScalarGridSpec(
            num_scalar_prefetch=1,
            grid=(),
            in_specs=[whole] * 2,
            out_specs=whole,
            scratch_shapes=[
                pltpu.VMEM((n, 2, e, e), f32),
                pltpu.VMEM((n, 2, e, e), f32),
                pltpu.VMEM((n, 2, 128, 128), f32),
            ],
        ),
        out_shape=jax.ShapeDtypeStruct(base.shape, f32),
        compiler_params=pltpu.CompilerParams(vmem_limit_bytes=56 << 20),
        name="soap_factor",
    )(flags, base, gram)


def soap_last(flags, left, right, moment, fresh):
    n, e = left.shape[:2]
    one = pl.BlockSpec((1, e, e), lambda i, *_: (i, 0, 0))
    two = pl.BlockSpec((1, 2, e, e), lambda i, *_: (i, 0, 0, 0))
    return pl.pallas_call(
        last_kernel,
        grid_spec=pltpu.PrefetchScalarGridSpec(
            num_scalar_prefetch=1, grid=(n,), in_specs=[one] * 3 + [two], out_specs=[one] * 3
        ),
        out_shape=[jax.ShapeDtypeStruct((n, e, e), f32)] * 3,
        compiler_params=pltpu.CompilerParams(vmem_limit_bytes=56 << 20),
        name="soap_last",
    )(flags, left, right, moment, fresh)


def block_places(shapes, edge):
    places = []
    for index, (height, breadth) in enumerate(shapes):
        for row in range(height // edge):
            for column in range(breadth // edge):
                places.append((index, row, column))
    return places


def gather_matrices(slots, second, table):
    edge = table.shape[-1]
    shapes = enc_shapes() + pred_shapes()
    places = block_places(shapes, edge)

    def body(slots_ref, second_ref, table_ref, *rest):
        outs, sems = rest[:-1], rest[-1]

        def copy(j):
            index, row, column = places[j]
            spot = outs[index].at[pl.ds(row * edge, edge), pl.ds(column * edge, edge)]
            return pltpu.make_async_copy(table_ref.at[slots_ref[j]], spot, sems.at[j])

        for j in range(NBE):
            copy(j).start()

        @pl.when(second_ref[0] != 0)
        def more():
            for j in range(NBE, NBE + NBP):
                copy(j).start()
            for j in range(NBE, NBE + NBP):
                copy(j).wait()

        for j in range(NBE):
            copy(j).wait()

    result = pl.pallas_call(
        body,
        grid_spec=pltpu.PrefetchScalarGridSpec(
            num_scalar_prefetch=2,
            grid=(),
            in_specs=[pl.BlockSpec(memory_space=pl.ANY)],
            out_specs=[pl.BlockSpec(memory_space=pltpu.VMEM)] * len(shapes),
            scratch_shapes=[pltpu.SemaphoreType.DMA((len(places),))],
        ),
        out_shape=[jax.ShapeDtypeStruct(shape, table.dtype) for shape in shapes],
        compiler_params=pltpu.CompilerParams(vmem_limit_bytes=56 << 20),
        name="gather_matrices",
    )(slots, second, table)
    return result[: len(enc_shapes())], result[len(enc_shapes()) :]


def place_shares(slots, second, enc_share, pred_share, slot_rows):
    depth, edge = enc_share.shape[1:]

    def body(slots_ref, second_ref, enc_ref, pred_ref, out_ref):
        def run(source, first, count):
            def copy(j, carry):
                out_ref[slots_ref[first + j]] = source[j]
                return carry

            lax.fori_loop(0, count, copy, 0)

        @pl.when(second_ref[0] == 0)
        def enc():
            run(enc_ref, 0, NBE)

        @pl.when(second_ref[0] != 0)
        def pred():
            run(pred_ref, NBE, NBP)

    return pl.pallas_call(
        body,
        grid_spec=pltpu.PrefetchScalarGridSpec(
            num_scalar_prefetch=2,
            grid=(),
            in_specs=[pl.BlockSpec(memory_space=pltpu.VMEM)] * 2,
            out_specs=pl.BlockSpec(memory_space=pltpu.VMEM),
        ),
        out_shape=jax.ShapeDtypeStruct((slot_rows, depth, edge), f32),
        compiler_params=pltpu.CompilerParams(vmem_limit_bytes=40 << 20),
        name="place_shares",
    )(slots, second, enc_share, pred_share)


class Exchange:
    def __init__(self, sections):
        self.ranks = lax.axis_size("dp")
        self.bits = self.ranks.bit_length() - 1
        self.sections = sections

    def swap(self, value, bit):
        pairs = [
            (s * self.ranks + i, s * self.ranks + (i ^ (1 << bit)))
            for s in self.sections
            for i in range(self.ranks)
        ]
        return lax.ppermute(value, ("section", "dp"), pairs)

    def total(self, value):
        for bit in range(self.bits):
            value = value + self.swap(value, bit)
        return value


def power_scale(bound):
    return jnp.exp2(jnp.floor(jnp.log2(WIRE_TOP / jnp.maximum(bound, 1e-30))))


def halve(exchange, grads, orders):
    ranks, bits = exchange.ranks, exchange.bits
    me = lax.axis_index("dp")
    bounds = [jnp.max(jnp.abs(g)) for g in grads]
    parts = []
    for g in grads:
        lead, edge, columns = g.shape
        parts.append(g.reshape((lead,) + (2,) * bits + (edge // ranks, columns)))
    left = [list(range(bits - 1, -1, -1)) for _ in grads]
    for stage in range(bits):
        sent, tiny = [], {}
        for k, part in enumerate(parts):
            bit = orders[k][stage]
            axis = 1 + left[k].index(bit)
            mine = (me >> bit) & 1
            give = lax.dynamic_index_in_dim(part, 1 - mine, axis, keepdims=False)
            keep = lax.dynamic_index_in_dim(part, mine, axis, keepdims=False)
            scale = power_scale(bounds[k])
            low = (give.reshape(-1, give.shape[-1]) * scale).astype(WIRE)
            sent.append((exchange.swap(low, bit), keep))
            tiny.setdefault(bit, []).append(k)
            left[k].remove(bit)
        for bit, members in tiny.items():
            packed = jnp.stack([bounds[k] for k in members])
            packed = jnp.pad(packed, (0, 128 - len(members)))
            theirs = exchange.swap(packed, bit)
            for place, k in enumerate(members):
                other = theirs[place]
                low, keep = sent[k]
                got = low.astype(f32) * (1.0 / power_scale(other))
                parts[k] = keep + got.reshape(keep.shape)
                bounds[k] = bounds[k] + other
    return parts


def split_columns(share, edge):
    lead, depth, columns = share.shape
    cut = share.reshape(lead, depth, columns // edge, edge)
    return cut.transpose(0, 2, 1, 3).reshape(-1, depth, edge)


def zeros_of(shapes):
    return jax.tree.map(lambda leaf: jnp.zeros(leaf.shape, leaf.dtype), shapes)


def on_device(
    pixels,
    ctx_idx,
    ctx_len,
    tgt_idx,
    tgt_len,
    slot_of,
    weights,
    first_moment,
    second_moment,
    left_basis,
    right_basis,
    left_stats,
    right_stats,
    vectors,
    vector_first,
    vector_second,
):
    section_index = lax.axis_index("section")
    owner_index = lax.axis_index("dp")
    ranks = lax.axis_size("dp")
    is_first = section_index == 0
    second = section_index.astype(jnp.int32).reshape(1)
    slot_count = weights.shape[1]
    edge = weights.shape[-1]
    slot_rows = slot_count * ranks
    gathered = lax.all_gather(weights[0].astype(bf), "dp", axis=0, tiled=True)
    enc_mats, pred_mats = gather_matrices(slot_of, second, gathered)
    enc_slots = slot_of[:NBE]
    pred_slots = slot_of[NBE:]
    row_now = vectors[0]
    enc_vectors = unpack_vec(
        lax.dynamic_slice_in_dim(row_now, section_index * VP, VE), enc_lengths()
    )
    pred_vectors = unpack_vec(row_now[:VP], pred_lengths())
    pos_enc = sincos(D)
    pos_pred = sincos(PD)
    images = ctx_idx.shape[0]
    ctx_valid = jnp.arange(LC)[None, :] < ctx_len[:, None]
    tgt_flat = tgt_idx.reshape(images, NT * LT)
    tgt_valid = (jnp.arange(LT)[None, None, :] < tgt_len[:, :, None]).reshape(images, NT * LT)

    def pick(index, count):
        return (index[..., None] == jnp.arange(count)).astype(f32)

    ctx_hot = pick(ctx_idx, P_SIZE)
    tgt_hot = pick(tgt_flat, P_SIZE)

    def choose(hot, table):
        return jnp.einsum(
            "njp,pd->njd", hot, table, precision=lax.Precision.HIGHEST, preferred_element_type=f32
        )

    pixel_rows = jnp.einsum(
        "njp,npd->njd", ctx_hot.astype(bf), pixels, preferred_element_type=f32
    ).astype(bf)

    def run_encoder(unused):
        encoded, kept = encode_forward(
            pixel_rows, choose(ctx_hot, pos_enc), ctx_valid, enc_mats, enc_vectors
        )
        return encoded.astype(bf), kept

    kept_shapes = jax.eval_shape(run_encoder, 0)[1]

    def enc_branch(unused):
        encoded, kept = run_encoder(0)
        return encoded, kept, jnp.zeros((images, NT * LT, D), f32)

    def tgt_branch(unused):
        valid = jnp.ones(pixels.shape[:2], jnp.bool_)
        encoded, _ = encode_forward(pixels, pos_enc[None], valid, enc_mats, enc_vectors)
        target = jnp.einsum(
            "njp,npd->njd",
            tgt_hot,
            plain_norm(encoded),
            precision=lax.Precision.HIGHEST,
            preferred_element_type=f32,
        )
        return jnp.zeros((images, LC, D), bf), zeros_of(kept_shapes), target

    outgoing, kept, target = lax.cond(is_first, enc_branch, tgt_branch, 0)
    context = from_behind(outgoing, "section", 1)
    joined_valid = jnp.concatenate([ctx_valid, tgt_valid], 1)
    target_mask = tgt_valid.astype(f32)[:, :, None]

    def run_predictor(unused):
        predicted, saved = predict_forward(
            context,
            choose(ctx_hot, pos_pred),
            choose(tgt_hot, pos_pred),
            joined_valid,
            pred_mats,
            pred_vectors,
        )
        difference = predicted - target
        magnitude = jnp.abs(difference)
        loss_value = jnp.sum(
            jnp.where(magnitude < 1.0, 0.5 * difference * difference, magnitude - 0.5)
            * target_mask
        )
        grad_out = jnp.clip(difference, -1.0, 1.0) * target_mask
        grad_context, mats_grad, vecs_grad = predict_backward(
            context, saved, grad_out, pred_mats, pred_vectors
        )
        return grad_context.astype(bf), mats_grad, jnp.concatenate(vecs_grad), loss_value

    predictor_shapes = jax.eval_shape(run_predictor, 0)
    back_send, pred_grads, pred_vec, loss_local = lax.cond(
        is_first, lambda unused: zeros_of(predictor_shapes), run_predictor, 0
    )
    incoming = from_behind(back_send, "section", -1)

    low_order = list(range(Exchange((0,)).bits))
    swapped = [1, 0] + low_order[2:] if len(low_order) > 1 else low_order
    g_in, g_qkv, g_out, g_up, g_down, g_last = pred_grads
    pred_leaves = [
        jnp.concatenate([g_qkv, g_out, g_up, g_last], 1)[None],
        jnp.concatenate([g_in, g_down], 0).reshape(-1, edge, PD),
    ]
    pred_wide, pred_tall = halve(Exchange((1,)), pred_leaves, [low_order, swapped])

    def run_encoder_back(unused):
        mats_grad, vecs_grad = encode_backward(
            pixel_rows, kept, incoming.astype(f32), enc_mats, enc_vectors
        )
        return mats_grad, jnp.concatenate(vecs_grad)

    back_shapes = jax.eval_shape(run_encoder_back, 0)
    enc_grads, enc_vec = lax.cond(
        is_first, run_encoder_back, lambda unused: zeros_of(back_shapes), 0
    )
    enc_leaves = [g.reshape(-1, edge, g.shape[1]) for g in enc_grads]
    e_patch, e_qkv, e_out, e_up, e_down = enc_leaves
    s_up, s_down = halve(Exchange((0,)), [e_up, e_down], [low_order, swapped])
    s_qkv, s_out, s_patch = halve(
        Exchange((0,)), [e_qkv, e_out, e_patch], [low_order, swapped, swapped]
    )
    enc_share = jnp.concatenate(
        [split_columns(s, edge) for s in (s_patch, s_qkv, s_out, s_up, s_down)], 0
    )
    wide = split_columns(pred_wide, edge)
    pred_share = jnp.concatenate([pred_tall[:2], wide[:8], pred_tall[2:], wide[8:]], 0)

    both = Exchange((0, 1))
    vec_local = jnp.where(is_first, enc_vec, jnp.pad(pred_vec, (0, VE - VP)))
    count_local = jnp.where(is_first, 0, jnp.sum(tgt_len)).astype(f32)
    scalars = jnp.pad(jnp.stack([loss_local, count_local]), (0, 126))
    summed = both.total(jnp.concatenate([vec_local, scalars]))
    vec_total = jnp.pad(summed[:VE], (0, VW - VE))
    share_squares = jnp.where(
        is_first, jnp.sum(enc_share * enc_share), jnp.sum(pred_share * pred_share)
    )
    squares = both.total(jnp.full((128,), share_squares))
    facts = jnp.stack([squares[0] + jnp.sum(summed[:VE] ** 2), summed[VE], summed[VE + 1]])
    facts = jnp.pad(facts, (0, 125))
    swap_sections = [(i, 1 - i) for i in range(2)]
    facts = facts + lax.ppermute(facts, "section", swap_sections)
    square_total, loss_total, count_total = facts[0], facts[1], facts[2]

    placed = place_shares(slot_of, second, enc_share, pred_share, slot_rows)
    bound = jnp.where(is_first, jnp.max(jnp.abs(enc_share)), jnp.max(jnp.abs(pred_share)))
    exponent = jnp.floor(jnp.log2(WIRE_TOP / jnp.maximum(bound, 1e-30)))
    depth = edge // ranks
    payload = (placed * jnp.exp2(exponent)).reshape(ranks, slot_count * depth, edge)
    mark = jnp.full((ranks, 8, edge), exponent)
    payload = jnp.concatenate([payload, mark], 1).astype(WIRE)
    owned = lax.all_to_all(payload, "dp", split_axis=0, concat_axis=0, tiled=True).astype(f32)
    unscale = 1.0 / jnp.exp2(owned[:, -1:, :1])
    owned = (owned[:, : slot_count * depth] * unscale).reshape(ranks, slot_count, depth, edge)
    owned_sum = owned.transpose(1, 0, 2, 3).reshape(slot_count, edge, edge)

    own_ids = owner_index * slot_count + jnp.arange(slot_count)
    enc_here = jnp.any(own_ids[:, None] == enc_slots[None, :], 1)
    pred_here = jnp.any(own_ids[:, None] == pred_slots[None, :], 1)
    trained = jnp.where(is_first, enc_here, pred_here)
    ema_here = jnp.logical_and(jnp.logical_not(is_first), enc_here)
    positions = jnp.arange(VW)
    vec_trained = positions < jnp.where(is_first, VE, VP)
    vec_ema = jnp.logical_and(jnp.logical_not(is_first), positions >= VP)
    grad_norm = jnp.sqrt(square_total) / count_total
    factor = jnp.minimum(1.0, CLIP_LIMIT / (grad_norm + 1e-06)) / count_total

    flags = trained.astype(jnp.int32)
    new_weight, moment, new_second, new_estat, new_fstat, base, gram = soap_first(
        flags,
        factor.reshape(1),
        owned_sum,
        weights[0],
        first_moment[0],
        second_moment[0],
        left_basis[0],
        right_basis[0],
        left_stats[0],
        right_stats[0],
    )
    fresh_bases = soap_factor(flags, base, gram)
    new_left, new_right, new_first = soap_last(
        flags, left_basis[0], right_basis[0], moment, fresh_bases
    )

    correct_one = 1.0 - BETA_FIRST**STEP
    correct_two = 1.0 - BETA_SECOND**STEP
    vec_clipped = vec_total * factor
    fresh_first = BETA_FIRST * vector_first[0] + (1.0 - BETA_FIRST) * vec_clipped
    fresh_second = BETA_SECOND * vector_second[0] + (1.0 - BETA_SECOND) * vec_clipped * vec_clipped
    stepped = row_now - RATE_VECTOR * (fresh_first / correct_one) / (
        jnp.sqrt(fresh_second / correct_two) + ADAM_EPS
    )
    new_vec = jnp.where(vec_trained, stepped, row_now)
    new_vec_first = jnp.where(vec_trained, fresh_first, vector_first[0])
    new_vec_second = jnp.where(vec_trained, fresh_second, vector_second[0])
    from_encoder = from_behind(new_weight.astype(bf), "section", 1).astype(f32)
    vec_from_encoder = from_behind(new_vec.astype(bf), "section", 1).astype(f32)
    new_weight = jnp.where(
        ema_here[:, None, None], EMA_KEEP * weights[0] + (1.0 - EMA_KEEP) * from_encoder, new_weight
    )
    aligned = jnp.concatenate([jnp.zeros((VP,), f32), vec_from_encoder[:VE]])
    new_vec = jnp.where(vec_ema, EMA_KEEP * row_now + (1.0 - EMA_KEEP) * aligned, new_vec)
    return (
        loss_total,
        count_total,
        grad_norm,
        new_weight[None],
        new_first[None],
        new_second[None],
        new_left[None],
        new_right[None],
        new_estat[None],
        new_fstat[None],
        new_vec[None],
        new_vec_first[None],
        new_vec_second[None],
    )


def solution(mesh):
    in_specs = (
        P("dp", None, None),
        P("dp", None),
        P("dp"),
        P("dp", None, None),
        P("dp", None),
        P(),
        P("section", "dp", None, None),
        P("section", "dp", None, None),
        P("section", "dp", None, None),
        P("section", "dp", None, None),
        P("section", "dp", None, None),
        P("section", "dp", None, None),
        P("section", "dp", None, None),
        P("section", None),
        P("section", None),
        P("section", None),
    )
    out_specs = (
        P(),
        P(),
        P(),
        P("section", "dp", None, None),
        P("section", "dp", None, None),
        P("section", "dp", None, None),
        P("section", "dp", None, None),
        P("section", "dp", None, None),
        P("section", "dp", None, None),
        P("section", "dp", None, None),
        P("section", None),
        P("section", None),
        P("section", None),
    )
    return jax.shard_map(
        on_device, mesh=mesh, in_specs=in_specs, out_specs=out_specs, check_vma=False
    )
```

```python
import functools
import math

import jax
import jax.numpy as jnp
from jax import lax
from jax.experimental import pallas as pl
from jax.experimental.pallas import tpu as pltpu
from jax.sharding import PartitionSpec as P

D = 768
FF = 3072
H = 12
PD = 384
PFF = 1536
PH = 12
PIX = 768
GRID = 14
NT = 4
LC = 128
STEP = 10
P_SIZE = 196
LT = 36
NBE = 52
NBP = 16
VE = 11520
VP = 6912
VW = 18432


NORM_EPS = 1e-06
ADAM_EPS = 1e-08
BETA_FIRST = 0.5
BETA_SECOND = 0.5
BETA_STATS = 0.95
RATE_MATRIX = 0.02
RATE_VECTOR = 0.05
DECAY_MATRIX = 0.04
EMA_KEEP = 0.996
CLIP_LIMIT = 1.0
NEG_FILL = -1000000000.0
WIRE = jnp.float16
WIRE_TOP = 16384.0
f32 = jnp.float32
bf = jnp.bfloat16


def from_behind(shard, axis, by):
    size = lax.axis_size(axis)
    pairs = [(i, i + by) for i in range(size) if 0 <= i + by < size]
    return lax.ppermute(shard, axis, pairs)


def enc_shapes():
    return [(PIX, D), (D, 3 * D), (D, D), (D, FF), (FF, D)]


def pred_shapes():
    return [(D, PD), (PD, 3 * PD), (PD, PD), (PD, PFF), (PFF, PD), (PD, D)]


def enc_lengths():
    return [D] * 8 + [FF, D, D, D]


def pred_lengths():
    return [PD] * 8 + [PFF, PD, PD, PD, D, PD]


def sincos(width):
    quarter = width // 4
    frequency = 1.0 / 10000.0 ** (jnp.arange(quarter, dtype=jnp.float32) / quarter)
    cell_ids = jnp.arange(P_SIZE)
    row_pos = (cell_ids // GRID).astype(jnp.float32)[:, None] * frequency
    column_pos = (cell_ids % GRID).astype(jnp.float32)[:, None] * frequency
    return jnp.concatenate(
        [jnp.sin(row_pos), jnp.cos(row_pos), jnp.sin(column_pos), jnp.cos(column_pos)], 1
    )


DIMS = {"nn": (1, 0), "nt": (1, 1), "tn": (0, 0)}

def parts_of(a, count):
    found = []
    for index in range(count):
        piece = a.astype(bf)
        found.append(piece)
        if index + 1 < count:
            a = a - piece.astype(f32)
    return found

def product(left, right, form, pairs):
    ld, rd = DIMS[form]
    lhs = jnp.concatenate([left[i] for i, _ in pairs], ld)
    rhs = jnp.concatenate([right[j] for _, j in pairs], rd)
    return lax.dot_general(lhs, rhs, (((ld,), (rd,)), ((), ())), preferred_element_type=f32)

THREE = ((0, 1), (1, 0), (0, 0))
SIX = ((0, 2), (2, 0), (1, 1), (0, 1), (1, 0), (0, 0))
def mul3(left, right, form="nn"):
    return product(left, right, form, THREE)
def mul6(left, right, form="nn"):
    return product(left, right, form, SIX)

def invert_factors(mats):
    n = mats[0].shape[0]
    lane = lax.broadcasted_iota(jnp.int32, (8, n), 1)
    sub = lax.broadcasted_iota(jnp.int32, (8, n), 0)
    groups = [[a[8 * t : 8 * t + 8, :] for t in range(n // 8)] for a in mats]
    for j in range(n):
        top, at_row = divmod(j, 8)
        here = lane == j
        pick = jnp.full((8, n), j, jnp.int32)
        for tiles in groups:
            column = jnp.take_along_axis(tiles[top], pick, axis=1)
            pivot = jnp.broadcast_to(column[at_row : at_row + 1, :], (8, n))
            row = jnp.broadcast_to(tiles[top][at_row : at_row + 1, :], (8, n))
            scaled = jnp.where(here, 1.0, row) * (1.0 / pivot)
            for t in range(top, n // 8):
                if t > top:
                    column = jnp.take_along_axis(tiles[t], pick, axis=1)
                fresh = jnp.where(here, 0.0, tiles[t]) - column * scaled
                tiles[t] = jnp.where(sub > at_row, fresh, tiles[t]) if t == top else fresh
    results = []
    for tiles in groups:
        rows = []
        for t in range(n // 8):
            at = sub + 8 * t
            pivots = jnp.sum(jnp.where(lane == at, tiles[t], 0.0), axis=1, keepdims=True)
            unit = jnp.where(lane < at, tiles[t], jnp.where(lane == at, 1.0, 0.0))
            rows.append(unit * lax.rsqrt(pivots))
        results.append(jnp.concatenate(rows, 0))
    return results

def first_kernel(flag, factor, g_ref, w_ref, m_ref, v_ref, l_ref, r_ref, e_ref, f_ref,
                 w_out, m_out, v_out, e_out, f_out, base_out, gram_out):
    on = flag[pl.program_id(0)] != 0

    @pl.when(jnp.logical_not(on))
    def keep():
        for source, target in ((w_ref, w_out), (m_ref, m_out), (v_ref, v_out), (e_ref, e_out), (f_ref, f_out)):
            target[...] = source[...]

    @pl.when(on)
    def update():
        correct_one = 1.0 - BETA_FIRST**STEP
        correct_two = 1.0 - BETA_SECOND**STEP
        grad = parts_of(g_ref[0] * factor[0], 3)
        left = parts_of(l_ref[0], 3)
        right = parts_of(r_ref[0], 3)
        rotated = mul3(left, parts_of(mul3(grad, right), 2), "tn")
        moment = BETA_FIRST * m_ref[0] + (1.0 - BETA_FIRST) * rotated
        second = BETA_SECOND * v_ref[0] + (1.0 - BETA_SECOND) * rotated * rotated
        m_out[0] = moment
        v_out[0] = second
        normed = moment / correct_one / (jnp.sqrt(second / correct_two) + ADAM_EPS)
        weight = w_ref[0]
        step = mul3(left, parts_of(mul3(parts_of(normed, 2), right, "nt"), 2))
        w_out[0] = weight - RATE_MATRIX * (step + DECAY_MATRIX * weight)
        for index, (stat, target, basis, form) in enumerate(
            ((e_ref, e_out, left, "nt"), (f_ref, f_out, right, "tn"))
        ):
            fresh = BETA_STATS * stat[0] + (1.0 - BETA_STATS) * mul6(grad, grad, form)
            target[0] = fresh
            moved = mul6(parts_of(fresh, 3), basis)
            base_out[0, index] = moved
            pieces = parts_of(moved, 3)
            gram_out[0, index] = mul6(pieces, pieces, "tn")

def factor_kernel(flag, base_ref, gram_ref, q_out, base, gram, inverse):
    blocks, edge = base_ref.shape[0], base_ref.shape[-1]
    panel = 128
    count = edge // panel
    base[...] = base_ref[...]
    gram[...] = gram_ref[...]

    def stage(k):
        at = pl.ds(panel * k, panel)
        start = panel * k
        spot = slice(start, start + panel)
        rest = slice(start + panel, edge)

        def block(b, carry):
            @pl.when(flag[b] != 0)
            def run():
                for side in range(2):
                    inv = parts_of(inverse[b, side], 3)
                    q = mul6(parts_of(base[b, side, :, spot], 3), inv, "nt")
                    q_out[b, side, :, spot] = q
                    if k + 1 < count:
                        p = parts_of(mul6(inv, parts_of(gram[b, side, spot, rest], 3)), 3)
                        gram[b, side, rest, rest] = gram[b, side, rest, rest] - mul6(p, p, "tn")
                        base[b, side, :, rest] = base[b, side, :, rest] - mul6(parts_of(q, 3), p)
            return carry

        lax.fori_loop(0, blocks, block, 0)

    def turn(k, carry):
        for which in range(count):
            @pl.when(k == which)
            def load():
                spot = slice(panel * which, panel * which + panel)
                for b in range(blocks):
                    for side in range(2):
                        inverse[b, side] = gram[b, side, spot, spot]
        mats = invert_factors([inverse[b, side] for b in range(blocks) for side in range(2)])
        for b in range(blocks):
            for side in range(2):
                inverse[b, side] = mats[2 * b + side]
        for which in range(count):
            @pl.when(k == which)
            def run():
                stage(which)
        return carry

    lax.fori_loop(0, count, turn, 0)

def last_kernel(flag, l_ref, r_ref, m_ref, q_ref, l_out, r_out, m_out):
    on = flag[pl.program_id(0)] != 0

    @pl.when(jnp.logical_not(on))
    def keep():
        l_out[...] = l_ref[...]
        r_out[...] = r_ref[...]
        m_out[...] = m_ref[...]

    @pl.when(on)
    def update():
        l_out[0] = q_ref[0, 0]
        r_out[0] = q_ref[0, 1]
        turn_left = mul3(parts_of(q_ref[0, 0], 2), parts_of(l_ref[0], 2), "tn")
        turn_right = mul3(parts_of(r_ref[0], 2), parts_of(q_ref[0, 1], 2), "tn")
        half = mul3(parts_of(turn_left, 2), parts_of(m_ref[0], 2))
        m_out[0] = mul3(parts_of(half, 2), parts_of(turn_right, 2))

PLAIN = (((1,), (0,)), ((), ()))
RIGHT_T = (((1,), (1,)), ((), ()))
LEFT_T = (((0,), (0,)), ((), ()))
ROOT_HALF = 0.7071067811865476
ROOT_TWO_PI = 2.5066282746310002


def mm(left, right, dims=PLAIN):
    return lax.dot_general(left, right, dims, preferred_element_type=f32)


def norm_parts(x):
    center = x - jnp.mean(x, -1, keepdims=True)
    inverse = lax.rsqrt(jnp.mean(center * center, -1, keepdims=True) + NORM_EPS)
    return center * inverse, inverse


def norm(x, gain, shift):
    return norm_parts(x)[0] * gain + shift


def norm_back(x, gain, grad):
    unit, inverse = norm_parts(x)
    grad_unit = grad * gain
    mean_one = jnp.mean(grad_unit, -1, keepdims=True)
    mean_two = jnp.mean(grad_unit * unit, -1, keepdims=True)
    back = inverse * (grad_unit - mean_one - unit * mean_two)
    return back, col_sum(grad * unit), col_sum(grad)


def col_sum(x):
    return jnp.sum(x, 0, keepdims=True)


def gelu(x):
    return 0.5 * x * (1.0 + lax.erf(x * ROOT_HALF))


def gelu_slope(x):
    return 0.5 * (1.0 + lax.erf(x * ROOT_HALF)) + x * jnp.exp(-0.5 * x * x) * (1.0 / ROOT_TWO_PI)


def offsets(lengths):
    result = [0]
    for length in lengths:
        result.append(result[-1] + length)
    return result


class Vec:
    def __init__(self, ref, lengths):
        self.ref, self.at = ref, offsets(lengths)

    def __getitem__(self, k):
        return self.ref[:, self.at[k] : self.at[k + 1]]

    def __setitem__(self, k, value):
        self.ref[:, self.at[k] : self.at[k + 1]] = value

    def part(self, k, start, size):
        return self.ref[:, pl.ds(pl.multiple_of(self.at[k] + start, 128), size)]

    def put_part(self, k, start, size, value):
        self.ref[:, pl.ds(pl.multiple_of(self.at[k] + start, 128), size)] = value


def load_blocks(table, slots, sems, first, shapes, targets):
    edge = table.shape[-1]
    groups = []
    j = first
    for (height, breadth), target in zip(shapes, targets):
        group = []
        for row in range(height // edge):
            for column in range(breadth // edge):
                if target is not None:
                    spot = target.at[pl.ds(row * edge, edge), pl.ds(column * edge, edge)]
                    group.append(pltpu.make_async_copy(table.at[slots[j]], spot, sems.at[j]))
                j += 1
        groups.append(group)
    return groups


def start_all(groups):
    for group in groups:
        for copy in group:
            copy.start()


def wait_group(group):
    for copy in group:
        copy.wait()


def head_masks(rows, heads, width):
    lane = lax.broadcasted_iota(jnp.int32, (rows, 128), 1)
    size = width // heads
    return [(lane >= size * h) & (lane < size * h + size) for h in range(128 // size)]


def as_factors(masks):
    return [jnp.where(mask, 1.0, 0.0).astype(bf) for mask in masks]


def soft(scores, allowed):
    scores = jnp.where(allowed, scores, NEG_FILL)
    top = jnp.max(scores, -1, keepdims=True)
    raised = jnp.exp(scores - top)
    return raised * (1.0 / jnp.sum(raised, -1, keepdims=True))


def attend(q_ref, k_ref, v_ref, valid_ref, out_ref, heads):
    images, rows, width = q_ref.shape
    keys = k_ref.shape[1]
    masks = head_masks(rows, heads, width)
    factors = as_factors(masks)

    def group(p, carry):
        lanes = pl.ds(pl.multiple_of(128 * p, 128), 128)
        for i in range(images):
            q, k, v = q_ref[i, :, lanes], k_ref[i, :, lanes], v_ref[i, :, lanes]
            allowed = jnp.broadcast_to(valid_ref[i], (rows, keys)) > 0.0
            result = jnp.zeros((rows, 128), f32)
            for mask, factor in zip(masks, factors):
                probs = soft(mm(q * factor, k, RIGHT_T), allowed)
                result = jnp.where(mask, mm(probs.astype(bf), v), result)
            out_ref[i, :, lanes] = result.astype(bf)
        return carry

    lax.fori_loop(0, width // 128, group, 0)


def attend_back(q_ref, k_ref, v_ref, valid_ref, go_ref, dq_ref, dk_ref, dv_ref, heads):
    images, rows, width = q_ref.shape
    keys = k_ref.shape[1]
    masks = head_masks(rows, heads, width)
    key_masks = head_masks(keys, heads, width)
    factors = as_factors(masks)
    scale = 1.0 / math.sqrt(width // heads)

    def group(p, carry):
        lanes = pl.ds(pl.multiple_of(128 * p, 128), 128)
        for i in range(images):
            q, k, v = q_ref[i, :, lanes], k_ref[i, :, lanes], v_ref[i, :, lanes]
            go = go_ref[i, :, lanes]
            allowed = jnp.broadcast_to(valid_ref[i], (rows, keys)) > 0.0
            dq = jnp.zeros((rows, 128), f32)
            dk = jnp.zeros((keys, 128), f32)
            dv = jnp.zeros((keys, 128), f32)
            for mask, key_mask, factor in zip(masks, key_masks, factors):
                probs = soft(mm(q * factor, k, RIGHT_T), allowed)
                dv = jnp.where(key_mask, mm(probs.astype(bf), go, LEFT_T), dv)
                dprobs = mm(go * factor, v, RIGHT_T)
                dscores = probs * (dprobs - jnp.sum(dprobs * probs, -1, keepdims=True))
                low = dscores.astype(bf)
                dq = jnp.where(mask, mm(low, k) * scale, dq)
                dk = jnp.where(key_mask, mm(low, q, LEFT_T), dk)
            dq_ref[i, :, lanes] = dq
            dk_ref[i, :, lanes] = dk
            dv_ref[i, :, lanes] = dv
        return carry

    lax.fori_loop(0, width // 128, group, 0)


def split_rows(ref, value):
    images, rows, _ = ref.shape
    for i in range(images):
        ref[i] = value[rows * i : rows * i + rows].astype(ref.dtype)


def flat(ref):
    return jnp.concatenate([ref[i] for i in range(ref.shape[0])], 0)


STRIP = 384


def feed_forward(normed, mid, up, down, vec, pre_ref, acc_ref):
    acc_ref[...] = mid

    def strip(c, carry):
        lanes = pl.ds(pl.multiple_of(c * STRIP, 128), STRIP)
        pre = mm(normed, up[:, lanes]) + vec.part(8, c * STRIP, STRIP)
        if pre_ref is not None:
            pre_ref[:, lanes] = pre
        acc_ref[...] += mm(gelu(pre).astype(bf), down[lanes, :])
        return carry

    lax.fori_loop(0, up.shape[1] // STRIP, strip, 0)
    return acc_ref[...] + vec[9]


def encoder_kernel(
    slots, table, rows_ref, pos_ref, valid_ref, vec_ref,
    z_out, e_out, q_out, k_out, v_out, att_out, mid_out, pre_out, hid_out,
    wp, wqkv, wo, w1, w2, acc, sems,
):
    vec = Vec(vec_ref, enc_lengths())
    groups = load_blocks(table, slots, sems, 0, enc_shapes(), (wp, wqkv, wo, w1, w2))
    start_all(groups)
    wait_group(groups[0])
    e = mm(rows_ref[...], wp[...]) + vec[0] + pos_ref[...]
    e_out[...] = e
    normed = norm(e, vec[1], vec[2]).astype(bf)
    wait_group(groups[1])
    split_rows(q_out, (mm(normed, wqkv[:, :D]) + vec[3]) * (1.0 / math.sqrt(D // H)))
    split_rows(k_out, mm(normed, wqkv[:, D : 2 * D]))
    split_rows(v_out, mm(normed, wqkv[:, 2 * D :]) + vec[4])
    attend(q_out, k_out, v_out, valid_ref, att_out, H)
    wait_group(groups[2])
    mid = e + mm(flat(att_out), wo[...]) + vec[5]
    mid_out[...] = mid
    hidden = norm(mid, vec[6], vec[7]).astype(bf)
    wait_group(groups[3])
    wait_group(groups[4])
    hid = feed_forward(hidden, mid, w1, w2, vec, pre_out, acc)
    hid_out[...] = hid
    z_out[...] = norm(hid, vec[10], vec[11]).astype(bf)


def target_kernel(
    slots, table, all_ref, pos_all_ref, some_ref, pos_some_ref, valid_ref, vec_ref,
    out_ref, wp, wqkv, wo, w1, w2, q, k, v, att, acc, sems,
):
    vec = Vec(vec_ref, enc_lengths())
    groups = load_blocks(table, slots, sems, 0, enc_shapes(), (wp, wqkv, wo, w1, w2))
    start_all(groups)
    wait_group(groups[0])
    e = mm(all_ref[...], wp[...]) + vec[0] + pos_all_ref[...]
    normed = norm(e, vec[1], vec[2]).astype(bf)
    wait_group(groups[1])
    split_rows(k, mm(normed, wqkv[:, D : 2 * D]))
    split_rows(v, mm(normed, wqkv[:, 2 * D :]) + vec[4])
    e = mm(some_ref[...], wp[...]) + vec[0] + pos_some_ref[...]
    normed = norm(e, vec[1], vec[2]).astype(bf)
    split_rows(q, (mm(normed, wqkv[:, :D]) + vec[3]) * (1.0 / math.sqrt(D // H)))
    attend(q, k, v, valid_ref, att, H)
    wait_group(groups[2])
    mid = e + mm(flat(att), wo[...]) + vec[5]
    hidden = norm(mid, vec[6], vec[7]).astype(bf)
    wait_group(groups[3])
    wait_group(groups[4])
    hid = feed_forward(hidden, mid, w1, w2, vec, None, acc)
    out_ref[...] = norm_parts(norm(hid, vec[10], vec[11]))[0]


def put_block(ref, value, j, depth):
    edge = value.shape[-1]
    if depth % 8:
        ref[j] = value
    else:
        ref[:, depth * j : depth * j + depth, :] = value.reshape(edge // depth, depth, edge)


def raise_top(top_ref, value):
    top_ref[...] = jnp.maximum(top_ref[...], jnp.max(jnp.abs(value), 0, keepdims=True))


def predictor_kernel(
    depth, slots, table, z_ref, pos_c_ref, pos_t_ref, valid_ref, tgt_ref, tmask_ref, vec_ref,
    dz_out, flow_a, flow_b, vec_out, loss_out, top_out,
    win, wqkv, wo, w1, w2, wout, q, k, v, att, go, dq, dk, dv, pre_ref, act_ref, dpre_ref, acc, sems,
):
    vec, grads = Vec(vec_ref, pred_lengths()), Vec(vec_out, pred_lengths())
    edge = table.shape[-1]
    half = flow_split(NBP)
    images = z_ref.shape[0] // LC
    groups = load_blocks(table, slots, sems, NBE, pred_shapes(), (win, wqkv, wo, w1, w2, wout))
    start_all(groups)
    for group in groups:
        wait_group(group)
    firsts = offsets([h * b // (edge * edge) for h, b in pred_shapes()])

    def store(index, matrix):
        for row in range(matrix.shape[0] // edge):
            for column in range(matrix.shape[1] // edge):
                j = firsts[index] + row * (pred_shapes()[index][1] // edge) + column
                value = matrix[row * edge : row * edge + edge, column * edge : column * edge + edge]
                raise_top(top_out, value)
                if j < half:
                    put_block(flow_a, value, j, depth)
                else:
                    put_block(flow_b, value, j - half, depth)

    top_out[...] = jnp.zeros_like(top_out)
    z = z_ref[...]
    x_c = mm(z, win[...]) + vec[0] + pos_c_ref[...]
    x_t = vec[13] + pos_t_ref[...]
    n_c = norm(x_c, vec[1], vec[2]).astype(bf)
    n_t = norm(x_t, vec[1], vec[2]).astype(bf)
    split_rows(q, (mm(n_t, wqkv[:, :PD]) + vec[3]) * (1.0 / math.sqrt(PD // PH)))
    for ref, start, bias in ((k, PD, 0.0), (v, 2 * PD, vec[4])):
        of_c = mm(n_c, wqkv[:, start : start + PD]) + bias
        of_t = mm(n_t, wqkv[:, start : start + PD]) + bias
        count = NT * LT
        for i in range(images):
            ref[i, :LC, :] = of_c[LC * i : LC * i + LC].astype(bf)
            ref[i, LC:, :] = of_t[count * i : count * i + count].astype(bf)
    attend(q, k, v, valid_ref, att, PH)
    mid = x_t + mm(flat(att), wo[...]) + vec[5]
    n_two = norm(mid, vec[6], vec[7]).astype(bf)
    y = feed_forward(n_two, mid, w1, w2, vec, pre_ref, acc)
    n_three = norm(y, vec[10], vec[11]).astype(bf)
    difference = mm(n_three, wout[...]) + vec[12] - tgt_ref[...]
    tmask = tmask_ref[...]
    magnitude = jnp.abs(difference)
    loss = jnp.where(magnitude < 1.0, 0.5 * difference * difference, magnitude - 0.5) * tmask
    loss_out[...] = col_sum(loss)
    grad = jnp.clip(difference, -1.0, 1.0) * tmask

    grads[12] = col_sum(grad)
    low = grad.astype(bf)
    store(5, mm(n_three.T, low))
    dy, grads[10], grads[11] = norm_back(y, vec[10], mm(low, wout[...], RIGHT_T))
    grads[9] = col_sum(dy)
    low = dy.astype(bf)
    acc[...] = jnp.zeros_like(acc)

    def strip(c, carry):
        lanes = pl.ds(pl.multiple_of(c * STRIP, 128), STRIP)
        pre = pre_ref[:, lanes]
        act_ref[:, lanes] = gelu(pre).astype(bf)
        dpre = mm(low, w2[lanes, :], RIGHT_T) * gelu_slope(pre)
        grads.put_part(8, c * STRIP, STRIP, col_sum(dpre))
        dpre = dpre.astype(bf)
        dpre_ref[:, lanes] = dpre
        acc[...] += mm(dpre, w1[:, lanes], RIGHT_T)
        return carry

    lax.fori_loop(0, PFF // STRIP, strip, 0)
    store(4, mm(act_ref[...].T, low))
    store(3, mm(n_two.T, dpre_ref[...]))
    dmid, grads[6], grads[7] = norm_back(mid, vec[6], acc[...])
    dmid = dmid + dy
    grads[5] = col_sum(dmid)
    low = dmid.astype(bf)
    split_rows(go, mm(low, wo[...], RIGHT_T))
    store(2, mm(flat(att).T, low))
    attend_back(q, k, v, valid_ref, go, dq, dk, dv, PH)
    d_q, d_k, d_v = flat(dq), [dk[i] for i in range(images)], [dv[i] for i in range(images)]
    grads[3] = col_sum(d_q)
    grads[4] = sum(col_sum(part) for part in d_v)
    q_low = d_q.astype(bf)
    k_c = jnp.concatenate([part[:LC] for part in d_k], 0).astype(bf)
    k_t = jnp.concatenate([part[LC:] for part in d_k], 0).astype(bf)
    v_c = jnp.concatenate([part[:LC] for part in d_v], 0).astype(bf)
    v_t = jnp.concatenate([part[LC:] for part in d_v], 0).astype(bf)
    n_c_t, n_t_t = n_c.T, n_t.T
    store(
        1,
        jnp.concatenate(
            [mm(n_t_t, q_low), mm(n_c_t, k_c) + mm(n_t_t, k_t), mm(n_c_t, v_c) + mm(n_t_t, v_t)], 1
        ),
    )
    wq, wk, wv = wqkv[:, :PD], wqkv[:, PD : 2 * PD], wqkv[:, 2 * PD :]
    dn_t = mm(q_low, wq, RIGHT_T) + mm(k_t, wk, RIGHT_T) + mm(v_t, wv, RIGHT_T)
    dn_c = mm(k_c, wk, RIGHT_T) + mm(v_c, wv, RIGHT_T)
    dx_t, gain_t, shift_t = norm_back(x_t, vec[1], dn_t)
    dx_c, gain_c, shift_c = norm_back(x_c, vec[1], dn_c)
    grads[1] = gain_t + gain_c
    grads[2] = shift_t + shift_c
    dx_t = dx_t + dmid
    grads[13] = col_sum(dx_t)
    grads[0] = col_sum(dx_c)
    low = dx_c.astype(bf)
    dz_out[...] = mm(low, win[...], RIGHT_T).astype(bf)
    store(0, mm(z.T, low))


def flow_split(count):
    return (count // 2 + 3) // 4 * 4


def encoder_back_kernel(
    depth, slots, table, dz_ref, rows_ref, e_ref, q, k, v, att_ref, mid_ref, pre_ref, hid_ref, valid_ref, vec_ref,
    flow_a, flow_b, vec_out, top_out,
    wqkv, wo, w1, w2, go, dq, dk, dv, act_t, dpre_ref, x_t, dqkv, acc, stage, sems, out_sems,
):
    vec, grads = Vec(vec_ref, enc_lengths()), Vec(vec_out, enc_lengths())
    edge = table.shape[-1]
    half = flow_split(NBE)
    groups = load_blocks(table, slots, sems, 0, enc_shapes(), (None, wqkv, wo, w1, w2))
    start_all(groups[::-1])
    firsts = offsets([h * b // (edge * edge) for h, b in enc_shapes()])
    sent = []

    def store(index, left_t, right):
        columns = enc_shapes()[index][1] // edge
        rows = enc_shapes()[index][0] // edge
        for first in range(0, rows * columns, 4):
            turn = len(sent)
            slot = turn % 2
            if turn >= 2:
                sent[turn - 2].wait()
            for b in range(4):
                row, column = divmod(first + b, columns)
                value = mm(
                    left_t[row * edge : row * edge + edge, :],
                    right[:, column * edge : column * edge + edge],
                )
                raise_top(top_out, value)
                put_block(stage.at[slot], value, b, depth)
            j = firsts[index] + first
            target, start = (flow_a, j) if j < half else (flow_b, j - half)
            if depth % 8:
                spot = target.at[pl.ds(start, 4)]
            else:
                spot = target.at[:, pl.ds(depth * start, 4 * depth), :]
            copy = pltpu.make_async_copy(stage.at[slot], spot, out_sems.at[turn])
            copy.start()
            sent.append(copy)

    top_out[...] = jnp.zeros_like(top_out)
    hid = hid_ref[...]
    dy, grads[10], grads[11] = norm_back(hid, vec[10], dz_ref[...].astype(f32))
    grads[9] = col_sum(dy)
    low = dy.astype(bf)
    wait_group(groups[4])
    wait_group(groups[3])
    acc[...] = jnp.zeros_like(acc)

    def strip(c, carry):
        lanes = pl.ds(pl.multiple_of(c * STRIP, 128), STRIP)
        pre = pre_ref[:, lanes]
        act_t[lanes, :] = gelu(pre).astype(bf).T
        dpre = mm(low, w2[lanes, :], RIGHT_T) * gelu_slope(pre)
        grads.put_part(8, c * STRIP, STRIP, col_sum(dpre))
        dpre = dpre.astype(bf)
        dpre_ref[:, lanes] = dpre
        acc[...] += mm(dpre, w1[:, lanes], RIGHT_T)
        return carry

    lax.fori_loop(0, FF // STRIP, strip, 0)
    dqkv[:, :D] = low
    store(4, act_t, dqkv)
    mid = mid_ref[...]
    unit, _ = norm_parts(mid)
    x_t[...] = (unit * vec[6] + vec[7]).astype(bf).T
    store(3, x_t, dpre_ref)
    dmid, grads[6], grads[7] = norm_back(mid, vec[6], acc[...])
    dmid = dmid + dy
    acc[...] = dmid
    grads[5] = col_sum(dmid)
    low = dmid.astype(bf)
    wait_group(groups[2])
    wait_group(groups[1])
    split_rows(go, mm(low, wo[...], RIGHT_T))
    x_t[...] = flat(att_ref).T
    dqkv[:, :D] = low
    store(2, x_t, dqkv)
    attend_back(q, k, v, valid_ref, go, dq, dk, dv, H)
    d_q, d_v = flat(dq), flat(dv)
    grads[3] = col_sum(d_q)
    grads[4] = col_sum(d_v)
    dqkv[:, :D] = d_q.astype(bf)
    dqkv[:, D : 2 * D] = flat(dk).astype(bf)
    dqkv[:, 2 * D :] = d_v.astype(bf)
    e = e_ref[...]
    x_t[...] = norm(e, vec[1], vec[2]).astype(bf).T
    store(1, x_t, dqkv)
    back, grads[1], grads[2] = norm_back(e, vec[1], mm(dqkv[...], wqkv[...], RIGHT_T))
    de = acc[...] + back
    grads[0] = col_sum(de)
    dqkv[:, :D] = de.astype(bf)
    x_t[...] = rows_ref[...].T
    store(0, x_t, dqkv)
    for copy in sent[-2:]:
        copy.wait()


def spaces(count):
    return [pl.BlockSpec(memory_space=pltpu.VMEM)] * count


ANYWHERE = pl.BlockSpec(memory_space=pl.ANY)


def weight_scratch(shapes):
    return [pltpu.VMEM(shape, bf) for shape in shapes]


def call_kernel(body, slots, args, any_args, outs, any_outs, scratch, name):
    specs = [ANYWHERE if i in any_args else spaces(1)[0] for i in range(len(args))]
    out_specs = [ANYWHERE if i in any_outs else spaces(1)[0] for i in range(len(outs))]
    return pl.pallas_call(
        body,
        grid_spec=pltpu.PrefetchScalarGridSpec(
            num_scalar_prefetch=1, grid=(), in_specs=specs, out_specs=out_specs, scratch_shapes=scratch
        ),
        out_shape=[jax.ShapeDtypeStruct(shape, kind) for shape, kind in outs],
        compiler_params=pltpu.CompilerParams(vmem_limit_bytes=58 << 20),
        name=name,
    )(slots, *args)


def flow_shapes(count, edge, ranks):
    half = flow_split(count)
    if (edge // ranks) % 8:
        return [((n, edge, edge), f32) for n in (half, count - half)]
    return [((ranks, edge // ranks * n, edge), f32) for n in (half, count - half)]


def encoder_call(slots, table, rows, pos, valid, vec):
    n = rows.shape[0]
    images = n // LC
    per = (images, LC, D)
    outs = [((n, D), bf), ((n, D), f32), (per, bf), (per, bf), (per, bf), (per, bf)]
    outs += [((n, D), f32), ((n, FF), f32), ((n, D), f32)]
    scratch = weight_scratch(enc_shapes()) + [pltpu.VMEM((n, D), f32), pltpu.SemaphoreType.DMA((NBE,))]
    return call_kernel(
        encoder_kernel, slots, (table, rows, pos, valid, vec), (0,), outs, (), scratch, "encoder_forward"
    )


def target_call(slots, table, rows, pos, some, pos_some, valid, vec, images):
    n = some.shape[0]
    keys = rows.shape[0] // images
    per, wide = (images, n // images, D), (images, keys, D)
    scratch = weight_scratch(enc_shapes()) + [
        pltpu.VMEM(per, bf),
        pltpu.VMEM(wide, bf),
        pltpu.VMEM(wide, bf),
        pltpu.VMEM(per, bf),
        pltpu.VMEM((n, D), f32),
        pltpu.SemaphoreType.DMA((NBE,)),
    ]
    args = (table, rows, pos, some, pos_some, valid, vec)
    return call_kernel(target_kernel, slots, args, (0,), [((n, D), f32)], (), scratch, "target_forward")[0]


def predictor_call(slots, table, z, pos_c, pos_t, valid, tgt, tmask, vec, ranks):
    n, m = z.shape[0], pos_t.shape[0]
    images = n // LC
    rows, keys = m // images, valid.shape[-1]
    edge = table.shape[-1]
    per, wide = (images, rows, PD), (images, keys, PD)
    outs = [((n, D), bf)] + flow_shapes(NBP, edge, ranks) + [((1, VP), f32), ((1, D), f32), ((1, edge), f32)]
    scratch = weight_scratch(pred_shapes()) + [
        pltpu.VMEM(per, bf),
        pltpu.VMEM(wide, bf),
        pltpu.VMEM(wide, bf),
        pltpu.VMEM(per, bf),
        pltpu.VMEM(per, bf),
        pltpu.VMEM(per, f32),
        pltpu.VMEM(wide, f32),
        pltpu.VMEM(wide, f32),
        pltpu.VMEM((m, PFF), f32),
        pltpu.VMEM((m, PFF), bf),
        pltpu.VMEM((m, PFF), bf),
        pltpu.VMEM((m, PD), f32),
        pltpu.SemaphoreType.DMA((NBE + NBP,)),
    ]
    args = (table, z, pos_c, pos_t, valid, tgt, tmask, vec)
    body = functools.partial(predictor_kernel, edge // ranks)
    return call_kernel(body, slots, args, (0,), outs, (), scratch, "predictor_step")


def encoder_back_call(slots, table, dz, rows, kept, valid, vec, ranks):
    n = rows.shape[0]
    images = n // LC
    edge = table.shape[-1]
    per = (images, LC, D)
    e, q, k, v, att, mid, pre, hid = kept
    depth = edge // ranks
    stage = (2, ranks, 4 * depth, edge) if depth % 8 == 0 else (2, 4, edge, edge)
    scratch = weight_scratch(enc_shapes()[1:]) + [
        pltpu.VMEM(per, bf),
        pltpu.VMEM(per, f32),
        pltpu.VMEM(per, f32),
        pltpu.VMEM(per, f32),
        pltpu.VMEM((FF, n), bf),
        pltpu.VMEM((n, FF), bf),
        pltpu.VMEM((D, n), bf),
        pltpu.VMEM((n, 3 * D), bf),
        pltpu.VMEM((n, D), f32),
        pltpu.VMEM(stage, f32),
        pltpu.SemaphoreType.DMA((NBE,)),
        pltpu.SemaphoreType.DMA((NBE // 4,)),
    ]
    outs = flow_shapes(NBE, edge, ranks) + [((1, VE), f32), ((1, edge), f32)]
    args = (table, dz, rows, e, q, k, v, att, mid, pre, hid, valid, vec)
    body = functools.partial(encoder_back_kernel, edge // ranks)
    return call_kernel(body, slots, args, (0,), outs, (0, 1), scratch, "encoder_backward")


def soap_first(flags, factor, *arrays):
    n, e = arrays[0].shape[:2]
    one = pl.BlockSpec((1, e, e), lambda i, *_: (i, 0, 0))
    two = pl.BlockSpec((1, 2, e, e), lambda i, *_: (i, 0, 0, 0))
    single = jax.ShapeDtypeStruct((n, e, e), f32)
    double = jax.ShapeDtypeStruct((n, 2, e, e), f32)
    return pl.pallas_call(
        first_kernel,
        grid_spec=pltpu.PrefetchScalarGridSpec(
            num_scalar_prefetch=2, grid=(n,), in_specs=[one] * 8, out_specs=[one] * 5 + [two] * 2
        ),
        out_shape=[single] * 5 + [double] * 2,
        compiler_params=pltpu.CompilerParams(vmem_limit_bytes=56 << 20),
        name="soap_first",
    )(flags, factor, *arrays)


def soap_factor(flags, base, gram):
    n, _, e, _ = base.shape
    whole = pl.BlockSpec(memory_space=pltpu.VMEM)
    return pl.pallas_call(
        factor_kernel,
        grid_spec=pltpu.PrefetchScalarGridSpec(
            num_scalar_prefetch=1,
            grid=(),
            in_specs=[whole] * 2,
            out_specs=whole,
            scratch_shapes=[
                pltpu.VMEM((n, 2, e, e), f32),
                pltpu.VMEM((n, 2, e, e), f32),
                pltpu.VMEM((n, 2, 128, 128), f32),
            ],
        ),
        out_shape=jax.ShapeDtypeStruct(base.shape, f32),
        compiler_params=pltpu.CompilerParams(vmem_limit_bytes=56 << 20),
        name="soap_factor",
    )(flags, base, gram)


def soap_last(flags, left, right, moment, fresh):
    n, e = left.shape[:2]
    one = pl.BlockSpec((1, e, e), lambda i, *_: (i, 0, 0))
    two = pl.BlockSpec((1, 2, e, e), lambda i, *_: (i, 0, 0, 0))
    return pl.pallas_call(
        last_kernel,
        grid_spec=pltpu.PrefetchScalarGridSpec(
            num_scalar_prefetch=1, grid=(n,), in_specs=[one] * 3 + [two], out_specs=[one] * 3
        ),
        out_shape=[jax.ShapeDtypeStruct((n, e, e), f32)] * 3,
        compiler_params=pltpu.CompilerParams(vmem_limit_bytes=56 << 20),
        name="soap_last",
    )(flags, left, right, moment, fresh)


def place_shares(slots, second, enc_share, pred_share, slot_rows):
    depth, edge = enc_share.shape[1:]

    def body(slots_ref, second_ref, enc_ref, pred_ref, out_ref):
        def run(source, first, count):
            def copy(j, carry):
                out_ref[slots_ref[first + j]] = source[j]
                return carry

            lax.fori_loop(0, count, copy, 0)

        @pl.when(second_ref[0] == 0)
        def enc():
            run(enc_ref, 0, NBE)

        @pl.when(second_ref[0] != 0)
        def pred():
            run(pred_ref, NBE, NBP)

    return pl.pallas_call(
        body,
        grid_spec=pltpu.PrefetchScalarGridSpec(
            num_scalar_prefetch=2,
            grid=(),
            in_specs=[pl.BlockSpec(memory_space=pltpu.VMEM)] * 2,
            out_specs=pl.BlockSpec(memory_space=pltpu.VMEM),
        ),
        out_shape=jax.ShapeDtypeStruct((slot_rows, depth, edge), f32),
        compiler_params=pltpu.CompilerParams(vmem_limit_bytes=40 << 20),
        name="place_shares",
    )(slots, second, enc_share, pred_share)


class Exchange:
    def __init__(self, sections):
        self.ranks = lax.axis_size("dp")
        self.bits = self.ranks.bit_length() - 1
        self.sections = sections

    def swap(self, value, bit):
        pairs = [
            (s * self.ranks + i, s * self.ranks + (i ^ (1 << bit)))
            for s in self.sections
            for i in range(self.ranks)
        ]
        return lax.ppermute(value, ("section", "dp"), pairs)

    def total(self, value):
        for bit in range(self.bits):
            value = value + self.swap(value, bit)
        return value


def wire_exponent(bound):
    return jnp.floor(jnp.log2(WIRE_TOP / jnp.maximum(bound, 1e-30)))


def pack(values, exponent, axis):
    shape = list(values.shape)
    shape[axis] = 16
    mark = jnp.full(shape, exponent)
    return jnp.concatenate([values * jnp.exp2(exponent), mark], axis).astype(WIRE)


def halve(exchange, flows, orders, bound):
    bits = exchange.bits
    me = lax.axis_index("dp")
    parts = [f.reshape((2,) * bits + f.shape[1:]) for f in flows]
    bounds = [bound for _ in flows]
    left = [list(range(bits - 1, -1, -1)) for _ in flows]
    for stage in range(bits):
        arrived = []
        for k, part in enumerate(parts):
            bit = orders[k][stage]
            axis = left[k].index(bit)
            give = lax.dynamic_index_in_dim(part, 1 - ((me >> bit) & 1), axis, keepdims=False)
            low = pack(give.reshape(-1, give.shape[-1]), wire_exponent(bounds[k]), 0)
            arrived.append(exchange.swap(low, bit))
        for k, part in enumerate(parts):
            bit = orders[k][stage]
            axis = left[k].index(bit)
            keep = lax.dynamic_index_in_dim(part, (me >> bit) & 1, axis, keepdims=False)
            unscale = jnp.exp2(-arrived[k][-1, 0].astype(f32))
            got = arrived[k][:-16].astype(f32) * unscale
            parts[k] = keep + got.reshape(keep.shape)
            bounds[k] = bounds[k] + WIRE_TOP * unscale
            left[k].remove(bit)
    return parts, sum(bounds)


def by_share(flow, ranks):
    if flow.shape[0] == ranks and flow.shape[1] != flow.shape[2]:
        return flow
    blocks, edge = flow.shape[:2]
    cut = flow.reshape(blocks, ranks, edge // ranks, edge)
    return cut.transpose(1, 0, 2, 3).reshape(ranks, -1, edge)


def zeros_of(shapes):
    return jax.tree.map(lambda leaf: jnp.zeros(leaf.shape, leaf.dtype), shapes)


def on_device(
    pixels,
    ctx_idx,
    ctx_len,
    tgt_idx,
    tgt_len,
    slot_of,
    weights,
    first_moment,
    second_moment,
    left_basis,
    right_basis,
    left_stats,
    right_stats,
    vectors,
    vector_first,
    vector_second,
):
    section_index = lax.axis_index("section")
    owner_index = lax.axis_index("dp")
    ranks = lax.axis_size("dp")
    is_first = section_index == 0
    second = section_index.astype(jnp.int32).reshape(1)
    slot_count = weights.shape[1]
    edge = weights.shape[-1]
    slot_rows = slot_count * ranks
    table = lax.all_gather(weights[0].astype(bf), "dp", axis=0, tiled=True)
    enc_slots = slot_of[:NBE]
    pred_slots = slot_of[NBE:]
    row_now = vectors[0]
    enc_vec_now = lax.dynamic_slice_in_dim(row_now, section_index * VP, VE)[None]
    pred_vec_now = row_now[None, :VP]
    pos_enc = sincos(D)
    pos_pred = sincos(PD)
    images = ctx_idx.shape[0]
    rows_all = -(-P_SIZE // 16) * 16
    tgt_flat = tgt_idx.reshape(images, NT * LT)
    ctx_valid = (jnp.arange(LC)[None, :] < ctx_len[:, None]).astype(f32)
    tgt_valid = (jnp.arange(LT)[None, None, :] < tgt_len[:, :, None]).astype(f32)
    tgt_valid = tgt_valid.reshape(images, NT * LT)
    joined_valid = jnp.concatenate([ctx_valid, tgt_valid], 1)[:, None, :]
    all_valid = (jnp.arange(rows_all) < P_SIZE).astype(f32)
    all_valid = jnp.broadcast_to(all_valid, (images, 1, rows_all))

    def pick(index):
        return (index[..., None] == jnp.arange(P_SIZE)).astype(f32)

    ctx_hot = pick(ctx_idx)
    tgt_hot = pick(tgt_flat)

    def choose(hot, values):
        return jnp.einsum(
            "njp,pd->njd", hot, values, precision=lax.Precision.HIGHEST, preferred_element_type=f32
        ).reshape(-1, values.shape[-1])

    def choose_pixels(hot):
        picked = jnp.einsum("njp,npd->njd", hot.astype(bf), pixels, preferred_element_type=f32)
        return picked.astype(bf).reshape(-1, PIX)

    pixel_rows = choose_pixels(ctx_hot)
    enc_pos_ctx = choose(ctx_hot, pos_enc)
    padding = ((0, 0), (0, rows_all - P_SIZE), (0, 0))
    pixel_all = jnp.pad(pixels, padding).reshape(-1, PIX)
    pos_all = jnp.broadcast_to(jnp.pad(pos_enc[None], padding), (images, rows_all, D)).reshape(-1, D)
    pixel_tgt = choose_pixels(tgt_hot)
    enc_pos_tgt = choose(tgt_hot, pos_enc)
    pred_pos_ctx = choose(ctx_hot, pos_pred)
    pred_pos_tgt = choose(tgt_hot, pos_pred)

    def run_encoder(unused):
        return encoder_call(slot_of, table, pixel_rows, enc_pos_ctx, ctx_valid[:, None, :], enc_vec_now)

    encoder_shapes = jax.eval_shape(run_encoder, 0)

    def enc_branch(unused):
        return run_encoder(0), jnp.zeros((images * NT * LT, D), f32)

    def tgt_branch(unused):
        target = target_call(
            slot_of, table, pixel_all, pos_all, pixel_tgt, enc_pos_tgt, all_valid, enc_vec_now, images
        )
        return zeros_of(encoder_shapes), target

    encoded, target = lax.cond(is_first, enc_branch, tgt_branch, 0)
    context = from_behind(encoded[0], "section", 1)

    def run_predictor(unused):
        return predictor_call(
            slot_of,
            table,
            context,
            pred_pos_ctx,
            pred_pos_tgt,
            joined_valid,
            target,
            tgt_valid.reshape(-1, 1),
            pred_vec_now,
            ranks,
        )

    predictor_shapes = jax.eval_shape(run_predictor, 0)
    back_send, pred_a, pred_b, pred_vec, loss_lanes, pred_top = lax.cond(
        is_first, lambda unused: zeros_of(predictor_shapes), run_predictor, 0
    )
    incoming = from_behind(back_send, "section", -1)
    loss_local = jnp.sum(loss_lanes)

    low_order = list(range(Exchange((0,)).bits))
    orders = [low_order, [1, 0] + low_order[2:] if len(low_order) > 1 else low_order]
    pred_flows = [by_share(flow, ranks) for flow in (pred_a, pred_b)]
    pred_parts, pred_bound = halve(Exchange((1,)), pred_flows, orders, jnp.max(pred_top))

    def run_encoder_back(unused):
        return encoder_back_call(
            slot_of,
            table,
            incoming,
            pixel_rows,
            encoded[1:],
            ctx_valid[:, None, :],
            enc_vec_now,
            ranks,
        )

    back_shapes = jax.eval_shape(run_encoder_back, 0)
    enc_a, enc_b, enc_vec, enc_top = lax.cond(
        is_first, run_encoder_back, lambda unused: zeros_of(back_shapes), 0
    )
    enc_flows = [by_share(flow, ranks) for flow in (enc_a, enc_b)]
    enc_parts, enc_bound = halve(Exchange((0,)), enc_flows, orders, jnp.max(enc_top))
    depth = edge // ranks
    enc_share = jnp.concatenate(enc_parts, 0).reshape(NBE, depth, edge)
    pred_share = jnp.concatenate(pred_parts, 0).reshape(NBP, depth, edge)

    both = Exchange((0, 1))
    vec_local = jnp.where(is_first, enc_vec[0], jnp.pad(pred_vec[0], (0, VE - VP)))
    count_local = jnp.where(is_first, 0, jnp.sum(tgt_len)).astype(f32)
    scalars = jnp.pad(jnp.stack([loss_local, count_local]), (0, 126))
    summed = both.total(jnp.concatenate([vec_local, scalars]))
    vec_total = jnp.pad(summed[:VE], (0, VW - VE))
    share_squares = jnp.where(
        is_first, jnp.sum(enc_share * enc_share), jnp.sum(pred_share * pred_share)
    )
    squares = both.total(jnp.full((128,), share_squares))
    facts = jnp.stack([squares[0] + jnp.sum(summed[:VE] ** 2), summed[VE], summed[VE + 1]])
    facts = jnp.pad(facts, (0, 125))
    swap_sections = [(i, 1 - i) for i in range(2)]
    facts = facts + lax.ppermute(facts, "section", swap_sections)
    square_total, loss_total, count_total = facts[0], facts[1], facts[2]

    placed = place_shares(slot_of, second, enc_share, pred_share, slot_rows)
    exponent = wire_exponent(jnp.where(is_first, enc_bound, pred_bound))
    payload = pack(placed.reshape(ranks, slot_count * depth, edge), exponent, 1)
    owned = lax.all_to_all(payload, "dp", split_axis=0, concat_axis=0, tiled=True).astype(f32)
    unscale = jnp.exp2(-owned[:, -1:, :1])
    owned = (owned[:, : slot_count * depth] * unscale).reshape(ranks, slot_count, depth, edge)
    owned_sum = owned.transpose(1, 0, 2, 3).reshape(slot_count, edge, edge)

    own_ids = owner_index * slot_count + jnp.arange(slot_count)
    enc_here = jnp.any(own_ids[:, None] == enc_slots[None, :], 1)
    pred_here = jnp.any(own_ids[:, None] == pred_slots[None, :], 1)
    trained = jnp.where(is_first, enc_here, pred_here)
    ema_here = jnp.logical_and(jnp.logical_not(is_first), enc_here)
    positions = jnp.arange(VW)
    vec_trained = positions < jnp.where(is_first, VE, VP)
    vec_ema = jnp.logical_and(jnp.logical_not(is_first), positions >= VP)
    grad_norm = jnp.sqrt(square_total) / count_total
    factor = jnp.minimum(1.0, CLIP_LIMIT / (grad_norm + 1e-06)) / count_total

    flags = trained.astype(jnp.int32)
    new_weight, moment, new_second, new_estat, new_fstat, base, gram = soap_first(
        flags,
        factor.reshape(1),
        owned_sum,
        weights[0],
        first_moment[0],
        second_moment[0],
        left_basis[0],
        right_basis[0],
        left_stats[0],
        right_stats[0],
    )
    fresh_bases = soap_factor(flags, base, gram)
    new_left, new_right, new_first = soap_last(
        flags, left_basis[0], right_basis[0], moment, fresh_bases
    )

    correct_one = 1.0 - BETA_FIRST**STEP
    correct_two = 1.0 - BETA_SECOND**STEP
    vec_clipped = vec_total * factor
    fresh_first = BETA_FIRST * vector_first[0] + (1.0 - BETA_FIRST) * vec_clipped
    fresh_second = BETA_SECOND * vector_second[0] + (1.0 - BETA_SECOND) * vec_clipped * vec_clipped
    stepped = row_now - RATE_VECTOR * (fresh_first / correct_one) / (
        jnp.sqrt(fresh_second / correct_two) + ADAM_EPS
    )
    new_vec = jnp.where(vec_trained, stepped, row_now)
    new_vec_first = jnp.where(vec_trained, fresh_first, vector_first[0])
    new_vec_second = jnp.where(vec_trained, fresh_second, vector_second[0])
    from_encoder = from_behind(new_weight.astype(bf), "section", 1).astype(f32)
    vec_from_encoder = from_behind(new_vec.astype(bf), "section", 1).astype(f32)
    new_weight = jnp.where(
        ema_here[:, None, None], EMA_KEEP * weights[0] + (1.0 - EMA_KEEP) * from_encoder, new_weight
    )
    aligned = jnp.concatenate([jnp.zeros((VP,), f32), vec_from_encoder[:VE]])
    new_vec = jnp.where(vec_ema, EMA_KEEP * row_now + (1.0 - EMA_KEEP) * aligned, new_vec)
    return (
        loss_total,
        count_total,
        grad_norm,
        new_weight[None],
        new_first[None],
        new_second[None],
        new_left[None],
        new_right[None],
        new_estat[None],
        new_fstat[None],
        new_vec[None],
        new_vec_first[None],
        new_vec_second[None],
    )


def solution(mesh):
    in_specs = (
        P("dp", None, None),
        P("dp", None),
        P("dp"),
        P("dp", None, None),
        P("dp", None),
        P(),
        P("section", "dp", None, None),
        P("section", "dp", None, None),
        P("section", "dp", None, None),
        P("section", "dp", None, None),
        P("section", "dp", None, None),
        P("section", "dp", None, None),
        P("section", "dp", None, None),
        P("section", None),
        P("section", None),
        P("section", None),
    )
    out_specs = (
        P(),
        P(),
        P(),
        P("section", "dp", None, None),
        P("section", "dp", None, None),
        P("section", "dp", None, None),
        P("section", "dp", None, None),
        P("section", "dp", None, None),
        P("section", "dp", None, None),
        P("section", "dp", None, None),
        P("section", None),
        P("section", None),
        P("section", None),
    )
    return jax.shard_map(
        on_device, mesh=mesh, in_specs=in_specs, out_specs=out_specs, check_vma=False
    )
```

```python
import functools
import math

import jax
import jax.numpy as jnp
from jax import lax
from jax.experimental import pallas as pl
from jax.experimental.pallas import tpu as pltpu
from jax.sharding import PartitionSpec as P

D = 768
FF = 3072
H = 12
PD = 384
PFF = 1536
PH = 12
PIX = 768
GRID = 14
NT = 4
LC = 128
STEP = 10
P_SIZE = 196
LT = 36
NBE = 52
NBP = 16
VE = 11520
VP = 6912
VW = 18432


NORM_EPS = 1e-06
ADAM_EPS = 1e-08
BETA_FIRST = 0.5
BETA_SECOND = 0.5
BETA_STATS = 0.95
RATE_MATRIX = 0.02
RATE_VECTOR = 0.05
DECAY_MATRIX = 0.04
EMA_KEEP = 0.996
CLIP_LIMIT = 1.0
NEG_FILL = -1000000000.0
WIRE = jnp.float16
WIRE_TOP = 16384.0
f32 = jnp.float32
bf = jnp.bfloat16


def from_behind(shard, axis, by):
    size = lax.axis_size(axis)
    pairs = [(i, i + by) for i in range(size) if 0 <= i + by < size]
    return lax.ppermute(shard, axis, pairs)


def enc_shapes():
    return [(PIX, D), (D, 3 * D), (D, D), (D, FF), (FF, D)]


def pred_shapes():
    return [(D, PD), (PD, 3 * PD), (PD, PD), (PD, PFF), (PFF, PD), (PD, D)]


def enc_lengths():
    return [D] * 8 + [FF, D, D, D]


def pred_lengths():
    return [PD] * 8 + [PFF, PD, PD, PD, D, PD]


def sincos(width):
    quarter = width // 4
    frequency = 1.0 / 10000.0 ** (jnp.arange(quarter, dtype=jnp.float32) / quarter)
    cell_ids = jnp.arange(P_SIZE)
    row_pos = (cell_ids // GRID).astype(jnp.float32)[:, None] * frequency
    column_pos = (cell_ids % GRID).astype(jnp.float32)[:, None] * frequency
    return jnp.concatenate(
        [jnp.sin(row_pos), jnp.cos(row_pos), jnp.sin(column_pos), jnp.cos(column_pos)], 1
    )


DIMS = {"nn": (1, 0), "nt": (1, 1), "tn": (0, 0)}

def parts_of(a, count):
    found = []
    for index in range(count):
        piece = a.astype(bf)
        found.append(piece)
        if index + 1 < count:
            a = a - piece.astype(f32)
    return found

def product(left, right, form, pairs):
    ld, rd = DIMS[form]
    lhs = jnp.concatenate([left[i] for i, _ in pairs], ld)
    rhs = jnp.concatenate([right[j] for _, j in pairs], rd)
    return lax.dot_general(lhs, rhs, (((ld,), (rd,)), ((), ())), preferred_element_type=f32)

THREE = ((0, 1), (1, 0), (0, 0))
SIX = ((0, 2), (2, 0), (1, 1), (0, 1), (1, 0), (0, 0))
def mul3(left, right, form="nn"):
    return product(left, right, form, THREE)
def mul6(left, right, form="nn"):
    return product(left, right, form, SIX)

def invert_factors(mats):
    n = mats[0].shape[0]
    lane = lax.broadcasted_iota(jnp.int32, (8, n), 1)
    sub = lax.broadcasted_iota(jnp.int32, (8, n), 0)
    groups = [[a[8 * t : 8 * t + 8, :] for t in range(n // 8)] for a in mats]
    for j in range(n):
        top, at_row = divmod(j, 8)
        here = lane == j
        pick = jnp.full((8, n), j, jnp.int32)
        for tiles in groups:
            column = jnp.take_along_axis(tiles[top], pick, axis=1)
            pivot = jnp.broadcast_to(column[at_row : at_row + 1, :], (8, n))
            row = jnp.broadcast_to(tiles[top][at_row : at_row + 1, :], (8, n))
            scaled = jnp.where(here, 1.0, row) * (1.0 / pivot)
            for t in range(top, n // 8):
                if t > top:
                    column = jnp.take_along_axis(tiles[t], pick, axis=1)
                fresh = jnp.where(here, 0.0, tiles[t]) - column * scaled
                tiles[t] = jnp.where(sub > at_row, fresh, tiles[t]) if t == top else fresh
    results = []
    for tiles in groups:
        rows = []
        for t in range(n // 8):
            at = sub + 8 * t
            pivots = jnp.sum(jnp.where(lane == at, tiles[t], 0.0), axis=1, keepdims=True)
            unit = jnp.where(lane < at, tiles[t], jnp.where(lane == at, 1.0, 0.0))
            rows.append(unit * lax.rsqrt(pivots))
        results.append(jnp.concatenate(rows, 0))
    return results

def first_kernel(flag, factor, g_ref, w_ref, m_ref, v_ref, l_ref, r_ref, e_ref, f_ref,
                 w_out, m_out, v_out, e_out, f_out, base_out, gram_out):
    on = flag[pl.program_id(0)] != 0

    @pl.when(jnp.logical_not(on))
    def keep():
        for source, target in ((w_ref, w_out), (m_ref, m_out), (v_ref, v_out), (e_ref, e_out), (f_ref, f_out)):
            target[...] = source[...]

    @pl.when(on)
    def update():
        correct_one = 1.0 - BETA_FIRST**STEP
        correct_two = 1.0 - BETA_SECOND**STEP
        grad = parts_of(g_ref[0] * factor[0], 3)
        left = parts_of(l_ref[0], 3)
        right = parts_of(r_ref[0], 3)
        rotated = mul3(left, parts_of(mul3(grad, right), 2), "tn")
        moment = BETA_FIRST * m_ref[0] + (1.0 - BETA_FIRST) * rotated
        second = BETA_SECOND * v_ref[0] + (1.0 - BETA_SECOND) * rotated * rotated
        m_out[0] = moment
        v_out[0] = second
        normed = moment / correct_one / (jnp.sqrt(second / correct_two) + ADAM_EPS)
        weight = w_ref[0]
        step = mul3(left, parts_of(mul3(parts_of(normed, 2), right, "nt"), 2))
        w_out[0] = weight - RATE_MATRIX * (step + DECAY_MATRIX * weight)
        for index, (stat, target, basis, form) in enumerate(
            ((e_ref, e_out, left, "nt"), (f_ref, f_out, right, "tn"))
        ):
            fresh = BETA_STATS * stat[0] + (1.0 - BETA_STATS) * mul6(grad, grad, form)
            target[0] = fresh
            moved = mul6(parts_of(fresh, 3), basis)
            base_out[0, index] = moved
            pieces = parts_of(moved, 3)
            gram_out[0, index] = mul6(pieces, pieces, "tn")

def factor_kernel(flag, base_ref, gram_ref, q_out, base, gram, inverse):
    blocks, edge = base_ref.shape[0], base_ref.shape[-1]
    panel = 128
    count = edge // panel
    base[...] = base_ref[...]
    gram[...] = gram_ref[...]

    def stage(k):
        at = pl.ds(panel * k, panel)
        start = panel * k
        spot = slice(start, start + panel)
        rest = slice(start + panel, edge)

        def block(b, carry):
            @pl.when(flag[b] != 0)
            def run():
                for side in range(2):
                    inv = parts_of(inverse[b, side], 3)
                    q = mul6(parts_of(base[b, side, :, spot], 3), inv, "nt")
                    q_out[b, side, :, spot] = q
                    if k + 1 < count:
                        p = parts_of(mul6(inv, parts_of(gram[b, side, spot, rest], 3)), 3)
                        gram[b, side, rest, rest] = gram[b, side, rest, rest] - mul6(p, p, "tn")
                        base[b, side, :, rest] = base[b, side, :, rest] - mul6(parts_of(q, 3), p)
            return carry

        lax.fori_loop(0, blocks, block, 0)

    def turn(k, carry):
        for which in range(count):
            @pl.when(k == which)
            def load():
                spot = slice(panel * which, panel * which + panel)
                for b in range(blocks):
                    for side in range(2):
                        inverse[b, side] = gram[b, side, spot, spot]
        mats = invert_factors([inverse[b, side] for b in range(blocks) for side in range(2)])
        for b in range(blocks):
            for side in range(2):
                inverse[b, side] = mats[2 * b + side]
        for which in range(count):
            @pl.when(k == which)
            def run():
                stage(which)
        return carry

    lax.fori_loop(0, count, turn, 0)

def last_kernel(flag, l_ref, r_ref, m_ref, q_ref, l_out, r_out, m_out):
    on = flag[pl.program_id(0)] != 0

    @pl.when(jnp.logical_not(on))
    def keep():
        l_out[...] = l_ref[...]
        r_out[...] = r_ref[...]
        m_out[...] = m_ref[...]

    @pl.when(on)
    def update():
        l_out[0] = q_ref[0, 0]
        r_out[0] = q_ref[0, 1]
        turn_left = mul3(parts_of(q_ref[0, 0], 2), parts_of(l_ref[0], 2), "tn")
        turn_right = mul3(parts_of(r_ref[0], 2), parts_of(q_ref[0, 1], 2), "tn")
        half = mul3(parts_of(turn_left, 2), parts_of(m_ref[0], 2))
        m_out[0] = mul3(parts_of(half, 2), parts_of(turn_right, 2))

PLAIN = (((1,), (0,)), ((), ()))
RIGHT_T = (((1,), (1,)), ((), ()))
LEFT_T = (((0,), (0,)), ((), ()))
ROOT_HALF = 0.7071067811865476
ROOT_TWO_PI = 2.5066282746310002


def mm(left, right, dims=PLAIN):
    return lax.dot_general(left, right, dims, preferred_element_type=f32)


def norm_parts(x):
    center = x - jnp.mean(x, -1, keepdims=True)
    inverse = lax.rsqrt(jnp.mean(center * center, -1, keepdims=True) + NORM_EPS)
    return center * inverse, inverse


def norm(x, gain, shift):
    return norm_parts(x)[0] * gain + shift


def norm_back(x, gain, grad):
    unit, inverse = norm_parts(x)
    grad_unit = grad * gain
    mean_one = jnp.mean(grad_unit, -1, keepdims=True)
    mean_two = jnp.mean(grad_unit * unit, -1, keepdims=True)
    back = inverse * (grad_unit - mean_one - unit * mean_two)
    return back, col_sum(grad * unit), col_sum(grad)


def col_sum(x):
    return jnp.sum(x, 0, keepdims=True)


def gelu(x):
    return 0.5 * x * (1.0 + lax.erf(x * ROOT_HALF))


def gelu_slope(x):
    return 0.5 * (1.0 + lax.erf(x * ROOT_HALF)) + x * jnp.exp(-0.5 * x * x) * (1.0 / ROOT_TWO_PI)


def offsets(lengths):
    result = [0]
    for length in lengths:
        result.append(result[-1] + length)
    return result


class Vec:
    def __init__(self, ref, lengths):
        self.ref, self.at = ref, offsets(lengths)

    def __getitem__(self, k):
        return self.ref[:, self.at[k] : self.at[k + 1]]

    def __setitem__(self, k, value):
        self.ref[:, self.at[k] : self.at[k + 1]] = value

    def part(self, k, start, size):
        return self.ref[:, pl.ds(pl.multiple_of(self.at[k] + start, 128), size)]

    def put_part(self, k, start, size, value):
        self.ref[:, pl.ds(pl.multiple_of(self.at[k] + start, 128), size)] = value


class Fetch:
    def __init__(self, pieces, places, j, spot, sem):
        self.pieces, self.spot, self.sem = pieces, spot, sem
        self.which, self.index = places[j], places[NBE + NBP + j]

    def copy(self, piece, index):
        return pltpu.make_async_copy(piece.at[index], self.spot, self.sem)

    def start(self):
        if len(self.pieces) == 1:
            self.copy(self.pieces[0], self.index).start()
        else:
            self.start_among(0, len(self.pieces))

    def start_among(self, low, high):
        if high - low == 1:
            self.copy(self.pieces[low], self.index).start()
            return
        middle = (low + high) // 2

        @pl.when(self.which < middle)
        def below():
            self.start_among(low, middle)

        @pl.when(self.which >= middle)
        def above():
            self.start_among(middle, high)

    def wait(self):
        self.copy(self.pieces[0], 0).wait()


def load_blocks(pieces, places, sems, first, shapes, targets):
    edge = pieces[0].shape[-1]
    groups = []
    j = first
    for (height, breadth), target in zip(shapes, targets):
        group = []
        for row in range(height // edge):
            for column in range(breadth // edge):
                if target is not None:
                    spot = target.at[pl.ds(row * edge, edge), pl.ds(column * edge, edge)]
                    group.append(Fetch(pieces, places, j, spot, sems.at[j]))
                j += 1
        groups.append(group)
    return groups


def start_all(groups):
    for group in groups:
        for copy in group:
            copy.start()


def wait_group(group):
    for copy in group:
        copy.wait()


def head_masks(rows, heads, width):
    lane = lax.broadcasted_iota(jnp.int32, (rows, 128), 1)
    size = width // heads
    return [(lane >= size * h) & (lane < size * h + size) for h in range(128 // size)]


def as_factors(masks):
    return [jnp.where(mask, 1.0, 0.0).astype(bf) for mask in masks]


def soft(scores, allowed):
    scores = jnp.where(allowed, scores, NEG_FILL)
    top = jnp.max(scores, -1, keepdims=True)
    raised = jnp.exp(scores - top)
    return raised * (1.0 / jnp.sum(raised, -1, keepdims=True))


def attend(q_ref, k_ref, v_ref, valid_ref, out_ref, heads):
    images, rows, width = q_ref.shape
    keys = k_ref.shape[1]
    masks = head_masks(rows, heads, width)
    factors = as_factors(masks)

    def group(p, carry):
        lanes = pl.ds(pl.multiple_of(128 * p, 128), 128)
        for i in range(images):
            q, k, v = q_ref[i, :, lanes], k_ref[i, :, lanes], v_ref[i, :, lanes]
            allowed = jnp.broadcast_to(valid_ref[i], (rows, keys)) > 0.0
            result = jnp.zeros((rows, 128), f32)
            for mask, factor in zip(masks, factors):
                probs = soft(mm(q * factor, k, RIGHT_T), allowed)
                result = jnp.where(mask, mm(probs.astype(bf), v), result)
            out_ref[i, :, lanes] = result.astype(bf)
        return carry

    lax.fori_loop(0, width // 128, group, 0)


def attend_back(q_ref, k_ref, v_ref, valid_ref, go_ref, dq_ref, dk_ref, dv_ref, heads):
    images, rows, width = q_ref.shape
    keys = k_ref.shape[1]
    masks = head_masks(rows, heads, width)
    key_masks = head_masks(keys, heads, width)
    factors = as_factors(masks)
    scale = 1.0 / math.sqrt(width // heads)

    def group(p, carry):
        lanes = pl.ds(pl.multiple_of(128 * p, 128), 128)
        for i in range(images):
            q, k, v = q_ref[i, :, lanes], k_ref[i, :, lanes], v_ref[i, :, lanes]
            go = go_ref[i, :, lanes]
            allowed = jnp.broadcast_to(valid_ref[i], (rows, keys)) > 0.0
            dq = jnp.zeros((rows, 128), f32)
            dk = jnp.zeros((keys, 128), f32)
            dv = jnp.zeros((keys, 128), f32)
            for mask, key_mask, factor in zip(masks, key_masks, factors):
                probs = soft(mm(q * factor, k, RIGHT_T), allowed)
                dv = jnp.where(key_mask, mm(probs.astype(bf), go, LEFT_T), dv)
                dprobs = mm(go * factor, v, RIGHT_T)
                dscores = probs * (dprobs - jnp.sum(dprobs * probs, -1, keepdims=True))
                low = dscores.astype(bf)
                dq = jnp.where(mask, mm(low, k) * scale, dq)
                dk = jnp.where(key_mask, mm(low, q, LEFT_T), dk)
            dq_ref[i, :, lanes] = dq
            dk_ref[i, :, lanes] = dk
            dv_ref[i, :, lanes] = dv
        return carry

    lax.fori_loop(0, width // 128, group, 0)


def split_rows(ref, value):
    images, rows, _ = ref.shape
    for i in range(images):
        ref[i] = value[rows * i : rows * i + rows].astype(ref.dtype)


def flat(ref):
    return jnp.concatenate([ref[i] for i in range(ref.shape[0])], 0)


STRIP = 384


def feed_forward(normed, mid, up, down, vec, pre_ref, acc_ref):
    acc_ref[...] = mid

    def strip(c, carry):
        lanes = pl.ds(pl.multiple_of(c * STRIP, 128), STRIP)
        pre = mm(normed, up[:, lanes]) + vec.part(8, c * STRIP, STRIP)
        if pre_ref is not None:
            pre_ref[:, lanes] = pre
        acc_ref[...] += mm(gelu(pre).astype(bf), down[lanes, :])
        return carry

    lax.fori_loop(0, up.shape[1] // STRIP, strip, 0)
    return acc_ref[...] + vec[9]


def encoder_kernel(
    slots, table, rows_ref, pos_ref, valid_ref, vec_ref,
    z_out, e_out, q_out, k_out, v_out, att_out, mid_out, pre_out, hid_out,
    wp, wqkv, wo, w1, w2, acc, sems,
):
    vec = Vec(vec_ref, enc_lengths())
    groups = load_blocks(table, slots, sems, 0, enc_shapes(), (wp, wqkv, wo, w1, w2))
    start_all(groups)
    wait_group(groups[0])
    e = mm(rows_ref[...], wp[...]) + vec[0] + pos_ref[...]
    e_out[...] = e
    normed = norm(e, vec[1], vec[2]).astype(bf)
    wait_group(groups[1])
    split_rows(q_out, (mm(normed, wqkv[:, :D]) + vec[3]) * (1.0 / math.sqrt(D // H)))
    split_rows(k_out, mm(normed, wqkv[:, D : 2 * D]))
    split_rows(v_out, mm(normed, wqkv[:, 2 * D :]) + vec[4])
    attend(q_out, k_out, v_out, valid_ref, att_out, H)
    wait_group(groups[2])
    mid = e + mm(flat(att_out), wo[...]) + vec[5]
    mid_out[...] = mid
    hidden = norm(mid, vec[6], vec[7]).astype(bf)
    wait_group(groups[3])
    wait_group(groups[4])
    hid = feed_forward(hidden, mid, w1, w2, vec, pre_out, acc)
    hid_out[...] = hid
    z_out[...] = norm(hid, vec[10], vec[11]).astype(bf)


def target_kernel(
    slots, table, all_ref, pos_all_ref, some_ref, pos_some_ref, valid_ref, vec_ref,
    out_ref, wp, wqkv, wo, w1, w2, q, k, v, att, acc, sems,
):
    vec = Vec(vec_ref, enc_lengths())
    groups = load_blocks(table, slots, sems, 0, enc_shapes(), (wp, wqkv, wo, w1, w2))
    start_all(groups)
    wait_group(groups[0])
    e = mm(all_ref[...], wp[...]) + vec[0] + pos_all_ref[...]
    normed = norm(e, vec[1], vec[2]).astype(bf)
    wait_group(groups[1])
    split_rows(k, mm(normed, wqkv[:, D : 2 * D]))
    split_rows(v, mm(normed, wqkv[:, 2 * D :]) + vec[4])
    e = mm(some_ref[...], wp[...]) + vec[0] + pos_some_ref[...]
    normed = norm(e, vec[1], vec[2]).astype(bf)
    split_rows(q, (mm(normed, wqkv[:, :D]) + vec[3]) * (1.0 / math.sqrt(D // H)))
    attend(q, k, v, valid_ref, att, H)
    wait_group(groups[2])
    mid = e + mm(flat(att), wo[...]) + vec[5]
    hidden = norm(mid, vec[6], vec[7]).astype(bf)
    wait_group(groups[3])
    wait_group(groups[4])
    hid = feed_forward(hidden, mid, w1, w2, vec, None, acc)
    out_ref[...] = norm_parts(norm(hid, vec[10], vec[11]))[0]


def put_block(ref, value, j, depth):
    edge = value.shape[-1]
    if depth % 8:
        ref[j] = value
    else:
        ref[:, depth * j : depth * j + depth, :] = value.reshape(edge // depth, depth, edge)


def raise_top(top_ref, value):
    top_ref[...] = jnp.maximum(top_ref[...], jnp.max(jnp.abs(value), 0, keepdims=True))


def predictor_kernel(
    depth, slots, table, z_ref, pos_c_ref, pos_t_ref, valid_ref, tgt_ref, tmask_ref, vec_ref,
    dz_out, flow_a, flow_b, vec_out, loss_out, top_out,
    win, wqkv, wo, w1, w2, wout, q, k, v, att, go, dq, dk, dv, pre_ref, act_ref, dpre_ref, acc, sems,
):
    vec, grads = Vec(vec_ref, pred_lengths()), Vec(vec_out, pred_lengths())
    edge = table[0].shape[-1]
    half = flow_split(NBP)
    images = z_ref.shape[0] // LC
    groups = load_blocks(table, slots, sems, NBE, pred_shapes(), (win, wqkv, wo, w1, w2, wout))
    start_all(groups)
    for group in groups:
        wait_group(group)
    firsts = offsets([h * b // (edge * edge) for h, b in pred_shapes()])

    def store(index, matrix):
        for row in range(matrix.shape[0] // edge):
            for column in range(matrix.shape[1] // edge):
                j = firsts[index] + row * (pred_shapes()[index][1] // edge) + column
                value = matrix[row * edge : row * edge + edge, column * edge : column * edge + edge]
                raise_top(top_out, value)
                if j < half:
                    put_block(flow_a, value, j, depth)
                else:
                    put_block(flow_b, value, j - half, depth)

    top_out[...] = jnp.zeros_like(top_out)
    z = z_ref[...]
    x_c = mm(z, win[...]) + vec[0] + pos_c_ref[...]
    x_t = vec[13] + pos_t_ref[...]
    n_c = norm(x_c, vec[1], vec[2]).astype(bf)
    n_t = norm(x_t, vec[1], vec[2]).astype(bf)
    split_rows(q, (mm(n_t, wqkv[:, :PD]) + vec[3]) * (1.0 / math.sqrt(PD // PH)))
    for ref, start, bias in ((k, PD, 0.0), (v, 2 * PD, vec[4])):
        of_c = mm(n_c, wqkv[:, start : start + PD]) + bias
        of_t = mm(n_t, wqkv[:, start : start + PD]) + bias
        count = NT * LT
        for i in range(images):
            ref[i, :LC, :] = of_c[LC * i : LC * i + LC].astype(bf)
            ref[i, LC:, :] = of_t[count * i : count * i + count].astype(bf)
    attend(q, k, v, valid_ref, att, PH)
    mid = x_t + mm(flat(att), wo[...]) + vec[5]
    n_two = norm(mid, vec[6], vec[7]).astype(bf)
    y = feed_forward(n_two, mid, w1, w2, vec, pre_ref, acc)
    n_three = norm(y, vec[10], vec[11]).astype(bf)
    difference = mm(n_three, wout[...]) + vec[12] - tgt_ref[...]
    tmask = tmask_ref[...]
    magnitude = jnp.abs(difference)
    loss = jnp.where(magnitude < 1.0, 0.5 * difference * difference, magnitude - 0.5) * tmask
    loss_out[...] = col_sum(loss)
    grad = jnp.clip(difference, -1.0, 1.0) * tmask

    grads[12] = col_sum(grad)
    low = grad.astype(bf)
    store(5, mm(n_three.T, low))
    dy, grads[10], grads[11] = norm_back(y, vec[10], mm(low, wout[...], RIGHT_T))
    grads[9] = col_sum(dy)
    low = dy.astype(bf)
    acc[...] = jnp.zeros_like(acc)

    def strip(c, carry):
        lanes = pl.ds(pl.multiple_of(c * STRIP, 128), STRIP)
        pre = pre_ref[:, lanes]
        act_ref[:, lanes] = gelu(pre).astype(bf)
        dpre = mm(low, w2[lanes, :], RIGHT_T) * gelu_slope(pre)
        grads.put_part(8, c * STRIP, STRIP, col_sum(dpre))
        dpre = dpre.astype(bf)
        dpre_ref[:, lanes] = dpre
        acc[...] += mm(dpre, w1[:, lanes], RIGHT_T)
        return carry

    lax.fori_loop(0, PFF // STRIP, strip, 0)
    store(4, mm(act_ref[...].T, low))
    store(3, mm(n_two.T, dpre_ref[...]))
    dmid, grads[6], grads[7] = norm_back(mid, vec[6], acc[...])
    dmid = dmid + dy
    grads[5] = col_sum(dmid)
    low = dmid.astype(bf)
    split_rows(go, mm(low, wo[...], RIGHT_T))
    store(2, mm(flat(att).T, low))
    attend_back(q, k, v, valid_ref, go, dq, dk, dv, PH)
    d_q, d_k, d_v = flat(dq), [dk[i] for i in range(images)], [dv[i] for i in range(images)]
    grads[3] = col_sum(d_q)
    grads[4] = sum(col_sum(part) for part in d_v)
    q_low = d_q.astype(bf)
    k_c = jnp.concatenate([part[:LC] for part in d_k], 0).astype(bf)
    k_t = jnp.concatenate([part[LC:] for part in d_k], 0).astype(bf)
    v_c = jnp.concatenate([part[:LC] for part in d_v], 0).astype(bf)
    v_t = jnp.concatenate([part[LC:] for part in d_v], 0).astype(bf)
    n_c_t, n_t_t = n_c.T, n_t.T
    store(
        1,
        jnp.concatenate(
            [mm(n_t_t, q_low), mm(n_c_t, k_c) + mm(n_t_t, k_t), mm(n_c_t, v_c) + mm(n_t_t, v_t)], 1
        ),
    )
    wq, wk, wv = wqkv[:, :PD], wqkv[:, PD : 2 * PD], wqkv[:, 2 * PD :]
    dn_t = mm(q_low, wq, RIGHT_T) + mm(k_t, wk, RIGHT_T) + mm(v_t, wv, RIGHT_T)
    dn_c = mm(k_c, wk, RIGHT_T) + mm(v_c, wv, RIGHT_T)
    dx_t, gain_t, shift_t = norm_back(x_t, vec[1], dn_t)
    dx_c, gain_c, shift_c = norm_back(x_c, vec[1], dn_c)
    grads[1] = gain_t + gain_c
    grads[2] = shift_t + shift_c
    dx_t = dx_t + dmid
    grads[13] = col_sum(dx_t)
    grads[0] = col_sum(dx_c)
    low = dx_c.astype(bf)
    dz_out[...] = mm(low, win[...], RIGHT_T).astype(bf)
    store(0, mm(z.T, low))


def flow_split(count):
    return (count // 2 + 3) // 4 * 4


def encoder_back_kernel(
    depth, slots, table, dz_ref, rows_ref, e_ref, q, k, v, att_ref, mid_ref, pre_ref, hid_ref, valid_ref, vec_ref,
    flow_a, flow_b, vec_out, top_out,
    wqkv, wo, w1, w2, go, dq, dk, dv, act_t, dpre_ref, x_t, dqkv, acc, stage, sems, out_sems,
):
    vec, grads = Vec(vec_ref, enc_lengths()), Vec(vec_out, enc_lengths())
    edge = table[0].shape[-1]
    half = flow_split(NBE)
    groups = load_blocks(table, slots, sems, 0, enc_shapes(), (None, wqkv, wo, w1, w2))
    start_all(groups[::-1])
    firsts = offsets([h * b // (edge * edge) for h, b in enc_shapes()])
    sent = []

    def store(index, left_t, right):
        columns = enc_shapes()[index][1] // edge
        rows = enc_shapes()[index][0] // edge
        for first in range(0, rows * columns, 4):
            turn = len(sent)
            slot = turn % 2
            if turn >= 2:
                sent[turn - 2].wait()
            for b in range(4):
                row, column = divmod(first + b, columns)
                value = mm(
                    left_t[row * edge : row * edge + edge, :],
                    right[:, column * edge : column * edge + edge],
                )
                raise_top(top_out, value)
                put_block(stage.at[slot], value, b, depth)
            j = firsts[index] + first
            target, start = (flow_a, j) if j < half else (flow_b, j - half)
            if depth % 8:
                spot = target.at[pl.ds(start, 4)]
            else:
                spot = target.at[:, pl.ds(depth * start, 4 * depth), :]
            copy = pltpu.make_async_copy(stage.at[slot], spot, out_sems.at[turn])
            copy.start()
            sent.append(copy)

    top_out[...] = jnp.zeros_like(top_out)
    hid = hid_ref[...]
    dy, grads[10], grads[11] = norm_back(hid, vec[10], dz_ref[...].astype(f32))
    grads[9] = col_sum(dy)
    low = dy.astype(bf)
    wait_group(groups[4])
    wait_group(groups[3])
    acc[...] = jnp.zeros_like(acc)

    def strip(c, carry):
        lanes = pl.ds(pl.multiple_of(c * STRIP, 128), STRIP)
        pre = pre_ref[:, lanes]
        act_t[lanes, :] = gelu(pre).astype(bf).T
        dpre = mm(low, w2[lanes, :], RIGHT_T) * gelu_slope(pre)
        grads.put_part(8, c * STRIP, STRIP, col_sum(dpre))
        dpre = dpre.astype(bf)
        dpre_ref[:, lanes] = dpre
        acc[...] += mm(dpre, w1[:, lanes], RIGHT_T)
        return carry

    lax.fori_loop(0, FF // STRIP, strip, 0)
    dqkv[:, :D] = low
    store(4, act_t, dqkv)
    mid = mid_ref[...]
    unit, _ = norm_parts(mid)
    x_t[...] = (unit * vec[6] + vec[7]).astype(bf).T
    store(3, x_t, dpre_ref)
    dmid, grads[6], grads[7] = norm_back(mid, vec[6], acc[...])
    dmid = dmid + dy
    acc[...] = dmid
    grads[5] = col_sum(dmid)
    low = dmid.astype(bf)
    wait_group(groups[2])
    wait_group(groups[1])
    split_rows(go, mm(low, wo[...], RIGHT_T))
    x_t[...] = flat(att_ref).T
    dqkv[:, :D] = low
    store(2, x_t, dqkv)
    attend_back(q, k, v, valid_ref, go, dq, dk, dv, H)
    d_q, d_v = flat(dq), flat(dv)
    grads[3] = col_sum(d_q)
    grads[4] = col_sum(d_v)
    dqkv[:, :D] = d_q.astype(bf)
    dqkv[:, D : 2 * D] = flat(dk).astype(bf)
    dqkv[:, 2 * D :] = d_v.astype(bf)
    e = e_ref[...]
    x_t[...] = norm(e, vec[1], vec[2]).astype(bf).T
    store(1, x_t, dqkv)
    back, grads[1], grads[2] = norm_back(e, vec[1], mm(dqkv[...], wqkv[...], RIGHT_T))
    de = acc[...] + back
    grads[0] = col_sum(de)
    dqkv[:, :D] = de.astype(bf)
    x_t[...] = rows_ref[...].T
    store(0, x_t, dqkv)
    for copy in sent[-2:]:
        copy.wait()


def spaces(count):
    return [pl.BlockSpec(memory_space=pltpu.VMEM)] * count


ANYWHERE = pl.BlockSpec(memory_space=pl.ANY)


def weight_scratch(shapes):
    return [pltpu.VMEM(shape, bf) for shape in shapes]


def call_kernel(body, section, places, table, args, outs, any_outs, scratch, name):
    count = len(table)

    def guarded(places_ref, *refs):
        @pl.when(places_ref[2 * (NBE + NBP)] == section)
        def run():
            body(places_ref, refs[:count], *refs[count:])

    specs = [ANYWHERE] * count + spaces(len(args))
    out_specs = [ANYWHERE if i in any_outs else spaces(1)[0] for i in range(len(outs))]
    return pl.pallas_call(
        guarded,
        grid_spec=pltpu.PrefetchScalarGridSpec(
            num_scalar_prefetch=1, grid=(), in_specs=specs, out_specs=out_specs, scratch_shapes=scratch
        ),
        out_shape=[jax.ShapeDtypeStruct(shape, kind) for shape, kind in outs],
        compiler_params=pltpu.CompilerParams(vmem_limit_bytes=58 << 20),
        name=name,
    )(places, *table, *args)


MARKS = 16


def flow_shapes(count, edge, ranks):
    half = flow_split(count)
    if (edge // ranks) % 8:
        return [((n, edge, edge), f32) for n in (half, count - half)]
    return [((ranks, edge // ranks * n + MARKS, edge), f32) for n in (half, count - half)]


def encoder_call(slots, table, rows, pos, valid, vec):
    n = rows.shape[0]
    images = n // LC
    per = (images, LC, D)
    outs = [((n, D), bf), ((n, D), f32), (per, bf), (per, bf), (per, bf), (per, bf)]
    outs += [((n, D), f32), ((n, FF), f32), ((n, D), f32)]
    scratch = weight_scratch(enc_shapes()) + [pltpu.VMEM((n, D), f32), pltpu.SemaphoreType.DMA((NBE,))]
    args = (rows, pos, valid, vec)
    return call_kernel(encoder_kernel, 0, slots, table, args, outs, (), scratch, "encoder_forward")


def target_call(slots, table, rows, pos, some, pos_some, valid, vec, images):
    n = some.shape[0]
    keys = rows.shape[0] // images
    per, wide = (images, n // images, D), (images, keys, D)
    scratch = weight_scratch(enc_shapes()) + [
        pltpu.VMEM(per, bf),
        pltpu.VMEM(wide, bf),
        pltpu.VMEM(wide, bf),
        pltpu.VMEM(per, bf),
        pltpu.VMEM((n, D), f32),
        pltpu.SemaphoreType.DMA((NBE,)),
    ]
    args = (rows, pos, some, pos_some, valid, vec)
    outs = [((n, D), f32)]
    return call_kernel(target_kernel, 1, slots, table, args, outs, (), scratch, "target_forward")[0]


def predictor_call(slots, table, z, pos_c, pos_t, valid, tgt, tmask, vec, ranks):
    n, m = z.shape[0], pos_t.shape[0]
    images = n // LC
    rows, keys = m // images, valid.shape[-1]
    edge = table[0].shape[-1]
    per, wide = (images, rows, PD), (images, keys, PD)
    outs = [((n, D), bf)] + flow_shapes(NBP, edge, ranks) + [((1, VP), f32), ((1, D), f32), ((1, edge), f32)]
    scratch = weight_scratch(pred_shapes()) + [
        pltpu.VMEM(per, bf),
        pltpu.VMEM(wide, bf),
        pltpu.VMEM(wide, bf),
        pltpu.VMEM(per, bf),
        pltpu.VMEM(per, bf),
        pltpu.VMEM(per, f32),
        pltpu.VMEM(wide, f32),
        pltpu.VMEM(wide, f32),
        pltpu.VMEM((m, PFF), f32),
        pltpu.VMEM((m, PFF), bf),
        pltpu.VMEM((m, PFF), bf),
        pltpu.VMEM((m, PD), f32),
        pltpu.SemaphoreType.DMA((NBE + NBP,)),
    ]
    args = (z, pos_c, pos_t, valid, tgt, tmask, vec)
    body = functools.partial(predictor_kernel, edge // ranks)
    return call_kernel(body, 1, slots, table, args, outs, (), scratch, "predictor_step")


def encoder_back_call(slots, table, dz, rows, kept, valid, vec, ranks):
    n = rows.shape[0]
    images = n // LC
    edge = table[0].shape[-1]
    per = (images, LC, D)
    e, q, k, v, att, mid, pre, hid = kept
    depth = edge // ranks
    stage = (2, ranks, 4 * depth, edge) if depth % 8 == 0 else (2, 4, edge, edge)
    scratch = weight_scratch(enc_shapes()[1:]) + [
        pltpu.VMEM(per, bf),
        pltpu.VMEM(per, f32),
        pltpu.VMEM(per, f32),
        pltpu.VMEM(per, f32),
        pltpu.VMEM((FF, n), bf),
        pltpu.VMEM((n, FF), bf),
        pltpu.VMEM((D, n), bf),
        pltpu.VMEM((n, 3 * D), bf),
        pltpu.VMEM((n, D), f32),
        pltpu.VMEM(stage, f32),
        pltpu.SemaphoreType.DMA((NBE,)),
        pltpu.SemaphoreType.DMA((NBE // 4,)),
    ]
    outs = flow_shapes(NBE, edge, ranks) + [((1, VE), f32), ((1, edge), f32)]
    args = (dz, rows, e, q, k, v, att, mid, pre, hid, valid, vec)
    body = functools.partial(encoder_back_kernel, edge // ranks)
    return call_kernel(body, 0, slots, table, args, outs, (0, 1), scratch, "encoder_backward")


def soap_first(flags, factor, *arrays):
    n, e = arrays[0].shape[:2]
    one = pl.BlockSpec((1, e, e), lambda i, *_: (i, 0, 0))
    two = pl.BlockSpec((1, 2, e, e), lambda i, *_: (i, 0, 0, 0))
    single = jax.ShapeDtypeStruct((n, e, e), f32)
    double = jax.ShapeDtypeStruct((n, 2, e, e), f32)
    return pl.pallas_call(
        first_kernel,
        grid_spec=pltpu.PrefetchScalarGridSpec(
            num_scalar_prefetch=2, grid=(n,), in_specs=[one] * 8, out_specs=[one] * 5 + [two] * 2
        ),
        out_shape=[single] * 5 + [double] * 2,
        compiler_params=pltpu.CompilerParams(vmem_limit_bytes=56 << 20),
        name="soap_first",
    )(flags, factor, *arrays)


def soap_factor(flags, base, gram):
    n, _, e, _ = base.shape
    whole = pl.BlockSpec(memory_space=pltpu.VMEM)
    return pl.pallas_call(
        factor_kernel,
        grid_spec=pltpu.PrefetchScalarGridSpec(
            num_scalar_prefetch=1,
            grid=(),
            in_specs=[whole] * 2,
            out_specs=whole,
            scratch_shapes=[
                pltpu.VMEM((n, 2, e, e), f32),
                pltpu.VMEM((n, 2, e, e), f32),
                pltpu.VMEM((n, 2, 128, 128), f32),
            ],
        ),
        out_shape=jax.ShapeDtypeStruct(base.shape, f32),
        compiler_params=pltpu.CompilerParams(vmem_limit_bytes=56 << 20),
        name="soap_factor",
    )(flags, base, gram)


def soap_last(flags, left, right, moment, fresh):
    n, e = left.shape[:2]
    one = pl.BlockSpec((1, e, e), lambda i, *_: (i, 0, 0))
    two = pl.BlockSpec((1, 2, e, e), lambda i, *_: (i, 0, 0, 0))
    return pl.pallas_call(
        last_kernel,
        grid_spec=pltpu.PrefetchScalarGridSpec(
            num_scalar_prefetch=1, grid=(n,), in_specs=[one] * 3 + [two], out_specs=[one] * 3
        ),
        out_shape=[jax.ShapeDtypeStruct((n, e, e), f32)] * 3,
        compiler_params=pltpu.CompilerParams(vmem_limit_bytes=56 << 20),
        name="soap_last",
    )(flags, left, right, moment, fresh)


def place_shares(slots, second, enc_share, pred_share, ranks, slot_count):
    depth, edge = enc_share.shape[1:]

    def body(slots_ref, second_ref, enc_ref, pred_ref, out_ref):
        def run(source, first, count):
            def copy(j, carry):
                slot = slots_ref[first + j]
                rows = pl.ds(pl.multiple_of(slot % slot_count * depth, depth), depth)
                out_ref[slot // slot_count, rows, :] = source[j]
                return carry

            lax.fori_loop(0, count, copy, 0)

        @pl.when(second_ref[0] == 0)
        def enc():
            run(enc_ref, 0, NBE)

        @pl.when(second_ref[0] != 0)
        def pred():
            run(pred_ref, NBE, NBP)

    return pl.pallas_call(
        body,
        grid_spec=pltpu.PrefetchScalarGridSpec(
            num_scalar_prefetch=2, grid=(), in_specs=spaces(2), out_specs=spaces(1)[0]
        ),
        out_shape=jax.ShapeDtypeStruct((ranks, slot_count * depth + MARKS, edge), f32),
        compiler_params=pltpu.CompilerParams(vmem_limit_bytes=40 << 20),
        name="place_shares",
    )(slots, second, enc_share, pred_share)


ROUNDS = (
    (((1, 0), (2, 1), (4, 2)), ()),
    (((5, 0), (6, 1), (8, 3)), (1, 2, 4)),
    (((3, 0), (7, 1)), (5, 6)),
    (((9, 0), (10, 1), (12, 2)), (3, 7, 8)),
    (((13, 0), (14, 1)), (9, 10, 12)),
    (((11, 0), (15, 1)), (13, 14)),
)


def gather_pieces(own):
    both = Exchange((0, 1))
    if both.ranks != 16:
        return None
    held = {0: own}
    for moves, awaited in ROUNDS:
        names = sorted({piece ^ (1 << bit) for piece, bit in moves} | set(awaited))
        values = [held[name] for name in names]
        if awaited:
            values = lax.optimization_barrier(values)
        source = dict(zip(names, values))
        for piece, bit in moves:
            held[piece] = both.swap(source[piece ^ (1 << bit)], bit)
    return [held[piece] for piece in range(both.ranks)]


class Exchange:
    def __init__(self, sections):
        self.ranks = lax.axis_size("dp")
        self.bits = self.ranks.bit_length() - 1
        self.sections = sections

    def swap(self, value, bit):
        pairs = [
            (s * self.ranks + i, s * self.ranks + (i ^ (1 << bit)))
            for s in self.sections
            for i in range(self.ranks)
        ]
        return lax.ppermute(value, ("section", "dp"), pairs)

    def total(self, value):
        for bit in range(self.bits):
            value = value + self.swap(value, bit)
        return value


def wire_exponent(bound):
    return jnp.floor(jnp.log2(WIRE_TOP / jnp.maximum(bound, 1e-30)))


def pack(values, exponent):
    row = lax.broadcasted_iota(jnp.int32, values.shape, values.ndim - 2)
    marked = jnp.where(row < values.shape[-2] - MARKS, values * jnp.exp2(exponent), exponent)
    return marked.astype(WIRE)


def halve(exchange, flows, orders, bound):
    bits = exchange.bits
    me = lax.axis_index("dp")
    parts = [f.reshape((2,) * bits + f.shape[1:]) for f in flows]
    bounds = [bound for _ in flows]
    left = [list(range(bits - 1, -1, -1)) for _ in flows]
    for stage in range(bits):
        for k, part in enumerate(parts):
            bit = orders[k][stage]
            axis = left[k].index(bit)
            mine = (me >> bit) & 1
            give = lax.dynamic_index_in_dim(part, 1 - mine, axis, keepdims=False)
            arrived = exchange.swap(pack(give, wire_exponent(bounds[k])), bit)
            keep = lax.dynamic_index_in_dim(part, mine, axis, keepdims=False)
            unscale = jnp.exp2(-arrived[..., -1, 0].reshape(-1)[0].astype(f32))
            parts[k] = keep + arrived.astype(f32) * unscale
            bounds[k] = bounds[k] + WIRE_TOP * unscale
            left[k].remove(bit)
    return [part[:-MARKS] for part in parts], sum(bounds)


def by_share(flow, ranks):
    if flow.shape[0] == ranks and flow.shape[1] != flow.shape[2]:
        return flow
    blocks, edge = flow.shape[:2]
    cut = flow.reshape(blocks, ranks, edge // ranks, edge)
    cut = cut.transpose(1, 0, 2, 3).reshape(ranks, -1, edge)
    return jnp.pad(cut, ((0, 0), (0, MARKS), (0, 0)))


def on_device(
    pixels,
    ctx_idx,
    ctx_len,
    tgt_idx,
    tgt_len,
    slot_of,
    weights,
    first_moment,
    second_moment,
    left_basis,
    right_basis,
    left_stats,
    right_stats,
    vectors,
    vector_first,
    vector_second,
):
    section_index = lax.axis_index("section")
    owner_index = lax.axis_index("dp")
    ranks = lax.axis_size("dp")
    is_first = section_index == 0
    second = section_index.astype(jnp.int32).reshape(1)
    slot_count = weights.shape[1]
    edge = weights.shape[-1]
    own = weights[0].astype(bf)
    table = gather_pieces(own)
    if table is None:
        table = [lax.all_gather(own, "dp", axis=0, tiled=True)]
        places = jnp.concatenate([jnp.zeros_like(slot_of), slot_of, second])
    else:
        places = [jnp.bitwise_xor(slot_of // slot_count, owner_index), slot_of % slot_count, second]
        places = jnp.concatenate(places)
    enc_slots = slot_of[:NBE]
    pred_slots = slot_of[NBE:]
    row_now = vectors[0]
    enc_vec_now = lax.dynamic_slice_in_dim(row_now, section_index * VP, VE)[None]
    pred_vec_now = row_now[None, :VP]
    pos_enc = sincos(D)
    pos_pred = sincos(PD)
    images = ctx_idx.shape[0]
    rows_all = -(-P_SIZE // 16) * 16
    tgt_flat = tgt_idx.reshape(images, NT * LT)
    ctx_valid = (jnp.arange(LC)[None, :] < ctx_len[:, None]).astype(f32)
    tgt_valid = (jnp.arange(LT)[None, None, :] < tgt_len[:, :, None]).astype(f32)
    tgt_valid = tgt_valid.reshape(images, NT * LT)
    joined_valid = jnp.concatenate([ctx_valid, tgt_valid], 1)[:, None, :]
    all_valid = (jnp.arange(rows_all) < P_SIZE).astype(f32)
    all_valid = jnp.broadcast_to(all_valid, (images, 1, rows_all))

    def pick(index):
        return (index[..., None] == jnp.arange(P_SIZE)).astype(f32)

    ctx_hot = pick(ctx_idx)
    tgt_hot = pick(tgt_flat)

    def choose(hot, values):
        return jnp.einsum(
            "njp,pd->njd", hot, values, precision=lax.Precision.HIGHEST, preferred_element_type=f32
        ).reshape(-1, values.shape[-1])

    def choose_pixels(hot):
        picked = jnp.einsum("njp,npd->njd", hot.astype(bf), pixels, preferred_element_type=f32)
        return picked.astype(bf).reshape(-1, PIX)

    pixel_rows = choose_pixels(ctx_hot)
    enc_pos_ctx = choose(ctx_hot, pos_enc)
    padding = ((0, 0), (0, rows_all - P_SIZE), (0, 0))
    pixel_all = jnp.pad(pixels, padding).reshape(-1, PIX)
    pos_all = jnp.broadcast_to(jnp.pad(pos_enc[None], padding), (images, rows_all, D)).reshape(-1, D)
    pixel_tgt = choose_pixels(tgt_hot)
    enc_pos_tgt = choose(tgt_hot, pos_enc)
    pred_pos_ctx = choose(ctx_hot, pos_pred)
    pred_pos_tgt = choose(tgt_hot, pos_pred)

    ctx_keys = ctx_valid[:, None, :]
    encoded = encoder_call(places, table, pixel_rows, enc_pos_ctx, ctx_keys, enc_vec_now)
    context = from_behind(encoded[0], "section", 1)
    target = target_call(
        places, table, pixel_all, pos_all, pixel_tgt, enc_pos_tgt, all_valid, enc_vec_now, images
    )
    back_send, pred_a, pred_b, pred_vec, loss_lanes, pred_top = predictor_call(
        places,
        table,
        context,
        pred_pos_ctx,
        pred_pos_tgt,
        joined_valid,
        target,
        tgt_valid.reshape(-1, 1),
        pred_vec_now,
        ranks,
    )
    incoming = from_behind(back_send, "section", -1)
    loss_local = jnp.where(is_first, 0.0, jnp.sum(loss_lanes))

    low_order = list(range(Exchange((0,)).bits))
    orders = [low_order, low_order]
    if len(low_order) > 2:
        orders = [[0, 2, 1] + low_order[3:], [1, 0, 2] + low_order[3:]]
    pred_flows = [by_share(flow, ranks) for flow in (pred_a, pred_b)]
    pred_parts, pred_bound = halve(Exchange((1,)), pred_flows, orders, jnp.max(pred_top))

    enc_a, enc_b, enc_vec, enc_top = encoder_back_call(
        places, table, incoming, pixel_rows, encoded[1:], ctx_keys, enc_vec_now, ranks
    )
    enc_flows = [by_share(flow, ranks) for flow in (enc_a, enc_b)]
    enc_parts, enc_bound = halve(Exchange((0,)), enc_flows, orders, jnp.max(enc_top))
    depth = edge // ranks
    enc_share = jnp.concatenate(enc_parts, 0).reshape(NBE, depth, edge)
    pred_share = jnp.concatenate(pred_parts, 0).reshape(NBP, depth, edge)

    both = Exchange((0, 1))
    vec_local = jnp.where(is_first, enc_vec[0], jnp.pad(pred_vec[0], (0, VE - VP)))
    count_local = jnp.where(is_first, 0, jnp.sum(tgt_len)).astype(f32)
    scalars = jnp.pad(jnp.stack([loss_local, count_local]), (0, 126))
    summed = both.total(jnp.concatenate([vec_local, scalars]))
    vec_total = jnp.pad(summed[:VE], (0, VW - VE))
    share_squares = jnp.where(
        is_first, jnp.sum(enc_share * enc_share), jnp.sum(pred_share * pred_share)
    )
    squares = both.total(jnp.full((128,), share_squares))
    facts = jnp.stack([squares[0] + jnp.sum(summed[:VE] ** 2), summed[VE], summed[VE + 1]])
    facts = jnp.pad(facts, (0, 125))
    swap_sections = [(i, 1 - i) for i in range(2)]
    facts = facts + lax.ppermute(facts, "section", swap_sections)
    square_total, loss_total, count_total = facts[0], facts[1], facts[2]

    placed = place_shares(slot_of, second, enc_share, pred_share, ranks, slot_count)
    exponent = wire_exponent(jnp.where(is_first, enc_bound, pred_bound))
    payload = pack(placed, exponent)
    owned = lax.all_to_all(payload, "dp", split_axis=0, concat_axis=0, tiled=True).astype(f32)
    unscale = jnp.exp2(-owned[:, -1:, :1])
    owned = (owned[:, : slot_count * depth] * unscale).reshape(ranks, slot_count, depth, edge)
    owned_sum = owned.transpose(1, 0, 2, 3).reshape(slot_count, edge, edge)

    own_ids = owner_index * slot_count + jnp.arange(slot_count)
    enc_here = jnp.any(own_ids[:, None] == enc_slots[None, :], 1)
    pred_here = jnp.any(own_ids[:, None] == pred_slots[None, :], 1)
    trained = jnp.where(is_first, enc_here, pred_here)
    ema_here = jnp.logical_and(jnp.logical_not(is_first), enc_here)
    positions = jnp.arange(VW)
    vec_trained = positions < jnp.where(is_first, VE, VP)
    vec_ema = jnp.logical_and(jnp.logical_not(is_first), positions >= VP)
    grad_norm = jnp.sqrt(square_total) / count_total
    factor = jnp.minimum(1.0, CLIP_LIMIT / (grad_norm + 1e-06)) / count_total

    flags = trained.astype(jnp.int32)
    new_weight, moment, new_second, new_estat, new_fstat, base, gram = soap_first(
        flags,
        factor.reshape(1),
        owned_sum,
        weights[0],
        first_moment[0],
        second_moment[0],
        left_basis[0],
        right_basis[0],
        left_stats[0],
        right_stats[0],
    )
    fresh_bases = soap_factor(flags, base, gram)
    new_left, new_right, new_first = soap_last(
        flags, left_basis[0], right_basis[0], moment, fresh_bases
    )

    correct_one = 1.0 - BETA_FIRST**STEP
    correct_two = 1.0 - BETA_SECOND**STEP
    vec_clipped = vec_total * factor
    fresh_first = BETA_FIRST * vector_first[0] + (1.0 - BETA_FIRST) * vec_clipped
    fresh_second = BETA_SECOND * vector_second[0] + (1.0 - BETA_SECOND) * vec_clipped * vec_clipped
    stepped = row_now - RATE_VECTOR * (fresh_first / correct_one) / (
        jnp.sqrt(fresh_second / correct_two) + ADAM_EPS
    )
    new_vec = jnp.where(vec_trained, stepped, row_now)
    new_vec_first = jnp.where(vec_trained, fresh_first, vector_first[0])
    new_vec_second = jnp.where(vec_trained, fresh_second, vector_second[0])
    from_encoder = from_behind(new_weight.astype(bf), "section", 1).astype(f32)
    vec_from_encoder = from_behind(new_vec.astype(bf), "section", 1).astype(f32)
    new_weight = jnp.where(
        ema_here[:, None, None], EMA_KEEP * weights[0] + (1.0 - EMA_KEEP) * from_encoder, new_weight
    )
    aligned = jnp.concatenate([jnp.zeros((VP,), f32), vec_from_encoder[:VE]])
    new_vec = jnp.where(vec_ema, EMA_KEEP * row_now + (1.0 - EMA_KEEP) * aligned, new_vec)
    return (
        loss_total,
        count_total,
        grad_norm,
        new_weight[None],
        new_first[None],
        new_second[None],
        new_left[None],
        new_right[None],
        new_estat[None],
        new_fstat[None],
        new_vec[None],
        new_vec_first[None],
        new_vec_second[None],
    )


def solution(mesh):
    in_specs = (
        P("dp", None, None),
        P("dp", None),
        P("dp"),
        P("dp", None, None),
        P("dp", None),
        P(),
        P("section", "dp", None, None),
        P("section", "dp", None, None),
        P("section", "dp", None, None),
        P("section", "dp", None, None),
        P("section", "dp", None, None),
        P("section", "dp", None, None),
        P("section", "dp", None, None),
        P("section", None),
        P("section", None),
        P("section", None),
    )
    out_specs = (
        P(),
        P(),
        P(),
        P("section", "dp", None, None),
        P("section", "dp", None, None),
        P("section", "dp", None, None),
        P("section", "dp", None, None),
        P("section", "dp", None, None),
        P("section", "dp", None, None),
        P("section", "dp", None, None),
        P("section", None),
        P("section", None),
        P("section", None),
    )
    return jax.shard_map(
        on_device, mesh=mesh, in_specs=in_specs, out_specs=out_specs, check_vma=False
    )
```

```python
import functools
import math

import jax
import jax.numpy as jnp
from jax import lax
from jax.experimental import pallas as pl
from jax.experimental.pallas import tpu as pltpu
from jax.sharding import PartitionSpec as P

D = 768
FF = 3072
H = 12
PD = 384
PFF = 1536
PH = 12
PIX = 768
GRID = 14
NT = 4
LC = 128
STEP = 10
P_SIZE = 196
LT = 36
NBE = 52
NBP = 16
VE = 11520
VP = 6912
VW = 18432


NORM_EPS = 1e-06
ADAM_EPS = 1e-08
BETA_FIRST = 0.5
BETA_SECOND = 0.5
BETA_STATS = 0.95
RATE_MATRIX = 0.02
RATE_VECTOR = 0.05
DECAY_MATRIX = 0.04
EMA_KEEP = 0.996
CLIP_LIMIT = 1.0
NEG_FILL = -1000000000.0
WIRE = jnp.float16
WIRE_TOP = 16384.0
f32 = jnp.float32
bf = jnp.bfloat16


def from_behind(shard, axis, by):
    size = lax.axis_size(axis)
    pairs = [(i, i + by) for i in range(size) if 0 <= i + by < size]
    return lax.ppermute(shard, axis, pairs)


def enc_shapes():
    return [(PIX, D), (D, 3 * D), (D, D), (D, FF), (FF, D)]


def pred_shapes():
    return [(D, PD), (PD, 3 * PD), (PD, PD), (PD, PFF), (PFF, PD), (PD, D)]


def enc_lengths():
    return [D] * 8 + [FF, D, D, D]


def pred_lengths():
    return [PD] * 8 + [PFF, PD, PD, PD, D, PD]


def sincos(width):
    quarter = width // 4
    frequency = 1.0 / 10000.0 ** (jnp.arange(quarter, dtype=jnp.float32) / quarter)
    cell_ids = jnp.arange(P_SIZE)
    row_pos = (cell_ids // GRID).astype(jnp.float32)[:, None] * frequency
    column_pos = (cell_ids % GRID).astype(jnp.float32)[:, None] * frequency
    return jnp.concatenate(
        [jnp.sin(row_pos), jnp.cos(row_pos), jnp.sin(column_pos), jnp.cos(column_pos)], 1
    )


DIMS = {"nn": (1, 0), "nt": (1, 1), "tn": (0, 0)}

def parts_of(a, count):
    found = []
    for index in range(count):
        piece = a.astype(bf)
        found.append(piece)
        if index + 1 < count:
            a = a - piece.astype(f32)
    return found

def product(left, right, form, pairs):
    ld, rd = DIMS[form]
    lhs = jnp.concatenate([left[i] for i, _ in pairs], ld)
    rhs = jnp.concatenate([right[j] for _, j in pairs], rd)
    return lax.dot_general(lhs, rhs, (((ld,), (rd,)), ((), ())), preferred_element_type=f32)

THREE = ((0, 1), (1, 0), (0, 0))
SIX = ((0, 2), (2, 0), (1, 1), (0, 1), (1, 0), (0, 0))
def mul3(left, right, form="nn"):
    return product(left, right, form, THREE)
def mul6(left, right, form="nn"):
    return product(left, right, form, SIX)

def invert_factors(mats):
    n = mats[0].shape[0]
    lane = lax.broadcasted_iota(jnp.int32, (8, n), 1)
    sub = lax.broadcasted_iota(jnp.int32, (8, n), 0)
    groups = [[a[8 * t : 8 * t + 8, :] for t in range(n // 8)] for a in mats]
    for j in range(n):
        top, at_row = divmod(j, 8)
        here = lane == j
        pick = jnp.full((8, n), j, jnp.int32)
        for tiles in groups:
            column = jnp.take_along_axis(tiles[top], pick, axis=1)
            pivot = jnp.broadcast_to(column[at_row : at_row + 1, :], (8, n))
            row = jnp.broadcast_to(tiles[top][at_row : at_row + 1, :], (8, n))
            scaled = jnp.where(here, 1.0, row) * (1.0 / pivot)
            for t in range(top, n // 8):
                if t > top:
                    column = jnp.take_along_axis(tiles[t], pick, axis=1)
                fresh = jnp.where(here, 0.0, tiles[t]) - column * scaled
                tiles[t] = jnp.where(sub > at_row, fresh, tiles[t]) if t == top else fresh
    results = []
    for tiles in groups:
        rows = []
        for t in range(n // 8):
            at = sub + 8 * t
            pivots = jnp.sum(jnp.where(lane == at, tiles[t], 0.0), axis=1, keepdims=True)
            unit = jnp.where(lane < at, tiles[t], jnp.where(lane == at, 1.0, 0.0))
            rows.append(unit * lax.rsqrt(pivots))
        results.append(jnp.concatenate(rows, 0))
    return results

def first_kernel(flag, factor, g_ref, w_ref, m_ref, v_ref, l_ref, r_ref, e_ref, f_ref,
                 w_out, m_out, v_out, e_out, f_out, base_out, gram_out):
    on = flag[pl.program_id(0)] != 0

    @pl.when(jnp.logical_not(on))
    def keep():
        for source, target in ((w_ref, w_out), (m_ref, m_out), (v_ref, v_out), (e_ref, e_out), (f_ref, f_out)):
            target[...] = source[...]

    @pl.when(on)
    def update():
        correct_one = 1.0 - BETA_FIRST**STEP
        correct_two = 1.0 - BETA_SECOND**STEP
        grad = parts_of(g_ref[0] * factor[0], 3)
        left = parts_of(l_ref[0], 3)
        right = parts_of(r_ref[0], 3)
        rotated = mul3(left, parts_of(mul3(grad, right), 2), "tn")
        moment = BETA_FIRST * m_ref[0] + (1.0 - BETA_FIRST) * rotated
        second = BETA_SECOND * v_ref[0] + (1.0 - BETA_SECOND) * rotated * rotated
        m_out[0] = moment
        v_out[0] = second
        normed = moment / correct_one / (jnp.sqrt(second / correct_two) + ADAM_EPS)
        weight = w_ref[0]
        step = mul3(left, parts_of(mul3(parts_of(normed, 2), right, "nt"), 2))
        w_out[0] = weight - RATE_MATRIX * (step + DECAY_MATRIX * weight)
        for index, (stat, target, basis, form) in enumerate(
            ((e_ref, e_out, left, "nt"), (f_ref, f_out, right, "tn"))
        ):
            fresh = BETA_STATS * stat[0] + (1.0 - BETA_STATS) * mul6(grad, grad, form)
            target[0] = fresh
            moved = mul6(parts_of(fresh, 3), basis)
            base_out[0, index] = moved
            pieces = parts_of(moved, 3)
            gram_out[0, index] = mul6(pieces, pieces, "tn")

def factor_kernel(flag, base_ref, gram_ref, q_out, base, gram, inverse):
    blocks, edge = base_ref.shape[0], base_ref.shape[-1]
    panel = 128
    count = edge // panel
    base[...] = base_ref[...]
    gram[...] = gram_ref[...]

    def stage(k):
        at = pl.ds(panel * k, panel)
        start = panel * k
        spot = slice(start, start + panel)
        rest = slice(start + panel, edge)

        def block(b, carry):
            @pl.when(flag[b] != 0)
            def run():
                for side in range(2):
                    inv = parts_of(inverse[b, side], 3)
                    q = mul6(parts_of(base[b, side, :, spot], 3), inv, "nt")
                    q_out[b, side, :, spot] = q
                    if k + 1 < count:
                        p = parts_of(mul6(inv, parts_of(gram[b, side, spot, rest], 3)), 3)
                        gram[b, side, rest, rest] = gram[b, side, rest, rest] - mul6(p, p, "tn")
                        base[b, side, :, rest] = base[b, side, :, rest] - mul6(parts_of(q, 3), p)
            return carry

        lax.fori_loop(0, blocks, block, 0)

    def turn(k, carry):
        for which in range(count):
            @pl.when(k == which)
            def load():
                spot = slice(panel * which, panel * which + panel)
                for b in range(blocks):
                    for side in range(2):
                        inverse[b, side] = gram[b, side, spot, spot]
        mats = invert_factors([inverse[b, side] for b in range(blocks) for side in range(2)])
        for b in range(blocks):
            for side in range(2):
                inverse[b, side] = mats[2 * b + side]
        for which in range(count):
            @pl.when(k == which)
            def run():
                stage(which)
        return carry

    lax.fori_loop(0, count, turn, 0)

def last_kernel(flag, l_ref, r_ref, m_ref, q_ref, l_out, r_out, m_out):
    on = flag[pl.program_id(0)] != 0

    @pl.when(jnp.logical_not(on))
    def keep():
        l_out[...] = l_ref[...]
        r_out[...] = r_ref[...]
        m_out[...] = m_ref[...]

    @pl.when(on)
    def update():
        l_out[0] = q_ref[0, 0]
        r_out[0] = q_ref[0, 1]
        turn_left = mul3(parts_of(q_ref[0, 0], 2), parts_of(l_ref[0], 2), "tn")
        turn_right = mul3(parts_of(r_ref[0], 2), parts_of(q_ref[0, 1], 2), "tn")
        half = mul3(parts_of(turn_left, 2), parts_of(m_ref[0], 2))
        m_out[0] = mul3(parts_of(half, 2), parts_of(turn_right, 2))

PLAIN = (((1,), (0,)), ((), ()))
RIGHT_T = (((1,), (1,)), ((), ()))
LEFT_T = (((0,), (0,)), ((), ()))
ROOT_HALF = 0.7071067811865476
ROOT_TWO_PI = 2.5066282746310002


def mm(left, right, dims=PLAIN):
    return lax.dot_general(left, right, dims, preferred_element_type=f32)


def norm_parts(x):
    center = x - jnp.mean(x, -1, keepdims=True)
    inverse = lax.rsqrt(jnp.mean(center * center, -1, keepdims=True) + NORM_EPS)
    return center * inverse, inverse


def norm(x, gain, shift):
    return norm_parts(x)[0] * gain + shift


def norm_back(x, gain, grad):
    unit, inverse = norm_parts(x)
    grad_unit = grad * gain
    mean_one = jnp.mean(grad_unit, -1, keepdims=True)
    mean_two = jnp.mean(grad_unit * unit, -1, keepdims=True)
    back = inverse * (grad_unit - mean_one - unit * mean_two)
    return back, col_sum(grad * unit), col_sum(grad)


def col_sum(x):
    return jnp.sum(x, 0, keepdims=True)


def gelu(x):
    return 0.5 * x * (1.0 + lax.erf(x * ROOT_HALF))


def gelu_slope(x):
    return 0.5 * (1.0 + lax.erf(x * ROOT_HALF)) + x * jnp.exp(-0.5 * x * x) * (1.0 / ROOT_TWO_PI)


def offsets(lengths):
    result = [0]
    for length in lengths:
        result.append(result[-1] + length)
    return result


class Vec:
    def __init__(self, ref, lengths):
        self.ref, self.at = ref, offsets(lengths)

    def __getitem__(self, k):
        return self.ref[:, self.at[k] : self.at[k + 1]]

    def __setitem__(self, k, value):
        self.ref[:, self.at[k] : self.at[k + 1]] = value

    def part(self, k, start, size):
        return self.ref[:, pl.ds(pl.multiple_of(self.at[k] + start, 128), size)]

    def put_part(self, k, start, size, value):
        self.ref[:, pl.ds(pl.multiple_of(self.at[k] + start, 128), size)] = value


class Fetch:
    def __init__(self, pieces, places, j, spot, sem):
        self.pieces, self.spot, self.sem = pieces, spot, sem
        self.which, self.index = places[j], places[NBE + NBP + j]

    def copy(self, piece, index):
        return pltpu.make_async_copy(piece.at[index], self.spot, self.sem)

    def start(self):
        if len(self.pieces) == 1:
            self.copy(self.pieces[0], self.index).start()
        else:
            self.start_among(0, len(self.pieces))

    def start_among(self, low, high):
        if high - low == 1:
            self.copy(self.pieces[low], self.index).start()
            return
        middle = (low + high) // 2

        @pl.when(self.which < middle)
        def below():
            self.start_among(low, middle)

        @pl.when(self.which >= middle)
        def above():
            self.start_among(middle, high)

    def wait(self):
        self.copy(self.pieces[0], 0).wait()


def load_blocks(pieces, places, sems, first, shapes, targets):
    edge = pieces[0].shape[-1]
    groups = []
    j = first
    for (height, breadth), target in zip(shapes, targets):
        group = []
        for row in range(height // edge):
            for column in range(breadth // edge):
                if target is not None:
                    spot = target.at[pl.ds(row * edge, edge), pl.ds(column * edge, edge)]
                    group.append(Fetch(pieces, places, j, spot, sems.at[j]))
                j += 1
        groups.append(group)
    return groups


def start_all(groups):
    for group in groups:
        for copy in group:
            copy.start()


def wait_group(group):
    for copy in group:
        copy.wait()


def head_masks(rows, heads, width):
    lane = lax.broadcasted_iota(jnp.int32, (rows, 128), 1)
    size = width // heads
    return [(lane >= size * h) & (lane < size * h + size) for h in range(128 // size)]


def as_factors(masks):
    return [jnp.where(mask, 1.0, 0.0).astype(bf) for mask in masks]


def soft(scores, allowed):
    scores = jnp.where(allowed, scores, NEG_FILL)
    top = jnp.max(scores, -1, keepdims=True)
    raised = jnp.exp(scores - top)
    return raised * (1.0 / jnp.sum(raised, -1, keepdims=True))


def attend(q_ref, k_ref, v_ref, valid_ref, out_ref, heads):
    images, rows, width = q_ref.shape
    keys = k_ref.shape[1]
    masks = head_masks(rows, heads, width)
    factors = as_factors(masks)

    def group(p, carry):
        lanes = pl.ds(pl.multiple_of(128 * p, 128), 128)
        for i in range(images):
            q, k, v = q_ref[i, :, lanes], k_ref[i, :, lanes], v_ref[i, :, lanes]
            allowed = jnp.broadcast_to(valid_ref[i], (rows, keys)) > 0.0
            result = jnp.zeros((rows, 128), f32)
            for mask, factor in zip(masks, factors):
                probs = soft(mm(q * factor, k, RIGHT_T), allowed)
                result = jnp.where(mask, mm(probs.astype(bf), v), result)
            out_ref[i, :, lanes] = result.astype(bf)
        return carry

    lax.fori_loop(0, width // 128, group, 0)


def attend_back(q_ref, k_ref, v_ref, valid_ref, go_ref, dq_ref, dk_ref, dv_ref, heads):
    images, rows, width = q_ref.shape
    keys = k_ref.shape[1]
    masks = head_masks(rows, heads, width)
    key_masks = head_masks(keys, heads, width)
    factors = as_factors(masks)
    scale = 1.0 / math.sqrt(width // heads)

    def group(p, carry):
        lanes = pl.ds(pl.multiple_of(128 * p, 128), 128)
        for i in range(images):
            q, k, v = q_ref[i, :, lanes], k_ref[i, :, lanes], v_ref[i, :, lanes]
            go = go_ref[i, :, lanes]
            allowed = jnp.broadcast_to(valid_ref[i], (rows, keys)) > 0.0
            dq = jnp.zeros((rows, 128), f32)
            dk = jnp.zeros((keys, 128), f32)
            dv = jnp.zeros((keys, 128), f32)
            for mask, key_mask, factor in zip(masks, key_masks, factors):
                probs = soft(mm(q * factor, k, RIGHT_T), allowed)
                dv = jnp.where(key_mask, mm(probs.astype(bf), go, LEFT_T), dv)
                dprobs = mm(go * factor, v, RIGHT_T)
                dscores = probs * (dprobs - jnp.sum(dprobs * probs, -1, keepdims=True))
                low = dscores.astype(bf)
                dq = jnp.where(mask, mm(low, k) * scale, dq)
                dk = jnp.where(key_mask, mm(low, q, LEFT_T), dk)
            dq_ref[i, :, lanes] = dq
            dk_ref[i, :, lanes] = dk
            dv_ref[i, :, lanes] = dv
        return carry

    lax.fori_loop(0, width // 128, group, 0)


def split_rows(ref, value):
    images, rows, _ = ref.shape
    for i in range(images):
        ref[i] = value[rows * i : rows * i + rows].astype(ref.dtype)


def flat(ref):
    return jnp.concatenate([ref[i] for i in range(ref.shape[0])], 0)


STRIP = 384


def feed_forward(normed, mid, up, down, vec, pre_ref, acc_ref):
    acc_ref[...] = mid

    def strip(c, carry):
        lanes = pl.ds(pl.multiple_of(c * STRIP, 128), STRIP)
        pre = mm(normed, up[:, lanes]) + vec.part(8, c * STRIP, STRIP)
        if pre_ref is not None:
            pre_ref[:, lanes] = pre
        acc_ref[...] += mm(gelu(pre).astype(bf), down[lanes, :])
        return carry

    lax.fori_loop(0, up.shape[1] // STRIP, strip, 0)
    return acc_ref[...] + vec[9]


def encoder_kernel(
    slots, table, rows_ref, pos_ref, valid_ref, vec_ref,
    z_out, e_out, q_out, k_out, v_out, att_out, mid_out, pre_out, hid_out,
    wp, wqkv, wo, w1, w2, acc, sems,
):
    vec = Vec(vec_ref, enc_lengths())
    groups = load_blocks(table, slots, sems, 0, enc_shapes(), (wp, wqkv, wo, w1, w2))
    start_all(groups)
    wait_group(groups[0])
    e = mm(rows_ref[...], wp[...]) + vec[0] + pos_ref[...]
    e_out[...] = e
    normed = norm(e, vec[1], vec[2]).astype(bf)
    wait_group(groups[1])
    split_rows(q_out, (mm(normed, wqkv[:, :D]) + vec[3]) * (1.0 / math.sqrt(D // H)))
    split_rows(k_out, mm(normed, wqkv[:, D : 2 * D]))
    split_rows(v_out, mm(normed, wqkv[:, 2 * D :]) + vec[4])
    attend(q_out, k_out, v_out, valid_ref, att_out, H)
    wait_group(groups[2])
    mid = e + mm(flat(att_out), wo[...]) + vec[5]
    mid_out[...] = mid
    hidden = norm(mid, vec[6], vec[7]).astype(bf)
    wait_group(groups[3])
    wait_group(groups[4])
    hid = feed_forward(hidden, mid, w1, w2, vec, pre_out, acc)
    hid_out[...] = hid
    z_out[...] = norm(hid, vec[10], vec[11]).astype(bf)


def target_kernel(
    slots, table, all_ref, pos_all_ref, some_ref, pos_some_ref, valid_ref, vec_ref,
    out_ref, wp, wqkv, wo, w1, w2, q, k, v, att, acc, sems,
):
    vec = Vec(vec_ref, enc_lengths())
    groups = load_blocks(table, slots, sems, 0, enc_shapes(), (wp, wqkv, wo, w1, w2))
    start_all(groups)
    wait_group(groups[0])
    e = mm(all_ref[...], wp[...]) + vec[0] + pos_all_ref[...]
    normed = norm(e, vec[1], vec[2]).astype(bf)
    wait_group(groups[1])
    split_rows(k, mm(normed, wqkv[:, D : 2 * D]))
    split_rows(v, mm(normed, wqkv[:, 2 * D :]) + vec[4])
    e = mm(some_ref[...], wp[...]) + vec[0] + pos_some_ref[...]
    normed = norm(e, vec[1], vec[2]).astype(bf)
    split_rows(q, (mm(normed, wqkv[:, :D]) + vec[3]) * (1.0 / math.sqrt(D // H)))
    attend(q, k, v, valid_ref, att, H)
    wait_group(groups[2])
    mid = e + mm(flat(att), wo[...]) + vec[5]
    hidden = norm(mid, vec[6], vec[7]).astype(bf)
    wait_group(groups[3])
    wait_group(groups[4])
    hid = feed_forward(hidden, mid, w1, w2, vec, None, acc)
    out_ref[...] = norm_parts(norm(hid, vec[10], vec[11]))[0]


class Flow:
    def __init__(self, outs, stage, depth, me):
        self.outs, self.stage, self.depth, self.me = outs, stage, depth, me

    def put(self, value, j):
        edge, depth = value.shape[-1], self.depth
        if depth % 8:
            self.stage[j] = value
        else:
            cut = value.reshape(self.stage.shape[:2] + (depth, edge))
            self.stage[:, :, depth * j : depth * j + depth, :] = cut

    def copies(self, start, count, sems):
        depth = self.depth
        if depth % 8:
            target = self.outs[0].at[pl.ds(start, count)]
            return [pltpu.make_async_copy(self.stage.at[pl.ds(0, count)], target, sems[0])]
        group = len(self.outs)
        mine = self.me & (group - 1)
        made = []
        for p in range(group):
            source = self.stage.at[:, mine ^ p, pl.ds(0, depth * count), :]
            target = self.outs[p].at[:, pl.ds(depth * start, depth * count), :]
            made.append(pltpu.make_async_copy(source, target, sems[p]))
        return made


GROUP_BITS = 2
GROUP = 1 << GROUP_BITS


def sems_of(ref, turn):
    return [ref.at[turn, p] for p in range(GROUP)]


def raise_top(top_ref, value):
    top_ref[...] = jnp.maximum(top_ref[...], jnp.max(jnp.abs(value), 0, keepdims=True))


def predictor_kernel(
    depth, slots, table, z_ref, pos_c_ref, pos_t_ref, valid_ref, tgt_ref, tmask_ref, vec_ref,
    dz_out, out_0, out_1, out_2, out_3, vec_out, loss_out, top_out,
    win, wqkv, wo, w1, w2, wout, q, k, v, att, go, dq, dk, dv, pre_ref, act_ref, dpre_ref, acc, stage, sems, flow_sems,
):
    vec, grads = Vec(vec_ref, pred_lengths()), Vec(vec_out, pred_lengths())
    edge = table[0].shape[-1]
    flow = Flow((out_0, out_1, out_2, out_3), stage, depth, slots[2 * (NBE + NBP) + 1])
    images = z_ref.shape[0] // LC
    groups = load_blocks(table, slots, sems, NBE, pred_shapes(), (win, wqkv, wo, w1, w2, wout))
    start_all(groups)
    for group in groups:
        wait_group(group)
    firsts = offsets([h * b // (edge * edge) for h, b in pred_shapes()])

    def store(index, matrix):
        for row in range(matrix.shape[0] // edge):
            for column in range(matrix.shape[1] // edge):
                j = firsts[index] + row * (pred_shapes()[index][1] // edge) + column
                value = matrix[row * edge : row * edge + edge, column * edge : column * edge + edge]
                raise_top(top_out, value)
                flow.put(value, j)

    top_out[...] = jnp.zeros_like(top_out)
    z = z_ref[...]
    x_c = mm(z, win[...]) + vec[0] + pos_c_ref[...]
    x_t = vec[13] + pos_t_ref[...]
    n_c = norm(x_c, vec[1], vec[2]).astype(bf)
    n_t = norm(x_t, vec[1], vec[2]).astype(bf)
    split_rows(q, (mm(n_t, wqkv[:, :PD]) + vec[3]) * (1.0 / math.sqrt(PD // PH)))
    for ref, start, bias in ((k, PD, 0.0), (v, 2 * PD, vec[4])):
        of_c = mm(n_c, wqkv[:, start : start + PD]) + bias
        of_t = mm(n_t, wqkv[:, start : start + PD]) + bias
        count = NT * LT
        for i in range(images):
            ref[i, :LC, :] = of_c[LC * i : LC * i + LC].astype(bf)
            ref[i, LC:, :] = of_t[count * i : count * i + count].astype(bf)
    attend(q, k, v, valid_ref, att, PH)
    mid = x_t + mm(flat(att), wo[...]) + vec[5]
    n_two = norm(mid, vec[6], vec[7]).astype(bf)
    y = feed_forward(n_two, mid, w1, w2, vec, pre_ref, acc)
    n_three = norm(y, vec[10], vec[11]).astype(bf)
    difference = mm(n_three, wout[...]) + vec[12] - tgt_ref[...]
    tmask = tmask_ref[...]
    magnitude = jnp.abs(difference)
    loss = jnp.where(magnitude < 1.0, 0.5 * difference * difference, magnitude - 0.5) * tmask
    loss_out[...] = col_sum(loss)
    grad = jnp.clip(difference, -1.0, 1.0) * tmask

    grads[12] = col_sum(grad)
    low = grad.astype(bf)
    store(5, mm(n_three.T, low))
    dy, grads[10], grads[11] = norm_back(y, vec[10], mm(low, wout[...], RIGHT_T))
    grads[9] = col_sum(dy)
    low = dy.astype(bf)
    acc[...] = jnp.zeros_like(acc)

    def strip(c, carry):
        lanes = pl.ds(pl.multiple_of(c * STRIP, 128), STRIP)
        pre = pre_ref[:, lanes]
        act_ref[:, lanes] = gelu(pre).astype(bf)
        dpre = mm(low, w2[lanes, :], RIGHT_T) * gelu_slope(pre)
        grads.put_part(8, c * STRIP, STRIP, col_sum(dpre))
        dpre = dpre.astype(bf)
        dpre_ref[:, lanes] = dpre
        acc[...] += mm(dpre, w1[:, lanes], RIGHT_T)
        return carry

    lax.fori_loop(0, PFF // STRIP, strip, 0)
    store(4, mm(act_ref[...].T, low))
    store(3, mm(n_two.T, dpre_ref[...]))
    dmid, grads[6], grads[7] = norm_back(mid, vec[6], acc[...])
    dmid = dmid + dy
    grads[5] = col_sum(dmid)
    low = dmid.astype(bf)
    split_rows(go, mm(low, wo[...], RIGHT_T))
    store(2, mm(flat(att).T, low))
    attend_back(q, k, v, valid_ref, go, dq, dk, dv, PH)
    d_q, d_k, d_v = flat(dq), [dk[i] for i in range(images)], [dv[i] for i in range(images)]
    grads[3] = col_sum(d_q)
    grads[4] = sum(col_sum(part) for part in d_v)
    q_low = d_q.astype(bf)
    k_c = jnp.concatenate([part[:LC] for part in d_k], 0).astype(bf)
    k_t = jnp.concatenate([part[LC:] for part in d_k], 0).astype(bf)
    v_c = jnp.concatenate([part[:LC] for part in d_v], 0).astype(bf)
    v_t = jnp.concatenate([part[LC:] for part in d_v], 0).astype(bf)
    n_c_t, n_t_t = n_c.T, n_t.T
    store(
        1,
        jnp.concatenate(
            [mm(n_t_t, q_low), mm(n_c_t, k_c) + mm(n_t_t, k_t), mm(n_c_t, v_c) + mm(n_t_t, v_t)], 1
        ),
    )
    wq, wk, wv = wqkv[:, :PD], wqkv[:, PD : 2 * PD], wqkv[:, 2 * PD :]
    dn_t = mm(q_low, wq, RIGHT_T) + mm(k_t, wk, RIGHT_T) + mm(v_t, wv, RIGHT_T)
    dn_c = mm(k_c, wk, RIGHT_T) + mm(v_c, wv, RIGHT_T)
    dx_t, gain_t, shift_t = norm_back(x_t, vec[1], dn_t)
    dx_c, gain_c, shift_c = norm_back(x_c, vec[1], dn_c)
    grads[1] = gain_t + gain_c
    grads[2] = shift_t + shift_c
    dx_t = dx_t + dmid
    grads[13] = col_sum(dx_t)
    grads[0] = col_sum(dx_c)
    low = dx_c.astype(bf)
    dz_out[...] = mm(low, win[...], RIGHT_T).astype(bf)
    store(0, mm(z.T, low))
    leaving = flow.copies(0, NBP, sems_of(flow_sems, 0))
    for copy in leaving:
        copy.start()
    for copy in leaving:
        copy.wait()


class Store:
    def __init__(self, top, sems):
        self.top, self.sems, self.sent = top, sems, []

    def run(self, flow, slots, start, shape, left_t, right):
        edge = slots.shape[-1]
        columns, rows = shape[1] // edge, shape[0] // edge
        for first in range(0, rows * columns, 4):
            turn = len(self.sent)
            if turn >= 2:
                for copy in self.sent[turn - 2]:
                    copy.wait()
            flow.stage = slots.at[turn % 2]
            for b in range(4):
                row, column = divmod(first + b, columns)
                value = mm(
                    left_t[row * edge : row * edge + edge, :],
                    right[:, column * edge : column * edge + edge],
                )
                raise_top(self.top, value)
                flow.put(value, b)
            made = flow.copies(start + first, 4, sems_of(self.sems, turn))
            for copy in made:
                copy.start()
            self.sent.append(made)

    def finish(self):
        for made in self.sent[-2:]:
            for copy in made:
                copy.wait()


def feed_back_kernel(
    depth, slots, table, dz_ref, mid_ref, pre_ref, hid_ref, vec_ref,
    out_0, out_1, out_2, out_3, dmid_out, vec_out, top_out,
    w1, w2, act_t, dpre_ref, x_t, low_ref, acc, stage, sems, out_sems,
):
    vec, grads = Vec(vec_ref, enc_lengths()), Vec(vec_out, enc_lengths())
    flow = Flow((out_0, out_1, out_2, out_3), None, depth, slots[2 * (NBE + NBP) + 1])
    groups = load_blocks(table, slots, sems, 0, enc_shapes(), (None, None, None, w1, w2))
    start_all(groups)
    top_out[...] = jnp.zeros_like(top_out)
    hid = hid_ref[...]
    dy, grads[10], grads[11] = norm_back(hid, vec[10], dz_ref[...].astype(f32))
    grads[9] = col_sum(dy)
    low = dy.astype(bf)
    low_ref[...] = low
    wait_group(groups[4])
    wait_group(groups[3])
    acc[...] = jnp.zeros_like(acc)

    def strip(c, carry):
        lanes = pl.ds(pl.multiple_of(c * STRIP, 128), STRIP)
        pre = pre_ref[:, lanes]
        act_t[lanes, :] = gelu(pre).astype(bf).T
        dpre = mm(low, w2[lanes, :], RIGHT_T) * gelu_slope(pre)
        grads.put_part(8, c * STRIP, STRIP, col_sum(dpre))
        dpre = dpre.astype(bf)
        dpre_ref[:, lanes] = dpre
        acc[...] += mm(dpre, w1[:, lanes], RIGHT_T)
        return carry

    lax.fori_loop(0, FF // STRIP, strip, 0)
    mid = mid_ref[...]
    dmid, grads[6], grads[7] = norm_back(mid, vec[6], acc[...])
    dmid_out[...] = dmid + dy
    x_t[...] = (norm_parts(mid)[0] * vec[6] + vec[7]).astype(bf).T
    store = Store(top_out, out_sems)
    store.run(flow, stage, 16, (FF, D), act_t, low_ref)
    store.run(flow, stage, 0, (D, FF), x_t, dpre_ref)
    store.finish()


def attention_back_kernel(
    depth, slots, table, dmid_ref, rows_ref, e_ref, q, k, v, att_ref, valid_ref, vec_ref,
    out_0, out_1, out_2, out_3, vec_out, top_out,
    wqkv, wo, go, dq, dk, dv, x_t, dqkv, stage, sems, out_sems,
):
    vec, grads = Vec(vec_ref, enc_lengths()), Vec(vec_out, enc_lengths())
    flow = Flow((out_0, out_1, out_2, out_3), None, depth, slots[2 * (NBE + NBP) + 1])
    groups = load_blocks(table, slots, sems, 0, enc_shapes(), (None, wqkv, wo, None, None))
    start_all(groups[::-1])
    top_out[...] = jnp.zeros_like(top_out)
    store = Store(top_out, out_sems)
    dmid = dmid_ref[...]
    grads[5] = col_sum(dmid)
    low = dmid.astype(bf)
    wait_group(groups[2])
    wait_group(groups[1])
    split_rows(go, mm(low, wo[...], RIGHT_T))
    x_t[...] = flat(att_ref).T
    dqkv[:, :D] = low
    store.run(flow, stage, 16, (D, D), x_t, dqkv)
    attend_back(q, k, v, valid_ref, go, dq, dk, dv, H)
    d_q, d_v = flat(dq), flat(dv)
    grads[3] = col_sum(d_q)
    grads[4] = col_sum(d_v)
    dqkv[:, :D] = d_q.astype(bf)
    dqkv[:, D : 2 * D] = flat(dk).astype(bf)
    dqkv[:, 2 * D :] = d_v.astype(bf)
    e = e_ref[...]
    x_t[...] = norm(e, vec[1], vec[2]).astype(bf).T
    store.run(flow, stage, 4, (D, 3 * D), x_t, dqkv)
    back, grads[1], grads[2] = norm_back(e, vec[1], mm(dqkv[...], wqkv[...], RIGHT_T))
    de = dmid_ref[...] + back
    grads[0] = col_sum(de)
    dqkv[:, :D] = de.astype(bf)
    x_t[...] = rows_ref[...].T
    store.run(flow, stage, 0, (PIX, D), x_t, dqkv)
    store.finish()


def spaces(count):
    return [pl.BlockSpec(memory_space=pltpu.VMEM)] * count


ANYWHERE = pl.BlockSpec(memory_space=pl.ANY)


def weight_scratch(shapes):
    return [pltpu.VMEM(shape, bf) for shape in shapes]


def call_kernel(body, section, places, table, args, outs, any_outs, scratch, name, micros):
    pieces, n_in, n_out = len(table), len(args), len(outs)
    inside = [i for i in range(n_out) if i not in any_outs]
    held = [pltpu.VMEM(a.shape, a.dtype) for a in args]
    held += [pltpu.VMEM(outs[i][0], outs[i][1]) for i in inside]
    n_held = len(held)

    def guarded(places_ref, *refs):
        @pl.when(places_ref[2 * (NBE + NBP)] == section)
        def run():
            sources = refs[:pieces]
            given = refs[pieces : pieces + n_in]
            results = list(refs[pieces + n_in : pieces + n_in + n_out])
            local = refs[pieces + n_in + n_out :]
            mine, rest, sems = local[:n_held], local[n_held:-1], local[-1]
            loads = [
                pltpu.make_async_copy(given[i], mine[i], sems.at[i]) for i in range(n_in)
            ]
            for copy in loads:
                copy.start()
            stores = []
            for place, i in enumerate(inside):
                stores.append(
                    pltpu.make_async_copy(mine[n_in + place], results[i], sems.at[n_in + place])
                )
                results[i] = mine[n_in + place]
            for copy in loads:
                copy.wait()
            body(places_ref, sources, *mine[:n_in], *results, *rest)
            for copy in stores:
                copy.start()
            for copy in stores:
                copy.wait()

    return pl.pallas_call(
        guarded,
        grid_spec=pltpu.PrefetchScalarGridSpec(
            num_scalar_prefetch=1,
            grid=(),
            in_specs=[ANYWHERE] * (pieces + n_in),
            out_specs=[ANYWHERE] * n_out,
            scratch_shapes=held + scratch + [pltpu.SemaphoreType.DMA((n_held,))],
        ),
        out_shape=[jax.ShapeDtypeStruct(shape, kind) for shape, kind in outs],
        compiler_params=pltpu.CompilerParams(vmem_limit_bytes=58 << 20),
        cost_estimate=pl.CostEstimate(
            flops=0, transcendentals=0, bytes_accessed=int(micros * 3.0e6)
        ),
        name=name,
    )(places, *table, *args)


MARKS = 16


def flow_outs(count, edge, ranks):
    depth = edge // ranks
    if depth % 8:
        return [((count, edge, edge), f32)] + [((8, edge), f32)] * (GROUP - 1)
    return [((ranks // GROUP, depth * count + MARKS, edge), f32)] * GROUP


def stage_shape(count, edge, ranks):
    depth = edge // ranks
    return (count, edge, edge) if depth % 8 else (ranks // GROUP, GROUP, depth * count, edge)


def encoder_call(slots, table, rows, pos, valid, vec):
    n = rows.shape[0]
    images = n // LC
    per = (images, LC, D)
    outs = [((n, D), bf), ((n, D), f32), (per, bf), (per, bf), (per, bf), (per, bf)]
    outs += [((n, D), f32), ((n, FF), f32), ((n, D), f32)]
    scratch = weight_scratch(enc_shapes()) + [pltpu.VMEM((n, D), f32), pltpu.SemaphoreType.DMA((NBE,))]
    args = (rows, pos, valid, vec)
    return call_kernel(encoder_kernel, 0, slots, table, args, outs, (), scratch, "encoder_forward", 25)


def target_call(slots, table, rows, pos, some, pos_some, valid, vec, images):
    n = some.shape[0]
    keys = rows.shape[0] // images
    per, wide = (images, n // images, D), (images, keys, D)
    scratch = weight_scratch(enc_shapes()) + [
        pltpu.VMEM(per, bf),
        pltpu.VMEM(wide, bf),
        pltpu.VMEM(wide, bf),
        pltpu.VMEM(per, bf),
        pltpu.VMEM((n, D), f32),
        pltpu.SemaphoreType.DMA((NBE,)),
    ]
    args = (rows, pos, some, pos_some, valid, vec)
    outs = [((n, D), f32)]
    return call_kernel(target_kernel, 1, slots, table, args, outs, (), scratch, "target_forward", 25)[0]


def predictor_call(slots, table, z, pos_c, pos_t, valid, tgt, tmask, vec, ranks):
    n, m = z.shape[0], pos_t.shape[0]
    images = n // LC
    rows, keys = m // images, valid.shape[-1]
    edge = table[0].shape[-1]
    per, wide = (images, rows, PD), (images, keys, PD)
    outs = [((n, D), bf)] + flow_outs(NBP, edge, ranks)
    outs += [((1, VP), f32), ((1, D), f32), ((1, edge), f32)]
    scratch = weight_scratch(pred_shapes()) + [
        pltpu.VMEM(per, bf),
        pltpu.VMEM(wide, bf),
        pltpu.VMEM(wide, bf),
        pltpu.VMEM(per, bf),
        pltpu.VMEM(per, bf),
        pltpu.VMEM(per, f32),
        pltpu.VMEM(wide, f32),
        pltpu.VMEM(wide, f32),
        pltpu.VMEM((m, PFF), f32),
        pltpu.VMEM((m, PFF), bf),
        pltpu.VMEM((m, PFF), bf),
        pltpu.VMEM((m, PD), f32),
        pltpu.VMEM(stage_shape(NBP, edge, ranks), f32),
        pltpu.SemaphoreType.DMA((NBE + NBP,)),
        pltpu.SemaphoreType.DMA((1, GROUP)),
    ]
    args = (z, pos_c, pos_t, valid, tgt, tmask, vec)
    body = functools.partial(predictor_kernel, edge // ranks)
    return call_kernel(body, 1, slots, table, args, outs, (1, 2, 3, 4), scratch, "predictor_step", 50)


def feed_back_call(slots, table, dz, kept, vec, ranks):
    n = dz.shape[0]
    edge = table[0].shape[-1]
    mid, pre, hid = kept
    scratch = weight_scratch(enc_shapes()[3:]) + [
        pltpu.VMEM((FF, n), bf),
        pltpu.VMEM((n, FF), bf),
        pltpu.VMEM((D, n), bf),
        pltpu.VMEM((n, D), bf),
        pltpu.VMEM((n, D), f32),
        pltpu.VMEM((2,) + stage_shape(4, edge, ranks), f32),
        pltpu.SemaphoreType.DMA((NBE,)),
        pltpu.SemaphoreType.DMA((8, GROUP)),
    ]
    outs = flow_outs(32, edge, ranks)
    outs += [((n, D), f32), ((1, VE), f32), ((1, edge), f32)]
    args = (dz, mid, pre, hid, vec)
    body = functools.partial(feed_back_kernel, edge // ranks)
    return call_kernel(body, 0, slots, table, args, outs, (0, 1, 2, 3), scratch, "feed_backward", 25)


def attention_back_call(slots, table, dmid, rows, kept, valid, vec, ranks):
    n = rows.shape[0]
    images = n // LC
    edge = table[0].shape[-1]
    per = (images, LC, D)
    e, q, k, v, att = kept
    scratch = weight_scratch(enc_shapes()[1:3]) + [
        pltpu.VMEM(per, bf),
        pltpu.VMEM(per, f32),
        pltpu.VMEM(per, f32),
        pltpu.VMEM(per, f32),
        pltpu.VMEM((D, n), bf),
        pltpu.VMEM((n, 3 * D), bf),
        pltpu.VMEM((2,) + stage_shape(4, edge, ranks), f32),
        pltpu.SemaphoreType.DMA((NBE,)),
        pltpu.SemaphoreType.DMA((5, GROUP)),
    ]
    outs = flow_outs(20, edge, ranks) + [((1, VE), f32), ((1, edge), f32)]
    args = (dmid, rows, e, q, k, v, att, valid, vec)
    body = functools.partial(attention_back_kernel, edge // ranks)
    return call_kernel(body, 0, slots, table, args, outs, (0, 1, 2, 3), scratch, "attention_backward", 25)


def soap_first(flags, factor, *arrays):
    n, e = arrays[0].shape[:2]
    one = pl.BlockSpec((1, e, e), lambda i, *_: (i, 0, 0))
    two = pl.BlockSpec((1, 2, e, e), lambda i, *_: (i, 0, 0, 0))
    single = jax.ShapeDtypeStruct((n, e, e), f32)
    double = jax.ShapeDtypeStruct((n, 2, e, e), f32)
    return pl.pallas_call(
        first_kernel,
        grid_spec=pltpu.PrefetchScalarGridSpec(
            num_scalar_prefetch=2, grid=(n,), in_specs=[one] * 8, out_specs=[one] * 5 + [two] * 2
        ),
        out_shape=[single] * 5 + [double] * 2,
        compiler_params=pltpu.CompilerParams(vmem_limit_bytes=56 << 20),
        name="soap_first",
    )(flags, factor, *arrays)


def soap_factor(flags, base, gram):
    n, _, e, _ = base.shape
    whole = pl.BlockSpec(memory_space=pltpu.VMEM)
    return pl.pallas_call(
        factor_kernel,
        grid_spec=pltpu.PrefetchScalarGridSpec(
            num_scalar_prefetch=1,
            grid=(),
            in_specs=[whole] * 2,
            out_specs=whole,
            scratch_shapes=[
                pltpu.VMEM((n, 2, e, e), f32),
                pltpu.VMEM((n, 2, e, e), f32),
                pltpu.VMEM((n, 2, 128, 128), f32),
            ],
        ),
        out_shape=jax.ShapeDtypeStruct(base.shape, f32),
        compiler_params=pltpu.CompilerParams(vmem_limit_bytes=56 << 20),
        name="soap_factor",
    )(flags, base, gram)


def soap_last(flags, left, right, moment, fresh):
    n, e = left.shape[:2]
    one = pl.BlockSpec((1, e, e), lambda i, *_: (i, 0, 0))
    two = pl.BlockSpec((1, 2, e, e), lambda i, *_: (i, 0, 0, 0))
    return pl.pallas_call(
        last_kernel,
        grid_spec=pltpu.PrefetchScalarGridSpec(
            num_scalar_prefetch=1, grid=(n,), in_specs=[one] * 3 + [two], out_specs=[one] * 3
        ),
        out_shape=[jax.ShapeDtypeStruct((n, e, e), f32)] * 3,
        compiler_params=pltpu.CompilerParams(vmem_limit_bytes=56 << 20),
        name="soap_last",
    )(flags, left, right, moment, fresh)


def place_shares(slots, second, enc_share, pred_share, ranks, slot_count):
    depth, edge = enc_share.shape[1:]

    def body(slots_ref, second_ref, enc_ref, pred_ref, out_ref):
        def run(source, first, count):
            def copy(j, carry):
                slot = slots_ref[first + j]
                rows = pl.ds(pl.multiple_of(slot % slot_count * depth, depth), depth)
                out_ref[slot // slot_count, rows, :] = source[j]
                return carry

            lax.fori_loop(0, count, copy, 0)

        @pl.when(second_ref[0] == 0)
        def enc():
            run(enc_ref, 0, NBE)

        @pl.when(second_ref[0] != 0)
        def pred():
            run(pred_ref, NBE, NBP)

    return pl.pallas_call(
        body,
        grid_spec=pltpu.PrefetchScalarGridSpec(
            num_scalar_prefetch=2, grid=(), in_specs=spaces(2), out_specs=spaces(1)[0]
        ),
        out_shape=jax.ShapeDtypeStruct((ranks, slot_count * depth + MARKS, edge), f32),
        compiler_params=pltpu.CompilerParams(vmem_limit_bytes=40 << 20),
        name="place_shares",
    )(slots, second, enc_share, pred_share)


ROUNDS = (
    (((1, 0), (2, 1), (4, 2)), ()),
    (((5, 0), (6, 1), (8, 3)), (1, 2, 4)),
    (((3, 0), (7, 1)), (5, 6)),
    (((9, 0), (10, 1), (12, 2)), (3, 7, 8)),
    (((13, 0), (14, 1)), (9, 10, 12)),
    (((11, 0), (15, 1)), (13, 14)),
)


def gather_pieces(own, extra):
    both = Exchange((0, 1))
    if both.ranks != 16:
        return None, extra
    held = {0: own}
    for number, (moves, awaited) in enumerate(ROUNDS):
        names = sorted({piece ^ (1 << bit) for piece, bit in moves} | set(awaited))
        values = [held[name] for name in names]
        if number == 2:
            values, extra = lax.optimization_barrier((values, extra))
        elif awaited:
            values = lax.optimization_barrier(values)
        source = dict(zip(names, values))
        for piece, bit in moves:
            held[piece] = both.swap(source[piece ^ (1 << bit)], bit)
    return [held[piece] for piece in range(both.ranks)], extra


class Exchange:
    def __init__(self, sections):
        self.ranks = lax.axis_size("dp")
        self.bits = self.ranks.bit_length() - 1
        self.sections = sections

    def swap(self, value, bit):
        return self.trade(value, 1 << bit)

    def trade(self, value, flip):
        pairs = [
            (s * self.ranks + i, s * self.ranks + (i ^ flip))
            for s in self.sections
            for i in range(self.ranks)
        ]
        return lax.ppermute(value, ("section", "dp"), pairs)

    def total(self, value):
        for bit in range(self.bits):
            value = value + self.swap(value, bit)
        return value


def wire_exponent(bound):
    return jnp.floor(jnp.log2(WIRE_TOP / jnp.maximum(bound, 1e-30)))


def pack(values, exponent):
    row = lax.broadcasted_iota(jnp.int32, values.shape, values.ndim - 2)
    marked = jnp.where(row < values.shape[-2] - MARKS, values * jnp.exp2(exponent), exponent)
    return marked.astype(WIRE)


def flow_pieces(arrays, ranks):
    if arrays[1].ndim == 3:
        return list(arrays)
    blocks, edge = arrays[0].shape[:2]
    cut = arrays[0].reshape(blocks, ranks, edge // ranks, edge).transpose(1, 0, 2, 3)
    cut = jnp.pad(cut.reshape(ranks, -1, edge), ((0, 0), (0, MARKS), (0, 0)))
    return cut_pieces(cut, 0, GROUP)


def cut_pieces(shares, shift, size):
    mine = (lax.axis_index("dp") >> shift) & (size - 1)
    cut = shares.reshape((shares.shape[0] // size, size) + shares.shape[1:])
    return [lax.dynamic_index_in_dim(cut, mine ^ p, 1, keepdims=False) for p in range(size)]


def pack_pieces(pieces, bound):
    return [pack(piece, wire_exponent(bound)) for piece in pieces[1:]]


def send_packed(exchange, lows, shift):
    return [exchange.trade(low, (p + 1) << shift) for p, low in enumerate(lows)]


def send_pieces(exchange, pieces, shift, bound):
    return send_packed(exchange, pack_pieces(pieces, bound), shift)


def add_pieces(keep, arrived, bound):
    for got in arrived:
        unscale = jnp.exp2(-got[0, -1, 0].astype(f32))
        keep = keep + got.astype(f32) * unscale
        bound = bound + WIRE_TOP * unscale
    return keep, bound


def finish_sum(exchange, shares, bound):
    shift = GROUP_BITS
    while shares.shape[0] > 1:
        pieces = cut_pieces(shares, shift, min(GROUP, shares.shape[0]))
        arrived = send_pieces(exchange, pieces, shift, bound)
        shares, bound = add_pieces(pieces[0], arrived, bound)
        shift += GROUP_BITS
    return shares[0, :-MARKS], bound


def on_device(
    pixels,
    ctx_idx,
    ctx_len,
    tgt_idx,
    tgt_len,
    slot_of,
    weights,
    first_moment,
    second_moment,
    left_basis,
    right_basis,
    left_stats,
    right_stats,
    vectors,
    vector_first,
    vector_second,
):
    section_index = lax.axis_index("section")
    owner_index = lax.axis_index("dp")
    ranks = lax.axis_size("dp")
    is_first = section_index == 0
    second = section_index.astype(jnp.int32).reshape(1)
    slot_count = weights.shape[1]
    edge = weights.shape[-1]
    enc_slots = slot_of[:NBE]
    pred_slots = slot_of[NBE:]
    row_now = vectors[0]
    enc_vec_now = lax.dynamic_slice_in_dim(row_now, section_index * VP, VE)[None]
    pred_vec_now = row_now[None, :VP]
    pos_enc = sincos(D)
    pos_pred = sincos(PD)
    images = ctx_idx.shape[0]
    rows_all = -(-P_SIZE // 16) * 16
    tgt_flat = tgt_idx.reshape(images, NT * LT)
    ctx_valid = (jnp.arange(LC)[None, :] < ctx_len[:, None]).astype(f32)
    tgt_valid = (jnp.arange(LT)[None, None, :] < tgt_len[:, :, None]).astype(f32)
    tgt_valid = tgt_valid.reshape(images, NT * LT)
    joined_valid = jnp.concatenate([ctx_valid, tgt_valid], 1)[:, None, :]
    all_valid = (jnp.arange(rows_all) < P_SIZE).astype(f32)
    all_valid = jnp.broadcast_to(all_valid, (images, 1, rows_all))

    def pick(index):
        return (index[..., None] == jnp.arange(P_SIZE)).astype(f32)

    ctx_hot = pick(ctx_idx)
    tgt_hot = pick(tgt_flat)

    def choose(hot, values):
        return jnp.einsum(
            "njp,pd->njd", hot, values, precision=lax.Precision.HIGHEST, preferred_element_type=f32
        ).reshape(-1, values.shape[-1])

    def choose_pixels(hot):
        picked = jnp.einsum("njp,npd->njd", hot.astype(bf), pixels, preferred_element_type=f32)
        return picked.astype(bf).reshape(-1, PIX)

    pixel_rows = choose_pixels(ctx_hot)
    enc_pos_ctx = choose(ctx_hot, pos_enc)
    padding = ((0, 0), (0, rows_all - P_SIZE), (0, 0))
    pixel_all = jnp.pad(pixels, padding).reshape(-1, PIX)
    pos_all = jnp.broadcast_to(jnp.pad(pos_enc[None], padding), (images, rows_all, D)).reshape(-1, D)
    pixel_tgt = choose_pixels(tgt_hot)
    enc_pos_tgt = choose(tgt_hot, pos_enc)
    pred_pos_ctx = choose(ctx_hot, pos_pred)
    pred_pos_tgt = choose(tgt_hot, pos_pred)

    ctx_keys = ctx_valid[:, None, :]
    tgt_mask = tgt_valid.reshape(-1, 1)
    ready = (
        pixel_rows, enc_pos_ctx, ctx_keys, enc_vec_now, pixel_all, pos_all, pixel_tgt, enc_pos_tgt,
        all_valid, pred_pos_ctx, pred_pos_tgt, joined_valid, tgt_mask, pred_vec_now,
    )
    own = weights[0].astype(bf)
    place = [second, owner_index.astype(jnp.int32).reshape(1)]
    table, ready = gather_pieces(own, ready)
    if table is None:
        table = [lax.all_gather(own, "dp", axis=0, tiled=True)]
        places = jnp.concatenate([jnp.zeros_like(slot_of), slot_of] + place)
    else:
        sources = jnp.bitwise_xor(slot_of // slot_count, owner_index)
        places = jnp.concatenate([sources, slot_of % slot_count] + place)
    (
        pixel_rows, enc_pos_ctx, ctx_keys, enc_vec_now, pixel_all, pos_all, pixel_tgt, enc_pos_tgt,
        all_valid, pred_pos_ctx, pred_pos_tgt, joined_valid, tgt_mask, pred_vec_now,
    ) = ready

    z, *kept = encoder_call(places, table, pixel_rows, enc_pos_ctx, ctx_keys, enc_vec_now)
    context = from_behind(z, "section", 1)
    target = target_call(
        places, table, pixel_all, pos_all, pixel_tgt, enc_pos_tgt, all_valid, enc_vec_now, images
    )
    back_send, *pred_flows, pred_vec, loss_lanes, pred_top = predictor_call(
        places, table, context, pred_pos_ctx, pred_pos_tgt, joined_valid, target, tgt_mask, pred_vec_now, ranks
    )
    incoming = from_behind(back_send, "section", -1)
    loss_local = jnp.where(is_first, 0.0, jnp.sum(loss_lanes))

    behind = Exchange((1,))

    def sum_predictor(flows, top):
        bound = jnp.max(top)
        pieces = flow_pieces(flows, ranks)
        shares, bound = add_pieces(pieces[0], send_pieces(behind, pieces, 0, bound), bound)
        return finish_sum(behind, shares, bound)

    def skip_predictor(flows, top):
        return jnp.zeros((edge // ranks * NBP, edge), f32), jnp.zeros((), f32)

    incoming, pred_top = lax.optimization_barrier((incoming, pred_top))
    pred_sum, pred_bound = lax.cond(is_first, skip_predictor, sum_predictor, pred_flows, pred_top)
    incoming, pred_sum = lax.optimization_barrier((incoming, pred_sum))
    *feed_flow, grad_mid, feed_vec, feed_top = feed_back_call(
        places, table, incoming, kept[5:], enc_vec_now, ranks
    )
    ahead = Exchange((0,))
    feed_bound = jnp.max(feed_top)
    feed_pieces = flow_pieces(feed_flow, ranks)
    lows, grad_mid = lax.optimization_barrier((pack_pieces(feed_pieces, feed_bound), grad_mid))
    feed_arrived = send_packed(ahead, lows, 0)
    *rest_flow, rest_vec, rest_top = attention_back_call(
        places, table, grad_mid, pixel_rows, kept[:5], ctx_keys, enc_vec_now, ranks
    )
    rest_bound = jnp.max(rest_top)
    rest_pieces = flow_pieces(rest_flow, ranks)
    lows = pack_pieces(rest_pieces, rest_bound)
    feed_arrived, lows = lax.optimization_barrier((feed_arrived, lows))
    rest_arrived = send_packed(ahead, lows, 0)
    feed_shares, feed_bound = add_pieces(feed_pieces[0], feed_arrived, feed_bound)
    rest_shares, rest_bound = add_pieces(rest_pieces[0], rest_arrived, rest_bound)
    enc_shares = jnp.concatenate([rest_shares[:, :-MARKS], feed_shares], 1)
    enc_sum, enc_bound = finish_sum(ahead, enc_shares, jnp.maximum(rest_bound, feed_bound))
    cut_at = 6 * D
    enc_vec = jnp.concatenate([rest_vec[:, :cut_at], feed_vec[:, cut_at:]], 1)
    depth = edge // ranks
    enc_share = enc_sum.reshape(NBE, depth, edge)
    pred_share = pred_sum.reshape(NBP, depth, edge)

    both = Exchange((0, 1))
    vec_local = jnp.where(is_first, enc_vec[0], jnp.pad(pred_vec[0], (0, VE - VP)))
    count_local = jnp.where(is_first, 0, jnp.sum(tgt_len)).astype(f32)
    scalars = jnp.pad(jnp.stack([loss_local, count_local]), (0, 126))
    summed = both.total(jnp.concatenate([vec_local, scalars]))
    vec_total = jnp.pad(summed[:VE], (0, VW - VE))
    share_squares = jnp.where(
        is_first, jnp.sum(enc_share * enc_share), jnp.sum(pred_share * pred_share)
    )
    squares = both.total(jnp.full((128,), share_squares))
    facts = jnp.stack([squares[0] + jnp.sum(summed[:VE] ** 2), summed[VE], summed[VE + 1]])
    facts = jnp.pad(facts, (0, 125))
    swap_sections = [(i, 1 - i) for i in range(2)]
    facts = facts + lax.ppermute(facts, "section", swap_sections)
    square_total, loss_total, count_total = facts[0], facts[1], facts[2]

    placed = place_shares(slot_of, second, enc_share, pred_share, ranks, slot_count)
    exponent = wire_exponent(jnp.where(is_first, enc_bound, pred_bound))
    payload = pack(placed, exponent)
    owned = lax.all_to_all(payload, "dp", split_axis=0, concat_axis=0, tiled=True).astype(f32)
    unscale = jnp.exp2(-owned[:, -1:, :1])
    owned = (owned[:, : slot_count * depth] * unscale).reshape(ranks, slot_count, depth, edge)
    owned_sum = owned.transpose(1, 0, 2, 3).reshape(slot_count, edge, edge)

    own_ids = owner_index * slot_count + jnp.arange(slot_count)
    enc_here = jnp.any(own_ids[:, None] == enc_slots[None, :], 1)
    pred_here = jnp.any(own_ids[:, None] == pred_slots[None, :], 1)
    trained = jnp.where(is_first, enc_here, pred_here)
    ema_here = jnp.logical_and(jnp.logical_not(is_first), enc_here)
    positions = jnp.arange(VW)
    vec_trained = positions < jnp.where(is_first, VE, VP)
    vec_ema = jnp.logical_and(jnp.logical_not(is_first), positions >= VP)
    grad_norm = jnp.sqrt(square_total) / count_total
    factor = jnp.minimum(1.0, CLIP_LIMIT / (grad_norm + 1e-06)) / count_total

    flags = trained.astype(jnp.int32)
    new_weight, moment, new_second, new_estat, new_fstat, base, gram = soap_first(
        flags,
        factor.reshape(1),
        owned_sum,
        weights[0],
        first_moment[0],
        second_moment[0],
        left_basis[0],
        right_basis[0],
        left_stats[0],
        right_stats[0],
    )
    fresh_bases = soap_factor(flags, base, gram)
    new_left, new_right, new_first = soap_last(
        flags, left_basis[0], right_basis[0], moment, fresh_bases
    )

    correct_one = 1.0 - BETA_FIRST**STEP
    correct_two = 1.0 - BETA_SECOND**STEP
    vec_clipped = vec_total * factor
    fresh_first = BETA_FIRST * vector_first[0] + (1.0 - BETA_FIRST) * vec_clipped
    fresh_second = BETA_SECOND * vector_second[0] + (1.0 - BETA_SECOND) * vec_clipped * vec_clipped
    stepped = row_now - RATE_VECTOR * (fresh_first / correct_one) / (
        jnp.sqrt(fresh_second / correct_two) + ADAM_EPS
    )
    new_vec = jnp.where(vec_trained, stepped, row_now)
    new_vec_first = jnp.where(vec_trained, fresh_first, vector_first[0])
    new_vec_second = jnp.where(vec_trained, fresh_second, vector_second[0])
    from_encoder = from_behind(new_weight.astype(bf), "section", 1).astype(f32)
    vec_from_encoder = from_behind(new_vec.astype(bf), "section", 1).astype(f32)
    new_weight = jnp.where(
        ema_here[:, None, None], EMA_KEEP * weights[0] + (1.0 - EMA_KEEP) * from_encoder, new_weight
    )
    aligned = jnp.concatenate([jnp.zeros((VP,), f32), vec_from_encoder[:VE]])
    new_vec = jnp.where(vec_ema, EMA_KEEP * row_now + (1.0 - EMA_KEEP) * aligned, new_vec)
    return (
        loss_total,
        count_total,
        grad_norm,
        new_weight[None],
        new_first[None],
        new_second[None],
        new_left[None],
        new_right[None],
        new_estat[None],
        new_fstat[None],
        new_vec[None],
        new_vec_first[None],
        new_vec_second[None],
    )


def solution(mesh):
    in_specs = (
        P("dp", None, None),
        P("dp", None),
        P("dp"),
        P("dp", None, None),
        P("dp", None),
        P(),
        P("section", "dp", None, None),
        P("section", "dp", None, None),
        P("section", "dp", None, None),
        P("section", "dp", None, None),
        P("section", "dp", None, None),
        P("section", "dp", None, None),
        P("section", "dp", None, None),
        P("section", None),
        P("section", None),
        P("section", None),
    )
    out_specs = (
        P(),
        P(),
        P(),
        P("section", "dp", None, None),
        P("section", "dp", None, None),
        P("section", "dp", None, None),
        P("section", "dp", None, None),
        P("section", "dp", None, None),
        P("section", "dp", None, None),
        P("section", "dp", None, None),
        P("section", None),
        P("section", None),
        P("section", None),
    )
    return jax.shard_map(
        on_device, mesh=mesh, in_specs=in_specs, out_specs=out_specs, check_vma=False
    )
```

```python
import functools
import math

import jax
import jax.numpy as jnp
from jax import lax
from jax.experimental import pallas as pl
from jax.experimental.pallas import tpu as pltpu
from jax.sharding import PartitionSpec as P

D = 768
FF = 3072
H = 12
PD = 384
PFF = 1536
PH = 12
PIX = 768
GRID = 14
NT = 4
LC = 128
STEP = 10
P_SIZE = 196
LT = 36
NBE = 52
NBP = 16
VE = 11520
VP = 6912
VW = 18432


NORM_EPS = 1e-06
ADAM_EPS = 1e-08
BETA_FIRST = 0.5
BETA_SECOND = 0.5
BETA_STATS = 0.95
RATE_MATRIX = 0.02
RATE_VECTOR = 0.05
DECAY_MATRIX = 0.04
EMA_KEEP = 0.996
CLIP_LIMIT = 1.0
NEG_FILL = -1000000000.0
WIRE = jnp.float16
WIRE_TOP = 16384.0
f32 = jnp.float32
bf = jnp.bfloat16


def from_behind(shard, axis, by):
    size = lax.axis_size(axis)
    pairs = [(i, i + by) for i in range(size) if 0 <= i + by < size]
    return lax.ppermute(shard, axis, pairs)


def enc_shapes():
    return [(PIX, D), (D, 3 * D), (D, D), (D, FF), (FF, D)]


def pred_shapes():
    return [(D, PD), (PD, 3 * PD), (PD, PD), (PD, PFF), (PFF, PD), (PD, D)]


def enc_lengths():
    return [D] * 8 + [FF, D, D, D]


def pred_lengths():
    return [PD] * 8 + [PFF, PD, PD, PD, D, PD]


def sincos(width):
    quarter = width // 4
    frequency = 1.0 / 10000.0 ** (jnp.arange(quarter, dtype=jnp.float32) / quarter)
    cell_ids = jnp.arange(P_SIZE)
    row_pos = (cell_ids // GRID).astype(jnp.float32)[:, None] * frequency
    column_pos = (cell_ids % GRID).astype(jnp.float32)[:, None] * frequency
    return jnp.concatenate(
        [jnp.sin(row_pos), jnp.cos(row_pos), jnp.sin(column_pos), jnp.cos(column_pos)], 1
    )


DIMS = {"nn": (1, 0), "nt": (1, 1), "tn": (0, 0)}

def parts_of(a, count):
    found = []
    for index in range(count):
        piece = a.astype(bf)
        found.append(piece)
        if index + 1 < count:
            a = a - piece.astype(f32)
    return found

def product(left, right, form, pairs):
    ld, rd = DIMS[form]
    lhs = jnp.concatenate([left[i] for i, _ in pairs], ld)
    rhs = jnp.concatenate([right[j] for _, j in pairs], rd)
    return lax.dot_general(lhs, rhs, (((ld,), (rd,)), ((), ())), preferred_element_type=f32)

THREE = ((0, 1), (1, 0), (0, 0))
SIX = ((0, 2), (2, 0), (1, 1), (0, 1), (1, 0), (0, 0))
def mul3(left, right, form="nn"):
    return product(left, right, form, THREE)
def mul6(left, right, form="nn"):
    return product(left, right, form, SIX)

def invert_factors(mats):
    n = mats[0].shape[0]
    lane = lax.broadcasted_iota(jnp.int32, (8, n), 1)
    sub = lax.broadcasted_iota(jnp.int32, (8, n), 0)
    groups = [[a[8 * t : 8 * t + 8, :] for t in range(n // 8)] for a in mats]
    for j in range(n):
        top, at_row = divmod(j, 8)
        here = lane == j
        pick = jnp.full((8, n), j, jnp.int32)
        for tiles in groups:
            column = jnp.take_along_axis(tiles[top], pick, axis=1)
            pivot = jnp.broadcast_to(column[at_row : at_row + 1, :], (8, n))
            row = jnp.broadcast_to(tiles[top][at_row : at_row + 1, :], (8, n))
            scaled = jnp.where(here, 1.0, row) * (1.0 / pivot)
            for t in range(top, n // 8):
                if t > top:
                    column = jnp.take_along_axis(tiles[t], pick, axis=1)
                fresh = jnp.where(here, 0.0, tiles[t]) - column * scaled
                tiles[t] = jnp.where(sub > at_row, fresh, tiles[t]) if t == top else fresh
    results = []
    for tiles in groups:
        rows = []
        for t in range(n // 8):
            at = sub + 8 * t
            pivots = jnp.sum(jnp.where(lane == at, tiles[t], 0.0), axis=1, keepdims=True)
            unit = jnp.where(lane < at, tiles[t], jnp.where(lane == at, 1.0, 0.0))
            rows.append(unit * lax.rsqrt(pivots))
        results.append(jnp.concatenate(rows, 0))
    return results

def first_kernel(flag, factor, g_ref, w_ref, m_ref, v_ref, l_ref, r_ref, e_ref, f_ref,
                 w_out, m_out, v_out, e_out, f_out, base_out, gram_out):
    on = flag[pl.program_id(0)] != 0

    @pl.when(jnp.logical_not(on))
    def keep():
        for source, target in ((w_ref, w_out), (m_ref, m_out), (v_ref, v_out), (e_ref, e_out), (f_ref, f_out)):
            target[...] = source[...]

    @pl.when(on)
    def update():
        correct_one = 1.0 - BETA_FIRST**STEP
        correct_two = 1.0 - BETA_SECOND**STEP
        grad = parts_of(g_ref[0] * factor[0], 3)
        left = parts_of(l_ref[0], 3)
        right = parts_of(r_ref[0], 3)
        rotated = mul3(left, parts_of(mul3(grad, right), 2), "tn")
        moment = BETA_FIRST * m_ref[0] + (1.0 - BETA_FIRST) * rotated
        second = BETA_SECOND * v_ref[0] + (1.0 - BETA_SECOND) * rotated * rotated
        m_out[0] = moment
        v_out[0] = second
        normed = moment / correct_one / (jnp.sqrt(second / correct_two) + ADAM_EPS)
        weight = w_ref[0]
        step = mul3(left, parts_of(mul3(parts_of(normed, 2), right, "nt"), 2))
        w_out[0] = weight - RATE_MATRIX * (step + DECAY_MATRIX * weight)
        for index, (stat, target, basis, form) in enumerate(
            ((e_ref, e_out, left, "nt"), (f_ref, f_out, right, "tn"))
        ):
            fresh = BETA_STATS * stat[0] + (1.0 - BETA_STATS) * mul3(grad, grad, form)
            target[0] = fresh
            moved = mul6(parts_of(fresh, 3), basis)
            base_out[0, index] = moved
            pieces = parts_of(moved, 3)
            edge = moved.shape[-1]
            for start in range(0, edge, 128):
                rows = [piece[:, start : start + 128] for piece in pieces]
                upper = [piece[:, start:] for piece in pieces]
                gram_out[0, index, start : start + 128, start:] = mul6(rows, upper, "tn")

def factor_kernel(flag, base_ref, gram_ref, q_out, base, gram, inverse):
    blocks, edge = base_ref.shape[0], base_ref.shape[-1]
    panel = 128
    count = edge // panel
    base[...] = base_ref[...]
    gram[...] = gram_ref[...]

    def stage(k):
        at = pl.ds(panel * k, panel)
        start = panel * k
        spot = slice(start, start + panel)
        rest = slice(start + panel, edge)

        def block(b, carry):
            @pl.when(flag[b] != 0)
            def run():
                sides = range(2)
                inv = [parts_of(inverse[b, side], 3) for side in sides]
                q = [mul6(parts_of(base[b, side, :, spot], 3), inv[side], "nt") for side in sides]
                for side in sides:
                    q_out[b, side, :, spot] = q[side]
                if k + 1 < count:
                    tops = [mul6(inv[side], parts_of(gram[b, side, spot, rest], 3)) for side in sides]
                    p = [parts_of(top, 3) for top in tops]
                    minus = [mul6(p[side], p[side], "tn") for side in sides]
                    moved = [mul6(parts_of(q[side], 3), p[side]) for side in sides]
                    for side in sides:
                        gram[b, side, rest, rest] = gram[b, side, rest, rest] - minus[side]
                        base[b, side, :, rest] = base[b, side, :, rest] - moved[side]
            return carry

        lax.fori_loop(0, blocks, block, 0)

    def turn(k, carry):
        for which in range(count):
            @pl.when(k == which)
            def load():
                spot = slice(panel * which, panel * which + panel)
                for b in range(blocks):
                    for side in range(2):
                        inverse[b, side] = gram[b, side, spot, spot]
        mats = invert_factors([inverse[b, side] for b in range(blocks) for side in range(2)])
        for b in range(blocks):
            for side in range(2):
                inverse[b, side] = mats[2 * b + side]
        for which in range(count):
            @pl.when(k == which)
            def run():
                stage(which)
        return carry

    lax.fori_loop(0, count, turn, 0)

def last_kernel(flag, l_ref, r_ref, m_ref, q_ref, l_out, r_out, m_out):
    on = flag[pl.program_id(0)] != 0

    @pl.when(jnp.logical_not(on))
    def keep():
        l_out[...] = l_ref[...]
        r_out[...] = r_ref[...]
        m_out[...] = m_ref[...]

    @pl.when(on)
    def update():
        l_out[0] = q_ref[0, 0]
        r_out[0] = q_ref[0, 1]
        turn_left = mul3(parts_of(q_ref[0, 0], 2), parts_of(l_ref[0], 2), "tn")
        turn_right = mul3(parts_of(r_ref[0], 2), parts_of(q_ref[0, 1], 2), "tn")
        half = mul3(parts_of(turn_left, 2), parts_of(m_ref[0], 2))
        m_out[0] = mul3(parts_of(half, 2), parts_of(turn_right, 2))

PLAIN = (((1,), (0,)), ((), ()))
RIGHT_T = (((1,), (1,)), ((), ()))
LEFT_T = (((0,), (0,)), ((), ()))
ROOT_HALF = 0.7071067811865476
ROOT_TWO_PI = 2.5066282746310002


def mm(left, right, dims=PLAIN):
    return lax.dot_general(left, right, dims, preferred_element_type=f32)


def norm_parts(x):
    center = x - jnp.mean(x, -1, keepdims=True)
    inverse = lax.rsqrt(jnp.mean(center * center, -1, keepdims=True) + NORM_EPS)
    return center * inverse, inverse


def norm(x, gain, shift):
    return norm_parts(x)[0] * gain + shift


def norm_back(x, gain, grad):
    unit, inverse = norm_parts(x)
    grad_unit = grad * gain
    mean_one = jnp.mean(grad_unit, -1, keepdims=True)
    mean_two = jnp.mean(grad_unit * unit, -1, keepdims=True)
    back = inverse * (grad_unit - mean_one - unit * mean_two)
    return back, col_sum(grad * unit), col_sum(grad)


def col_sum(x):
    return jnp.sum(x, 0, keepdims=True)


def gelu(x):
    return 0.5 * x * (1.0 + lax.erf(x * ROOT_HALF))


def gelu_slope(x):
    return 0.5 * (1.0 + lax.erf(x * ROOT_HALF)) + x * jnp.exp(-0.5 * x * x) * (1.0 / ROOT_TWO_PI)


def offsets(lengths):
    result = [0]
    for length in lengths:
        result.append(result[-1] + length)
    return result


class Vec:
    def __init__(self, ref, lengths):
        self.ref, self.at = ref, offsets(lengths)

    def __getitem__(self, k):
        return self.ref[:, self.at[k] : self.at[k + 1]]

    def __setitem__(self, k, value):
        self.ref[:, self.at[k] : self.at[k + 1]] = value

    def part(self, k, start, size):
        return self.ref[:, pl.ds(pl.multiple_of(self.at[k] + start, 128), size)]

    def put_part(self, k, start, size, value):
        self.ref[:, pl.ds(pl.multiple_of(self.at[k] + start, 128), size)] = value


class Fetch:
    def __init__(self, pieces, places, j, spot, sem):
        self.pieces, self.spot, self.sem = pieces, spot, sem
        self.which, self.index = places[j], places[NBE + NBP + j]

    def copy(self, piece, index):
        return pltpu.make_async_copy(piece.at[index], self.spot, self.sem)

    def start(self):
        if len(self.pieces) == 1:
            self.copy(self.pieces[0], self.index).start()
        else:
            self.start_among(0, len(self.pieces))

    def start_among(self, low, high):
        if high - low == 1:
            self.copy(self.pieces[low], self.index).start()
            return
        middle = (low + high) // 2

        @pl.when(self.which < middle)
        def below():
            self.start_among(low, middle)

        @pl.when(self.which >= middle)
        def above():
            self.start_among(middle, high)

    def wait(self):
        self.copy(self.pieces[0], 0).wait()


def load_blocks(pieces, places, sems, first, shapes, targets):
    edge = pieces[0].shape[-1]
    groups = []
    j = first
    for (height, breadth), target in zip(shapes, targets):
        group = []
        for row in range(height // edge):
            for column in range(breadth // edge):
                if target is not None:
                    spot = target.at[pl.ds(row * edge, edge), pl.ds(column * edge, edge)]
                    group.append(Fetch(pieces, places, j, spot, sems.at[j]))
                j += 1
        groups.append(group)
    return groups


def start_all(groups):
    for group in groups:
        for copy in group:
            copy.start()


def wait_group(group):
    for copy in group:
        copy.wait()


def head_masks(rows, heads, width):
    lane = lax.broadcasted_iota(jnp.int32, (rows, 128), 1)
    size = width // heads
    return [(lane >= size * h) & (lane < size * h + size) for h in range(128 // size)]


def as_factors(masks):
    return [jnp.where(mask, 1.0, 0.0).astype(bf) for mask in masks]


def soft(scores, allowed):
    scores = jnp.where(allowed, scores, NEG_FILL)
    top = jnp.max(scores, -1, keepdims=True)
    raised = jnp.exp(scores - top)
    return raised * (1.0 / jnp.sum(raised, -1, keepdims=True))


def head_jobs(q_ref, k_ref, v_ref, p, span, factors):
    jobs = []
    for g in range(span):
        lanes = pl.ds(pl.multiple_of(128 * (span * p + g), 128), 128)
        for i in range(q_ref.shape[0]):
            q, k, v = q_ref[i, :, lanes], k_ref[i, :, lanes], v_ref[i, :, lanes]
            for h in range(len(factors)):
                jobs.append((i, lanes, h, q, k, v))
    return jobs


def attend(q_ref, k_ref, v_ref, valid_ref, out_ref, heads):
    images, rows, width = q_ref.shape
    keys = k_ref.shape[1]
    masks = head_masks(rows, heads, width)
    factors = as_factors(masks)
    span = 1 if width // 128 % 2 else 2

    def group(p, carry):
        allowed = [jnp.broadcast_to(valid_ref[i], (rows, keys)) > 0.0 for i in range(images)]
        jobs = head_jobs(q_ref, k_ref, v_ref, p, span, factors)
        scores = [mm(q * factors[h], k, RIGHT_T) for _, _, h, q, k, _ in jobs]
        probs = [soft(s, allowed[job[0]]).astype(bf) for s, job in zip(scores, jobs)]
        parts = [mm(probs[n], job[5]) for n, job in enumerate(jobs)]
        for n in range(0, len(jobs), len(masks)):
            result = parts[n]
            for h in range(1, len(masks)):
                result = jnp.where(masks[h], parts[n + h], result)
            out_ref[jobs[n][0], :, jobs[n][1]] = result.astype(bf)
        return carry

    lax.fori_loop(0, width // 128 // span, group, 0)


def attend_back(q_ref, k_ref, v_ref, valid_ref, go_ref, dq_ref, dk_ref, dv_ref, heads):
    images, rows, width = q_ref.shape
    keys = k_ref.shape[1]
    masks = head_masks(rows, heads, width)
    key_masks = head_masks(keys, heads, width)
    factors = as_factors(masks)
    scale = 1.0 / math.sqrt(width // heads)
    span = 1 if width // 128 % 2 else 2

    def group(p, carry):
        allowed = [jnp.broadcast_to(valid_ref[i], (rows, keys)) > 0.0 for i in range(images)]
        jobs = head_jobs(q_ref, k_ref, v_ref, p, span, factors)
        grads = [go_ref[job[0], :, job[1]] for job in jobs]
        scores = [mm(q * factors[h], k, RIGHT_T) for _, _, h, q, k, _ in jobs]
        dprobs = [mm(go * factors[job[2]], job[5], RIGHT_T) for go, job in zip(grads, jobs)]
        probs = [soft(s, allowed[job[0]]) for s, job in zip(scores, jobs)]
        lows = [
            (a * (da - jnp.sum(da * a, -1, keepdims=True))).astype(bf) for a, da in zip(probs, dprobs)
        ]
        dvs = [mm(a.astype(bf), go, LEFT_T) for a, go in zip(probs, grads)]
        dqs = [mm(low, job[4]) for low, job in zip(lows, jobs)]
        dks = [mm(low, job[3], LEFT_T) for low, job in zip(lows, jobs)]
        for n in range(0, len(jobs), len(masks)):
            dq, dk, dv = dqs[n], dks[n], dvs[n]
            for h in range(1, len(masks)):
                dq = jnp.where(masks[h], dqs[n + h], dq)
                dk = jnp.where(key_masks[h], dks[n + h], dk)
                dv = jnp.where(key_masks[h], dvs[n + h], dv)
            i, lanes = jobs[n][:2]
            dq_ref[i, :, lanes] = dq * scale
            dk_ref[i, :, lanes] = dk
            dv_ref[i, :, lanes] = dv
        return carry

    lax.fori_loop(0, width // 128 // span, group, 0)


def split_rows(ref, value):
    images, rows, _ = ref.shape
    for i in range(images):
        ref[i] = value[rows * i : rows * i + rows].astype(ref.dtype)


def flat(ref):
    return jnp.concatenate([ref[i] for i in range(ref.shape[0])], 0)


STRIP = 768


def feed_forward(normed, mid, up, down, vec, pre_ref, acc_ref):
    acc_ref[...] = mid

    def strip(c, carry):
        lanes = pl.ds(pl.multiple_of(c * STRIP, 128), STRIP)
        pre = mm(normed, up[:, lanes]) + vec.part(8, c * STRIP, STRIP)
        if pre_ref is not None:
            pre_ref[:, lanes] = pre
        acc_ref[...] += mm(gelu(pre).astype(bf), down[lanes, :])
        return carry

    lax.fori_loop(0, up.shape[1] // STRIP, strip, 0)
    return acc_ref[...] + vec[9]


def encoder_kernel(
    slots, table, rows_ref, pos_ref, valid_ref, vec_ref,
    z_out, e_out, q_out, k_out, v_out, att_out, mid_out, pre_out, hid_out,
    wp, wqkv, wo, w1, w2, acc, sems,
):
    vec = Vec(vec_ref, enc_lengths())
    groups = load_blocks(table, slots, sems, 0, enc_shapes(), (wp, wqkv, wo, w1, w2))
    start_all(groups)
    wait_group(groups[0])
    e = mm(rows_ref[...], wp[...]) + vec[0] + pos_ref[...]
    e_out[...] = e
    normed = norm(e, vec[1], vec[2]).astype(bf)
    wait_group(groups[1])
    split_rows(q_out, (mm(normed, wqkv[:, :D]) + vec[3]) * (1.0 / math.sqrt(D // H)))
    split_rows(k_out, mm(normed, wqkv[:, D : 2 * D]))
    split_rows(v_out, mm(normed, wqkv[:, 2 * D :]) + vec[4])
    attend(q_out, k_out, v_out, valid_ref, att_out, H)
    wait_group(groups[2])
    mid = e + mm(flat(att_out), wo[...]) + vec[5]
    mid_out[...] = mid
    hidden = norm(mid, vec[6], vec[7]).astype(bf)
    wait_group(groups[3])
    wait_group(groups[4])
    hid = feed_forward(hidden, mid, w1, w2, vec, pre_out, acc)
    hid_out[...] = hid
    z_out[...] = norm(hid, vec[10], vec[11]).astype(bf)


def target_kernel(
    slots, table, all_ref, pos_all_ref, some_ref, pos_some_ref, valid_ref, vec_ref,
    out_ref, wp, wqkv, wo, w1, w2, q, k, v, att, acc, sems,
):
    vec = Vec(vec_ref, enc_lengths())
    groups = load_blocks(table, slots, sems, 0, enc_shapes(), (wp, wqkv, wo, w1, w2))
    start_all(groups)
    wait_group(groups[0])
    e = mm(all_ref[...], wp[...]) + vec[0] + pos_all_ref[...]
    normed = norm(e, vec[1], vec[2]).astype(bf)
    wait_group(groups[1])
    split_rows(k, mm(normed, wqkv[:, D : 2 * D]))
    split_rows(v, mm(normed, wqkv[:, 2 * D :]) + vec[4])
    e = mm(some_ref[...], wp[...]) + vec[0] + pos_some_ref[...]
    normed = norm(e, vec[1], vec[2]).astype(bf)
    split_rows(q, (mm(normed, wqkv[:, :D]) + vec[3]) * (1.0 / math.sqrt(D // H)))
    attend(q, k, v, valid_ref, att, H)
    wait_group(groups[2])
    mid = e + mm(flat(att), wo[...]) + vec[5]
    hidden = norm(mid, vec[6], vec[7]).astype(bf)
    wait_group(groups[3])
    wait_group(groups[4])
    hid = feed_forward(hidden, mid, w1, w2, vec, None, acc)
    out_ref[...] = norm_parts(norm(hid, vec[10], vec[11]))[0]


class Flow:
    def __init__(self, outs, stage, depth, me):
        self.outs, self.stage, self.depth, self.me = outs, stage, depth, me

    def put(self, value, j):
        edge, depth = value.shape[-1], self.depth
        if depth % 8:
            self.stage[j] = value
        else:
            cut = value.reshape(self.stage.shape[:2] + (depth, edge))
            self.stage[:, :, depth * j : depth * j + depth, :] = cut

    def copies(self, start, count, sems):
        depth = self.depth
        if depth % 8:
            target = self.outs[0].at[pl.ds(start, count)]
            return [pltpu.make_async_copy(self.stage.at[pl.ds(0, count)], target, sems[0])]
        group = len(self.outs)
        mine = self.me & (group - 1)
        made = []
        for p in range(group):
            source = self.stage.at[:, mine ^ p, pl.ds(0, depth * count), :]
            target = self.outs[p].at[:, pl.ds(depth * start, depth * count), :]
            made.append(pltpu.make_async_copy(source, target, sems[p]))
        return made


GROUP_BITS = 2
GROUP = 1 << GROUP_BITS


def sems_of(ref, turn):
    return [ref.at[turn, p] for p in range(GROUP)]


def raise_top(top_ref, value):
    top_ref[...] = jnp.maximum(top_ref[...], jnp.max(jnp.abs(value), 0, keepdims=True))


def predictor_kernel(
    depth, slots, table, z_ref, pos_c_ref, pos_t_ref, valid_ref, tgt_ref, tmask_ref, vec_ref,
    dz_out, out_0, out_1, out_2, out_3, vec_out, loss_out, top_out,
    win, wqkv, wo, w1, w2, wout, q, k, v, att, go, dq, dk, dv, pre_ref, act_ref, dpre_ref, acc, stage, sems, flow_sems,
):
    vec, grads = Vec(vec_ref, pred_lengths()), Vec(vec_out, pred_lengths())
    edge = table[0].shape[-1]
    flow = Flow((out_0, out_1, out_2, out_3), stage, depth, slots[2 * (NBE + NBP) + 1])
    images = z_ref.shape[0] // LC
    groups = load_blocks(table, slots, sems, NBE, pred_shapes(), (win, wqkv, wo, w1, w2, wout))
    start_all(groups)
    for group in groups:
        wait_group(group)
    firsts = offsets([h * b // (edge * edge) for h, b in pred_shapes()])

    def store(index, matrix):
        for row in range(matrix.shape[0] // edge):
            for column in range(matrix.shape[1] // edge):
                j = firsts[index] + row * (pred_shapes()[index][1] // edge) + column
                value = matrix[row * edge : row * edge + edge, column * edge : column * edge + edge]
                raise_top(top_out, value)
                flow.put(value, j)

    top_out[...] = jnp.zeros_like(top_out)
    z = z_ref[...]
    x_c = mm(z, win[...]) + vec[0] + pos_c_ref[...]
    x_t = vec[13] + pos_t_ref[...]
    n_c = norm(x_c, vec[1], vec[2]).astype(bf)
    n_t = norm(x_t, vec[1], vec[2]).astype(bf)
    split_rows(q, (mm(n_t, wqkv[:, :PD]) + vec[3]) * (1.0 / math.sqrt(PD // PH)))
    for ref, start, bias in ((k, PD, 0.0), (v, 2 * PD, vec[4])):
        of_c = mm(n_c, wqkv[:, start : start + PD]) + bias
        of_t = mm(n_t, wqkv[:, start : start + PD]) + bias
        count = NT * LT
        for i in range(images):
            ref[i, :LC, :] = of_c[LC * i : LC * i + LC].astype(bf)
            ref[i, LC:, :] = of_t[count * i : count * i + count].astype(bf)
    attend(q, k, v, valid_ref, att, PH)
    mid = x_t + mm(flat(att), wo[...]) + vec[5]
    n_two = norm(mid, vec[6], vec[7]).astype(bf)
    y = feed_forward(n_two, mid, w1, w2, vec, pre_ref, acc)
    n_three = norm(y, vec[10], vec[11]).astype(bf)
    difference = mm(n_three, wout[...]) + vec[12] - tgt_ref[...]
    tmask = tmask_ref[...]
    magnitude = jnp.abs(difference)
    loss = jnp.where(magnitude < 1.0, 0.5 * difference * difference, magnitude - 0.5) * tmask
    loss_out[...] = col_sum(loss)
    grad = jnp.clip(difference, -1.0, 1.0) * tmask

    grads[12] = col_sum(grad)
    low = grad.astype(bf)
    store(5, mm(n_three.T, low))
    dy, grads[10], grads[11] = norm_back(y, vec[10], mm(low, wout[...], RIGHT_T))
    grads[9] = col_sum(dy)
    low = dy.astype(bf)
    acc[...] = jnp.zeros_like(acc)

    def strip(c, carry):
        lanes = pl.ds(pl.multiple_of(c * STRIP, 128), STRIP)
        pre = pre_ref[:, lanes]
        act_ref[:, lanes] = gelu(pre).astype(bf)
        dpre = mm(low, w2[lanes, :], RIGHT_T) * gelu_slope(pre)
        grads.put_part(8, c * STRIP, STRIP, col_sum(dpre))
        dpre = dpre.astype(bf)
        dpre_ref[:, lanes] = dpre
        acc[...] += mm(dpre, w1[:, lanes], RIGHT_T)
        return carry

    lax.fori_loop(0, PFF // STRIP, strip, 0)
    store(4, mm(act_ref[...].T, low))
    store(3, mm(n_two.T, dpre_ref[...]))
    dmid, grads[6], grads[7] = norm_back(mid, vec[6], acc[...])
    dmid = dmid + dy
    grads[5] = col_sum(dmid)
    low = dmid.astype(bf)
    split_rows(go, mm(low, wo[...], RIGHT_T))
    store(2, mm(flat(att).T, low))
    attend_back(q, k, v, valid_ref, go, dq, dk, dv, PH)
    d_q, d_k, d_v = flat(dq), [dk[i] for i in range(images)], [dv[i] for i in range(images)]
    grads[3] = col_sum(d_q)
    grads[4] = sum(col_sum(part) for part in d_v)
    q_low = d_q.astype(bf)
    k_c = jnp.concatenate([part[:LC] for part in d_k], 0).astype(bf)
    k_t = jnp.concatenate([part[LC:] for part in d_k], 0).astype(bf)
    v_c = jnp.concatenate([part[:LC] for part in d_v], 0).astype(bf)
    v_t = jnp.concatenate([part[LC:] for part in d_v], 0).astype(bf)
    n_c_t, n_t_t = n_c.T, n_t.T
    store(
        1,
        jnp.concatenate(
            [mm(n_t_t, q_low), mm(n_c_t, k_c) + mm(n_t_t, k_t), mm(n_c_t, v_c) + mm(n_t_t, v_t)], 1
        ),
    )
    wq, wk, wv = wqkv[:, :PD], wqkv[:, PD : 2 * PD], wqkv[:, 2 * PD :]
    dn_t = mm(q_low, wq, RIGHT_T) + mm(k_t, wk, RIGHT_T) + mm(v_t, wv, RIGHT_T)
    dn_c = mm(k_c, wk, RIGHT_T) + mm(v_c, wv, RIGHT_T)
    dx_t, gain_t, shift_t = norm_back(x_t, vec[1], dn_t)
    dx_c, gain_c, shift_c = norm_back(x_c, vec[1], dn_c)
    grads[1] = gain_t + gain_c
    grads[2] = shift_t + shift_c
    dx_t = dx_t + dmid
    grads[13] = col_sum(dx_t)
    grads[0] = col_sum(dx_c)
    low = dx_c.astype(bf)
    dz_out[...] = mm(low, win[...], RIGHT_T).astype(bf)
    store(0, mm(z.T, low))
    leaving = flow.copies(0, NBP, sems_of(flow_sems, 0))
    for copy in leaving:
        copy.start()
    for copy in leaving:
        copy.wait()


class Store:
    def __init__(self, top, sems):
        self.top, self.sems, self.sent = top, sems, []

    def run(self, flow, slots, start, shape, left_t, right):
        edge = slots.shape[-1]
        columns, rows = shape[1] // edge, shape[0] // edge
        for first in range(0, rows * columns, 4):
            turn = len(self.sent)
            if turn >= 2:
                for copy in self.sent[turn - 2]:
                    copy.wait()
            flow.stage = slots.at[turn % 2]
            for b in range(4):
                row, column = divmod(first + b, columns)
                value = mm(
                    left_t[row * edge : row * edge + edge, :],
                    right[:, column * edge : column * edge + edge],
                )
                raise_top(self.top, value)
                flow.put(value, b)
            made = flow.copies(start + first, 4, sems_of(self.sems, turn))
            for copy in made:
                copy.start()
            self.sent.append(made)

    def finish(self):
        for made in self.sent[-2:]:
            for copy in made:
                copy.wait()


def feed_back_kernel(
    depth, slots, table, dz_ref, mid_ref, pre_ref, hid_ref, vec_ref,
    out_0, out_1, out_2, out_3, dmid_out, vec_out, top_out,
    w1, w2, act_t, dpre_ref, x_t, low_ref, acc, stage, sems, out_sems,
):
    vec, grads = Vec(vec_ref, enc_lengths()), Vec(vec_out, enc_lengths())
    flow = Flow((out_0, out_1, out_2, out_3), None, depth, slots[2 * (NBE + NBP) + 1])
    groups = load_blocks(table, slots, sems, 0, enc_shapes(), (None, None, None, w1, w2))
    start_all(groups)
    top_out[...] = jnp.zeros_like(top_out)
    hid = hid_ref[...]
    dy, grads[10], grads[11] = norm_back(hid, vec[10], dz_ref[...].astype(f32))
    grads[9] = col_sum(dy)
    low = dy.astype(bf)
    low_ref[...] = low
    wait_group(groups[4])
    wait_group(groups[3])
    acc[...] = jnp.zeros_like(acc)

    def strip(c, carry):
        lanes = pl.ds(pl.multiple_of(c * STRIP, 128), STRIP)
        pre = pre_ref[:, lanes]
        act_t[lanes, :] = gelu(pre).astype(bf).T
        dpre = mm(low, w2[lanes, :], RIGHT_T) * gelu_slope(pre)
        grads.put_part(8, c * STRIP, STRIP, col_sum(dpre))
        dpre = dpre.astype(bf)
        dpre_ref[:, lanes] = dpre
        acc[...] += mm(dpre, w1[:, lanes], RIGHT_T)
        return carry

    lax.fori_loop(0, FF // STRIP, strip, 0)
    mid = mid_ref[...]
    dmid, grads[6], grads[7] = norm_back(mid, vec[6], acc[...])
    dmid_out[...] = dmid + dy
    x_t[...] = (norm_parts(mid)[0] * vec[6] + vec[7]).astype(bf).T
    store = Store(top_out, out_sems)
    store.run(flow, stage, 16, (FF, D), act_t, low_ref)
    store.run(flow, stage, 0, (D, FF), x_t, dpre_ref)
    store.finish()


def attention_back_kernel(
    depth, slots, table, dmid_ref, rows_ref, e_ref, q, k, v, att_ref, valid_ref, vec_ref,
    out_0, out_1, out_2, out_3, vec_out, top_out,
    wqkv, wo, go, dq, dk, dv, x_t, dqkv, stage, sems, out_sems,
):
    vec, grads = Vec(vec_ref, enc_lengths()), Vec(vec_out, enc_lengths())
    flow = Flow((out_0, out_1, out_2, out_3), None, depth, slots[2 * (NBE + NBP) + 1])
    groups = load_blocks(table, slots, sems, 0, enc_shapes(), (None, wqkv, wo, None, None))
    start_all(groups[::-1])
    top_out[...] = jnp.zeros_like(top_out)
    store = Store(top_out, out_sems)
    dmid = dmid_ref[...]
    grads[5] = col_sum(dmid)
    low = dmid.astype(bf)
    wait_group(groups[2])
    wait_group(groups[1])
    split_rows(go, mm(low, wo[...], RIGHT_T))
    x_t[...] = flat(att_ref).T
    dqkv[:, :D] = low
    store.run(flow, stage, 16, (D, D), x_t, dqkv)
    attend_back(q, k, v, valid_ref, go, dq, dk, dv, H)
    d_q, d_v = flat(dq), flat(dv)
    grads[3] = col_sum(d_q)
    grads[4] = col_sum(d_v)
    dqkv[:, :D] = d_q.astype(bf)
    dqkv[:, D : 2 * D] = flat(dk).astype(bf)
    dqkv[:, 2 * D :] = d_v.astype(bf)
    e = e_ref[...]
    x_t[...] = norm(e, vec[1], vec[2]).astype(bf).T
    store.run(flow, stage, 4, (D, 3 * D), x_t, dqkv)
    back, grads[1], grads[2] = norm_back(e, vec[1], mm(dqkv[...], wqkv[...], RIGHT_T))
    de = dmid_ref[...] + back
    grads[0] = col_sum(de)
    dqkv[:, :D] = de.astype(bf)
    x_t[...] = rows_ref[...].T
    store.run(flow, stage, 0, (PIX, D), x_t, dqkv)
    store.finish()


def spaces(count):
    return [pl.BlockSpec(memory_space=pltpu.VMEM)] * count


ANYWHERE = pl.BlockSpec(memory_space=pl.ANY)


def weight_scratch(shapes):
    return [pltpu.VMEM(shape, bf) for shape in shapes]


def call_kernel(body, section, places, table, args, outs, any_outs, scratch, name, micros):
    pieces, n_in, n_out = len(table), len(args), len(outs)
    inside = [i for i in range(n_out) if i not in any_outs]
    held = [pltpu.VMEM(a.shape, a.dtype) for a in args]
    held += [pltpu.VMEM(outs[i][0], outs[i][1]) for i in inside]
    n_held = len(held)

    def guarded(places_ref, *refs):
        @pl.when(places_ref[2 * (NBE + NBP)] == section)
        def run():
            sources = refs[:pieces]
            given = refs[pieces : pieces + n_in]
            results = list(refs[pieces + n_in : pieces + n_in + n_out])
            local = refs[pieces + n_in + n_out :]
            mine, rest, sems = local[:n_held], local[n_held:-1], local[-1]
            loads = [
                pltpu.make_async_copy(given[i], mine[i], sems.at[i]) for i in range(n_in)
            ]
            for copy in loads:
                copy.start()
            stores = []
            for place, i in enumerate(inside):
                stores.append(
                    pltpu.make_async_copy(mine[n_in + place], results[i], sems.at[n_in + place])
                )
                results[i] = mine[n_in + place]
            for copy in loads:
                copy.wait()
            body(places_ref, sources, *mine[:n_in], *results, *rest)
            for copy in stores:
                copy.start()
            for copy in stores:
                copy.wait()

    return pl.pallas_call(
        guarded,
        grid_spec=pltpu.PrefetchScalarGridSpec(
            num_scalar_prefetch=1,
            grid=(),
            in_specs=[ANYWHERE] * (pieces + n_in),
            out_specs=[ANYWHERE] * n_out,
            scratch_shapes=held + scratch + [pltpu.SemaphoreType.DMA((n_held,))],
        ),
        out_shape=[jax.ShapeDtypeStruct(shape, kind) for shape, kind in outs],
        compiler_params=pltpu.CompilerParams(vmem_limit_bytes=58 << 20),
        cost_estimate=pl.CostEstimate(
            flops=0, transcendentals=0, bytes_accessed=int(micros * 3.0e6)
        ),
        name=name,
    )(places, *table, *args)


MARKS = 16


def flow_outs(count, edge, ranks):
    depth = edge // ranks
    if depth % 8:
        return [((count, edge, edge), f32)] + [((8, edge), f32)] * (GROUP - 1)
    return [((ranks // GROUP, depth * count + MARKS, edge), f32)] * GROUP


def stage_shape(count, edge, ranks):
    depth = edge // ranks
    return (count, edge, edge) if depth % 8 else (ranks // GROUP, GROUP, depth * count, edge)


def encoder_call(slots, table, rows, pos, valid, vec):
    n = rows.shape[0]
    images = n // LC
    per = (images, LC, D)
    outs = [((n, D), bf), ((n, D), f32), (per, bf), (per, bf), (per, bf), (per, bf)]
    outs += [((n, D), f32), ((n, FF), f32), ((n, D), f32)]
    scratch = weight_scratch(enc_shapes()) + [pltpu.VMEM((n, D), f32), pltpu.SemaphoreType.DMA((NBE,))]
    args = (rows, pos, valid, vec)
    return call_kernel(encoder_kernel, 0, slots, table, args, outs, (), scratch, "encoder_forward", 25)


def target_call(slots, table, rows, pos, some, pos_some, valid, vec, images):
    n = some.shape[0]
    keys = rows.shape[0] // images
    per, wide = (images, n // images, D), (images, keys, D)
    scratch = weight_scratch(enc_shapes()) + [
        pltpu.VMEM(per, bf),
        pltpu.VMEM(wide, bf),
        pltpu.VMEM(wide, bf),
        pltpu.VMEM(per, bf),
        pltpu.VMEM((n, D), f32),
        pltpu.SemaphoreType.DMA((NBE,)),
    ]
    args = (rows, pos, some, pos_some, valid, vec)
    outs = [((n, D), f32)]
    return call_kernel(target_kernel, 1, slots, table, args, outs, (), scratch, "target_forward", 25)[0]


def predictor_call(slots, table, z, pos_c, pos_t, valid, tgt, tmask, vec, ranks):
    n, m = z.shape[0], pos_t.shape[0]
    images = n // LC
    rows, keys = m // images, valid.shape[-1]
    edge = table[0].shape[-1]
    per, wide = (images, rows, PD), (images, keys, PD)
    outs = [((n, D), bf)] + flow_outs(NBP, edge, ranks)
    outs += [((1, VP), f32), ((1, D), f32), ((1, edge), f32)]
    scratch = weight_scratch(pred_shapes()) + [
        pltpu.VMEM(per, bf),
        pltpu.VMEM(wide, bf),
        pltpu.VMEM(wide, bf),
        pltpu.VMEM(per, bf),
        pltpu.VMEM(per, bf),
        pltpu.VMEM(per, f32),
        pltpu.VMEM(wide, f32),
        pltpu.VMEM(wide, f32),
        pltpu.VMEM((m, PFF), f32),
        pltpu.VMEM((m, PFF), bf),
        pltpu.VMEM((m, PFF), bf),
        pltpu.VMEM((m, PD), f32),
        pltpu.VMEM(stage_shape(NBP, edge, ranks), f32),
        pltpu.SemaphoreType.DMA((NBE + NBP,)),
        pltpu.SemaphoreType.DMA((1, GROUP)),
    ]
    args = (z, pos_c, pos_t, valid, tgt, tmask, vec)
    body = functools.partial(predictor_kernel, edge // ranks)
    return call_kernel(body, 1, slots, table, args, outs, (1, 2, 3, 4), scratch, "predictor_step", 50)


def feed_back_call(slots, table, dz, kept, vec, ranks):
    n = dz.shape[0]
    edge = table[0].shape[-1]
    mid, pre, hid = kept
    scratch = weight_scratch(enc_shapes()[3:]) + [
        pltpu.VMEM((FF, n), bf),
        pltpu.VMEM((n, FF), bf),
        pltpu.VMEM((D, n), bf),
        pltpu.VMEM((n, D), bf),
        pltpu.VMEM((n, D), f32),
        pltpu.VMEM((2,) + stage_shape(4, edge, ranks), f32),
        pltpu.SemaphoreType.DMA((NBE,)),
        pltpu.SemaphoreType.DMA((8, GROUP)),
    ]
    outs = flow_outs(32, edge, ranks)
    outs += [((n, D), f32), ((1, VE), f32), ((1, edge), f32)]
    args = (dz, mid, pre, hid, vec)
    body = functools.partial(feed_back_kernel, edge // ranks)
    return call_kernel(body, 0, slots, table, args, outs, (0, 1, 2, 3), scratch, "feed_backward", 25)


def attention_back_call(slots, table, dmid, rows, kept, valid, vec, ranks):
    n = rows.shape[0]
    images = n // LC
    edge = table[0].shape[-1]
    per = (images, LC, D)
    e, q, k, v, att = kept
    scratch = weight_scratch(enc_shapes()[1:3]) + [
        pltpu.VMEM(per, bf),
        pltpu.VMEM(per, f32),
        pltpu.VMEM(per, f32),
        pltpu.VMEM(per, f32),
        pltpu.VMEM((D, n), bf),
        pltpu.VMEM((n, 3 * D), bf),
        pltpu.VMEM((2,) + stage_shape(4, edge, ranks), f32),
        pltpu.SemaphoreType.DMA((NBE,)),
        pltpu.SemaphoreType.DMA((5, GROUP)),
    ]
    outs = flow_outs(20, edge, ranks) + [((1, VE), f32), ((1, edge), f32)]
    args = (dmid, rows, e, q, k, v, att, valid, vec)
    body = functools.partial(attention_back_kernel, edge // ranks)
    return call_kernel(body, 0, slots, table, args, outs, (0, 1, 2, 3), scratch, "attention_backward", 25)


def soap_first(flags, factor, *arrays):
    n, e = arrays[0].shape[:2]
    one = pl.BlockSpec((1, e, e), lambda i, *_: (i, 0, 0))
    two = pl.BlockSpec((1, 2, e, e), lambda i, *_: (i, 0, 0, 0))
    single = jax.ShapeDtypeStruct((n, e, e), f32)
    double = jax.ShapeDtypeStruct((n, 2, e, e), f32)
    return pl.pallas_call(
        first_kernel,
        grid_spec=pltpu.PrefetchScalarGridSpec(
            num_scalar_prefetch=2, grid=(n,), in_specs=[one] * 8, out_specs=[one] * 5 + [two] * 2
        ),
        out_shape=[single] * 5 + [double] * 2,
        compiler_params=pltpu.CompilerParams(vmem_limit_bytes=56 << 20),
        name="soap_first",
    )(flags, factor, *arrays)


def soap_factor(flags, base, gram):
    n, _, e, _ = base.shape
    whole = pl.BlockSpec(memory_space=pltpu.VMEM)
    return pl.pallas_call(
        factor_kernel,
        grid_spec=pltpu.PrefetchScalarGridSpec(
            num_scalar_prefetch=1,
            grid=(),
            in_specs=[whole] * 2,
            out_specs=whole,
            scratch_shapes=[
                pltpu.VMEM((n, 2, e, e), f32),
                pltpu.VMEM((n, 2, e, e), f32),
                pltpu.VMEM((n, 2, 128, 128), f32),
            ],
        ),
        out_shape=jax.ShapeDtypeStruct(base.shape, f32),
        compiler_params=pltpu.CompilerParams(vmem_limit_bytes=56 << 20),
        name="soap_factor",
    )(flags, base, gram)


def soap_last(flags, left, right, moment, fresh):
    n, e = left.shape[:2]
    one = pl.BlockSpec((1, e, e), lambda i, *_: (i, 0, 0))
    two = pl.BlockSpec((1, 2, e, e), lambda i, *_: (i, 0, 0, 0))
    return pl.pallas_call(
        last_kernel,
        grid_spec=pltpu.PrefetchScalarGridSpec(
            num_scalar_prefetch=1, grid=(n,), in_specs=[one] * 3 + [two], out_specs=[one] * 3
        ),
        out_shape=[jax.ShapeDtypeStruct((n, e, e), f32)] * 3,
        compiler_params=pltpu.CompilerParams(vmem_limit_bytes=56 << 20),
        name="soap_last",
    )(flags, left, right, moment, fresh)


def place_shares(slots, second, enc_share, pred_share, ranks, slot_count):
    depth, edge = enc_share.shape[1:]

    def body(slots_ref, second_ref, enc_ref, pred_ref, out_ref):
        def run(source, first, count):
            def copy(j, carry):
                slot = slots_ref[first + j]
                rows = pl.ds(pl.multiple_of(slot % slot_count * depth, depth), depth)
                out_ref[slot // slot_count, rows, :] = source[j]
                return carry

            lax.fori_loop(0, count, copy, 0)

        @pl.when(second_ref[0] == 0)
        def enc():
            run(enc_ref, 0, NBE)

        @pl.when(second_ref[0] != 0)
        def pred():
            run(pred_ref, NBE, NBP)

    return pl.pallas_call(
        body,
        grid_spec=pltpu.PrefetchScalarGridSpec(
            num_scalar_prefetch=2, grid=(), in_specs=spaces(2), out_specs=spaces(1)[0]
        ),
        out_shape=jax.ShapeDtypeStruct((ranks, slot_count * depth + MARKS, edge), f32),
        compiler_params=pltpu.CompilerParams(vmem_limit_bytes=40 << 20),
        name="place_shares",
    )(slots, second, enc_share, pred_share)


ROUNDS = (
    (((1, 0), (2, 1), (4, 2)), ()),
    (((5, 0), (6, 1), (8, 3)), (1, 2, 4)),
    (((3, 0), (7, 1)), (5, 6)),
    (((9, 0), (10, 1), (12, 2)), (3, 7, 8)),
    (((11, 0), (14, 1), (13, 2)), (9, 10, 12)),
)
LAST = 15


def thirds(slot_count):
    size = -(-slot_count // 3)
    return size, [(start, min(start + size, slot_count)) for start in range(0, slot_count, size)]


def gather_pieces(own, extra):
    both = Exchange((0, 1))
    if both.ranks != 16:
        return None, extra
    held = {0: own}
    for number, (moves, awaited) in enumerate(ROUNDS):
        names = sorted({piece ^ (1 << bit) for piece, bit in moves} | set(awaited))
        values = [held[name] for name in names]
        if number == 2:
            values, extra = lax.optimization_barrier((values, extra))
        elif awaited:
            values = lax.optimization_barrier(values)
        source = dict(zip(names, values))
        for piece, bit in moves:
            held[piece] = both.swap(source[piece ^ (1 << bit)], bit)
    names = [LAST ^ 1, LAST ^ 2, LAST ^ 4]
    source = lax.optimization_barrier([held[name] for name in names])
    ends = [
        both.swap(source[bit][low:high], bit) for bit, (low, high) in enumerate(thirds(own.shape[0])[1])
    ]
    return [held[piece] for piece in range(LAST)] + ends, extra


class Exchange:
    def __init__(self, sections):
        self.ranks = lax.axis_size("dp")
        self.bits = self.ranks.bit_length() - 1
        self.sections = sections

    def swap(self, value, bit):
        return self.trade(value, 1 << bit)

    def trade(self, value, flip):
        pairs = [
            (s * self.ranks + i, s * self.ranks + (i ^ flip))
            for s in self.sections
            for i in range(self.ranks)
        ]
        return lax.ppermute(value, ("section", "dp"), pairs)

    def total(self, value):
        for bit in range(self.bits):
            value = value + self.swap(value, bit)
        return value


def wire_exponent(bound):
    return jnp.floor(jnp.log2(WIRE_TOP / jnp.maximum(bound, 1e-30)))


def pack(values, exponent):
    row = lax.broadcasted_iota(jnp.int32, values.shape, values.ndim - 2)
    marked = jnp.where(row < values.shape[-2] - MARKS, values * jnp.exp2(exponent), exponent)
    return marked.astype(WIRE)


def flow_pieces(arrays, ranks):
    if arrays[1].ndim == 3:
        return list(arrays)
    blocks, edge = arrays[0].shape[:2]
    cut = arrays[0].reshape(blocks, ranks, edge // ranks, edge).transpose(1, 0, 2, 3)
    cut = jnp.pad(cut.reshape(ranks, -1, edge), ((0, 0), (0, MARKS), (0, 0)))
    return cut_pieces(cut, 0, GROUP)


def cut_pieces(shares, shift, size):
    mine = (lax.axis_index("dp") >> shift) & (size - 1)
    cut = shares.reshape((shares.shape[0] // size, size) + shares.shape[1:])
    return [lax.dynamic_index_in_dim(cut, mine ^ p, 1, keepdims=False) for p in range(size)]


def pack_pieces(pieces, bound):
    return [pack(piece, wire_exponent(bound)) for piece in pieces[1:]]


def send_packed(exchange, lows, shift):
    return [exchange.trade(low, (p + 1) << shift) for p, low in enumerate(lows)]


def send_pieces(exchange, pieces, shift, bound):
    return send_packed(exchange, pack_pieces(pieces, bound), shift)


def add_pieces(keep, arrived, bound):
    for got in arrived:
        unscale = jnp.exp2(-got[0, -1, 0].astype(f32))
        keep = keep + got.astype(f32) * unscale
        bound = bound + WIRE_TOP * unscale
    return keep, bound


def finish_sum(exchange, shares, bound):
    shift = GROUP_BITS
    while shares.shape[0] > 1:
        pieces = cut_pieces(shares, shift, min(GROUP, shares.shape[0]))
        arrived = send_pieces(exchange, pieces, shift, bound)
        shares, bound = add_pieces(pieces[0], arrived, bound)
        shift += GROUP_BITS
    return shares[0, :-MARKS], bound


def on_device(
    pixels,
    ctx_idx,
    ctx_len,
    tgt_idx,
    tgt_len,
    slot_of,
    weights,
    first_moment,
    second_moment,
    left_basis,
    right_basis,
    left_stats,
    right_stats,
    vectors,
    vector_first,
    vector_second,
):
    section_index = lax.axis_index("section")
    owner_index = lax.axis_index("dp")
    ranks = lax.axis_size("dp")
    is_first = section_index == 0
    second = section_index.astype(jnp.int32).reshape(1)
    slot_count = weights.shape[1]
    edge = weights.shape[-1]
    enc_slots = slot_of[:NBE]
    pred_slots = slot_of[NBE:]
    row_now = vectors[0]
    enc_vec_now = lax.dynamic_slice_in_dim(row_now, section_index * VP, VE)[None]
    pred_vec_now = row_now[None, :VP]
    pos_enc = sincos(D)
    pos_pred = sincos(PD)
    images = ctx_idx.shape[0]
    rows_all = -(-P_SIZE // 16) * 16
    tgt_flat = tgt_idx.reshape(images, NT * LT)
    ctx_valid = (jnp.arange(LC)[None, :] < ctx_len[:, None]).astype(f32)
    tgt_valid = (jnp.arange(LT)[None, None, :] < tgt_len[:, :, None]).astype(f32)
    tgt_valid = tgt_valid.reshape(images, NT * LT)
    joined_valid = jnp.concatenate([ctx_valid, tgt_valid], 1)[:, None, :]
    all_valid = (jnp.arange(rows_all) < P_SIZE).astype(f32)
    all_valid = jnp.broadcast_to(all_valid, (images, 1, rows_all))

    def pick(index):
        return (index[..., None] == jnp.arange(P_SIZE)).astype(f32)

    ctx_hot = pick(ctx_idx)
    tgt_hot = pick(tgt_flat)

    def choose(hot, values):
        return jnp.einsum(
            "njp,pd->njd", hot, values, precision=lax.Precision.HIGHEST, preferred_element_type=f32
        ).reshape(-1, values.shape[-1])

    def choose_pixels(hot):
        picked = jnp.einsum("njp,npd->njd", hot.astype(bf), pixels, preferred_element_type=f32)
        return picked.astype(bf).reshape(-1, PIX)

    pixel_rows = choose_pixels(ctx_hot)
    enc_pos_ctx = choose(ctx_hot, pos_enc)
    padding = ((0, 0), (0, rows_all - P_SIZE), (0, 0))
    pixel_all = jnp.pad(pixels, padding).reshape(-1, PIX)
    pos_all = jnp.broadcast_to(jnp.pad(pos_enc[None], padding), (images, rows_all, D)).reshape(-1, D)
    pixel_tgt = choose_pixels(tgt_hot)
    enc_pos_tgt = choose(tgt_hot, pos_enc)
    pred_pos_ctx = choose(ctx_hot, pos_pred)
    pred_pos_tgt = choose(tgt_hot, pos_pred)

    ctx_keys = ctx_valid[:, None, :]
    tgt_mask = tgt_valid.reshape(-1, 1)
    ready = (
        pixel_rows, enc_pos_ctx, ctx_keys, enc_vec_now, pixel_all, pos_all, pixel_tgt, enc_pos_tgt,
        all_valid, pred_pos_ctx, pred_pos_tgt, joined_valid, tgt_mask, pred_vec_now,
    )
    own = weights[0].astype(bf)
    place = [second, owner_index.astype(jnp.int32).reshape(1)]
    table, ready = gather_pieces(own, ready)
    if table is None:
        table = [lax.all_gather(own, "dp", axis=0, tiled=True)]
        places = jnp.concatenate([jnp.zeros_like(slot_of), slot_of] + place)
    else:
        sources = jnp.bitwise_xor(slot_of // slot_count, owner_index)
        indices = slot_of % slot_count
        size, _ = thirds(slot_count)
        is_last = sources == LAST
        sources = jnp.where(is_last, LAST + indices // size, sources)
        places = jnp.concatenate([sources, jnp.where(is_last, indices % size, indices)] + place)
    (
        pixel_rows, enc_pos_ctx, ctx_keys, enc_vec_now, pixel_all, pos_all, pixel_tgt, enc_pos_tgt,
        all_valid, pred_pos_ctx, pred_pos_tgt, joined_valid, tgt_mask, pred_vec_now,
    ) = ready

    z, *kept = encoder_call(places, table, pixel_rows, enc_pos_ctx, ctx_keys, enc_vec_now)
    context = from_behind(z, "section", 1)
    target = target_call(
        places, table, pixel_all, pos_all, pixel_tgt, enc_pos_tgt, all_valid, enc_vec_now, images
    )
    back_send, *pred_flows, pred_vec, loss_lanes, pred_top = predictor_call(
        places, table, context, pred_pos_ctx, pred_pos_tgt, joined_valid, target, tgt_mask, pred_vec_now, ranks
    )
    incoming = from_behind(back_send, "section", -1)
    loss_local = jnp.where(is_first, 0.0, jnp.sum(loss_lanes))

    behind = Exchange((1,))

    def sum_predictor(flows, top):
        bound = jnp.max(top)
        pieces = flow_pieces(flows, ranks)
        shares, bound = add_pieces(pieces[0], send_pieces(behind, pieces, 0, bound), bound)
        return finish_sum(behind, shares, bound)

    def skip_predictor(flows, top):
        return jnp.zeros((edge // ranks * NBP, edge), f32), jnp.zeros((), f32)

    incoming, pred_top = lax.optimization_barrier((incoming, pred_top))
    pred_sum, pred_bound = lax.cond(is_first, skip_predictor, sum_predictor, pred_flows, pred_top)
    incoming, pred_sum = lax.optimization_barrier((incoming, pred_sum))
    *feed_flow, grad_mid, feed_vec, feed_top = feed_back_call(
        places, table, incoming, kept[5:], enc_vec_now, ranks
    )
    ahead = Exchange((0,))
    feed_bound = jnp.max(feed_top)
    feed_pieces = flow_pieces(feed_flow, ranks)
    lows, grad_mid = lax.optimization_barrier((pack_pieces(feed_pieces, feed_bound), grad_mid))
    feed_arrived = send_packed(ahead, lows, 0)
    *rest_flow, rest_vec, rest_top = attention_back_call(
        places, table, grad_mid, pixel_rows, kept[:5], ctx_keys, enc_vec_now, ranks
    )
    rest_bound = jnp.max(rest_top)
    rest_pieces = flow_pieces(rest_flow, ranks)
    lows = pack_pieces(rest_pieces, rest_bound)
    feed_arrived, lows = lax.optimization_barrier((feed_arrived, lows))
    rest_arrived = send_packed(ahead, lows, 0)
    feed_shares, feed_bound = add_pieces(feed_pieces[0], feed_arrived, feed_bound)
    rest_shares, rest_bound = add_pieces(rest_pieces[0], rest_arrived, rest_bound)
    enc_shares = jnp.concatenate([rest_shares[:, :-MARKS], feed_shares], 1)
    enc_sum, enc_bound = finish_sum(ahead, enc_shares, jnp.maximum(rest_bound, feed_bound))
    cut_at = 6 * D
    enc_vec = jnp.concatenate([rest_vec[:, :cut_at], feed_vec[:, cut_at:]], 1)
    depth = edge // ranks
    enc_share = enc_sum.reshape(NBE, depth, edge)
    pred_share = pred_sum.reshape(NBP, depth, edge)

    both = Exchange((0, 1))
    vec_local = jnp.where(is_first, enc_vec[0], jnp.pad(pred_vec[0], (0, VE - VP)))
    count_local = jnp.where(is_first, 0, jnp.sum(tgt_len)).astype(f32)
    scalars = jnp.pad(jnp.stack([loss_local, count_local]), (0, 126))
    summed = both.total(jnp.concatenate([vec_local, scalars]))
    vec_total = jnp.pad(summed[:VE], (0, VW - VE))
    share_squares = jnp.where(
        is_first, jnp.sum(enc_share * enc_share), jnp.sum(pred_share * pred_share)
    )
    squares = both.total(jnp.full((128,), share_squares))
    facts = jnp.stack([squares[0] + jnp.sum(summed[:VE] ** 2), summed[VE], summed[VE + 1]])
    facts = jnp.pad(facts, (0, 125))
    swap_sections = [(i, 1 - i) for i in range(2)]
    facts = facts + lax.ppermute(facts, "section", swap_sections)
    square_total, loss_total, count_total = facts[0], facts[1], facts[2]

    placed = place_shares(slot_of, second, enc_share, pred_share, ranks, slot_count)
    exponent = wire_exponent(jnp.where(is_first, enc_bound, pred_bound))
    payload = pack(placed, exponent)
    owned = lax.all_to_all(payload, "dp", split_axis=0, concat_axis=0, tiled=True).astype(f32)
    unscale = jnp.exp2(-owned[:, -1:, :1])
    owned = (owned[:, : slot_count * depth] * unscale).reshape(ranks, slot_count, depth, edge)
    owned_sum = owned.transpose(1, 0, 2, 3).reshape(slot_count, edge, edge)

    own_ids = owner_index * slot_count + jnp.arange(slot_count)
    enc_here = jnp.any(own_ids[:, None] == enc_slots[None, :], 1)
    pred_here = jnp.any(own_ids[:, None] == pred_slots[None, :], 1)
    trained = jnp.where(is_first, enc_here, pred_here)
    ema_here = jnp.logical_and(jnp.logical_not(is_first), enc_here)
    positions = jnp.arange(VW)
    vec_trained = positions < jnp.where(is_first, VE, VP)
    vec_ema = jnp.logical_and(jnp.logical_not(is_first), positions >= VP)
    grad_norm = jnp.sqrt(square_total) / count_total
    factor = jnp.minimum(1.0, CLIP_LIMIT / (grad_norm + 1e-06)) / count_total

    flags = trained.astype(jnp.int32)
    new_weight, moment, new_second, new_estat, new_fstat, base, gram = soap_first(
        flags,
        factor.reshape(1),
        owned_sum,
        weights[0],
        first_moment[0],
        second_moment[0],
        left_basis[0],
        right_basis[0],
        left_stats[0],
        right_stats[0],
    )
    fresh_bases = soap_factor(flags, base, gram)
    new_left, new_right, new_first = soap_last(
        flags, left_basis[0], right_basis[0], moment, fresh_bases
    )

    correct_one = 1.0 - BETA_FIRST**STEP
    correct_two = 1.0 - BETA_SECOND**STEP
    vec_clipped = vec_total * factor
    fresh_first = BETA_FIRST * vector_first[0] + (1.0 - BETA_FIRST) * vec_clipped
    fresh_second = BETA_SECOND * vector_second[0] + (1.0 - BETA_SECOND) * vec_clipped * vec_clipped
    stepped = row_now - RATE_VECTOR * (fresh_first / correct_one) / (
        jnp.sqrt(fresh_second / correct_two) + ADAM_EPS
    )
    new_vec = jnp.where(vec_trained, stepped, row_now)
    new_vec_first = jnp.where(vec_trained, fresh_first, vector_first[0])
    new_vec_second = jnp.where(vec_trained, fresh_second, vector_second[0])
    from_encoder = from_behind(new_weight.astype(bf), "section", 1).astype(f32)
    vec_from_encoder = from_behind(new_vec.astype(bf), "section", 1).astype(f32)
    new_weight = jnp.where(
        ema_here[:, None, None], EMA_KEEP * weights[0] + (1.0 - EMA_KEEP) * from_encoder, new_weight
    )
    aligned = jnp.concatenate([jnp.zeros((VP,), f32), vec_from_encoder[:VE]])
    new_vec = jnp.where(vec_ema, EMA_KEEP * row_now + (1.0 - EMA_KEEP) * aligned, new_vec)
    return (
        loss_total,
        count_total,
        grad_norm,
        new_weight[None],
        new_first[None],
        new_second[None],
        new_left[None],
        new_right[None],
        new_estat[None],
        new_fstat[None],
        new_vec[None],
        new_vec_first[None],
        new_vec_second[None],
    )


def solution(mesh):
    in_specs = (
        P("dp", None, None),
        P("dp", None),
        P("dp"),
        P("dp", None, None),
        P("dp", None),
        P(),
        P("section", "dp", None, None),
        P("section", "dp", None, None),
        P("section", "dp", None, None),
        P("section", "dp", None, None),
        P("section", "dp", None, None),
        P("section", "dp", None, None),
        P("section", "dp", None, None),
        P("section", None),
        P("section", None),
        P("section", None),
    )
    out_specs = (
        P(),
        P(),
        P(),
        P("section", "dp", None, None),
        P("section", "dp", None, None),
        P("section", "dp", None, None),
        P("section", "dp", None, None),
        P("section", "dp", None, None),
        P("section", "dp", None, None),
        P("section", "dp", None, None),
        P("section", None),
        P("section", None),
        P("section", None),
    )
    return jax.shard_map(
        on_device, mesh=mesh, in_specs=in_specs, out_specs=out_specs, check_vma=False
    )
```

```python
import functools
import math

import jax
import jax.numpy as jnp
from jax import lax
from jax.experimental import pallas as pl
from jax.experimental.pallas import tpu as pltpu
from jax.sharding import PartitionSpec as P

D = 768
FF = 3072
H = 12
PD = 384
PFF = 1536
PH = 12
PIX = 768
GRID = 14
NT = 4
LC = 128
STEP = 10
P_SIZE = 196
LT = 36
NBE = 52
NBP = 16
VE = 11520
VP = 6912
VW = 18432


NORM_EPS = 1e-06
ADAM_EPS = 1e-08
BETA_FIRST = 0.5
BETA_SECOND = 0.5
BETA_STATS = 0.95
RATE_MATRIX = 0.02
RATE_VECTOR = 0.05
DECAY_MATRIX = 0.04
EMA_KEEP = 0.996
CLIP_LIMIT = 1.0
NEG_FILL = -1000000000.0
WIRE = jnp.float16
WIRE_TOP = 16384.0
f32 = jnp.float32
bf = jnp.bfloat16


def from_behind(shard, axis, by):
    size = lax.axis_size(axis)
    pairs = [(i, i + by) for i in range(size) if 0 <= i + by < size]
    return lax.ppermute(shard, axis, pairs)


def enc_shapes():
    return [(PIX, D), (D, 3 * D), (D, D), (D, FF), (FF, D)]


def pred_shapes():
    return [(D, PD), (PD, 3 * PD), (PD, PD), (PD, PFF), (PFF, PD), (PD, D)]


def enc_lengths():
    return [D] * 8 + [FF, D, D, D]


def pred_lengths():
    return [PD] * 8 + [PFF, PD, PD, PD, D, PD]


def sincos(width):
    quarter = width // 4
    frequency = 1.0 / 10000.0 ** (jnp.arange(quarter, dtype=jnp.float32) / quarter)
    cell_ids = jnp.arange(P_SIZE)
    row_pos = (cell_ids // GRID).astype(jnp.float32)[:, None] * frequency
    column_pos = (cell_ids % GRID).astype(jnp.float32)[:, None] * frequency
    return jnp.concatenate(
        [jnp.sin(row_pos), jnp.cos(row_pos), jnp.sin(column_pos), jnp.cos(column_pos)], 1
    )


DIMS = {"nn": (1, 0), "nt": (1, 1), "tn": (0, 0)}

def parts_of(a, count):
    found = []
    for index in range(count):
        piece = a.astype(bf)
        found.append(piece)
        if index + 1 < count:
            a = a - piece.astype(f32)
    return found

def product(left, right, form, pairs):
    ld, rd = DIMS[form]
    lhs = jnp.concatenate([left[i] for i, _ in pairs], ld)
    rhs = jnp.concatenate([right[j] for _, j in pairs], rd)
    return lax.dot_general(lhs, rhs, (((ld,), (rd,)), ((), ())), preferred_element_type=f32)

THREE = ((0, 1), (1, 0), (0, 0))
SIX = ((0, 2), (2, 0), (1, 1), (0, 1), (1, 0), (0, 0))
def mul3(left, right, form="nn"):
    return product(left, right, form, THREE)
def mul6(left, right, form="nn"):
    return product(left, right, form, SIX)

def invert_factors(mats):
    n = mats[0].shape[0]
    lane = lax.broadcasted_iota(jnp.int32, (8, n), 1)
    sub = lax.broadcasted_iota(jnp.int32, (8, n), 0)
    groups = [[a[8 * t : 8 * t + 8, :] for t in range(n // 8)] for a in mats]
    for j in range(n):
        top, at_row = divmod(j, 8)
        here = lane == j
        pick = jnp.full((8, n), j, jnp.int32)
        for tiles in groups:
            column = jnp.take_along_axis(tiles[top], pick, axis=1)
            pivot = jnp.broadcast_to(column[at_row : at_row + 1, :], (8, n))
            row = jnp.broadcast_to(tiles[top][at_row : at_row + 1, :], (8, n))
            scaled = jnp.where(here, 1.0, row) * (1.0 / pivot)
            for t in range(top, n // 8):
                if t > top:
                    column = jnp.take_along_axis(tiles[t], pick, axis=1)
                fresh = jnp.where(here, 0.0, tiles[t]) - column * scaled
                tiles[t] = jnp.where(sub > at_row, fresh, tiles[t]) if t == top else fresh
    results = []
    for tiles in groups:
        rows = []
        for t in range(n // 8):
            at = sub + 8 * t
            pivots = jnp.sum(jnp.where(lane == at, tiles[t], 0.0), axis=1, keepdims=True)
            unit = jnp.where(lane < at, tiles[t], jnp.where(lane == at, 1.0, 0.0))
            rows.append(unit * lax.rsqrt(pivots))
        results.append(jnp.concatenate(rows, 0))
    return results

def first_kernel(flag, factor, g_ref, w_ref, m_ref, v_ref, l_ref, r_ref, e_ref, f_ref,
                 w_out, m_out, v_out, e_out, f_out, base_out, gram_out):
    on = flag[pl.program_id(0)] != 0

    @pl.when(jnp.logical_not(on))
    def keep():
        for source, target in ((w_ref, w_out), (m_ref, m_out), (v_ref, v_out), (e_ref, e_out), (f_ref, f_out)):
            target[...] = source[...]

    @pl.when(on)
    def update():
        correct_one = 1.0 - BETA_FIRST**STEP
        correct_two = 1.0 - BETA_SECOND**STEP
        grad = parts_of(g_ref[0] * factor[0], 3)
        left = parts_of(l_ref[0], 3)
        right = parts_of(r_ref[0], 3)
        rotated = mul3(left, parts_of(mul3(grad, right), 2), "tn")
        moment = BETA_FIRST * m_ref[0] + (1.0 - BETA_FIRST) * rotated
        second = BETA_SECOND * v_ref[0] + (1.0 - BETA_SECOND) * rotated * rotated
        m_out[0] = moment
        v_out[0] = second
        normed = moment / correct_one / (jnp.sqrt(second / correct_two) + ADAM_EPS)
        weight = w_ref[0]
        step = mul3(left, parts_of(mul3(parts_of(normed, 2), right, "nt"), 2))
        w_out[0] = weight - RATE_MATRIX * (step + DECAY_MATRIX * weight)
        for index, (stat, target, basis, form) in enumerate(
            ((e_ref, e_out, left, "nt"), (f_ref, f_out, right, "tn"))
        ):
            fresh = BETA_STATS * stat[0] + (1.0 - BETA_STATS) * mul3(grad, grad, form)
            target[0] = fresh
            moved = mul6(parts_of(fresh, 3), basis)
            base_out[0, index] = moved
            pieces = parts_of(moved, 3)
            edge = moved.shape[-1]
            for start in range(0, edge, 128):
                rows = [piece[:, start : start + 128] for piece in pieces]
                upper = [piece[:, start:] for piece in pieces]
                gram_out[0, index, start : start + 128, start:] = mul6(rows, upper, "tn")

def factor_kernel(flag, base_ref, gram_ref, q_out, base, gram, inverse):
    blocks, edge = base_ref.shape[0], base_ref.shape[-1]
    panel = 128
    count = edge // panel
    base[...] = base_ref[...]
    gram[...] = gram_ref[...]

    def stage(k):
        at = pl.ds(panel * k, panel)
        start = panel * k
        spot = slice(start, start + panel)
        rest = slice(start + panel, edge)

        def block(b, carry):
            @pl.when(flag[b] != 0)
            def run():
                sides = range(2)
                inv = [parts_of(inverse[b, side], 3) for side in sides]
                q = [mul6(parts_of(base[b, side, :, spot], 3), inv[side], "nt") for side in sides]
                for side in sides:
                    q_out[b, side, :, spot] = q[side]
                if k + 1 < count:
                    tops = [mul6(inv[side], parts_of(gram[b, side, spot, rest], 3)) for side in sides]
                    p = [parts_of(top, 3) for top in tops]
                    minus = [mul6(p[side], p[side], "tn") for side in sides]
                    moved = [mul6(parts_of(q[side], 3), p[side]) for side in sides]
                    for side in sides:
                        gram[b, side, rest, rest] = gram[b, side, rest, rest] - minus[side]
                        base[b, side, :, rest] = base[b, side, :, rest] - moved[side]
            return carry

        lax.fori_loop(0, blocks, block, 0)

    def turn(k, carry):
        for which in range(count):
            @pl.when(k == which)
            def load():
                spot = slice(panel * which, panel * which + panel)
                for b in range(blocks):
                    for side in range(2):
                        inverse[b, side] = gram[b, side, spot, spot]
        mats = invert_factors([inverse[b, side] for b in range(blocks) for side in range(2)])
        for b in range(blocks):
            for side in range(2):
                inverse[b, side] = mats[2 * b + side]
        for which in range(count):
            @pl.when(k == which)
            def run():
                stage(which)
        return carry

    lax.fori_loop(0, count, turn, 0)

def last_kernel(flag, l_ref, r_ref, m_ref, q_ref, l_out, r_out, m_out):
    on = flag[pl.program_id(0)] != 0

    @pl.when(jnp.logical_not(on))
    def keep():
        l_out[...] = l_ref[...]
        r_out[...] = r_ref[...]
        m_out[...] = m_ref[...]

    @pl.when(on)
    def update():
        l_out[0] = q_ref[0, 0]
        r_out[0] = q_ref[0, 1]
        turn_left = mul3(parts_of(q_ref[0, 0], 2), parts_of(l_ref[0], 2), "tn")
        turn_right = mul3(parts_of(r_ref[0], 2), parts_of(q_ref[0, 1], 2), "tn")
        half = mul3(parts_of(turn_left, 2), parts_of(m_ref[0], 2))
        m_out[0] = mul3(parts_of(half, 2), parts_of(turn_right, 2))

PLAIN = (((1,), (0,)), ((), ()))
RIGHT_T = (((1,), (1,)), ((), ()))
LEFT_T = (((0,), (0,)), ((), ()))
ROOT_HALF = 0.7071067811865476
ROOT_TWO_PI = 2.5066282746310002


def mm(left, right, dims=PLAIN):
    return lax.dot_general(left, right, dims, preferred_element_type=f32)


def norm_parts(x):
    center = x - jnp.mean(x, -1, keepdims=True)
    inverse = lax.rsqrt(jnp.mean(center * center, -1, keepdims=True) + NORM_EPS)
    return center * inverse, inverse


def norm(x, gain, shift):
    return norm_parts(x)[0] * gain + shift


def norm_back(x, gain, grad):
    unit, inverse = norm_parts(x)
    grad_unit = grad * gain
    mean_one = jnp.mean(grad_unit, -1, keepdims=True)
    mean_two = jnp.mean(grad_unit * unit, -1, keepdims=True)
    back = inverse * (grad_unit - mean_one - unit * mean_two)
    return back, col_sum(grad * unit), col_sum(grad)


def col_sum(x):
    return jnp.sum(x, 0, keepdims=True)


def gelu(x):
    return 0.5 * x * (1.0 + lax.erf(x * ROOT_HALF))


def gelu_slope(x):
    return 0.5 * (1.0 + lax.erf(x * ROOT_HALF)) + x * jnp.exp(-0.5 * x * x) * (1.0 / ROOT_TWO_PI)


def offsets(lengths):
    result = [0]
    for length in lengths:
        result.append(result[-1] + length)
    return result


class Vec:
    def __init__(self, ref, lengths):
        self.ref, self.at = ref, offsets(lengths)

    def __getitem__(self, k):
        return self.ref[:, self.at[k] : self.at[k + 1]]

    def __setitem__(self, k, value):
        self.ref[:, self.at[k] : self.at[k + 1]] = value

    def part(self, k, start, size):
        return self.ref[:, pl.ds(pl.multiple_of(self.at[k] + start, 128), size)]

    def put_part(self, k, start, size, value):
        self.ref[:, pl.ds(pl.multiple_of(self.at[k] + start, 128), size)] = value


class Fetch:
    def __init__(self, pieces, places, j, spot, sem):
        self.pieces, self.spot, self.sem = pieces, spot, sem
        self.which, self.index = places[j], places[NBE + NBP + j]

    def copy(self, piece, index):
        return pltpu.make_async_copy(piece.at[index], self.spot, self.sem)

    def start(self):
        if len(self.pieces) == 1:
            self.copy(self.pieces[0], self.index).start()
        else:
            self.start_among(0, len(self.pieces))

    def start_among(self, low, high):
        if high - low == 1:
            self.copy(self.pieces[low], self.index).start()
            return
        middle = (low + high) // 2

        @pl.when(self.which < middle)
        def below():
            self.start_among(low, middle)

        @pl.when(self.which >= middle)
        def above():
            self.start_among(middle, high)

    def wait(self):
        self.copy(self.pieces[0], 0).wait()


def load_blocks(pieces, places, sems, first, shapes, targets):
    edge = pieces[0].shape[-1]
    groups = []
    j = first
    for (height, breadth), target in zip(shapes, targets):
        group = []
        for row in range(height // edge):
            for column in range(breadth // edge):
                if target is not None:
                    spot = target.at[pl.ds(row * edge, edge), pl.ds(column * edge, edge)]
                    group.append(Fetch(pieces, places, j, spot, sems.at[j]))
                j += 1
        groups.append(group)
    return groups


def start_all(groups):
    for group in groups:
        for copy in group:
            copy.start()


def wait_group(group):
    for copy in group:
        copy.wait()


def head_masks(rows, heads, width):
    lane = lax.broadcasted_iota(jnp.int32, (rows, 128), 1)
    size = width // heads
    return [(lane >= size * h) & (lane < size * h + size) for h in range(128 // size)]


def as_factors(masks):
    return [jnp.where(mask, 1.0, 0.0).astype(bf) for mask in masks]


def soft(scores, allowed):
    scores = jnp.where(allowed, scores, NEG_FILL)
    top = jnp.max(scores, -1, keepdims=True)
    raised = jnp.exp(scores - top)
    return raised * (1.0 / jnp.sum(raised, -1, keepdims=True))


def head_jobs(q_ref, k_ref, v_ref, p, span, factors):
    jobs = []
    for g in range(span):
        lanes = pl.ds(pl.multiple_of(128 * (span * p + g), 128), 128)
        for i in range(q_ref.shape[0]):
            q, k, v = q_ref[i, :, lanes], k_ref[i, :, lanes], v_ref[i, :, lanes]
            for h in range(len(factors)):
                jobs.append((i, lanes, h, q, k, v))
    return jobs


def attend(q_ref, k_ref, v_ref, valid_ref, out_ref, heads):
    images, rows, width = q_ref.shape
    keys = k_ref.shape[1]
    masks = head_masks(rows, heads, width)
    factors = as_factors(masks)
    span = 1 if width // 128 % 2 else 2

    def group(p, carry):
        allowed = [jnp.broadcast_to(valid_ref[i], (rows, keys)) > 0.0 for i in range(images)]
        jobs = head_jobs(q_ref, k_ref, v_ref, p, span, factors)
        scores = [mm(q * factors[h], k, RIGHT_T) for _, _, h, q, k, _ in jobs]
        probs = [soft(s, allowed[job[0]]).astype(bf) for s, job in zip(scores, jobs)]
        parts = [mm(probs[n], job[5]) for n, job in enumerate(jobs)]
        for n in range(0, len(jobs), len(masks)):
            result = parts[n]
            for h in range(1, len(masks)):
                result = jnp.where(masks[h], parts[n + h], result)
            out_ref[jobs[n][0], :, jobs[n][1]] = result.astype(bf)
        return carry

    lax.fori_loop(0, width // 128 // span, group, 0)


def attend_back(q_ref, k_ref, v_ref, valid_ref, go_ref, dq_ref, dk_ref, dv_ref, heads):
    images, rows, width = q_ref.shape
    keys = k_ref.shape[1]
    masks = head_masks(rows, heads, width)
    key_masks = head_masks(keys, heads, width)
    factors = as_factors(masks)
    scale = 1.0 / math.sqrt(width // heads)
    span = 1 if width // 128 % 2 else 2

    def group(p, carry):
        allowed = [jnp.broadcast_to(valid_ref[i], (rows, keys)) > 0.0 for i in range(images)]
        jobs = head_jobs(q_ref, k_ref, v_ref, p, span, factors)
        grads = [go_ref[job[0], :, job[1]] for job in jobs]
        scores = [mm(q * factors[h], k, RIGHT_T) for _, _, h, q, k, _ in jobs]
        dprobs = [mm(go * factors[job[2]], job[5], RIGHT_T) for go, job in zip(grads, jobs)]
        probs = [soft(s, allowed[job[0]]) for s, job in zip(scores, jobs)]
        lows = [
            (a * (da - jnp.sum(da * a, -1, keepdims=True))).astype(bf) for a, da in zip(probs, dprobs)
        ]
        dvs = [mm(a.astype(bf), go, LEFT_T) for a, go in zip(probs, grads)]
        dqs = [mm(low, job[4]) for low, job in zip(lows, jobs)]
        dks = [mm(low, job[3], LEFT_T) for low, job in zip(lows, jobs)]
        for n in range(0, len(jobs), len(masks)):
            dq, dk, dv = dqs[n], dks[n], dvs[n]
            for h in range(1, len(masks)):
                dq = jnp.where(masks[h], dqs[n + h], dq)
                dk = jnp.where(key_masks[h], dks[n + h], dk)
                dv = jnp.where(key_masks[h], dvs[n + h], dv)
            i, lanes = jobs[n][:2]
            dq_ref[i, :, lanes] = dq * scale
            dk_ref[i, :, lanes] = dk
            dv_ref[i, :, lanes] = dv
        return carry

    lax.fori_loop(0, width // 128 // span, group, 0)


def split_rows(ref, value):
    images, rows, _ = ref.shape
    for i in range(images):
        ref[i] = value[rows * i : rows * i + rows].astype(ref.dtype)


def flat(ref):
    return jnp.concatenate([ref[i] for i in range(ref.shape[0])], 0)


STRIP = 768


def feed_forward(normed, mid, up, down, vec, pre_ref, acc_ref):
    acc_ref[...] = mid

    def strip(c, carry):
        lanes = pl.ds(pl.multiple_of(c * STRIP, 128), STRIP)
        pre = mm(normed, up[:, lanes]) + vec.part(8, c * STRIP, STRIP)
        if pre_ref is not None:
            pre_ref[:, lanes] = pre
        acc_ref[...] += mm(gelu(pre).astype(bf), down[lanes, :])
        return carry

    lax.fori_loop(0, up.shape[1] // STRIP, strip, 0)
    return acc_ref[...] + vec[9]


def encoder_kernel(
    slots, table, rows_ref, pos_ref, valid_ref, vec_ref,
    z_out, e_out, q_out, k_out, v_out, att_out, mid_out, pre_out, hid_out,
    wp, wqkv, wo, w1, w2, acc, sems,
):
    vec = Vec(vec_ref, enc_lengths())
    groups = load_blocks(table, slots, sems, 0, enc_shapes(), (wp, wqkv, wo, w1, w2))
    start_all(groups)
    wait_group(groups[0])
    e = mm(rows_ref[...], wp[...]) + vec[0] + pos_ref[...]
    e_out[...] = e
    normed = norm(e, vec[1], vec[2]).astype(bf)
    wait_group(groups[1])
    split_rows(q_out, (mm(normed, wqkv[:, :D]) + vec[3]) * (1.0 / math.sqrt(D // H)))
    split_rows(k_out, mm(normed, wqkv[:, D : 2 * D]))
    split_rows(v_out, mm(normed, wqkv[:, 2 * D :]) + vec[4])
    attend(q_out, k_out, v_out, valid_ref, att_out, H)
    wait_group(groups[2])
    mid = e + mm(flat(att_out), wo[...]) + vec[5]
    mid_out[...] = mid
    hidden = norm(mid, vec[6], vec[7]).astype(bf)
    wait_group(groups[3])
    wait_group(groups[4])
    hid = feed_forward(hidden, mid, w1, w2, vec, pre_out, acc)
    hid_out[...] = hid
    z_out[...] = norm(hid, vec[10], vec[11]).astype(bf)


def target_kernel(
    slots, table, all_ref, pos_all_ref, some_ref, pos_some_ref, valid_ref, vec_ref,
    out_ref, wp, wqkv, wo, w1, w2, q, k, v, att, acc, sems,
):
    vec = Vec(vec_ref, enc_lengths())
    groups = load_blocks(table, slots, sems, 0, enc_shapes(), (wp, wqkv, wo, w1, w2))
    start_all(groups)
    wait_group(groups[0])
    e = mm(all_ref[...], wp[...]) + vec[0] + pos_all_ref[...]
    normed = norm(e, vec[1], vec[2]).astype(bf)
    wait_group(groups[1])
    split_rows(k, mm(normed, wqkv[:, D : 2 * D]))
    split_rows(v, mm(normed, wqkv[:, 2 * D :]) + vec[4])
    e = mm(some_ref[...], wp[...]) + vec[0] + pos_some_ref[...]
    normed = norm(e, vec[1], vec[2]).astype(bf)
    split_rows(q, (mm(normed, wqkv[:, :D]) + vec[3]) * (1.0 / math.sqrt(D // H)))
    attend(q, k, v, valid_ref, att, H)
    wait_group(groups[2])
    mid = e + mm(flat(att), wo[...]) + vec[5]
    hidden = norm(mid, vec[6], vec[7]).astype(bf)
    wait_group(groups[3])
    wait_group(groups[4])
    hid = feed_forward(hidden, mid, w1, w2, vec, None, acc)
    out_ref[...] = norm_parts(norm(hid, vec[10], vec[11]))[0]


class Flow:
    def __init__(self, outs, stage, depth, me):
        self.outs, self.stage, self.depth, self.me = outs, stage, depth, me

    def put(self, value, j):
        edge, depth = value.shape[-1], self.depth
        if depth % 8:
            self.stage[j] = value
        else:
            cut = value.reshape(self.stage.shape[:2] + (depth, edge))
            self.stage[:, :, depth * j : depth * j + depth, :] = cut

    def copies(self, start, count, sems):
        depth = self.depth
        if depth % 8:
            target = self.outs[0].at[pl.ds(start, count)]
            return [pltpu.make_async_copy(self.stage.at[pl.ds(0, count)], target, sems[0])]
        group = len(self.outs)
        mine = self.me & (group - 1)
        made = []
        for p in range(group):
            source = self.stage.at[:, mine ^ p, pl.ds(0, depth * count), :]
            target = self.outs[p].at[:, pl.ds(depth * start, depth * count), :]
            made.append(pltpu.make_async_copy(source, target, sems[p]))
        return made


GROUP_BITS = 2
GROUP = 1 << GROUP_BITS


def sems_of(ref, turn):
    return [ref.at[turn, p] for p in range(GROUP)]


def raise_top(top_ref, value):
    top_ref[...] = jnp.maximum(top_ref[...], jnp.max(jnp.abs(value), 0, keepdims=True))


def predictor_kernel(
    depth, slots, table, z_ref, pos_c_ref, pos_t_ref, valid_ref, tgt_ref, tmask_ref, vec_ref,
    dz_out, out_0, out_1, out_2, out_3, vec_out, loss_out, top_out,
    win, wqkv, wo, w1, w2, wout, q, k, v, att, go, dq, dk, dv, pre_ref, act_ref, dpre_ref, acc, stage, sems, flow_sems,
):
    vec, grads = Vec(vec_ref, pred_lengths()), Vec(vec_out, pred_lengths())
    edge = table[0].shape[-1]
    flow = Flow((out_0, out_1, out_2, out_3), stage, depth, slots[2 * (NBE + NBP) + 1])
    images = z_ref.shape[0] // LC
    groups = load_blocks(table, slots, sems, NBE, pred_shapes(), (win, wqkv, wo, w1, w2, wout))
    start_all(groups)
    for group in groups:
        wait_group(group)
    firsts = offsets([h * b // (edge * edge) for h, b in pred_shapes()])

    def store(index, matrix):
        for row in range(matrix.shape[0] // edge):
            for column in range(matrix.shape[1] // edge):
                j = firsts[index] + row * (pred_shapes()[index][1] // edge) + column
                value = matrix[row * edge : row * edge + edge, column * edge : column * edge + edge]
                raise_top(top_out, value)
                flow.put(value, j)

    top_out[...] = jnp.zeros_like(top_out)
    z = z_ref[...]
    x_c = mm(z, win[...]) + vec[0] + pos_c_ref[...]
    x_t = vec[13] + pos_t_ref[...]
    n_c = norm(x_c, vec[1], vec[2]).astype(bf)
    n_t = norm(x_t, vec[1], vec[2]).astype(bf)
    split_rows(q, (mm(n_t, wqkv[:, :PD]) + vec[3]) * (1.0 / math.sqrt(PD // PH)))
    for ref, start, bias in ((k, PD, 0.0), (v, 2 * PD, vec[4])):
        of_c = mm(n_c, wqkv[:, start : start + PD]) + bias
        of_t = mm(n_t, wqkv[:, start : start + PD]) + bias
        count = NT * LT
        for i in range(images):
            ref[i, :LC, :] = of_c[LC * i : LC * i + LC].astype(bf)
            ref[i, LC:, :] = of_t[count * i : count * i + count].astype(bf)
    attend(q, k, v, valid_ref, att, PH)
    mid = x_t + mm(flat(att), wo[...]) + vec[5]
    n_two = norm(mid, vec[6], vec[7]).astype(bf)
    y = feed_forward(n_two, mid, w1, w2, vec, pre_ref, acc)
    n_three = norm(y, vec[10], vec[11]).astype(bf)
    difference = mm(n_three, wout[...]) + vec[12] - tgt_ref[...]
    tmask = tmask_ref[...]
    magnitude = jnp.abs(difference)
    loss = jnp.where(magnitude < 1.0, 0.5 * difference * difference, magnitude - 0.5) * tmask
    loss_out[...] = col_sum(loss)
    grad = jnp.clip(difference, -1.0, 1.0) * tmask

    grads[12] = col_sum(grad)
    low = grad.astype(bf)
    store(5, mm(n_three.T, low))
    dy, grads[10], grads[11] = norm_back(y, vec[10], mm(low, wout[...], RIGHT_T))
    grads[9] = col_sum(dy)
    low = dy.astype(bf)
    acc[...] = jnp.zeros_like(acc)

    def strip(c, carry):
        lanes = pl.ds(pl.multiple_of(c * STRIP, 128), STRIP)
        pre = pre_ref[:, lanes]
        act_ref[:, lanes] = gelu(pre).astype(bf)
        dpre = mm(low, w2[lanes, :], RIGHT_T) * gelu_slope(pre)
        grads.put_part(8, c * STRIP, STRIP, col_sum(dpre))
        dpre = dpre.astype(bf)
        dpre_ref[:, lanes] = dpre
        acc[...] += mm(dpre, w1[:, lanes], RIGHT_T)
        return carry

    lax.fori_loop(0, PFF // STRIP, strip, 0)
    store(4, mm(act_ref[...].T, low))
    store(3, mm(n_two.T, dpre_ref[...]))
    dmid, grads[6], grads[7] = norm_back(mid, vec[6], acc[...])
    dmid = dmid + dy
    grads[5] = col_sum(dmid)
    low = dmid.astype(bf)
    split_rows(go, mm(low, wo[...], RIGHT_T))
    store(2, mm(flat(att).T, low))
    attend_back(q, k, v, valid_ref, go, dq, dk, dv, PH)
    d_q, d_k, d_v = flat(dq), [dk[i] for i in range(images)], [dv[i] for i in range(images)]
    grads[3] = col_sum(d_q)
    grads[4] = sum(col_sum(part) for part in d_v)
    q_low = d_q.astype(bf)
    k_c = jnp.concatenate([part[:LC] for part in d_k], 0).astype(bf)
    k_t = jnp.concatenate([part[LC:] for part in d_k], 0).astype(bf)
    v_c = jnp.concatenate([part[:LC] for part in d_v], 0).astype(bf)
    v_t = jnp.concatenate([part[LC:] for part in d_v], 0).astype(bf)
    n_c_t, n_t_t = n_c.T, n_t.T
    store(
        1,
        jnp.concatenate(
            [mm(n_t_t, q_low), mm(n_c_t, k_c) + mm(n_t_t, k_t), mm(n_c_t, v_c) + mm(n_t_t, v_t)], 1
        ),
    )
    wq, wk, wv = wqkv[:, :PD], wqkv[:, PD : 2 * PD], wqkv[:, 2 * PD :]
    dn_t = mm(q_low, wq, RIGHT_T) + mm(k_t, wk, RIGHT_T) + mm(v_t, wv, RIGHT_T)
    dn_c = mm(k_c, wk, RIGHT_T) + mm(v_c, wv, RIGHT_T)
    dx_t, gain_t, shift_t = norm_back(x_t, vec[1], dn_t)
    dx_c, gain_c, shift_c = norm_back(x_c, vec[1], dn_c)
    grads[1] = gain_t + gain_c
    grads[2] = shift_t + shift_c
    dx_t = dx_t + dmid
    grads[13] = col_sum(dx_t)
    grads[0] = col_sum(dx_c)
    low = dx_c.astype(bf)
    dz_out[...] = mm(low, win[...], RIGHT_T).astype(bf)
    store(0, mm(z.T, low))
    leaving = flow.copies(0, NBP, sems_of(flow_sems, 0))
    for copy in leaving:
        copy.start()
    for copy in leaving:
        copy.wait()


class Store:
    def __init__(self, top, sems):
        self.top, self.sems, self.sent = top, sems, []

    def run(self, flow, slots, start, shape, left_t, right):
        edge = slots.shape[-1]
        columns, rows = shape[1] // edge, shape[0] // edge
        for first in range(0, rows * columns, 4):
            turn = len(self.sent)
            if turn >= 2:
                for copy in self.sent[turn - 2]:
                    copy.wait()
            flow.stage = slots.at[turn % 2]
            for b in range(4):
                row, column = divmod(first + b, columns)
                value = mm(
                    left_t[row * edge : row * edge + edge, :],
                    right[:, column * edge : column * edge + edge],
                )
                raise_top(self.top, value)
                flow.put(value, b)
            made = flow.copies(start + first, 4, sems_of(self.sems, turn))
            for copy in made:
                copy.start()
            self.sent.append(made)

    def finish(self):
        for made in self.sent[-2:]:
            for copy in made:
                copy.wait()


def feed_back_kernel(
    depth, slots, table, dz_ref, mid_ref, pre_ref, hid_ref, vec_ref,
    out_0, out_1, out_2, out_3, dmid_out, vec_out, top_out,
    w1, w2, act_t, dpre_ref, x_t, low_ref, acc, stage, sems, out_sems,
):
    vec, grads = Vec(vec_ref, enc_lengths()), Vec(vec_out, enc_lengths())
    flow = Flow((out_0, out_1, out_2, out_3), None, depth, slots[2 * (NBE + NBP) + 1])
    groups = load_blocks(table, slots, sems, 0, enc_shapes(), (None, None, None, w1, w2))
    start_all(groups)
    top_out[...] = jnp.zeros_like(top_out)
    hid = hid_ref[...]
    dy, grads[10], grads[11] = norm_back(hid, vec[10], dz_ref[...].astype(f32))
    grads[9] = col_sum(dy)
    low = dy.astype(bf)
    low_ref[...] = low
    wait_group(groups[4])
    wait_group(groups[3])
    acc[...] = jnp.zeros_like(acc)

    def strip(c, carry):
        lanes = pl.ds(pl.multiple_of(c * STRIP, 128), STRIP)
        pre = pre_ref[:, lanes]
        act_t[lanes, :] = gelu(pre).astype(bf).T
        dpre = mm(low, w2[lanes, :], RIGHT_T) * gelu_slope(pre)
        grads.put_part(8, c * STRIP, STRIP, col_sum(dpre))
        dpre = dpre.astype(bf)
        dpre_ref[:, lanes] = dpre
        acc[...] += mm(dpre, w1[:, lanes], RIGHT_T)
        return carry

    lax.fori_loop(0, FF // STRIP, strip, 0)
    mid = mid_ref[...]
    dmid, grads[6], grads[7] = norm_back(mid, vec[6], acc[...])
    dmid_out[...] = dmid + dy
    x_t[...] = (norm_parts(mid)[0] * vec[6] + vec[7]).astype(bf).T
    store = Store(top_out, out_sems)
    store.run(flow, stage, 16, (FF, D), act_t, low_ref)
    store.run(flow, stage, 0, (D, FF), x_t, dpre_ref)
    store.finish()


def attention_back_kernel(
    depth, slots, table, dmid_ref, rows_ref, e_ref, q, k, v, att_ref, valid_ref, vec_ref,
    out_0, out_1, out_2, out_3, vec_out, top_out,
    wqkv, wo, go, dq, dk, dv, x_t, dqkv, stage, sems, out_sems,
):
    vec, grads = Vec(vec_ref, enc_lengths()), Vec(vec_out, enc_lengths())
    flow = Flow((out_0, out_1, out_2, out_3), None, depth, slots[2 * (NBE + NBP) + 1])
    groups = load_blocks(table, slots, sems, 0, enc_shapes(), (None, wqkv, wo, None, None))
    start_all(groups[::-1])
    top_out[...] = jnp.zeros_like(top_out)
    store = Store(top_out, out_sems)
    dmid = dmid_ref[...]
    grads[5] = col_sum(dmid)
    low = dmid.astype(bf)
    wait_group(groups[2])
    wait_group(groups[1])
    split_rows(go, mm(low, wo[...], RIGHT_T))
    x_t[...] = flat(att_ref).T
    dqkv[:, :D] = low
    store.run(flow, stage, 16, (D, D), x_t, dqkv)
    attend_back(q, k, v, valid_ref, go, dq, dk, dv, H)
    d_q, d_v = flat(dq), flat(dv)
    grads[3] = col_sum(d_q)
    grads[4] = col_sum(d_v)
    dqkv[:, :D] = d_q.astype(bf)
    dqkv[:, D : 2 * D] = flat(dk).astype(bf)
    dqkv[:, 2 * D :] = d_v.astype(bf)
    e = e_ref[...]
    x_t[...] = norm(e, vec[1], vec[2]).astype(bf).T
    store.run(flow, stage, 4, (D, 3 * D), x_t, dqkv)
    back, grads[1], grads[2] = norm_back(e, vec[1], mm(dqkv[...], wqkv[...], RIGHT_T))
    de = dmid_ref[...] + back
    grads[0] = col_sum(de)
    dqkv[:, :D] = de.astype(bf)
    x_t[...] = rows_ref[...].T
    store.run(flow, stage, 0, (PIX, D), x_t, dqkv)
    store.finish()


def spaces(count):
    return [pl.BlockSpec(memory_space=pltpu.VMEM)] * count


ANYWHERE = pl.BlockSpec(memory_space=pl.ANY)


def weight_scratch(shapes):
    return [pltpu.VMEM(shape, bf) for shape in shapes]


def call_kernel(body, section, places, table, args, outs, any_outs, scratch, name, micros):
    pieces, n_in, n_out = len(table), len(args), len(outs)
    inside = [i for i in range(n_out) if i not in any_outs]
    held = [pltpu.VMEM(a.shape, a.dtype) for a in args]
    held += [pltpu.VMEM(outs[i][0], outs[i][1]) for i in inside]
    n_held = len(held)

    def guarded(places_ref, *refs):
        @pl.when(places_ref[2 * (NBE + NBP)] == section)
        def run():
            sources = refs[:pieces]
            given = refs[pieces : pieces + n_in]
            results = list(refs[pieces + n_in : pieces + n_in + n_out])
            local = refs[pieces + n_in + n_out :]
            mine, rest, sems = local[:n_held], local[n_held:-1], local[-1]
            loads = [
                pltpu.make_async_copy(given[i], mine[i], sems.at[i]) for i in range(n_in)
            ]
            for copy in loads:
                copy.start()
            stores = []
            for place, i in enumerate(inside):
                stores.append(
                    pltpu.make_async_copy(mine[n_in + place], results[i], sems.at[n_in + place])
                )
                results[i] = mine[n_in + place]
            for copy in loads:
                copy.wait()
            body(places_ref, sources, *mine[:n_in], *results, *rest)
            for copy in stores:
                copy.start()
            for copy in stores:
                copy.wait()

    return pl.pallas_call(
        guarded,
        grid_spec=pltpu.PrefetchScalarGridSpec(
            num_scalar_prefetch=1,
            grid=(),
            in_specs=[ANYWHERE] * (pieces + n_in),
            out_specs=[ANYWHERE] * n_out,
            scratch_shapes=held + scratch + [pltpu.SemaphoreType.DMA((n_held,))],
        ),
        out_shape=[jax.ShapeDtypeStruct(shape, kind) for shape, kind in outs],
        compiler_params=pltpu.CompilerParams(vmem_limit_bytes=58 << 20),
        cost_estimate=pl.CostEstimate(
            flops=0, transcendentals=0, bytes_accessed=int(micros * 3.0e6)
        ),
        name=name,
    )(places, *table, *args)


MARKS = 16


def flow_outs(count, edge, ranks):
    depth = edge // ranks
    if depth % 8:
        return [((count, edge, edge), f32)] + [((8, edge), f32)] * (GROUP - 1)
    return [((ranks // GROUP, depth * count + MARKS, edge), f32)] * GROUP


def stage_shape(count, edge, ranks):
    depth = edge // ranks
    return (count, edge, edge) if depth % 8 else (ranks // GROUP, GROUP, depth * count, edge)


def encoder_call(slots, table, rows, pos, valid, vec):
    n = rows.shape[0]
    images = n // LC
    per = (images, LC, D)
    outs = [((n, D), bf), ((n, D), f32), (per, bf), (per, bf), (per, bf), (per, bf)]
    outs += [((n, D), f32), ((n, FF), f32), ((n, D), f32)]
    scratch = weight_scratch(enc_shapes()) + [pltpu.VMEM((n, D), f32), pltpu.SemaphoreType.DMA((NBE,))]
    args = (rows, pos, valid, vec)
    return call_kernel(encoder_kernel, 0, slots, table, args, outs, (), scratch, "encoder_forward", 25)


def target_call(slots, table, rows, pos, some, pos_some, valid, vec, images):
    n = some.shape[0]
    keys = rows.shape[0] // images
    per, wide = (images, n // images, D), (images, keys, D)
    scratch = weight_scratch(enc_shapes()) + [
        pltpu.VMEM(per, bf),
        pltpu.VMEM(wide, bf),
        pltpu.VMEM(wide, bf),
        pltpu.VMEM(per, bf),
        pltpu.VMEM((n, D), f32),
        pltpu.SemaphoreType.DMA((NBE,)),
    ]
    args = (rows, pos, some, pos_some, valid, vec)
    outs = [((n, D), f32)]
    return call_kernel(target_kernel, 1, slots, table, args, outs, (), scratch, "target_forward", 25)[0]


def predictor_call(slots, table, z, pos_c, pos_t, valid, tgt, tmask, vec, ranks):
    n, m = z.shape[0], pos_t.shape[0]
    images = n // LC
    rows, keys = m // images, valid.shape[-1]
    edge = table[0].shape[-1]
    per, wide = (images, rows, PD), (images, keys, PD)
    outs = [((n, D), bf)] + flow_outs(NBP, edge, ranks)
    outs += [((1, VP), f32), ((1, D), f32), ((1, edge), f32)]
    scratch = weight_scratch(pred_shapes()) + [
        pltpu.VMEM(per, bf),
        pltpu.VMEM(wide, bf),
        pltpu.VMEM(wide, bf),
        pltpu.VMEM(per, bf),
        pltpu.VMEM(per, bf),
        pltpu.VMEM(per, f32),
        pltpu.VMEM(wide, f32),
        pltpu.VMEM(wide, f32),
        pltpu.VMEM((m, PFF), f32),
        pltpu.VMEM((m, PFF), bf),
        pltpu.VMEM((m, PFF), bf),
        pltpu.VMEM((m, PD), f32),
        pltpu.VMEM(stage_shape(NBP, edge, ranks), f32),
        pltpu.SemaphoreType.DMA((NBE + NBP,)),
        pltpu.SemaphoreType.DMA((1, GROUP)),
    ]
    args = (z, pos_c, pos_t, valid, tgt, tmask, vec)
    body = functools.partial(predictor_kernel, edge // ranks)
    return call_kernel(body, 1, slots, table, args, outs, (1, 2, 3, 4), scratch, "predictor_step", 50)


def feed_back_call(slots, table, dz, kept, vec, ranks):
    n = dz.shape[0]
    edge = table[0].shape[-1]
    mid, pre, hid = kept
    scratch = weight_scratch(enc_shapes()[3:]) + [
        pltpu.VMEM((FF, n), bf),
        pltpu.VMEM((n, FF), bf),
        pltpu.VMEM((D, n), bf),
        pltpu.VMEM((n, D), bf),
        pltpu.VMEM((n, D), f32),
        pltpu.VMEM((2,) + stage_shape(4, edge, ranks), f32),
        pltpu.SemaphoreType.DMA((NBE,)),
        pltpu.SemaphoreType.DMA((8, GROUP)),
    ]
    outs = flow_outs(32, edge, ranks)
    outs += [((n, D), f32), ((1, VE), f32), ((1, edge), f32)]
    args = (dz, mid, pre, hid, vec)
    body = functools.partial(feed_back_kernel, edge // ranks)
    return call_kernel(body, 0, slots, table, args, outs, (0, 1, 2, 3), scratch, "feed_backward", 25)


def attention_back_call(slots, table, dmid, rows, kept, valid, vec, ranks):
    n = rows.shape[0]
    images = n // LC
    edge = table[0].shape[-1]
    per = (images, LC, D)
    e, q, k, v, att = kept
    scratch = weight_scratch(enc_shapes()[1:3]) + [
        pltpu.VMEM(per, bf),
        pltpu.VMEM(per, f32),
        pltpu.VMEM(per, f32),
        pltpu.VMEM(per, f32),
        pltpu.VMEM((D, n), bf),
        pltpu.VMEM((n, 3 * D), bf),
        pltpu.VMEM((2,) + stage_shape(4, edge, ranks), f32),
        pltpu.SemaphoreType.DMA((NBE,)),
        pltpu.SemaphoreType.DMA((5, GROUP)),
    ]
    outs = flow_outs(20, edge, ranks) + [((1, VE), f32), ((1, edge), f32)]
    args = (dmid, rows, e, q, k, v, att, valid, vec)
    body = functools.partial(attention_back_kernel, edge // ranks)
    return call_kernel(body, 0, slots, table, args, outs, (0, 1, 2, 3), scratch, "attention_backward", 25)


def soap_first(flags, factor, *arrays):
    n, e = arrays[0].shape[:2]
    one = pl.BlockSpec((1, e, e), lambda i, *_: (i, 0, 0))
    two = pl.BlockSpec((1, 2, e, e), lambda i, *_: (i, 0, 0, 0))
    single = jax.ShapeDtypeStruct((n, e, e), f32)
    double = jax.ShapeDtypeStruct((n, 2, e, e), f32)
    return pl.pallas_call(
        first_kernel,
        grid_spec=pltpu.PrefetchScalarGridSpec(
            num_scalar_prefetch=2, grid=(n,), in_specs=[one] * 8, out_specs=[one] * 5 + [two] * 2
        ),
        out_shape=[single] * 5 + [double] * 2,
        compiler_params=pltpu.CompilerParams(vmem_limit_bytes=56 << 20),
        name="soap_first",
    )(flags, factor, *arrays)


def soap_factor(flags, base, gram):
    n, _, e, _ = base.shape
    whole = pl.BlockSpec(memory_space=pltpu.VMEM)
    return pl.pallas_call(
        factor_kernel,
        grid_spec=pltpu.PrefetchScalarGridSpec(
            num_scalar_prefetch=1,
            grid=(),
            in_specs=[whole] * 2,
            out_specs=whole,
            scratch_shapes=[
                pltpu.VMEM((n, 2, e, e), f32),
                pltpu.VMEM((n, 2, e, e), f32),
                pltpu.VMEM((n, 2, 128, 128), f32),
            ],
        ),
        out_shape=jax.ShapeDtypeStruct(base.shape, f32),
        compiler_params=pltpu.CompilerParams(vmem_limit_bytes=56 << 20),
        name="soap_factor",
    )(flags, base, gram)


def soap_last(flags, left, right, moment, fresh):
    n, e = left.shape[:2]
    one = pl.BlockSpec((1, e, e), lambda i, *_: (i, 0, 0))
    two = pl.BlockSpec((1, 2, e, e), lambda i, *_: (i, 0, 0, 0))
    return pl.pallas_call(
        last_kernel,
        grid_spec=pltpu.PrefetchScalarGridSpec(
            num_scalar_prefetch=1, grid=(n,), in_specs=[one] * 3 + [two], out_specs=[one] * 3
        ),
        out_shape=[jax.ShapeDtypeStruct((n, e, e), f32)] * 3,
        compiler_params=pltpu.CompilerParams(vmem_limit_bytes=56 << 20),
        name="soap_last",
    )(flags, left, right, moment, fresh)


def place_shares(slots, second, enc_share, pred_share, ranks, slot_count):
    depth, edge = enc_share.shape[1:]

    def body(slots_ref, second_ref, enc_ref, pred_ref, out_ref):
        def run(source, first, count):
            def copy(j, carry):
                slot = slots_ref[first + j]
                rows = pl.ds(pl.multiple_of(slot % slot_count * depth, depth), depth)
                out_ref[slot // slot_count, rows, :] = source[j]
                return carry

            lax.fori_loop(0, count, copy, 0)

        @pl.when(second_ref[0] == 0)
        def enc():
            run(enc_ref, 0, NBE)

        @pl.when(second_ref[0] != 0)
        def pred():
            run(pred_ref, NBE, NBP)

    return pl.pallas_call(
        body,
        grid_spec=pltpu.PrefetchScalarGridSpec(
            num_scalar_prefetch=2, grid=(), in_specs=spaces(2), out_specs=spaces(1)[0]
        ),
        out_shape=jax.ShapeDtypeStruct((ranks, slot_count * depth + MARKS, edge), f32),
        compiler_params=pltpu.CompilerParams(vmem_limit_bytes=40 << 20),
        name="place_shares",
    )(slots, second, enc_share, pred_share)


ROUNDS = (
    (((1, 0), (2, 1), (4, 2)), ()),
    (((5, 0), (6, 1), (8, 3)), (1, 2, 4)),
    (((3, 0), (7, 1)), (5, 6)),
    (((9, 0), (10, 1), (12, 2)), (3, 7, 8)),
    (((11, 0), (14, 1), (13, 2)), (9, 10, 12)),
)
LAST = 15


def thirds(slot_count):
    size = -(-slot_count // 3)
    return size, [(start, min(start + size, slot_count)) for start in range(0, slot_count, size)]


def gather_pieces(own, extra):
    both = Exchange((0, 1))
    if both.ranks != 16:
        return None, extra
    held = {0: own}
    for number, (moves, awaited) in enumerate(ROUNDS):
        names = sorted({piece ^ (1 << bit) for piece, bit in moves} | set(awaited))
        values = [held[name] for name in names]
        if number == 2:
            values, extra = lax.optimization_barrier((values, extra))
        elif awaited:
            values = lax.optimization_barrier(values)
        source = dict(zip(names, values))
        for piece, bit in moves:
            held[piece] = both.swap(source[piece ^ (1 << bit)], bit)
    names = [LAST ^ 1, LAST ^ 2, LAST ^ 4]
    source = lax.optimization_barrier([held[name] for name in names])
    ends = [
        both.swap(source[bit][low:high], bit) for bit, (low, high) in enumerate(thirds(own.shape[0])[1])
    ]
    return [held[piece] for piece in range(LAST)] + ends, extra


class Exchange:
    def __init__(self, sections):
        self.ranks = lax.axis_size("dp")
        self.bits = self.ranks.bit_length() - 1
        self.sections = sections

    def swap(self, value, bit):
        return self.trade(value, 1 << bit)

    def trade(self, value, flip):
        pairs = [
            (s * self.ranks + i, s * self.ranks + (i ^ flip))
            for s in self.sections
            for i in range(self.ranks)
        ]
        return lax.ppermute(value, ("section", "dp"), pairs)

    def total(self, value):
        for bit in range(self.bits):
            value = value + self.swap(value, bit)
        return value


def wire_exponent(bound):
    return jnp.floor(jnp.log2(WIRE_TOP / jnp.maximum(bound, 1e-30)))


def pack(values, exponent):
    row = lax.broadcasted_iota(jnp.int32, values.shape, values.ndim - 2)
    marked = jnp.where(row < values.shape[-2] - MARKS, values * jnp.exp2(exponent), exponent)
    return marked.astype(WIRE)


def flow_pieces(arrays, ranks):
    if arrays[1].ndim == 3:
        return list(arrays)
    blocks, edge = arrays[0].shape[:2]
    cut = arrays[0].reshape(blocks, ranks, edge // ranks, edge).transpose(1, 0, 2, 3)
    cut = jnp.pad(cut.reshape(ranks, -1, edge), ((0, 0), (0, MARKS), (0, 0)))
    return cut_pieces(cut, 0, GROUP)


def cut_pieces(shares, shift, size):
    mine = (lax.axis_index("dp") >> shift) & (size - 1)
    cut = shares.reshape((shares.shape[0] // size, size) + shares.shape[1:])
    return [lax.dynamic_index_in_dim(cut, mine ^ p, 1, keepdims=False) for p in range(size)]


def pack_pieces(pieces, bound):
    return [pack(piece, wire_exponent(bound)) for piece in pieces[1:]]


def send_packed(exchange, lows, shift):
    return [exchange.trade(low, (p + 1) << shift) for p, low in enumerate(lows)]


def send_pieces(exchange, pieces, shift, bound):
    return send_packed(exchange, pack_pieces(pieces, bound), shift)


def add_pieces(keep, arrived, bound):
    for got in arrived:
        unscale = jnp.exp2(-got[0, -1, 0].astype(f32))
        keep = keep + got.astype(f32) * unscale
        bound = bound + WIRE_TOP * unscale
    return keep, bound


def finish_sum(exchange, shares, bound):
    shift = GROUP_BITS
    while shares.shape[0] > 1:
        pieces = cut_pieces(shares, shift, min(GROUP, shares.shape[0]))
        arrived = send_pieces(exchange, pieces, shift, bound)
        shares, bound = add_pieces(pieces[0], arrived, bound)
        shift += GROUP_BITS
    return shares[0, :-MARKS], bound


def on_device(
    pixels,
    ctx_idx,
    ctx_len,
    tgt_idx,
    tgt_len,
    slot_of,
    weights,
    first_moment,
    second_moment,
    left_basis,
    right_basis,
    left_stats,
    right_stats,
    vectors,
    vector_first,
    vector_second,
):
    section_index = lax.axis_index("section")
    owner_index = lax.axis_index("dp")
    ranks = lax.axis_size("dp")
    is_first = section_index == 0
    second = section_index.astype(jnp.int32).reshape(1)
    slot_count = weights.shape[1]
    edge = weights.shape[-1]
    enc_slots = slot_of[:NBE]
    pred_slots = slot_of[NBE:]
    row_now = vectors[0]
    enc_vec_now = lax.dynamic_slice_in_dim(row_now, section_index * VP, VE)[None]
    pred_vec_now = row_now[None, :VP]
    pos_enc = sincos(D)
    pos_pred = sincos(PD)
    images = ctx_idx.shape[0]
    rows_all = -(-P_SIZE // 16) * 16
    tgt_flat = tgt_idx.reshape(images, NT * LT)
    ctx_valid = (jnp.arange(LC)[None, :] < ctx_len[:, None]).astype(f32)
    tgt_valid = (jnp.arange(LT)[None, None, :] < tgt_len[:, :, None]).astype(f32)
    tgt_valid = tgt_valid.reshape(images, NT * LT)
    joined_valid = jnp.concatenate([ctx_valid, tgt_valid], 1)[:, None, :]
    all_valid = (jnp.arange(rows_all) < P_SIZE).astype(f32)
    all_valid = jnp.broadcast_to(all_valid, (images, 1, rows_all))

    def pick(index):
        return (index[..., None] == jnp.arange(P_SIZE)).astype(f32)

    ctx_hot = pick(ctx_idx)
    tgt_hot = pick(tgt_flat)

    def choose(hot, values):
        return jnp.einsum(
            "njp,pd->njd", hot, values, precision=lax.Precision.HIGHEST, preferred_element_type=f32
        ).reshape(-1, values.shape[-1])

    def choose_pixels(hot):
        picked = jnp.einsum("njp,npd->njd", hot.astype(bf), pixels, preferred_element_type=f32)
        return picked.astype(bf).reshape(-1, PIX)

    pixel_rows = choose_pixels(ctx_hot)
    enc_pos_ctx = choose(ctx_hot, pos_enc)
    padding = ((0, 0), (0, rows_all - P_SIZE), (0, 0))
    pixel_all = jnp.pad(pixels, padding).reshape(-1, PIX)
    pos_all = jnp.broadcast_to(jnp.pad(pos_enc[None], padding), (images, rows_all, D)).reshape(-1, D)
    pixel_tgt = choose_pixels(tgt_hot)
    enc_pos_tgt = choose(tgt_hot, pos_enc)
    pred_pos_ctx = choose(ctx_hot, pos_pred)
    pred_pos_tgt = choose(tgt_hot, pos_pred)

    ctx_keys = ctx_valid[:, None, :]
    tgt_mask = tgt_valid.reshape(-1, 1)
    ready = (
        pixel_rows, enc_pos_ctx, ctx_keys, enc_vec_now, pixel_all, pos_all, pixel_tgt, enc_pos_tgt,
        all_valid, pred_pos_ctx, pred_pos_tgt, joined_valid, tgt_mask, pred_vec_now,
    )
    own = weights[0].astype(bf)
    place = [second, owner_index.astype(jnp.int32).reshape(1)]
    table, ready = gather_pieces(own, ready)
    if table is None:
        table = [lax.all_gather(own, "dp", axis=0, tiled=True)]
        places = jnp.concatenate([jnp.zeros_like(slot_of), slot_of] + place)
    else:
        sources = jnp.bitwise_xor(slot_of // slot_count, owner_index)
        indices = slot_of % slot_count
        size, _ = thirds(slot_count)
        is_last = sources == LAST
        sources = jnp.where(is_last, LAST + indices // size, sources)
        places = jnp.concatenate([sources, jnp.where(is_last, indices % size, indices)] + place)
    (
        pixel_rows, enc_pos_ctx, ctx_keys, enc_vec_now, pixel_all, pos_all, pixel_tgt, enc_pos_tgt,
        all_valid, pred_pos_ctx, pred_pos_tgt, joined_valid, tgt_mask, pred_vec_now,
    ) = ready

    z, *kept = encoder_call(places, table, pixel_rows, enc_pos_ctx, ctx_keys, enc_vec_now)
    context = from_behind(z, "section", 1)
    target = target_call(
        places, table, pixel_all, pos_all, pixel_tgt, enc_pos_tgt, all_valid, enc_vec_now, images
    )
    back_send, *pred_flows, pred_vec, loss_lanes, pred_top = predictor_call(
        places, table, context, pred_pos_ctx, pred_pos_tgt, joined_valid, target, tgt_mask, pred_vec_now, ranks
    )
    incoming = from_behind(back_send, "section", -1)
    loss_local = jnp.where(is_first, 0.0, jnp.sum(loss_lanes))

    behind = Exchange((1,))

    def sum_predictor(flows, top):
        bound = jnp.max(top)
        pieces = flow_pieces(flows, ranks)
        shares, bound = add_pieces(pieces[0], send_pieces(behind, pieces, 0, bound), bound)
        return finish_sum(behind, shares, bound)

    def skip_predictor(flows, top):
        return jnp.zeros((edge // ranks * NBP, edge), f32), jnp.zeros((), f32)

    incoming, pred_top = lax.optimization_barrier((incoming, pred_top))
    pred_sum, pred_bound = lax.cond(is_first, skip_predictor, sum_predictor, pred_flows, pred_top)
    incoming, pred_sum = lax.optimization_barrier((incoming, pred_sum))
    *feed_flow, grad_mid, feed_vec, feed_top = feed_back_call(
        places, table, incoming, kept[5:], enc_vec_now, ranks
    )
    ahead = Exchange((0,))
    feed_bound = jnp.max(feed_top)
    feed_pieces = flow_pieces(feed_flow, ranks)
    lows, grad_mid = lax.optimization_barrier((pack_pieces(feed_pieces, feed_bound), grad_mid))
    feed_arrived = send_packed(ahead, lows, 0)
    *rest_flow, rest_vec, rest_top = attention_back_call(
        places, table, grad_mid, pixel_rows, kept[:5], ctx_keys, enc_vec_now, ranks
    )
    rest_bound = jnp.max(rest_top)
    rest_pieces = flow_pieces(rest_flow, ranks)
    lows = pack_pieces(rest_pieces, rest_bound)
    feed_arrived, lows = lax.optimization_barrier((feed_arrived, lows))
    rest_arrived = send_packed(ahead, lows, 0)
    feed_shares, feed_bound = add_pieces(feed_pieces[0], feed_arrived, feed_bound)
    rest_shares, rest_bound = add_pieces(rest_pieces[0], rest_arrived, rest_bound)
    feed_sum, feed_bound = finish_sum(ahead, feed_shares, feed_bound)
    rest_sum, rest_bound = finish_sum(ahead, rest_shares, rest_bound)
    enc_sum = jnp.concatenate([rest_sum, feed_sum], 0)
    enc_bound = jnp.maximum(rest_bound, feed_bound)
    cut_at = 6 * D
    enc_vec = jnp.concatenate([rest_vec[:, :cut_at], feed_vec[:, cut_at:]], 1)
    depth = edge // ranks
    enc_share = enc_sum.reshape(NBE, depth, edge)
    pred_share = pred_sum.reshape(NBP, depth, edge)

    both = Exchange((0, 1))
    vec_local = jnp.where(is_first, enc_vec[0], jnp.pad(pred_vec[0], (0, VE - VP)))
    count_local = jnp.where(is_first, 0, jnp.sum(tgt_len)).astype(f32)
    scalars = jnp.pad(jnp.stack([loss_local, count_local]), (0, 126))
    summed = both.total(jnp.concatenate([vec_local, scalars]))
    vec_total = jnp.pad(summed[:VE], (0, VW - VE))
    share_squares = jnp.where(
        is_first, jnp.sum(enc_share * enc_share), jnp.sum(pred_share * pred_share)
    )
    squares = both.total(jnp.full((128,), share_squares))
    facts = jnp.stack([squares[0] + jnp.sum(summed[:VE] ** 2), summed[VE], summed[VE + 1]])
    facts = jnp.pad(facts, (0, 125))
    swap_sections = [(i, 1 - i) for i in range(2)]
    facts = facts + lax.ppermute(facts, "section", swap_sections)
    square_total, loss_total, count_total = facts[0], facts[1], facts[2]

    placed = place_shares(slot_of, second, enc_share, pred_share, ranks, slot_count)
    exponent = wire_exponent(jnp.where(is_first, enc_bound, pred_bound))
    payload = pack(placed, exponent)
    owned = lax.all_to_all(payload, "dp", split_axis=0, concat_axis=0, tiled=True).astype(f32)
    unscale = jnp.exp2(-owned[:, -1:, :1])
    owned = (owned[:, : slot_count * depth] * unscale).reshape(ranks, slot_count, depth, edge)
    owned_sum = owned.transpose(1, 0, 2, 3).reshape(slot_count, edge, edge)

    own_ids = owner_index * slot_count + jnp.arange(slot_count)
    enc_here = jnp.any(own_ids[:, None] == enc_slots[None, :], 1)
    pred_here = jnp.any(own_ids[:, None] == pred_slots[None, :], 1)
    trained = jnp.where(is_first, enc_here, pred_here)
    ema_here = jnp.logical_and(jnp.logical_not(is_first), enc_here)
    positions = jnp.arange(VW)
    vec_trained = positions < jnp.where(is_first, VE, VP)
    vec_ema = jnp.logical_and(jnp.logical_not(is_first), positions >= VP)
    grad_norm = jnp.sqrt(square_total) / count_total
    factor = jnp.minimum(1.0, CLIP_LIMIT / (grad_norm + 1e-06)) / count_total

    flags = trained.astype(jnp.int32)
    new_weight, moment, new_second, new_estat, new_fstat, base, gram = soap_first(
        flags,
        factor.reshape(1),
        owned_sum,
        weights[0],
        first_moment[0],
        second_moment[0],
        left_basis[0],
        right_basis[0],
        left_stats[0],
        right_stats[0],
    )
    fresh_bases = soap_factor(flags, base, gram)
    new_left, new_right, new_first = soap_last(
        flags, left_basis[0], right_basis[0], moment, fresh_bases
    )

    correct_one = 1.0 - BETA_FIRST**STEP
    correct_two = 1.0 - BETA_SECOND**STEP
    vec_clipped = vec_total * factor
    fresh_first = BETA_FIRST * vector_first[0] + (1.0 - BETA_FIRST) * vec_clipped
    fresh_second = BETA_SECOND * vector_second[0] + (1.0 - BETA_SECOND) * vec_clipped * vec_clipped
    stepped = row_now - RATE_VECTOR * (fresh_first / correct_one) / (
        jnp.sqrt(fresh_second / correct_two) + ADAM_EPS
    )
    new_vec = jnp.where(vec_trained, stepped, row_now)
    new_vec_first = jnp.where(vec_trained, fresh_first, vector_first[0])
    new_vec_second = jnp.where(vec_trained, fresh_second, vector_second[0])
    from_encoder = from_behind(new_weight.astype(bf), "section", 1).astype(f32)
    vec_from_encoder = from_behind(new_vec.astype(bf), "section", 1).astype(f32)
    new_weight = jnp.where(
        ema_here[:, None, None], EMA_KEEP * weights[0] + (1.0 - EMA_KEEP) * from_encoder, new_weight
    )
    aligned = jnp.concatenate([jnp.zeros((VP,), f32), vec_from_encoder[:VE]])
    new_vec = jnp.where(vec_ema, EMA_KEEP * row_now + (1.0 - EMA_KEEP) * aligned, new_vec)
    return (
        loss_total,
        count_total,
        grad_norm,
        new_weight[None],
        new_first[None],
        new_second[None],
        new_left[None],
        new_right[None],
        new_estat[None],
        new_fstat[None],
        new_vec[None],
        new_vec_first[None],
        new_vec_second[None],
    )


def solution(mesh):
    in_specs = (
        P("dp", None, None),
        P("dp", None),
        P("dp"),
        P("dp", None, None),
        P("dp", None),
        P(),
        P("section", "dp", None, None),
        P("section", "dp", None, None),
        P("section", "dp", None, None),
        P("section", "dp", None, None),
        P("section", "dp", None, None),
        P("section", "dp", None, None),
        P("section", "dp", None, None),
        P("section", None),
        P("section", None),
        P("section", None),
    )
    out_specs = (
        P(),
        P(),
        P(),
        P("section", "dp", None, None),
        P("section", "dp", None, None),
        P("section", "dp", None, None),
        P("section", "dp", None, None),
        P("section", "dp", None, None),
        P("section", "dp", None, None),
        P("section", "dp", None, None),
        P("section", None),
        P("section", None),
        P("section", None),
    )
    return jax.shard_map(
        on_device, mesh=mesh, in_specs=in_specs, out_specs=out_specs, check_vma=False
    )
```

```python
import functools
import math

import jax
import jax.numpy as jnp
from jax import lax
from jax.experimental import pallas as pl
from jax.experimental.pallas import tpu as pltpu
from jax.sharding import PartitionSpec as P

D = 768
FF = 3072
H = 12
PD = 384
PFF = 1536
PH = 12
PIX = 768
GRID = 14
NT = 4
LC = 128
STEP = 10
P_SIZE = 196
LT = 36
NBE = 52
NBP = 16
VE = 11520
VP = 6912
VW = 18432


NORM_EPS = 1e-06
ADAM_EPS = 1e-08
BETA_FIRST = 0.5
BETA_SECOND = 0.5
BETA_STATS = 0.95
RATE_MATRIX = 0.02
RATE_VECTOR = 0.05
DECAY_MATRIX = 0.04
EMA_KEEP = 0.996
CLIP_LIMIT = 1.0
NEG_FILL = -1000000000.0
WIRE = jnp.float16
WIRE_TOP = 16384.0
f32 = jnp.float32
bf = jnp.bfloat16


def from_behind(shard, axis, by):
    size = lax.axis_size(axis)
    pairs = [(i, i + by) for i in range(size) if 0 <= i + by < size]
    return lax.ppermute(shard, axis, pairs)


def enc_shapes():
    return [(PIX, D), (D, 3 * D), (D, D), (D, FF), (FF, D)]


def pred_shapes():
    return [(D, PD), (PD, 3 * PD), (PD, PD), (PD, PFF), (PFF, PD), (PD, D)]


def enc_lengths():
    return [D] * 8 + [FF, D, D, D]


def pred_lengths():
    return [PD] * 8 + [PFF, PD, PD, PD, D, PD]


def sincos(width):
    quarter = width // 4
    frequency = 1.0 / 10000.0 ** (jnp.arange(quarter, dtype=jnp.float32) / quarter)
    cell_ids = jnp.arange(P_SIZE)
    row_pos = (cell_ids // GRID).astype(jnp.float32)[:, None] * frequency
    column_pos = (cell_ids % GRID).astype(jnp.float32)[:, None] * frequency
    return jnp.concatenate(
        [jnp.sin(row_pos), jnp.cos(row_pos), jnp.sin(column_pos), jnp.cos(column_pos)], 1
    )


DIMS = {"nn": (1, 0), "nt": (1, 1), "tn": (0, 0)}

def parts_of(a, count):
    found = []
    for index in range(count):
        piece = a.astype(bf)
        found.append(piece)
        if index + 1 < count:
            a = a - piece.astype(f32)
    return found

def product(left, right, form, pairs):
    ld, rd = DIMS[form]
    lhs = jnp.concatenate([left[i] for i, _ in pairs], ld)
    rhs = jnp.concatenate([right[j] for _, j in pairs], rd)
    return lax.dot_general(lhs, rhs, (((ld,), (rd,)), ((), ())), preferred_element_type=f32)

THREE = ((0, 1), (1, 0), (0, 0))
SIX = ((0, 2), (2, 0), (1, 1), (0, 1), (1, 0), (0, 0))
def mul3(left, right, form="nn"):
    return product(left, right, form, THREE)
def mul6(left, right, form="nn"):
    return product(left, right, form, SIX)

def invert_factors(mats):
    n = mats[0].shape[0]
    lane = lax.broadcasted_iota(jnp.int32, (8, n), 1)
    sub = lax.broadcasted_iota(jnp.int32, (8, n), 0)
    groups = [[a[8 * t : 8 * t + 8, :] for t in range(n // 8)] for a in mats]
    for j in range(n):
        top, at_row = divmod(j, 8)
        here = lane == j
        pick = jnp.full((8, n), j, jnp.int32)
        for tiles in groups:
            column = jnp.take_along_axis(tiles[top], pick, axis=1)
            pivot = jnp.broadcast_to(column[at_row : at_row + 1, :], (8, n))
            row = jnp.broadcast_to(tiles[top][at_row : at_row + 1, :], (8, n))
            scaled = jnp.where(here, 1.0, row) * (1.0 / pivot)
            for t in range(top, n // 8):
                if t > top:
                    column = jnp.take_along_axis(tiles[t], pick, axis=1)
                fresh = jnp.where(here, 0.0, tiles[t]) - column * scaled
                tiles[t] = jnp.where(sub > at_row, fresh, tiles[t]) if t == top else fresh
    results = []
    for tiles in groups:
        rows = []
        for t in range(n // 8):
            at = sub + 8 * t
            pivots = jnp.sum(jnp.where(lane == at, tiles[t], 0.0), axis=1, keepdims=True)
            unit = jnp.where(lane < at, tiles[t], jnp.where(lane == at, 1.0, 0.0))
            rows.append(unit * lax.rsqrt(pivots))
        results.append(jnp.concatenate(rows, 0))
    return results

def first_kernel(flag, factor, g_ref, w_ref, m_ref, v_ref, l_ref, r_ref, e_ref, f_ref,
                 w_out, m_out, v_out, e_out, f_out, base_out, gram_out):
    on = flag[pl.program_id(0)] != 0

    @pl.when(jnp.logical_not(on))
    def keep():
        for source, target in ((w_ref, w_out), (m_ref, m_out), (v_ref, v_out), (e_ref, e_out), (f_ref, f_out)):
            target[...] = source[...]

    @pl.when(on)
    def update():
        correct_one = 1.0 - BETA_FIRST**STEP
        correct_two = 1.0 - BETA_SECOND**STEP
        grad = parts_of(g_ref[0] * factor[0], 3)
        left = parts_of(l_ref[0], 3)
        right = parts_of(r_ref[0], 3)
        rotated = mul3(left, parts_of(mul3(grad, right), 2), "tn")
        moment = BETA_FIRST * m_ref[0] + (1.0 - BETA_FIRST) * rotated
        second = BETA_SECOND * v_ref[0] + (1.0 - BETA_SECOND) * rotated * rotated
        m_out[0] = moment
        v_out[0] = second
        normed = moment / correct_one / (jnp.sqrt(second / correct_two) + ADAM_EPS)
        weight = w_ref[0]
        step = mul3(left, parts_of(mul3(parts_of(normed, 2), right, "nt"), 2))
        w_out[0] = weight - RATE_MATRIX * (step + DECAY_MATRIX * weight)
        for index, (stat, target, basis, form) in enumerate(
            ((e_ref, e_out, left, "nt"), (f_ref, f_out, right, "tn"))
        ):
            fresh = BETA_STATS * stat[0] + (1.0 - BETA_STATS) * mul3(grad, grad, form)
            target[0] = fresh
            moved = mul6(parts_of(fresh, 3), basis)
            base_out[0, index] = moved
            pieces = parts_of(moved, 3)
            edge = moved.shape[-1]
            for start in range(0, edge, 128):
                rows = [piece[:, start : start + 128] for piece in pieces]
                upper = [piece[:, start:] for piece in pieces]
                gram_out[0, index, start : start + 128, start:] = mul6(rows, upper, "tn")

def factor_kernel(flag, base_ref, gram_ref, q_out, base, gram, inverse):
    blocks, edge = base_ref.shape[0], base_ref.shape[-1]
    panel = 128
    count = edge // panel
    base[...] = base_ref[...]
    gram[...] = gram_ref[...]

    def stage(k):
        at = pl.ds(panel * k, panel)
        start = panel * k
        spot = slice(start, start + panel)
        rest = slice(start + panel, edge)

        def block(b, carry):
            @pl.when(flag[b] != 0)
            def run():
                sides = range(2)
                inv = [parts_of(inverse[b, side], 3) for side in sides]
                q = [mul6(parts_of(base[b, side, :, spot], 3), inv[side], "nt") for side in sides]
                for side in sides:
                    q_out[b, side, :, spot] = q[side]
                if k + 1 < count:
                    tops = [mul6(inv[side], parts_of(gram[b, side, spot, rest], 3)) for side in sides]
                    p = [parts_of(top, 3) for top in tops]
                    minus = [mul6(p[side], p[side], "tn") for side in sides]
                    moved = [mul6(parts_of(q[side], 3), p[side]) for side in sides]
                    for side in sides:
                        gram[b, side, rest, rest] = gram[b, side, rest, rest] - minus[side]
                        base[b, side, :, rest] = base[b, side, :, rest] - moved[side]
            return carry

        lax.fori_loop(0, blocks, block, 0)

    def turn(k, carry):
        for which in range(count):
            @pl.when(k == which)
            def load():
                spot = slice(panel * which, panel * which + panel)
                for b in range(blocks):
                    for side in range(2):
                        inverse[b, side] = gram[b, side, spot, spot]
        mats = invert_factors([inverse[b, side] for b in range(blocks) for side in range(2)])
        for b in range(blocks):
            for side in range(2):
                inverse[b, side] = mats[2 * b + side]
        for which in range(count):
            @pl.when(k == which)
            def run():
                stage(which)
        return carry

    lax.fori_loop(0, count, turn, 0)

def last_kernel(flag, l_ref, r_ref, m_ref, q_ref, l_out, r_out, m_out):
    on = flag[pl.program_id(0)] != 0

    @pl.when(jnp.logical_not(on))
    def keep():
        l_out[...] = l_ref[...]
        r_out[...] = r_ref[...]
        m_out[...] = m_ref[...]

    @pl.when(on)
    def update():
        l_out[0] = q_ref[0, 0]
        r_out[0] = q_ref[0, 1]
        turn_left = mul3(parts_of(q_ref[0, 0], 2), parts_of(l_ref[0], 2), "tn")
        turn_right = mul3(parts_of(r_ref[0], 2), parts_of(q_ref[0, 1], 2), "tn")
        half = mul3(parts_of(turn_left, 2), parts_of(m_ref[0], 2))
        m_out[0] = mul3(parts_of(half, 2), parts_of(turn_right, 2))

PLAIN = (((1,), (0,)), ((), ()))
RIGHT_T = (((1,), (1,)), ((), ()))
LEFT_T = (((0,), (0,)), ((), ()))
ROOT_HALF = 0.7071067811865476
ROOT_TWO_PI = 2.5066282746310002


def mm(left, right, dims=PLAIN):
    return lax.dot_general(left, right, dims, preferred_element_type=f32)


def norm_parts(x):
    center = x - jnp.mean(x, -1, keepdims=True)
    inverse = lax.rsqrt(jnp.mean(center * center, -1, keepdims=True) + NORM_EPS)
    return center * inverse, inverse


def norm(x, gain, shift):
    return norm_parts(x)[0] * gain + shift


def norm_back(x, gain, grad):
    unit, inverse = norm_parts(x)
    grad_unit = grad * gain
    mean_one = jnp.mean(grad_unit, -1, keepdims=True)
    mean_two = jnp.mean(grad_unit * unit, -1, keepdims=True)
    back = inverse * (grad_unit - mean_one - unit * mean_two)
    return back, col_sum(grad * unit), col_sum(grad)


def col_sum(x):
    return jnp.sum(x, 0, keepdims=True)


def gelu(x):
    return 0.5 * x * (1.0 + lax.erf(x * ROOT_HALF))


def gelu_slope(x):
    return 0.5 * (1.0 + lax.erf(x * ROOT_HALF)) + x * jnp.exp(-0.5 * x * x) * (1.0 / ROOT_TWO_PI)


def offsets(lengths):
    result = [0]
    for length in lengths:
        result.append(result[-1] + length)
    return result


class Vec:
    def __init__(self, ref, lengths):
        self.ref, self.at = ref, offsets(lengths)

    def __getitem__(self, k):
        return self.ref[:, self.at[k] : self.at[k + 1]]

    def __setitem__(self, k, value):
        self.ref[:, self.at[k] : self.at[k + 1]] = value

    def part(self, k, start, size):
        return self.ref[:, pl.ds(pl.multiple_of(self.at[k] + start, 128), size)]

    def put_part(self, k, start, size, value):
        self.ref[:, pl.ds(pl.multiple_of(self.at[k] + start, 128), size)] = value


class Fetch:
    def __init__(self, pieces, places, j, spot, sem):
        self.pieces, self.spot, self.sem = pieces, spot, sem
        self.which, self.index = places[j], places[NBE + NBP + j]

    def copy(self, piece, index):
        return pltpu.make_async_copy(piece.at[index], self.spot, self.sem)

    def start(self):
        if len(self.pieces) == 1:
            self.copy(self.pieces[0], self.index).start()
        else:
            self.start_among(0, len(self.pieces))

    def start_among(self, low, high):
        if high - low == 1:
            self.copy(self.pieces[low], self.index).start()
            return
        middle = (low + high) // 2

        @pl.when(self.which < middle)
        def below():
            self.start_among(low, middle)

        @pl.when(self.which >= middle)
        def above():
            self.start_among(middle, high)

    def wait(self):
        self.copy(self.pieces[0], 0).wait()


def load_blocks(pieces, places, sems, first, shapes, targets):
    edge = pieces[0].shape[-1]
    groups = []
    j = first
    for (height, breadth), target in zip(shapes, targets):
        group = []
        for row in range(height // edge):
            for column in range(breadth // edge):
                if target is not None:
                    spot = target.at[pl.ds(row * edge, edge), pl.ds(column * edge, edge)]
                    group.append(Fetch(pieces, places, j, spot, sems.at[j]))
                j += 1
        groups.append(group)
    return groups


def start_all(groups, loads):
    for group in groups:
        for copy in group:
            copy.start()
    for copy in loads:
        copy.wait()


def wait_group(group):
    for copy in group:
        copy.wait()


def head_masks(rows, heads, width):
    lane = lax.broadcasted_iota(jnp.int32, (rows, 128), 1)
    size = width // heads
    return [(lane >= size * h) & (lane < size * h + size) for h in range(128 // size)]


def as_factors(masks):
    return [jnp.where(mask, 1.0, 0.0).astype(bf) for mask in masks]


def soft(scores, allowed):
    scores = jnp.where(allowed, scores, NEG_FILL)
    top = jnp.max(scores, -1, keepdims=True)
    raised = jnp.exp(scores - top)
    return raised * (1.0 / jnp.sum(raised, -1, keepdims=True))


def head_jobs(q_ref, k_ref, v_ref, p, span, factors):
    jobs = []
    for g in range(span):
        lanes = pl.ds(pl.multiple_of(128 * (span * p + g), 128), 128)
        for i in range(q_ref.shape[0]):
            q, k, v = q_ref[i, :, lanes], k_ref[i, :, lanes], v_ref[i, :, lanes]
            for h in range(len(factors)):
                jobs.append((i, lanes, h, q, k, v))
    return jobs


def attend(q_ref, k_ref, v_ref, valid_ref, out_ref, heads):
    images, rows, width = q_ref.shape
    keys = k_ref.shape[1]
    masks = head_masks(rows, heads, width)
    factors = as_factors(masks)
    span = 3 if width // 128 % 3 == 0 else 1

    def group(p, carry):
        allowed = [jnp.broadcast_to(valid_ref[i], (rows, keys)) > 0.0 for i in range(images)]
        jobs = head_jobs(q_ref, k_ref, v_ref, p, span, factors)
        scores = [mm(q * factors[h], k, RIGHT_T) for _, _, h, q, k, _ in jobs]
        probs = [soft(s, allowed[job[0]]).astype(bf) for s, job in zip(scores, jobs)]
        parts = [mm(probs[n], job[5]) for n, job in enumerate(jobs)]
        for n in range(0, len(jobs), len(masks)):
            result = parts[n]
            for h in range(1, len(masks)):
                result = jnp.where(masks[h], parts[n + h], result)
            out_ref[jobs[n][0], :, jobs[n][1]] = result.astype(bf)
        return carry

    lax.fori_loop(0, width // 128 // span, group, 0)


def attend_back(q_ref, k_ref, v_ref, valid_ref, go_ref, dq_ref, dk_ref, dv_ref, heads):
    images, rows, width = q_ref.shape
    keys = k_ref.shape[1]
    masks = head_masks(rows, heads, width)
    key_masks = head_masks(keys, heads, width)
    factors = as_factors(masks)
    scale = 1.0 / math.sqrt(width // heads)
    span = 3 if width // 128 % 3 == 0 else 1

    def group(p, carry):
        allowed = [jnp.broadcast_to(valid_ref[i], (rows, keys)) > 0.0 for i in range(images)]
        jobs = head_jobs(q_ref, k_ref, v_ref, p, span, factors)
        grads = [go_ref[job[0], :, job[1]] for job in jobs]
        scores = [mm(q * factors[h], k, RIGHT_T) for _, _, h, q, k, _ in jobs]
        dprobs = [mm(go * factors[job[2]], job[5], RIGHT_T) for go, job in zip(grads, jobs)]
        probs = [soft(s, allowed[job[0]]) for s, job in zip(scores, jobs)]
        lows = [
            (a * (da - jnp.sum(da * a, -1, keepdims=True))).astype(bf) for a, da in zip(probs, dprobs)
        ]
        dvs = [mm(a.astype(bf), go, LEFT_T) for a, go in zip(probs, grads)]
        dqs = [mm(low, job[4]) for low, job in zip(lows, jobs)]
        dks = [mm(low, job[3], LEFT_T) for low, job in zip(lows, jobs)]
        for n in range(0, len(jobs), len(masks)):
            dq, dk, dv = dqs[n], dks[n], dvs[n]
            for h in range(1, len(masks)):
                dq = jnp.where(masks[h], dqs[n + h], dq)
                dk = jnp.where(key_masks[h], dks[n + h], dk)
                dv = jnp.where(key_masks[h], dvs[n + h], dv)
            i, lanes = jobs[n][:2]
            dq_ref[i, :, lanes] = dq * scale
            dk_ref[i, :, lanes] = dk
            dv_ref[i, :, lanes] = dv
        return carry

    lax.fori_loop(0, width // 128 // span, group, 0)


def split_rows(ref, value):
    images, rows, _ = ref.shape
    for i in range(images):
        ref[i] = value[rows * i : rows * i + rows].astype(ref.dtype)


def flat(ref):
    return jnp.concatenate([ref[i] for i in range(ref.shape[0])], 0)


STRIP = 768


def feed_forward(normed, mid, up, down, vec, pre_ref, acc_ref):
    acc_ref[...] = mid

    def strip(c, carry):
        lanes = pl.ds(pl.multiple_of(c * STRIP, 128), STRIP)
        pre = mm(normed, up[:, lanes]) + vec.part(8, c * STRIP, STRIP)
        if pre_ref is not None:
            pre_ref[:, lanes] = pre
        acc_ref[...] += mm(gelu(pre).astype(bf), down[lanes, :])
        return carry

    lax.fori_loop(0, up.shape[1] // STRIP, strip, 0)
    return acc_ref[...] + vec[9]


def encoder_kernel(
    loads, slots, table, rows_ref, pos_ref, valid_ref, vec_ref,
    z_out, e_out, q_out, k_out, v_out, att_out, mid_out, pre_out, hid_out,
    wp, wqkv, wo, w1, w2, acc, sems,
):
    vec = Vec(vec_ref, enc_lengths())
    groups = load_blocks(table, slots, sems, 0, enc_shapes(), (wp, wqkv, wo, w1, w2))
    start_all((), loads)
    start_all(groups, ())
    wait_group(groups[0])
    e = mm(rows_ref[...], wp[...]) + vec[0] + pos_ref[...]
    e_out[...] = e
    normed = norm(e, vec[1], vec[2]).astype(bf)
    wait_group(groups[1])
    split_rows(q_out, (mm(normed, wqkv[:, :D]) + vec[3]) * (1.0 / math.sqrt(D // H)))
    split_rows(k_out, mm(normed, wqkv[:, D : 2 * D]))
    split_rows(v_out, mm(normed, wqkv[:, 2 * D :]) + vec[4])
    attend(q_out, k_out, v_out, valid_ref, att_out, H)
    wait_group(groups[2])
    mid = e + mm(flat(att_out), wo[...]) + vec[5]
    mid_out[...] = mid
    hidden = norm(mid, vec[6], vec[7]).astype(bf)
    wait_group(groups[3])
    wait_group(groups[4])
    hid = feed_forward(hidden, mid, w1, w2, vec, pre_out, acc)
    hid_out[...] = hid
    z_out[...] = norm(hid, vec[10], vec[11]).astype(bf)


def target_kernel(
    loads, slots, table, all_ref, pos_all_ref, some_ref, pos_some_ref, valid_ref, vec_ref,
    out_ref, wp, wqkv, wo, w1, w2, q, k, v, att, acc, sems,
):
    vec = Vec(vec_ref, enc_lengths())
    groups = load_blocks(table, slots, sems, 0, enc_shapes(), (wp, wqkv, wo, w1, w2))
    start_all((), loads)
    start_all(groups, ())
    wait_group(groups[0])
    e = mm(all_ref[...], wp[...]) + vec[0] + pos_all_ref[...]
    normed = norm(e, vec[1], vec[2]).astype(bf)
    wait_group(groups[1])
    split_rows(k, mm(normed, wqkv[:, D : 2 * D]))
    split_rows(v, mm(normed, wqkv[:, 2 * D :]) + vec[4])
    e = mm(some_ref[...], wp[...]) + vec[0] + pos_some_ref[...]
    normed = norm(e, vec[1], vec[2]).astype(bf)
    split_rows(q, (mm(normed, wqkv[:, :D]) + vec[3]) * (1.0 / math.sqrt(D // H)))
    attend(q, k, v, valid_ref, att, H)
    wait_group(groups[2])
    mid = e + mm(flat(att), wo[...]) + vec[5]
    hidden = norm(mid, vec[6], vec[7]).astype(bf)
    wait_group(groups[3])
    wait_group(groups[4])
    hid = feed_forward(hidden, mid, w1, w2, vec, None, acc)
    out_ref[...] = norm_parts(norm(hid, vec[10], vec[11]))[0]


class Flow:
    def __init__(self, outs, stage, depth, me):
        self.outs, self.stage, self.depth, self.me = outs, stage, depth, me

    def put(self, value, j):
        edge, depth = value.shape[-1], self.depth
        if depth % 8:
            self.stage[j] = value
        else:
            cut = value.reshape(self.stage.shape[:2] + (depth, edge))
            self.stage[:, :, depth * j : depth * j + depth, :] = cut

    def copies(self, start, count, sems):
        depth = self.depth
        if depth % 8:
            target = self.outs[0].at[pl.ds(start, count)]
            return [pltpu.make_async_copy(self.stage.at[pl.ds(0, count)], target, sems[0])]
        group = len(self.outs)
        mine = self.me & (group - 1)
        made = []
        for p in range(group):
            source = self.stage.at[:, mine ^ p, pl.ds(0, depth * count), :]
            target = self.outs[p].at[:, pl.ds(depth * start, depth * count), :]
            made.append(pltpu.make_async_copy(source, target, sems[p]))
        return made


GROUP_BITS = 2
GROUP = 1 << GROUP_BITS


def sems_of(ref, turn):
    return [ref.at[turn, p] for p in range(GROUP)]


def raise_top(top_ref, value):
    top_ref[...] = jnp.maximum(top_ref[...], jnp.max(jnp.abs(value), 0, keepdims=True))


def predictor_kernel(
    depth, loads, slots, table, z_ref, pos_c_ref, pos_t_ref, valid_ref, tgt_ref, tmask_ref, vec_ref,
    dz_out, out_0, out_1, out_2, out_3, vec_out, loss_out, top_out,
    win, wqkv, wo, w1, w2, wout, q, k, v, att, go, dq, dk, dv, pre_ref, act_ref, dpre_ref, acc, stage, sems, flow_sems,
):
    vec, grads = Vec(vec_ref, pred_lengths()), Vec(vec_out, pred_lengths())
    edge = table[0].shape[-1]
    flow = Flow((out_0, out_1, out_2, out_3), stage, depth, slots[2 * (NBE + NBP) + 1])
    images = z_ref.shape[0] // LC
    groups = load_blocks(table, slots, sems, NBE, pred_shapes(), (win, wqkv, wo, w1, w2, wout))
    start_all(groups, loads)
    for group in groups:
        wait_group(group)
    firsts = offsets([h * b // (edge * edge) for h, b in pred_shapes()])

    def store(index, matrix):
        for row in range(matrix.shape[0] // edge):
            for column in range(matrix.shape[1] // edge):
                j = firsts[index] + row * (pred_shapes()[index][1] // edge) + column
                value = matrix[row * edge : row * edge + edge, column * edge : column * edge + edge]
                raise_top(top_out, value)
                flow.put(value, j)

    top_out[...] = jnp.zeros_like(top_out)
    z = z_ref[...]
    x_c = mm(z, win[...]) + vec[0] + pos_c_ref[...]
    x_t = vec[13] + pos_t_ref[...]
    n_c = norm(x_c, vec[1], vec[2]).astype(bf)
    n_t = norm(x_t, vec[1], vec[2]).astype(bf)
    split_rows(q, (mm(n_t, wqkv[:, :PD]) + vec[3]) * (1.0 / math.sqrt(PD // PH)))
    for ref, start, bias in ((k, PD, 0.0), (v, 2 * PD, vec[4])):
        of_c = mm(n_c, wqkv[:, start : start + PD]) + bias
        of_t = mm(n_t, wqkv[:, start : start + PD]) + bias
        count = NT * LT
        for i in range(images):
            ref[i, :LC, :] = of_c[LC * i : LC * i + LC].astype(bf)
            ref[i, LC:, :] = of_t[count * i : count * i + count].astype(bf)
    attend(q, k, v, valid_ref, att, PH)
    mid = x_t + mm(flat(att), wo[...]) + vec[5]
    n_two = norm(mid, vec[6], vec[7]).astype(bf)
    y = feed_forward(n_two, mid, w1, w2, vec, pre_ref, acc)
    n_three = norm(y, vec[10], vec[11]).astype(bf)
    difference = mm(n_three, wout[...]) + vec[12] - tgt_ref[...]
    tmask = tmask_ref[...]
    magnitude = jnp.abs(difference)
    loss = jnp.where(magnitude < 1.0, 0.5 * difference * difference, magnitude - 0.5) * tmask
    loss_out[...] = col_sum(loss)
    grad = jnp.clip(difference, -1.0, 1.0) * tmask

    grads[12] = col_sum(grad)
    low = grad.astype(bf)
    store(5, mm(n_three.T, low))
    dy, grads[10], grads[11] = norm_back(y, vec[10], mm(low, wout[...], RIGHT_T))
    grads[9] = col_sum(dy)
    low = dy.astype(bf)
    acc[...] = jnp.zeros_like(acc)

    def strip(c, carry):
        lanes = pl.ds(pl.multiple_of(c * STRIP, 128), STRIP)
        pre = pre_ref[:, lanes]
        act_ref[:, lanes] = gelu(pre).astype(bf)
        dpre = mm(low, w2[lanes, :], RIGHT_T) * gelu_slope(pre)
        grads.put_part(8, c * STRIP, STRIP, col_sum(dpre))
        dpre = dpre.astype(bf)
        dpre_ref[:, lanes] = dpre
        acc[...] += mm(dpre, w1[:, lanes], RIGHT_T)
        return carry

    lax.fori_loop(0, PFF // STRIP, strip, 0)
    store(4, mm(act_ref[...].T, low))
    store(3, mm(n_two.T, dpre_ref[...]))
    dmid, grads[6], grads[7] = norm_back(mid, vec[6], acc[...])
    dmid = dmid + dy
    grads[5] = col_sum(dmid)
    low = dmid.astype(bf)
    split_rows(go, mm(low, wo[...], RIGHT_T))
    store(2, mm(flat(att).T, low))
    attend_back(q, k, v, valid_ref, go, dq, dk, dv, PH)
    d_q, d_k, d_v = flat(dq), [dk[i] for i in range(images)], [dv[i] for i in range(images)]
    grads[3] = col_sum(d_q)
    grads[4] = sum(col_sum(part) for part in d_v)
    q_low = d_q.astype(bf)
    k_c = jnp.concatenate([part[:LC] for part in d_k], 0).astype(bf)
    k_t = jnp.concatenate([part[LC:] for part in d_k], 0).astype(bf)
    v_c = jnp.concatenate([part[:LC] for part in d_v], 0).astype(bf)
    v_t = jnp.concatenate([part[LC:] for part in d_v], 0).astype(bf)
    n_c_t, n_t_t = n_c.T, n_t.T
    store(
        1,
        jnp.concatenate(
            [mm(n_t_t, q_low), mm(n_c_t, k_c) + mm(n_t_t, k_t), mm(n_c_t, v_c) + mm(n_t_t, v_t)], 1
        ),
    )
    wq, wk, wv = wqkv[:, :PD], wqkv[:, PD : 2 * PD], wqkv[:, 2 * PD :]
    dn_t = mm(q_low, wq, RIGHT_T) + mm(k_t, wk, RIGHT_T) + mm(v_t, wv, RIGHT_T)
    dn_c = mm(k_c, wk, RIGHT_T) + mm(v_c, wv, RIGHT_T)
    dx_t, gain_t, shift_t = norm_back(x_t, vec[1], dn_t)
    dx_c, gain_c, shift_c = norm_back(x_c, vec[1], dn_c)
    grads[1] = gain_t + gain_c
    grads[2] = shift_t + shift_c
    dx_t = dx_t + dmid
    grads[13] = col_sum(dx_t)
    grads[0] = col_sum(dx_c)
    low = dx_c.astype(bf)
    dz_out[...] = mm(low, win[...], RIGHT_T).astype(bf)
    store(0, mm(z.T, low))
    leaving = flow.copies(0, NBP, sems_of(flow_sems, 0))
    for copy in leaving:
        copy.start()
    for copy in leaving:
        copy.wait()


class Store:
    def __init__(self, top, sems):
        self.top, self.sems, self.sent = top, sems, []

    def run(self, flow, slots, start, shape, left_t, right):
        edge = slots.shape[-1]
        columns, rows = shape[1] // edge, shape[0] // edge
        for first in range(0, rows * columns, 4):
            turn = len(self.sent)
            if turn >= 2:
                for copy in self.sent[turn - 2]:
                    copy.wait()
            flow.stage = slots.at[turn % 2]
            for b in range(4):
                row, column = divmod(first + b, columns)
                value = mm(
                    left_t[row * edge : row * edge + edge, :],
                    right[:, column * edge : column * edge + edge],
                )
                raise_top(self.top, value)
                flow.put(value, b)
            made = flow.copies(start + first, 4, sems_of(self.sems, turn))
            for copy in made:
                copy.start()
            self.sent.append(made)

    def finish(self):
        for made in self.sent[-2:]:
            for copy in made:
                copy.wait()


def feed_back_kernel(
    depth, loads, slots, table, dz_ref, mid_ref, pre_ref, hid_ref, vec_ref,
    out_0, out_1, out_2, out_3, dmid_out, vec_out, top_out,
    w1, w2, act_t, dpre_ref, x_t, low_ref, acc, stage, sems, out_sems,
):
    vec, grads = Vec(vec_ref, enc_lengths()), Vec(vec_out, enc_lengths())
    flow = Flow((out_0, out_1, out_2, out_3), None, depth, slots[2 * (NBE + NBP) + 1])
    groups = load_blocks(table, slots, sems, 0, enc_shapes(), (None, None, None, w1, w2))
    start_all(groups, loads)
    top_out[...] = jnp.zeros_like(top_out)
    hid = hid_ref[...]
    dy, grads[10], grads[11] = norm_back(hid, vec[10], dz_ref[...].astype(f32))
    grads[9] = col_sum(dy)
    low = dy.astype(bf)
    low_ref[...] = low
    wait_group(groups[4])
    wait_group(groups[3])
    acc[...] = jnp.zeros_like(acc)

    def strip(c, carry):
        lanes = pl.ds(pl.multiple_of(c * STRIP, 128), STRIP)
        pre = pre_ref[:, lanes]
        act_t[lanes, :] = gelu(pre).astype(bf).T
        dpre = mm(low, w2[lanes, :], RIGHT_T) * gelu_slope(pre)
        grads.put_part(8, c * STRIP, STRIP, col_sum(dpre))
        dpre = dpre.astype(bf)
        dpre_ref[:, lanes] = dpre
        acc[...] += mm(dpre, w1[:, lanes], RIGHT_T)
        return carry

    lax.fori_loop(0, FF // STRIP, strip, 0)
    mid = mid_ref[...]
    dmid, grads[6], grads[7] = norm_back(mid, vec[6], acc[...])
    dmid_out[...] = dmid + dy
    x_t[...] = (norm_parts(mid)[0] * vec[6] + vec[7]).astype(bf).T
    store = Store(top_out, out_sems)
    store.run(flow, stage, 16, (FF, D), act_t, low_ref)
    store.run(flow, stage, 0, (D, FF), x_t, dpre_ref)
    store.finish()


def attention_back_kernel(
    depth, loads, slots, table, dmid_ref, rows_ref, e_ref, q, k, v, att_ref, valid_ref, vec_ref,
    out_0, out_1, out_2, out_3, vec_out, top_out,
    wqkv, wo, go, dq, dk, dv, x_t, dqkv, stage, sems, out_sems,
):
    vec, grads = Vec(vec_ref, enc_lengths()), Vec(vec_out, enc_lengths())
    flow = Flow((out_0, out_1, out_2, out_3), None, depth, slots[2 * (NBE + NBP) + 1])
    groups = load_blocks(table, slots, sems, 0, enc_shapes(), (None, wqkv, wo, None, None))
    start_all(groups[::-1], loads)
    top_out[...] = jnp.zeros_like(top_out)
    store = Store(top_out, out_sems)
    dmid = dmid_ref[...]
    grads[5] = col_sum(dmid)
    low = dmid.astype(bf)
    wait_group(groups[2])
    wait_group(groups[1])
    split_rows(go, mm(low, wo[...], RIGHT_T))
    x_t[...] = flat(att_ref).T
    dqkv[:, :D] = low
    store.run(flow, stage, 16, (D, D), x_t, dqkv)
    attend_back(q, k, v, valid_ref, go, dq, dk, dv, H)
    d_q, d_v = flat(dq), flat(dv)
    grads[3] = col_sum(d_q)
    grads[4] = col_sum(d_v)
    dqkv[:, :D] = d_q.astype(bf)
    dqkv[:, D : 2 * D] = flat(dk).astype(bf)
    dqkv[:, 2 * D :] = d_v.astype(bf)
    e = e_ref[...]
    x_t[...] = norm(e, vec[1], vec[2]).astype(bf).T
    store.run(flow, stage, 4, (D, 3 * D), x_t, dqkv)
    back, grads[1], grads[2] = norm_back(e, vec[1], mm(dqkv[...], wqkv[...], RIGHT_T))
    de = dmid_ref[...] + back
    grads[0] = col_sum(de)
    dqkv[:, :D] = de.astype(bf)
    x_t[...] = rows_ref[...].T
    store.run(flow, stage, 0, (PIX, D), x_t, dqkv)
    store.finish()


def spaces(count):
    return [pl.BlockSpec(memory_space=pltpu.VMEM)] * count


ANYWHERE = pl.BlockSpec(memory_space=pl.ANY)


def weight_scratch(shapes):
    return [pltpu.VMEM(shape, bf) for shape in shapes]


def call_kernel(body, section, places, table, args, outs, any_outs, scratch, name, micros):
    pieces, n_in, n_out = len(table), len(args), len(outs)
    inside = [i for i in range(n_out) if i not in any_outs]
    held = [pltpu.VMEM(a.shape, a.dtype) for a in args]
    held += [pltpu.VMEM(outs[i][0], outs[i][1]) for i in inside]
    n_held = len(held)

    def guarded(places_ref, *refs):
        @pl.when(places_ref[2 * (NBE + NBP)] == section)
        def run():
            sources = refs[:pieces]
            given = refs[pieces : pieces + n_in]
            results = list(refs[pieces + n_in : pieces + n_in + n_out])
            local = refs[pieces + n_in + n_out :]
            mine, rest, sems = local[:n_held], local[n_held:-1], local[-1]
            loads = [
                pltpu.make_async_copy(given[i], mine[i], sems.at[i]) for i in range(n_in)
            ]
            for copy in loads:
                copy.start()
            stores = []
            for place, i in enumerate(inside):
                stores.append(
                    pltpu.make_async_copy(mine[n_in + place], results[i], sems.at[n_in + place])
                )
                results[i] = mine[n_in + place]
            body(loads, places_ref, sources, *mine[:n_in], *results, *rest)
            for copy in stores:
                copy.start()
            for copy in stores:
                copy.wait()

    return pl.pallas_call(
        guarded,
        grid_spec=pltpu.PrefetchScalarGridSpec(
            num_scalar_prefetch=1,
            grid=(),
            in_specs=[ANYWHERE] * (pieces + n_in),
            out_specs=[ANYWHERE] * n_out,
            scratch_shapes=held + scratch + [pltpu.SemaphoreType.DMA((n_held,))],
        ),
        out_shape=[jax.ShapeDtypeStruct(shape, kind) for shape, kind in outs],
        compiler_params=pltpu.CompilerParams(vmem_limit_bytes=58 << 20),
        cost_estimate=pl.CostEstimate(
            flops=0, transcendentals=0, bytes_accessed=int(micros * 3.0e6)
        ),
        name=name,
    )(places, *table, *args)


MARKS = 16


def flow_outs(count, edge, ranks):
    depth = edge // ranks
    if depth % 8:
        return [((count, edge, edge), f32)] + [((8, edge), f32)] * (GROUP - 1)
    return [((ranks // GROUP, depth * count + MARKS, edge), f32)] * GROUP


def stage_shape(count, edge, ranks):
    depth = edge // ranks
    return (count, edge, edge) if depth % 8 else (ranks // GROUP, GROUP, depth * count, edge)


def encoder_call(slots, table, rows, pos, valid, vec):
    n = rows.shape[0]
    images = n // LC
    per = (images, LC, D)
    outs = [((n, D), bf), ((n, D), f32), (per, bf), (per, bf), (per, bf), (per, bf)]
    outs += [((n, D), f32), ((n, FF), f32), ((n, D), f32)]
    scratch = weight_scratch(enc_shapes()) + [pltpu.VMEM((n, D), f32), pltpu.SemaphoreType.DMA((NBE,))]
    args = (rows, pos, valid, vec)
    return call_kernel(encoder_kernel, 0, slots, table, args, outs, (), scratch, "encoder_forward", 25)


def target_call(slots, table, rows, pos, some, pos_some, valid, vec, images):
    n = some.shape[0]
    keys = rows.shape[0] // images
    per, wide = (images, n // images, D), (images, keys, D)
    scratch = weight_scratch(enc_shapes()) + [
        pltpu.VMEM(per, bf),
        pltpu.VMEM(wide, bf),
        pltpu.VMEM(wide, bf),
        pltpu.VMEM(per, bf),
        pltpu.VMEM((n, D), f32),
        pltpu.SemaphoreType.DMA((NBE,)),
    ]
    args = (rows, pos, some, pos_some, valid, vec)
    outs = [((n, D), f32)]
    return call_kernel(target_kernel, 1, slots, table, args, outs, (), scratch, "target_forward", 25)[0]


def predictor_call(slots, table, z, pos_c, pos_t, valid, tgt, tmask, vec, ranks):
    n, m = z.shape[0], pos_t.shape[0]
    images = n // LC
    rows, keys = m // images, valid.shape[-1]
    edge = table[0].shape[-1]
    per, wide = (images, rows, PD), (images, keys, PD)
    outs = [((n, D), bf)] + flow_outs(NBP, edge, ranks)
    outs += [((1, VP), f32), ((1, D), f32), ((1, edge), f32)]
    scratch = weight_scratch(pred_shapes()) + [
        pltpu.VMEM(per, bf),
        pltpu.VMEM(wide, bf),
        pltpu.VMEM(wide, bf),
        pltpu.VMEM(per, bf),
        pltpu.VMEM(per, bf),
        pltpu.VMEM(per, f32),
        pltpu.VMEM(wide, f32),
        pltpu.VMEM(wide, f32),
        pltpu.VMEM((m, PFF), f32),
        pltpu.VMEM((m, PFF), bf),
        pltpu.VMEM((m, PFF), bf),
        pltpu.VMEM((m, PD), f32),
        pltpu.VMEM(stage_shape(NBP, edge, ranks), f32),
        pltpu.SemaphoreType.DMA((NBE + NBP,)),
        pltpu.SemaphoreType.DMA((1, GROUP)),
    ]
    args = (z, pos_c, pos_t, valid, tgt, tmask, vec)
    body = functools.partial(predictor_kernel, edge // ranks)
    return call_kernel(body, 1, slots, table, args, outs, (1, 2, 3, 4), scratch, "predictor_step", 50)


def feed_back_call(slots, table, dz, kept, vec, ranks):
    n = dz.shape[0]
    edge = table[0].shape[-1]
    mid, pre, hid = kept
    scratch = weight_scratch(enc_shapes()[3:]) + [
        pltpu.VMEM((FF, n), bf),
        pltpu.VMEM((n, FF), bf),
        pltpu.VMEM((D, n), bf),
        pltpu.VMEM((n, D), bf),
        pltpu.VMEM((n, D), f32),
        pltpu.VMEM((2,) + stage_shape(4, edge, ranks), f32),
        pltpu.SemaphoreType.DMA((NBE,)),
        pltpu.SemaphoreType.DMA((8, GROUP)),
    ]
    outs = flow_outs(32, edge, ranks)
    outs += [((n, D), f32), ((1, VE), f32), ((1, edge), f32)]
    args = (dz, mid, pre, hid, vec)
    body = functools.partial(feed_back_kernel, edge // ranks)
    return call_kernel(body, 0, slots, table, args, outs, (0, 1, 2, 3), scratch, "feed_backward", 25)


def attention_back_call(slots, table, dmid, rows, kept, valid, vec, ranks):
    n = rows.shape[0]
    images = n // LC
    edge = table[0].shape[-1]
    per = (images, LC, D)
    e, q, k, v, att = kept
    scratch = weight_scratch(enc_shapes()[1:3]) + [
        pltpu.VMEM(per, bf),
        pltpu.VMEM(per, f32),
        pltpu.VMEM(per, f32),
        pltpu.VMEM(per, f32),
        pltpu.VMEM((D, n), bf),
        pltpu.VMEM((n, 3 * D), bf),
        pltpu.VMEM((2,) + stage_shape(4, edge, ranks), f32),
        pltpu.SemaphoreType.DMA((NBE,)),
        pltpu.SemaphoreType.DMA((5, GROUP)),
    ]
    outs = flow_outs(20, edge, ranks) + [((1, VE), f32), ((1, edge), f32)]
    args = (dmid, rows, e, q, k, v, att, valid, vec)
    body = functools.partial(attention_back_kernel, edge // ranks)
    return call_kernel(body, 0, slots, table, args, outs, (0, 1, 2, 3), scratch, "attention_backward", 25)


def soap_first(flags, factor, *arrays):
    n, e = arrays[0].shape[:2]
    one = pl.BlockSpec((1, e, e), lambda i, *_: (i, 0, 0))
    two = pl.BlockSpec((1, 2, e, e), lambda i, *_: (i, 0, 0, 0))
    single = jax.ShapeDtypeStruct((n, e, e), f32)
    double = jax.ShapeDtypeStruct((n, 2, e, e), f32)
    return pl.pallas_call(
        first_kernel,
        grid_spec=pltpu.PrefetchScalarGridSpec(
            num_scalar_prefetch=2, grid=(n,), in_specs=[one] * 8, out_specs=[one] * 5 + [two] * 2
        ),
        out_shape=[single] * 5 + [double] * 2,
        compiler_params=pltpu.CompilerParams(vmem_limit_bytes=56 << 20),
        name="soap_first",
    )(flags, factor, *arrays)


def soap_factor(flags, base, gram):
    n, _, e, _ = base.shape
    whole = pl.BlockSpec(memory_space=pltpu.VMEM)
    return pl.pallas_call(
        factor_kernel,
        grid_spec=pltpu.PrefetchScalarGridSpec(
            num_scalar_prefetch=1,
            grid=(),
            in_specs=[whole] * 2,
            out_specs=whole,
            scratch_shapes=[
                pltpu.VMEM((n, 2, e, e), f32),
                pltpu.VMEM((n, 2, e, e), f32),
                pltpu.VMEM((n, 2, 128, 128), f32),
            ],
        ),
        out_shape=jax.ShapeDtypeStruct(base.shape, f32),
        compiler_params=pltpu.CompilerParams(vmem_limit_bytes=56 << 20),
        name="soap_factor",
    )(flags, base, gram)


def soap_last(flags, left, right, moment, fresh):
    n, e = left.shape[:2]
    one = pl.BlockSpec((1, e, e), lambda i, *_: (i, 0, 0))
    two = pl.BlockSpec((1, 2, e, e), lambda i, *_: (i, 0, 0, 0))
    return pl.pallas_call(
        last_kernel,
        grid_spec=pltpu.PrefetchScalarGridSpec(
            num_scalar_prefetch=1, grid=(n,), in_specs=[one] * 3 + [two], out_specs=[one] * 3
        ),
        out_shape=[jax.ShapeDtypeStruct((n, e, e), f32)] * 3,
        compiler_params=pltpu.CompilerParams(vmem_limit_bytes=56 << 20),
        name="soap_last",
    )(flags, left, right, moment, fresh)


def place_shares(slots, second, enc_share, pred_share, ranks, slot_count):
    depth, edge = enc_share.shape[1:]

    def body(slots_ref, second_ref, enc_ref, pred_ref, out_ref):
        def run(source, first, count):
            def copy(j, carry):
                slot = slots_ref[first + j]
                rows = pl.ds(pl.multiple_of(slot % slot_count * depth, depth), depth)
                out_ref[slot // slot_count, rows, :] = source[j]
                return carry

            lax.fori_loop(0, count, copy, 0)

        @pl.when(second_ref[0] == 0)
        def enc():
            run(enc_ref, 0, NBE)

        @pl.when(second_ref[0] != 0)
        def pred():
            run(pred_ref, NBE, NBP)

    return pl.pallas_call(
        body,
        grid_spec=pltpu.PrefetchScalarGridSpec(
            num_scalar_prefetch=2, grid=(), in_specs=spaces(2), out_specs=spaces(1)[0]
        ),
        out_shape=jax.ShapeDtypeStruct((ranks, slot_count * depth + MARKS, edge), f32),
        compiler_params=pltpu.CompilerParams(vmem_limit_bytes=40 << 20),
        name="place_shares",
    )(slots, second, enc_share, pred_share)


ROUNDS = (
    (((1, 0), (2, 1), (4, 2)), ()),
    (((5, 0), (6, 1), (8, 3)), (1, 2, 4)),
    (((3, 0), (7, 1)), (5, 6)),
    (((9, 0), (10, 1), (12, 2)), (3, 7, 8)),
    (((11, 0), (14, 1), (13, 2)), (9, 10, 12)),
)
LAST = 15


def thirds(slot_count):
    size = -(-slot_count // 3)
    return size, [(start, min(start + size, slot_count)) for start in range(0, slot_count, size)]


def gather_pieces(own, extra):
    both = Exchange((0, 1))
    if both.ranks != 16:
        return None, extra
    held = {0: own}
    for number, (moves, awaited) in enumerate(ROUNDS):
        names = sorted({piece ^ (1 << bit) for piece, bit in moves} | set(awaited))
        values = [held[name] for name in names]
        if number == 2:
            values, extra = lax.optimization_barrier((values, extra))
        elif awaited:
            values = lax.optimization_barrier(values)
        source = dict(zip(names, values))
        for piece, bit in moves:
            held[piece] = both.swap(source[piece ^ (1 << bit)], bit)
    names = [LAST ^ 1, LAST ^ 2, LAST ^ 4]
    source = lax.optimization_barrier([held[name] for name in names])
    ends = [
        both.swap(source[bit][low:high], bit) for bit, (low, high) in enumerate(thirds(own.shape[0])[1])
    ]
    return [held[piece] for piece in range(LAST)] + ends, extra


class Exchange:
    def __init__(self, sections):
        self.ranks = lax.axis_size("dp")
        self.bits = self.ranks.bit_length() - 1
        self.sections = sections

    def swap(self, value, bit):
        return self.trade(value, 1 << bit)

    def trade(self, value, flip):
        pairs = [
            (s * self.ranks + i, s * self.ranks + (i ^ flip))
            for s in self.sections
            for i in range(self.ranks)
        ]
        return lax.ppermute(value, ("section", "dp"), pairs)

    def total(self, value):
        for bit in range(self.bits):
            value = value + self.swap(value, bit)
        return value


def wire_exponent(bound):
    return jnp.floor(jnp.log2(WIRE_TOP / jnp.maximum(bound, 1e-30)))


def pack(values, exponent):
    row = lax.broadcasted_iota(jnp.int32, values.shape, values.ndim - 2)
    marked = jnp.where(row < values.shape[-2] - MARKS, values * jnp.exp2(exponent), exponent)
    return marked.astype(WIRE)


def flow_pieces(arrays, ranks):
    if arrays[1].ndim == 3:
        return list(arrays)
    blocks, edge = arrays[0].shape[:2]
    cut = arrays[0].reshape(blocks, ranks, edge // ranks, edge).transpose(1, 0, 2, 3)
    cut = jnp.pad(cut.reshape(ranks, -1, edge), ((0, 0), (0, MARKS), (0, 0)))
    return cut_pieces(cut, 0, GROUP)


def cut_pieces(shares, shift, size):
    mine = (lax.axis_index("dp") >> shift) & (size - 1)
    cut = shares.reshape((shares.shape[0] // size, size) + shares.shape[1:])
    return [lax.dynamic_index_in_dim(cut, mine ^ p, 1, keepdims=False) for p in range(size)]


def pack_pieces(pieces, bound):
    return [pack(piece, wire_exponent(bound)) for piece in pieces[1:]]


def send_packed(exchange, lows, shift):
    return [exchange.trade(low, (p + 1) << shift) for p, low in enumerate(lows)]


def send_pieces(exchange, pieces, shift, bound):
    return send_packed(exchange, pack_pieces(pieces, bound), shift)


def add_pieces(keep, arrived, bound):
    for got in arrived:
        unscale = jnp.exp2(-got[0, -1, 0].astype(f32))
        keep = keep + got.astype(f32) * unscale
        bound = bound + WIRE_TOP * unscale
    return keep, bound


def finish_sum(exchange, shares, bound):
    shift = GROUP_BITS
    while shares.shape[0] > 1:
        pieces = cut_pieces(shares, shift, min(GROUP, shares.shape[0]))
        arrived = send_pieces(exchange, pieces, shift, bound)
        shares, bound = add_pieces(pieces[0], arrived, bound)
        shift += GROUP_BITS
    return shares[0, :-MARKS], bound


def on_device(
    pixels,
    ctx_idx,
    ctx_len,
    tgt_idx,
    tgt_len,
    slot_of,
    weights,
    first_moment,
    second_moment,
    left_basis,
    right_basis,
    left_stats,
    right_stats,
    vectors,
    vector_first,
    vector_second,
):
    section_index = lax.axis_index("section")
    owner_index = lax.axis_index("dp")
    ranks = lax.axis_size("dp")
    is_first = section_index == 0
    second = section_index.astype(jnp.int32).reshape(1)
    slot_count = weights.shape[1]
    edge = weights.shape[-1]
    enc_slots = slot_of[:NBE]
    pred_slots = slot_of[NBE:]
    row_now = vectors[0]
    enc_vec_now = lax.dynamic_slice_in_dim(row_now, section_index * VP, VE)[None]
    pred_vec_now = row_now[None, :VP]
    pos_enc = sincos(D)
    pos_pred = sincos(PD)
    images = ctx_idx.shape[0]
    rows_all = -(-P_SIZE // 16) * 16
    tgt_flat = tgt_idx.reshape(images, NT * LT)
    ctx_valid = (jnp.arange(LC)[None, :] < ctx_len[:, None]).astype(f32)
    tgt_valid = (jnp.arange(LT)[None, None, :] < tgt_len[:, :, None]).astype(f32)
    tgt_valid = tgt_valid.reshape(images, NT * LT)
    joined_valid = jnp.concatenate([ctx_valid, tgt_valid], 1)[:, None, :]
    all_valid = (jnp.arange(rows_all) < P_SIZE).astype(f32)
    all_valid = jnp.broadcast_to(all_valid, (images, 1, rows_all))

    def pick(index):
        return (index[..., None] == jnp.arange(P_SIZE)).astype(f32)

    ctx_hot = pick(ctx_idx)
    tgt_hot = pick(tgt_flat)

    def choose(hot, values):
        return jnp.einsum(
            "njp,pd->njd", hot, values, precision=lax.Precision.HIGHEST, preferred_element_type=f32
        ).reshape(-1, values.shape[-1])

    def choose_pixels(hot):
        picked = jnp.einsum("njp,npd->njd", hot.astype(bf), pixels, preferred_element_type=f32)
        return picked.astype(bf).reshape(-1, PIX)

    pixel_rows = choose_pixels(ctx_hot)
    enc_pos_ctx = choose(ctx_hot, pos_enc)
    padding = ((0, 0), (0, rows_all - P_SIZE), (0, 0))
    pixel_all = jnp.pad(pixels, padding).reshape(-1, PIX)
    pos_all = jnp.broadcast_to(jnp.pad(pos_enc[None], padding), (images, rows_all, D)).reshape(-1, D)
    pixel_tgt = choose_pixels(tgt_hot)
    enc_pos_tgt = choose(tgt_hot, pos_enc)
    pred_pos_ctx = choose(ctx_hot, pos_pred)
    pred_pos_tgt = choose(tgt_hot, pos_pred)

    ctx_keys = ctx_valid[:, None, :]
    tgt_mask = tgt_valid.reshape(-1, 1)
    ready = (
        pixel_rows, enc_pos_ctx, ctx_keys, enc_vec_now, pixel_all, pos_all, pixel_tgt, enc_pos_tgt,
        all_valid, pred_pos_ctx, pred_pos_tgt, joined_valid, tgt_mask, pred_vec_now,
    )
    own = weights[0].astype(bf)
    place = [second, owner_index.astype(jnp.int32).reshape(1)]
    table, ready = gather_pieces(own, ready)
    if table is None:
        table = [lax.all_gather(own, "dp", axis=0, tiled=True)]
        places = jnp.concatenate([jnp.zeros_like(slot_of), slot_of] + place)
    else:
        sources = jnp.bitwise_xor(slot_of // slot_count, owner_index)
        indices = slot_of % slot_count
        size, _ = thirds(slot_count)
        is_last = sources == LAST
        sources = jnp.where(is_last, LAST + indices // size, sources)
        places = jnp.concatenate([sources, jnp.where(is_last, indices % size, indices)] + place)
    (
        pixel_rows, enc_pos_ctx, ctx_keys, enc_vec_now, pixel_all, pos_all, pixel_tgt, enc_pos_tgt,
        all_valid, pred_pos_ctx, pred_pos_tgt, joined_valid, tgt_mask, pred_vec_now,
    ) = ready

    z, *kept = encoder_call(places, table, pixel_rows, enc_pos_ctx, ctx_keys, enc_vec_now)
    context = from_behind(z, "section", 1)
    target = target_call(
        places, table, pixel_all, pos_all, pixel_tgt, enc_pos_tgt, all_valid, enc_vec_now, images
    )
    back_send, *pred_flows, pred_vec, loss_lanes, pred_top = predictor_call(
        places, table, context, pred_pos_ctx, pred_pos_tgt, joined_valid, target, tgt_mask, pred_vec_now, ranks
    )
    incoming = from_behind(back_send, "section", -1)
    loss_local = jnp.where(is_first, 0.0, jnp.sum(loss_lanes))

    behind = Exchange((1,))

    def sum_predictor(flows, top):
        bound = jnp.max(top)
        pieces = flow_pieces(flows, ranks)
        shares, bound = add_pieces(pieces[0], send_pieces(behind, pieces, 0, bound), bound)
        return finish_sum(behind, shares, bound)

    def skip_predictor(flows, top):
        return jnp.zeros((edge // ranks * NBP, edge), f32), jnp.zeros((), f32)

    incoming, pred_top = lax.optimization_barrier((incoming, pred_top))
    pred_sum, pred_bound = lax.cond(is_first, skip_predictor, sum_predictor, pred_flows, pred_top)
    incoming, pred_sum = lax.optimization_barrier((incoming, pred_sum))
    *feed_flow, grad_mid, feed_vec, feed_top = feed_back_call(
        places, table, incoming, kept[5:], enc_vec_now, ranks
    )
    ahead = Exchange((0,))
    feed_bound = jnp.max(feed_top)
    feed_pieces = flow_pieces(feed_flow, ranks)
    lows, grad_mid = lax.optimization_barrier((pack_pieces(feed_pieces, feed_bound), grad_mid))
    feed_arrived = send_packed(ahead, lows, 0)
    *rest_flow, rest_vec, rest_top = attention_back_call(
        places, table, grad_mid, pixel_rows, kept[:5], ctx_keys, enc_vec_now, ranks
    )
    rest_bound = jnp.max(rest_top)
    rest_pieces = flow_pieces(rest_flow, ranks)
    lows = pack_pieces(rest_pieces, rest_bound)
    feed_arrived, lows = lax.optimization_barrier((feed_arrived, lows))
    rest_arrived = send_packed(ahead, lows, 0)
    feed_shares, feed_bound = add_pieces(feed_pieces[0], feed_arrived, feed_bound)
    rest_shares, rest_bound = add_pieces(rest_pieces[0], rest_arrived, rest_bound)
    feed_sum, feed_bound = finish_sum(ahead, feed_shares, feed_bound)
    rest_sum, rest_bound = finish_sum(ahead, rest_shares, rest_bound)
    enc_sum = jnp.concatenate([rest_sum, feed_sum], 0)
    enc_bound = jnp.maximum(rest_bound, feed_bound)
    cut_at = 6 * D
    enc_vec = jnp.concatenate([rest_vec[:, :cut_at], feed_vec[:, cut_at:]], 1)
    depth = edge // ranks
    enc_share = enc_sum.reshape(NBE, depth, edge)
    pred_share = pred_sum.reshape(NBP, depth, edge)

    both = Exchange((0, 1))
    vec_local = jnp.where(is_first, enc_vec[0], jnp.pad(pred_vec[0], (0, VE - VP)))
    count_local = jnp.where(is_first, 0, jnp.sum(tgt_len)).astype(f32)
    scalars = jnp.pad(jnp.stack([loss_local, count_local]), (0, 126))
    summed = both.total(jnp.concatenate([vec_local, scalars]))
    vec_total = jnp.pad(summed[:VE], (0, VW - VE))
    share_squares = jnp.where(
        is_first, jnp.sum(enc_share * enc_share), jnp.sum(pred_share * pred_share)
    )
    squares = both.total(jnp.full((128,), share_squares))
    facts = jnp.stack([squares[0] + jnp.sum(summed[:VE] ** 2), summed[VE], summed[VE + 1]])
    facts = jnp.pad(facts, (0, 125))
    swap_sections = [(i, 1 - i) for i in range(2)]
    facts = facts + lax.ppermute(facts, "section", swap_sections)
    square_total, loss_total, count_total = facts[0], facts[1], facts[2]

    placed = place_shares(slot_of, second, enc_share, pred_share, ranks, slot_count)
    exponent = wire_exponent(jnp.where(is_first, enc_bound, pred_bound))
    payload = pack(placed, exponent)
    owned = lax.all_to_all(payload, "dp", split_axis=0, concat_axis=0, tiled=True).astype(f32)
    unscale = jnp.exp2(-owned[:, -1:, :1])
    owned = (owned[:, : slot_count * depth] * unscale).reshape(ranks, slot_count, depth, edge)
    owned_sum = owned.transpose(1, 0, 2, 3).reshape(slot_count, edge, edge)

    own_ids = owner_index * slot_count + jnp.arange(slot_count)
    enc_here = jnp.any(own_ids[:, None] == enc_slots[None, :], 1)
    pred_here = jnp.any(own_ids[:, None] == pred_slots[None, :], 1)
    trained = jnp.where(is_first, enc_here, pred_here)
    ema_here = jnp.logical_and(jnp.logical_not(is_first), enc_here)
    positions = jnp.arange(VW)
    vec_trained = positions < jnp.where(is_first, VE, VP)
    vec_ema = jnp.logical_and(jnp.logical_not(is_first), positions >= VP)
    grad_norm = jnp.sqrt(square_total) / count_total
    factor = jnp.minimum(1.0, CLIP_LIMIT / (grad_norm + 1e-06)) / count_total

    flags = trained.astype(jnp.int32)
    new_weight, moment, new_second, new_estat, new_fstat, base, gram = soap_first(
        flags,
        factor.reshape(1),
        owned_sum,
        weights[0],
        first_moment[0],
        second_moment[0],
        left_basis[0],
        right_basis[0],
        left_stats[0],
        right_stats[0],
    )
    fresh_bases = soap_factor(flags, base, gram)
    new_left, new_right, new_first = soap_last(
        flags, left_basis[0], right_basis[0], moment, fresh_bases
    )

    correct_one = 1.0 - BETA_FIRST**STEP
    correct_two = 1.0 - BETA_SECOND**STEP
    vec_clipped = vec_total * factor
    fresh_first = BETA_FIRST * vector_first[0] + (1.0 - BETA_FIRST) * vec_clipped
    fresh_second = BETA_SECOND * vector_second[0] + (1.0 - BETA_SECOND) * vec_clipped * vec_clipped
    stepped = row_now - RATE_VECTOR * (fresh_first / correct_one) / (
        jnp.sqrt(fresh_second / correct_two) + ADAM_EPS
    )
    new_vec = jnp.where(vec_trained, stepped, row_now)
    new_vec_first = jnp.where(vec_trained, fresh_first, vector_first[0])
    new_vec_second = jnp.where(vec_trained, fresh_second, vector_second[0])
    from_encoder = from_behind(new_weight.astype(bf), "section", 1).astype(f32)
    vec_from_encoder = from_behind(new_vec.astype(bf), "section", 1).astype(f32)
    new_weight = jnp.where(
        ema_here[:, None, None], EMA_KEEP * weights[0] + (1.0 - EMA_KEEP) * from_encoder, new_weight
    )
    aligned = jnp.concatenate([jnp.zeros((VP,), f32), vec_from_encoder[:VE]])
    new_vec = jnp.where(vec_ema, EMA_KEEP * row_now + (1.0 - EMA_KEEP) * aligned, new_vec)
    return (
        loss_total,
        count_total,
        grad_norm,
        new_weight[None],
        new_first[None],
        new_second[None],
        new_left[None],
        new_right[None],
        new_estat[None],
        new_fstat[None],
        new_vec[None],
        new_vec_first[None],
        new_vec_second[None],
    )


def solution(mesh):
    in_specs = (
        P("dp", None, None),
        P("dp", None),
        P("dp"),
        P("dp", None, None),
        P("dp", None),
        P(),
        P("section", "dp", None, None),
        P("section", "dp", None, None),
        P("section", "dp", None, None),
        P("section", "dp", None, None),
        P("section", "dp", None, None),
        P("section", "dp", None, None),
        P("section", "dp", None, None),
        P("section", None),
        P("section", None),
        P("section", None),
    )
    out_specs = (
        P(),
        P(),
        P(),
        P("section", "dp", None, None),
        P("section", "dp", None, None),
        P("section", "dp", None, None),
        P("section", "dp", None, None),
        P("section", "dp", None, None),
        P("section", "dp", None, None),
        P("section", "dp", None, None),
        P("section", None),
        P("section", None),
        P("section", None),
    )
    return jax.shard_map(
        on_device, mesh=mesh, in_specs=in_specs, out_specs=out_specs, check_vma=False
    )
```
